32 devices in a mesh: seq: 4 (over x, core), fsdp: 8 (over z, y).
Axes of the slice: x: 2, y: 2, z: 4, core: 2. Of those that a mesh axis runs over, the one named last changes fastest.
Arguments:
- hidden_states: bfloat16 [16, 1024, 1536], P('fsdp', 'seq'), may hold values from -15 to 15
- text_states: bfloat16 [16, 64, 1536], P('fsdp'), may hold values from -6 to 6
- self_gain: bfloat16 [1536], P('fsdp'), may hold values from 0.5 to 1.5
- self_bias: bfloat16 [1536], P('fsdp'), may hold values from -3 to 3
- query_key_value: bfloat16 [1536, 4608], P('fsdp'), may hold values from -0.15625 to 0.15625
- self_output: bfloat16 [1536, 1536], P('fsdp'), may hold values from -2.5 to 2.5
- cross_gain: bfloat16 [1536], P('fsdp'), may hold values from 0.5 to 1.5
- cross_bias: bfloat16 [1536], P('fsdp'), may hold values from -3 to 3
- cross_query: bfloat16 [1536, 1536], P('fsdp'), may hold values from -0.15625 to 0.15625
- cross_memory: bfloat16 [1536, 3072], P('fsdp'), may hold values from -0.15625 to 0.15625
- cross_output: bfloat16 [1536, 1536], P('fsdp'), may hold values from -0.875 to 0.875
- final_gain: bfloat16 [1536], P('fsdp'), may hold values from 0.5 to 1.5
- final_bias: bfloat16 [1536], P('fsdp'), may hold values from -3 to 3
- expand_weight: bfloat16 [1536, 6144], P('fsdp'), may hold values from -0.15625 to 0.15625
- contract_weight: bfloat16 [6144, 1536], P('fsdp'), may hold values from -0.109375 to 0.109375
- output_cotangent: bfloat16 [16, 1024, 1536], P('fsdp', 'seq'), may hold values from -6 to 6
Outputs:
- block_output: bfloat16 [16, 1024, 1536], P('fsdp', 'seq')
- hidden_gradient: float32 [16, 1024, 1536], P('fsdp', 'seq')
- self_gain_gradient: float32 [1536], P('fsdp')
- self_bias_gradient: float32 [1536], P('fsdp')
- qkv_gradient: float32 [1536, 4608], P('fsdp')
- self_output_gradient: float32 [1536, 1536], P('fsdp')
- cross_gain_gradient: float32 [1536], P('fsdp')
- cross_bias_gradient: float32 [1536], P('fsdp')
- cross_query_gradient: float32 [1536, 1536], P('fsdp')
- cross_memory_gradient: float32 [1536, 3072], P('fsdp')
- cross_output_gradient: float32 [1536, 1536], P('fsdp')
- final_gain_gradient: float32 [1536], P('fsdp')
- final_bias_gradient: float32 [1536], P('fsdp')
- expand_gradient: float32 [1536, 6144], P('fsdp')
- contract_gradient: float32 [6144, 1536], P('fsdp')
- layer_rms: float32 [4], replicated
The draws below stay inside these ranges and needn't reach their ends.
All inputs are finite; a program needn't handle non-finite values.
Results may differ from the reference program's by a relative error of at most 0.023.
Values may be sent and summed in bfloat16 or wider, within the bound.
A program may use at most 320 MiB of HBM per device.

```python
import jax
import jax.numpy as jnp
from jax import lax

D = 1536
H = 24
HD = 64
FF = 6144
TEXT = 64
LEN = 1024
CLIPS = 16
QB = 512


def draw_hidden_states(key, part):
    clip_place = jnp.arange(CLIPS, dtype=jnp.float32)[:, None, None] / (CLIPS - 1)
    frame_place = jnp.arange(LEN, dtype=jnp.float32)[None, :, None] / (LEN - 1)
    base = jnp.clip(jax.random.normal(key, (CLIPS, LEN, D), jnp.float32), -6.0, 6.0)
    factor = 0.5 * jnp.exp(jnp.log(5.0) * 0.5 * (clip_place + frame_place))
    return (base * factor).astype(jnp.bfloat16)


def shard_levels(rng, dims, pieces, least, largest):
    def one(dim, blocks):
        steps = jax.random.uniform(jax.random.fold_in(jax.random.fold_in(rng, 6), dim), (blocks,), jnp.float32, least / len(pieces), largest / len(pieces))
        return jnp.repeat(jnp.exp(steps), dims[dim] // blocks).reshape((-1,) + (1,) * (len(dims) - dim - 1))

    level = one(*pieces[0])
    for cut in pieces[1:]:
        level = level * one(*cut)
    return level


def gaussian(stream_key, shape, width, most, shards=(), held_as=jnp.bfloat16):
    values = width * jax.random.normal(stream_key, shape, jnp.float32)
    if shards:
        values = values * shard_levels(stream_key, shape, shards, -0.22, 0.18)
    return jnp.clip(values, -most, most).astype(held_as)


def setup_inputs(seed: int = 0) -> dict:
    key_list = jax.random.split(jax.random.key(seed), 17)
    return {
        "hidden_states": draw_hidden_states(jax.random.fold_in(key_list[16], 71), 0),
        "text_states": gaussian(key_list[1], (CLIPS, TEXT, D), 1.0, 6.0, ((0, 8),)),
        "self_gain": jnp.clip(1.0 + 0.1 * jax.random.normal(key_list[2], (D,), jnp.float32), 0.5, 1.5).astype(jnp.bfloat16),
        "self_bias": gaussian(key_list[3], (D,), 0.3, 3.0, ((0, 8),)),
        "query_key_value": gaussian(key_list[4], (D, 3 * D), D ** -0.5, 0.15625, ((0, 8),)),
        "self_output": gaussian(key_list[5], (D, D), (max(1, D // 256)) ** -0.5, 2.5, ((0, 8),)),
        "cross_gain": jnp.clip(1.0 + 0.1 * jax.random.normal(key_list[6], (D,), jnp.float32), 0.5, 1.5).astype(jnp.bfloat16),
        "cross_bias": gaussian(key_list[7], (D,), 0.3, 3.0, ((0, 8),)),
        "cross_query": gaussian(key_list[8], (D, D), D ** -0.5, 0.15625, ((0, 8),)),
        "cross_memory": gaussian(key_list[9], (D, 2 * D), D ** -0.5, 0.15625, ((0, 8),)),
        "cross_output": gaussian(key_list[10], (D, D), (max(1, D // 32)) ** -0.5, 0.875, ((0, 8),)),
        "final_gain": jnp.clip(1.0 + 0.1 * jax.random.normal(key_list[11], (D,), jnp.float32), 0.5, 1.5).astype(jnp.bfloat16),
        "final_bias": gaussian(key_list[12], (D,), 0.3, 3.0, ((0, 8),)),
        "expand_weight": gaussian(key_list[13], (D, FF), D ** -0.5, 0.15625, ((0, 8),)),
        "contract_weight": gaussian(key_list[14], (FF, D), (FF // 2) ** -0.5, 0.109375, ((0, 8),)),
        "output_cotangent": gaussian(key_list[15], (CLIPS, LEN, D), 1.0, 6.0, ((0, 8), (1, 4))),
    }


@jax.custom_vjp
def low(v):
    return lax.optimization_barrier(v.astype(jnp.bfloat16)).astype(jnp.float32)

@jax.custom_vjp
def low_back(v):
    return v

def low_keep(v):
    return (low(v), None)

def low_pass(kept, grad):
    return (grad,)

def back_keep(v):
    return (v, None)

def back_low(kept, grad):
    return (low(grad),)
low.defvjp(low_keep, low_pass)
low_back.defvjp(back_keep, back_low)

def matmul(left, right):
    return jnp.dot(left, right, precision=lax.Precision.HIGHEST, preferred_element_type=jnp.float32)

def layer_norm(values, gain, offset):
    center = values - lax.optimization_barrier(jnp.mean(values, axis=-1, keepdims=True))
    spread = lax.optimization_barrier(jnp.mean(center * center, axis=-1, keepdims=True))
    return center * lax.rsqrt(spread + 1e-05) * gain + offset

def self_attention(queries, keys, values):
    scale = HD ** (-0.5)
    blocks = queries.reshape(LEN // QB, QB, H, HD)
    starts = jnp.arange(LEN // QB, dtype=jnp.int32) * QB
    columns = jnp.arange(LEN, dtype=jnp.int32)

    def one_block(inputs):
        block, start = inputs
        scores = jnp.einsum('qhd,khd->hqk', block, keys, precision=lax.Precision.HIGHEST) * scale
        scores = low_back(scores)
        positions = start + jnp.arange(QB, dtype=jnp.int32)
        allowed = columns[None, :] <= positions[:, None]
        scores = jnp.where(allowed[None], scores, -1e+30)
        weights = jax.nn.softmax(scores, axis=-1)
        return jnp.einsum('hqk,khd->qhd', low(weights), values, precision=lax.Precision.HIGHEST)
    result = lax.map(jax.checkpoint(one_block), (blocks, starts))
    return result.reshape(LEN, H * HD)

def clip_layer(params, hidden, text):
    self_gain, self_bias, query_key_value, self_output, cross_gain, cross_bias, cross_query, cross_memory, cross_output, final_gain, final_bias, expand_weight, contract_weight = params
    scale = HD ** (-0.5)
    normed_one = low(layer_norm(hidden, self_gain, self_bias))
    projected = low_back(low(matmul(normed_one, query_key_value)))
    queries = projected[:, :D].reshape(LEN, H, HD)
    keys = projected[:, D:2 * D].reshape(LEN, H, HD)
    values = projected[:, 2 * D:].reshape(LEN, H, HD)
    context = low_back(low(self_attention(queries, keys, values)))
    attended = low_back(matmul(context, self_output))
    first = hidden + attended
    normed_two = low(layer_norm(first, cross_gain, cross_bias))
    cross_q = low_back(low(matmul(normed_two, cross_query))).reshape(LEN, H, HD)
    memory = low(matmul(text, cross_memory))
    cross_keys = memory[:, :D].reshape(TEXT, H, HD)
    cross_values = memory[:, D:].reshape(TEXT, H, HD)
    cross_scores = low_back(jnp.einsum('qhd,khd->hqk', cross_q, cross_keys, precision=lax.Precision.HIGHEST) * scale)
    cross_weights = jax.nn.softmax(cross_scores, axis=-1)
    cross_context = jnp.einsum('hqk,khd->qhd', low(cross_weights), cross_values, precision=lax.Precision.HIGHEST)
    cross_context = low_back(low(cross_context.reshape(LEN, D)))
    crossed = low_back(matmul(cross_context, cross_output))
    second = first + crossed
    normed_three = low(layer_norm(second, final_gain, final_bias))
    preact = low_back(matmul(normed_three, expand_weight))
    activated = low(jax.nn.gelu(preact, approximate=False))
    mixed = low_back(matmul(activated, contract_weight))
    output = second + mixed
    squares = jnp.stack([jnp.sum(output * output), jnp.sum(attended * attended), jnp.sum(crossed * crossed), jnp.sum(mixed * mixed)])
    return (output, squares)

def reference(hidden_states, text_states, self_gain, self_bias, query_key_value, self_output, cross_gain, cross_bias, cross_query, cross_memory, cross_output, final_gain, final_bias, expand_weight, contract_weight, output_cotangent):
    params = tuple((item.astype(jnp.float32) for item in (self_gain, self_bias, query_key_value, self_output, cross_gain, cross_bias, cross_query, cross_memory, cross_output, final_gain, final_bias, expand_weight, contract_weight)))
    hidden = hidden_states.astype(jnp.float32)
    text = text_states.astype(jnp.float32)
    upstream = output_cotangent.astype(jnp.float32)

    def forward(hidden_all, params_all):

        def step(totals, pair):
            output, squares = jax.checkpoint(clip_layer)(params_all, pair[0], pair[1])
            return (totals + squares, output)
        totals, outputs = lax.scan(step, jnp.zeros((4,), jnp.float32), (hidden_all, text))
        return (outputs, totals)
    outputs, backward, totals = jax.vjp(forward, hidden, params, has_aux=True)
    hidden_gradient, grads = backward(upstream)
    layer_rms = jnp.sqrt(totals / (CLIPS * LEN * D))
    return (outputs.astype(jnp.bfloat16), hidden_gradient, grads[0], grads[1], grads[2], grads[3], grads[4], grads[5], grads[6], grads[7], grads[8], grads[9], grads[10], grads[11], grads[12], layer_rms)
```

```python
import functools

import jax
import jax.numpy as jnp
from jax import lax
from jax.experimental import pallas as pl
from jax.experimental.pallas import tpu as pltpu
from jax.sharding import PartitionSpec as P

H = 24
HD = 64
TEXT = 64

NEGATIVE = -1e30
BF16 = jnp.bfloat16
F32 = jnp.float32
MESH = pl.DeviceIdType.MESH


def layer_norm(values, gain, offset):
    center = values - jnp.mean(values, axis=-1, keepdims=True)
    spread = jnp.mean(center * center, axis=-1, keepdims=True)
    return center * lax.rsqrt(spread + 1e-05) * gain + offset


def gelu_exact(values):
    return jax.nn.gelu(values, approximate=False)


def product(left, right):
    return jnp.dot(left, right, preferred_element_type=jnp.float32)


def product_left(left, right):
    return lax.dot_general(
        left, right, (((0,), (0,)), ((), ())), preferred_element_type=jnp.float32
    )


def product_right(left, right):
    return lax.dot_general(
        left, right, (((1,), (1,)), ((), ())), preferred_element_type=jnp.float32
    )


def causal_forward(queries, keys, values, rows_block, scale):
    clips, length, heads_local, head_width = queries.shape
    count = length // rows_block
    columns = jnp.arange(length, dtype=jnp.int32)

    def one_block(start):
        block = lax.dynamic_slice_in_dim(queries, start, rows_block, 1)
        scores = (
            jnp.einsum("cqhd,ckhd->chqk", block, keys, preferred_element_type=jnp.float32) * scale
        )
        positions = start + jnp.arange(rows_block, dtype=jnp.int32)
        allowed = columns[None, :] <= positions[:, None]
        scores = jnp.where(allowed, scores, NEGATIVE)
        highest = jnp.max(scores, axis=-1, keepdims=True)
        raised = jnp.exp(scores - highest)
        summed = jnp.sum(raised, axis=-1, keepdims=True)
        weights = (raised / summed).astype(jnp.bfloat16)
        result = jnp.einsum("chqk,ckhd->cqhd", weights, values, preferred_element_type=jnp.float32)
        return (result.astype(jnp.bfloat16), (highest + jnp.log(summed))[..., 0])

    starts = jnp.arange(count, dtype=jnp.int32) * rows_block
    results, logsum = lax.map(one_block, starts)
    results = jnp.moveaxis(results, 0, 1).reshape(clips, length, heads_local * head_width)
    return (results, logsum)


def causal_backward(queries, keys, values, logsum, grad_heads, rows_block, scale):
    clips, length, heads_local, head_width = queries.shape
    count = length // rows_block
    columns = jnp.arange(length, dtype=jnp.int32)
    starts = jnp.arange(count, dtype=jnp.int32) * rows_block

    def one_block(carry, inputs):
        grad_keys, grad_values = carry
        start, block_logsum = inputs
        block = lax.dynamic_slice_in_dim(queries, start, rows_block, 1)
        block_grad = lax.dynamic_slice_in_dim(grad_heads, start, rows_block, 1)
        scores = (
            jnp.einsum("cqhd,ckhd->chqk", block, keys, preferred_element_type=jnp.float32) * scale
        )
        positions = start + jnp.arange(rows_block, dtype=jnp.int32)
        allowed = columns[None, :] <= positions[:, None]
        scores = jnp.where(allowed, scores, NEGATIVE)
        weights = jnp.exp(scores - block_logsum[..., None])
        rounded = weights.astype(jnp.bfloat16)
        grad_weights = jnp.einsum(
            "cqhd,ckhd->chqk", block_grad, values, preferred_element_type=jnp.float32
        )
        inner = jnp.sum(weights * grad_weights, axis=-1, keepdims=True)
        grad_scores = (weights * (grad_weights - inner)).astype(jnp.bfloat16)
        grad_query = (
            jnp.einsum("chqk,ckhd->cqhd", grad_scores, keys, preferred_element_type=jnp.float32)
            * scale
        )
        grad_keys = (
            grad_keys
            + jnp.einsum("chqk,cqhd->ckhd", grad_scores, block, preferred_element_type=jnp.float32)
            * scale
        )
        grad_values = grad_values + jnp.einsum(
            "chqk,cqhd->ckhd", rounded, block_grad, preferred_element_type=jnp.float32
        )
        return ((grad_keys, grad_values), grad_query.astype(jnp.bfloat16))

    zeros = jnp.zeros(queries.shape, jnp.float32)
    (grad_keys, grad_values), grad_queries = lax.scan(one_block, (zeros, zeros), (starts, logsum))
    local_width = heads_local * head_width
    grad_queries = jnp.moveaxis(grad_queries, 0, 1).reshape(clips, length, local_width)
    grad_keys = grad_keys.astype(jnp.bfloat16).reshape(clips, length, local_width)
    grad_values = grad_values.astype(jnp.bfloat16).reshape(clips, length, local_width)
    return jnp.stack([grad_queries, grad_keys, grad_values], axis=2)


def on_any_mesh(
    hidden_states,
    text_states,
    self_gain,
    self_bias,
    query_key_value,
    self_output,
    cross_gain,
    cross_bias,
    cross_query,
    cross_memory,
    cross_output,
    final_gain,
    final_bias,
    expand_weight,
    contract_weight,
    output_cotangent,
):
    clips, frames, width = hidden_states.shape
    rows = clips * frames
    groups = lax.axis_size("seq")
    fsdp_count = lax.axis_size("fsdp")
    heads_local = H // groups
    length = frames * groups
    rows_block = min(512, length)
    scale = HD ** (-0.5)
    entries = rows * groups * fsdp_count * width
    self_set = (
        lax.all_gather(self_gain, "fsdp", axis=0, tiled=True),
        lax.all_gather(self_bias, "fsdp", axis=0, tiled=True),
        lax.all_gather(query_key_value, "fsdp", axis=0, tiled=True),
        lax.all_gather(self_output, "fsdp", axis=0, tiled=True),
    )
    hidden = hidden_states.reshape(rows, width).astype(jnp.float32)
    normed_one, norm_one_back = jax.vjp(
        layer_norm, hidden, self_set[0].astype(jnp.float32), self_set[1].astype(jnp.float32)
    )
    normed_one = normed_one.astype(jnp.bfloat16)
    projected = (
        product(normed_one, self_set[2]).astype(jnp.bfloat16).reshape(clips, frames, 3, width)
    )
    regrouped = lax.all_to_all(projected, "seq", split_axis=3, concat_axis=1, tiled=True)
    regrouped = regrouped.reshape(clips, length, 3, heads_local, HD)
    queries = regrouped[:, :, 0]
    keys = regrouped[:, :, 1]
    values = regrouped[:, :, 2]
    context_heads, logsum = causal_forward(queries, keys, values, rows_block, scale)
    context = lax.all_to_all(context_heads, "seq", split_axis=1, concat_axis=2, tiled=True).reshape(
        rows, width
    )
    attended = product(context, self_set[3])
    first = hidden + attended
    rest_set = (
        lax.all_gather(cross_gain, "fsdp", axis=0, tiled=True),
        lax.all_gather(cross_bias, "fsdp", axis=0, tiled=True),
        lax.all_gather(cross_query, "fsdp", axis=0, tiled=True),
        lax.all_gather(cross_memory, "fsdp", axis=0, tiled=True),
        lax.all_gather(cross_output, "fsdp", axis=0, tiled=True),
        lax.all_gather(final_gain, "fsdp", axis=0, tiled=True),
        lax.all_gather(final_bias, "fsdp", axis=0, tiled=True),
        lax.all_gather(expand_weight, "fsdp", axis=0, tiled=True),
        lax.all_gather(contract_weight, "fsdp", axis=0, tiled=True),
    )
    normed_two, norm_two_back = jax.vjp(
        layer_norm, first, rest_set[0].astype(jnp.float32), rest_set[1].astype(jnp.float32)
    )
    normed_two = normed_two.astype(jnp.bfloat16)
    cross_q = product(normed_two, rest_set[2]).astype(jnp.bfloat16).reshape(clips, frames, H, HD)
    text_rows = text_states.reshape(clips * TEXT, width)
    memory = product(text_rows, rest_set[3]).astype(jnp.bfloat16).reshape(clips, TEXT, 2, H, HD)
    cross_keys = memory[:, :, 0]
    cross_values = memory[:, :, 1]
    cross_scores = (
        jnp.einsum("cqhd,ckhd->chqk", cross_q, cross_keys, preferred_element_type=jnp.float32)
        * scale
    )
    highest = jnp.max(cross_scores, axis=-1, keepdims=True)
    raised = jnp.exp(cross_scores - highest)
    cross_weights = raised / jnp.sum(raised, axis=-1, keepdims=True)
    cross_rounded = cross_weights.astype(jnp.bfloat16)
    cross_context = jnp.einsum(
        "chqk,ckhd->cqhd", cross_rounded, cross_values, preferred_element_type=jnp.float32
    )
    cross_context = cross_context.astype(jnp.bfloat16).reshape(rows, width)
    crossed = product(cross_context, rest_set[4])
    second = first + crossed
    normed_three, norm_three_back = jax.vjp(
        layer_norm, second, rest_set[5].astype(jnp.float32), rest_set[6].astype(jnp.float32)
    )
    normed_three = normed_three.astype(jnp.bfloat16)
    preact = product(normed_three, rest_set[7])
    activated, gelu_back = jax.vjp(gelu_exact, preact)
    activated = activated.astype(jnp.bfloat16)
    mixed = product(activated, rest_set[8])
    output = second + mixed
    squares = jnp.stack(
        [
            jnp.sum(output * output),
            jnp.sum(attended * attended),
            jnp.sum(crossed * crossed),
            jnp.sum(mixed * mixed),
        ]
    )
    square_totals = lax.psum(squares, ("seq", "fsdp"))
    back_rest = (
        lax.all_gather(cross_gain, "fsdp", axis=0, tiled=True),
        lax.all_gather(cross_bias, "fsdp", axis=0, tiled=True),
        lax.all_gather(cross_query, "fsdp", axis=0, tiled=True),
        lax.all_gather(cross_memory, "fsdp", axis=0, tiled=True),
        lax.all_gather(cross_output, "fsdp", axis=0, tiled=True),
        lax.all_gather(final_gain, "fsdp", axis=0, tiled=True),
        lax.all_gather(final_bias, "fsdp", axis=0, tiled=True),
        lax.all_gather(expand_weight, "fsdp", axis=0, tiled=True),
        lax.all_gather(contract_weight, "fsdp", axis=0, tiled=True),
    )
    upstream = output_cotangent.reshape(rows, width).astype(jnp.float32)
    grad_mixed = upstream.astype(jnp.bfloat16)
    contract_term = product_left(activated, grad_mixed)
    grad_activated = product_right(grad_mixed, back_rest[8])
    grad_preact = gelu_back(grad_activated)[0].astype(jnp.bfloat16)
    expand_term = product_left(normed_three, grad_preact)
    grad_normed_three = product_right(grad_preact, back_rest[7])
    grad_second, final_gain_term, final_bias_term = norm_three_back(grad_normed_three)
    grad_second = upstream + grad_second
    grad_crossed = grad_second.astype(jnp.bfloat16)
    cross_output_term = product_left(cross_context, grad_crossed)
    grad_cross_context = (
        product_right(grad_crossed, back_rest[4]).astype(jnp.bfloat16).reshape(clips, frames, H, HD)
    )
    grad_cross_weights = jnp.einsum(
        "cqhd,ckhd->chqk", grad_cross_context, cross_values, preferred_element_type=jnp.float32
    )
    cross_inner = jnp.sum(cross_weights * grad_cross_weights, axis=-1, keepdims=True)
    grad_cross_scores = (cross_weights * (grad_cross_weights - cross_inner)).astype(jnp.bfloat16)
    grad_cross_q = (
        jnp.einsum(
            "chqk,ckhd->cqhd", grad_cross_scores, cross_keys, preferred_element_type=jnp.float32
        )
        * scale
    )
    grad_cross_q = grad_cross_q.astype(jnp.bfloat16).reshape(rows, width)
    grad_cross_keys = (
        jnp.einsum(
            "chqk,cqhd->ckhd", grad_cross_scores, cross_q, preferred_element_type=jnp.float32
        )
        * scale
    )
    grad_cross_values = jnp.einsum(
        "chqk,cqhd->ckhd", cross_rounded, grad_cross_context, preferred_element_type=jnp.float32
    )
    grad_memory = jnp.stack([grad_cross_keys, grad_cross_values], axis=2).reshape(
        clips * TEXT, 2 * width
    )
    memory_term = lax.dot_general(
        text_rows.astype(jnp.float32),
        grad_memory,
        (((0,), (0,)), ((), ())),
        precision=lax.Precision.HIGHEST,
        preferred_element_type=jnp.float32,
    )
    query_term = product_left(normed_two, grad_cross_q)
    grad_normed_two = product_right(grad_cross_q, back_rest[2])
    grad_first, cross_gain_term, cross_bias_term = norm_two_back(grad_normed_two)
    grad_first = grad_second + grad_first
    rest_sums = (
        lax.psum_scatter(
            cross_gain_term.astype(jnp.bfloat16), "fsdp", scatter_dimension=0, tiled=True
        ).astype(jnp.float32),
        lax.psum_scatter(
            cross_bias_term.astype(jnp.bfloat16), "fsdp", scatter_dimension=0, tiled=True
        ).astype(jnp.float32),
        lax.psum_scatter(
            query_term.astype(jnp.bfloat16), "fsdp", scatter_dimension=0, tiled=True
        ).astype(jnp.float32),
        lax.psum_scatter(
            memory_term.astype(jnp.bfloat16), "fsdp", scatter_dimension=0, tiled=True
        ).astype(jnp.float32),
        lax.psum_scatter(
            cross_output_term.astype(jnp.bfloat16), "fsdp", scatter_dimension=0, tiled=True
        ).astype(jnp.float32),
        lax.psum_scatter(
            final_gain_term.astype(jnp.bfloat16), "fsdp", scatter_dimension=0, tiled=True
        ).astype(jnp.float32),
        lax.psum_scatter(
            final_bias_term.astype(jnp.bfloat16), "fsdp", scatter_dimension=0, tiled=True
        ).astype(jnp.float32),
        lax.psum_scatter(
            expand_term.astype(jnp.bfloat16), "fsdp", scatter_dimension=0, tiled=True
        ).astype(jnp.float32),
        lax.psum_scatter(
            contract_term.astype(jnp.bfloat16), "fsdp", scatter_dimension=0, tiled=True
        ).astype(jnp.float32),
    )
    back_self = (
        lax.all_gather(self_gain, "fsdp", axis=0, tiled=True),
        lax.all_gather(self_bias, "fsdp", axis=0, tiled=True),
        lax.all_gather(query_key_value, "fsdp", axis=0, tiled=True),
        lax.all_gather(self_output, "fsdp", axis=0, tiled=True),
    )
    grad_attended = grad_first.astype(jnp.bfloat16)
    self_output_term = product_left(context, grad_attended)
    grad_context = (
        product_right(grad_attended, back_self[3])
        .astype(jnp.bfloat16)
        .reshape(clips, frames, width)
    )
    grad_heads = lax.all_to_all(grad_context, "seq", split_axis=2, concat_axis=1, tiled=True)
    grad_heads = grad_heads.reshape(clips, length, heads_local, HD)
    grad_regrouped = causal_backward(queries, keys, values, logsum, grad_heads, rows_block, scale)
    grad_projected = lax.all_to_all(
        grad_regrouped, "seq", split_axis=1, concat_axis=3, tiled=True
    ).reshape(rows, 3 * width)
    qkv_term = product_left(normed_one, grad_projected)
    grad_normed_one = product_right(grad_projected, back_self[2])
    grad_hidden, gain_one_term, bias_one_term = norm_one_back(grad_normed_one)
    grad_hidden = grad_first + grad_hidden
    self_sums = (
        lax.psum_scatter(
            gain_one_term.astype(jnp.bfloat16), "fsdp", scatter_dimension=0, tiled=True
        ).astype(jnp.float32),
        lax.psum_scatter(
            bias_one_term.astype(jnp.bfloat16), "fsdp", scatter_dimension=0, tiled=True
        ).astype(jnp.float32),
        lax.psum_scatter(
            qkv_term.astype(jnp.bfloat16), "fsdp", scatter_dimension=0, tiled=True
        ).astype(jnp.float32),
        lax.psum_scatter(
            self_output_term.astype(jnp.bfloat16), "fsdp", scatter_dimension=0, tiled=True
        ).astype(jnp.float32),
    )
    finals = (
        lax.psum(self_sums[0].astype(jnp.bfloat16), "seq").astype(jnp.float32),
        lax.psum(self_sums[1].astype(jnp.bfloat16), "seq").astype(jnp.float32),
        lax.psum(self_sums[2].astype(jnp.bfloat16), "seq").astype(jnp.float32),
        lax.psum(self_sums[3].astype(jnp.bfloat16), "seq").astype(jnp.float32),
        lax.psum(rest_sums[0].astype(jnp.bfloat16), "seq").astype(jnp.float32),
        lax.psum(rest_sums[1].astype(jnp.bfloat16), "seq").astype(jnp.float32),
        lax.psum(rest_sums[2].astype(jnp.bfloat16), "seq").astype(jnp.float32),
        lax.psum(rest_sums[3].astype(jnp.bfloat16), "seq").astype(jnp.float32),
        lax.psum(rest_sums[4].astype(jnp.bfloat16), "seq").astype(jnp.float32),
        lax.psum(rest_sums[5].astype(jnp.bfloat16), "seq").astype(jnp.float32),
        lax.psum(rest_sums[6].astype(jnp.bfloat16), "seq").astype(jnp.float32),
        lax.psum(rest_sums[7].astype(jnp.bfloat16), "seq").astype(jnp.float32),
        lax.psum(rest_sums[8].astype(jnp.bfloat16), "seq").astype(jnp.float32),
    )
    layer_rms = jnp.sqrt(square_totals / entries)
    return (
        output.astype(jnp.bfloat16).reshape(clips, frames, width),
        grad_hidden.reshape(clips, frames, width),
        finals[0],
        finals[1],
        finals[2],
        finals[3],
        finals[4],
        finals[5],
        finals[6],
        finals[7],
        finals[8],
        finals[9],
        finals[10],
        finals[11],
        finals[12],
        layer_rms,
    )


CORE_PAIRS = [(0, 1), (1, 0), (2, 3), (3, 2)]
X_PAIRS = [(0, 2), (2, 0), (1, 3), (3, 1)]
Y_PAIRS = [(i, i ^ 1) for i in range(8)]
Z_SHIFTS = [[(i, (i + 2 * k) % 8) for i in range(8)] for k in (1, 2, 3)]


def gather_kernel(plan, has_vectors, *refs):
    weights = len({entry[0] for entry in plan})
    inputs = refs[:weights]
    refs = refs[weights:]
    if has_vectors:
        vector_in, refs = refs[0], refs[1:]
    outputs = refs[:weights]
    refs = refs[weights:]
    if has_vectors:
        vector_out, refs = refs[0], refs[1:]
    zs_sem, zr_sem, ys_sem, yr_sem, xs_sem, xr_sem, cs_sem, cr_sem, own_sem, vs_sem, vr_sem = refs
    seq = lax.axis_index("seq")
    fsdp = lax.axis_index("fsdp")
    x, c = seq // 2, seq % 2
    z, y = fsdp // 2, fsdp % 2
    x_seq = 2 * (1 - x) + c
    c_seq = 2 * x + 1 - c
    y_fsdp = 2 * z + 1 - y

    def at_z(k):
        return 2 * ((z + k) % 4) + y

    barrier = pltpu.get_barrier_semaphore()
    partners = [(x_seq, fsdp), (c_seq, fsdp), (seq, y_fsdp)] + [(seq, at_z(k)) for k in (1, 2, 3)]
    if has_vectors:
        partners += [(seq, 2 * ((z + k) % 4) + 1 - y) for k in (1, 2, 3)]
    for partner in partners:
        pl.semaphore_signal(barrier, inc=1, device_id=partner, device_id_type=MESH)
    pl.semaphore_wait(barrier, len(partners))

    if has_vectors:
        vector_sends = []
        for k in range(1, 8):
            copy = pltpu.make_async_remote_copy(
                src_ref=vector_in,
                dst_ref=vector_out.at[fsdp],
                send_sem=vs_sem.at[k],
                recv_sem=vr_sem.at[k],
                device_id=(seq, (fsdp + k) % 8),
                device_id_type=MESH,
            )
            copy.start()
            vector_sends.append(copy)
        own = pltpu.make_async_copy(vector_in, vector_out.at[fsdp], vs_sem.at[0])
        own.start()

    def part(entry):
        weight, block, column, split = entry
        first = 2 * c + x if split else 2 * c
        count = 1 if split else 2
        return weight, block, pl.ds(column, 1536), pl.ds(first, count)

    def remote(region, send, recv, device):
        return pltpu.make_async_remote_copy(
            src_ref=region,
            dst_ref=region,
            send_sem=send,
            recv_sem=recv,
            device_id=device,
            device_id_type=MESH,
        )

    sends = []

    def send(copy):
        copy.start()
        sends.append(copy)

    def start_z(i):
        weight, block, columns, mine = part(plan[i])
        source = inputs[weight].at[block, mine, :, columns]
        target = outputs[weight].at[z, y, block, mine, :, columns]
        for k in (1, 2, 3):
            copy = pltpu.make_async_remote_copy(
                src_ref=source,
                dst_ref=target,
                send_sem=zs_sem.at[i, k],
                recv_sem=zr_sem.at[i, k],
                device_id=(seq, at_z(k)),
                device_id_type=MESH,
            )
            send(copy)
        pltpu.make_async_copy(source, target, own_sem.at[i]).start()

    def start_y(i):
        weight, block, columns, mine = part(plan[i])
        output = outputs[weight]
        for k in (1, 2, 3):
            region = output.at[(z + 4 - k) % 4, y, block, mine, :, columns]
            remote(region, zs_sem.at[i, k], zr_sem.at[i, k], (seq, at_z(k))).wait_recv()
        source = inputs[weight].at[block, mine, :, columns]
        target = output.at[z, y, block, mine, :, columns]
        pltpu.make_async_copy(source, target, own_sem.at[i]).wait()
        region = output.at[:, y, block, mine, :, columns]
        send(remote(region, ys_sem.at[i], yr_sem.at[i], (seq, y_fsdp)))

    def start_x(i):
        weight, block, columns, mine = part(plan[i])
        output = outputs[weight]
        region = output.at[:, 1 - y, block, mine, :, columns]
        remote(region, ys_sem.at[i], yr_sem.at[i], (seq, y_fsdp)).wait_recv()
        region = output.at[:, :, block, mine, :, columns]
        if plan[i][3]:
            send(remote(region, xs_sem.at[i], xr_sem.at[i], (x_seq, fsdp)))
        send(remote(region, cs_sem.at[i, 0], cr_sem.at[i, 0], (c_seq, fsdp)))

    def start_core(i):
        if plan[i][3]:
            weight, block, columns, _ = part(plan[i])
            region = outputs[weight].at[:, :, block, pl.ds(2 * c + 1 - x, 1), :, columns]
            remote(region, xs_sem.at[i], xr_sem.at[i], (x_seq, fsdp)).wait_recv()
            send(remote(region, cs_sem.at[i, 1], cr_sem.at[i, 1], (c_seq, fsdp)))

    def finish(i):
        weight, block, columns, _ = part(plan[i])
        other = 2 * (1 - c)
        output = outputs[weight]
        if plan[i][3]:
            for j, quarter in ((0, other + x), (1, other + 1 - x)):
                region = output.at[:, :, block, pl.ds(quarter, 1), :, columns]
                remote(region, cs_sem.at[i, j], cr_sem.at[i, j], (c_seq, fsdp)).wait_recv()
        else:
            region = output.at[:, :, block, pl.ds(other, 2), :, columns]
            remote(region, cs_sem.at[i, 0], cr_sem.at[i, 0], (c_seq, fsdp)).wait_recv()

    chunks = len(plan)
    ahead = 2
    for i in range(min(ahead, chunks)):
        start_z(i)
    for t in range(chunks + 2):
        if t + ahead < chunks:
            start_z(t + ahead)
        if t < chunks:
            start_y(t)
        if 0 <= t - 1 < chunks:
            start_x(t - 1)
        if 0 <= t - 2 < chunks:
            start_core(t - 2)
    for i in range(chunks):
        finish(i)
    for copy in sends:
        copy.wait_send()
    if has_vectors:
        own.wait()
        for k in range(1, 8):
            vector_sends[k - 1].wait_send()
            region = vector_out.at[(fsdp + 8 - k) % 8]
            remote(region, vs_sem.at[k], vr_sem.at[k], (seq, (fsdp + k) % 8)).wait_recv()


def gather_plan(shapes):
    plan = []
    for weight, (rows, columns) in enumerate(shapes):
        for block in range(rows // 192):
            for column in range(0, columns, 1536):
                plan.append((weight, block, column, len(plan) % 3 != 2))
    return tuple(plan)


def gather_weights(shards, vectors, collective_id):
    shapes = [shard.shape for shard in shards]
    plan = gather_plan(shapes)
    chunks = len(plan)
    inputs = [shard.reshape(rows // 192, 4, 48, columns) for shard, (rows, columns) in zip(shards, shapes)]
    out_shapes = [
        jax.ShapeDtypeStruct((4, 2, rows // 192, 4, 48, columns), BF16) for rows, columns in shapes
    ]
    if vectors is not None:
        inputs.append(vectors)
        out_shapes.append(jax.ShapeDtypeStruct((8,) + vectors.shape, vectors.dtype))
    anywhere = pl.BlockSpec(memory_space=pl.ANY)
    dma = pltpu.SemaphoreType.DMA
    results = pl.pallas_call(
        functools.partial(gather_kernel, plan, vectors is not None),
        out_shape=out_shapes,
        in_specs=[anywhere] * len(inputs),
        out_specs=[anywhere] * len(out_shapes),
        scratch_shapes=[
            dma((chunks, 4)),
            dma((chunks, 4)),
            dma((chunks,)),
            dma((chunks,)),
            dma((chunks,)),
            dma((chunks,)),
            dma((chunks, 2)),
            dma((chunks, 2)),
            dma((chunks,)),
            dma((8,)),
            dma((8,)),
        ],
        compiler_params=pltpu.CompilerParams(collective_id=collective_id, has_side_effects=True),
        name="gather_weights",
    )(*inputs)
    whole = [result.reshape(8 * rows, columns) for result, (rows, columns) in zip(results, shapes)]
    return whole, results[-1]


def pack_vectors(vectors):
    stacked = jnp.stack([vector.astype(F32) for vector in vectors])
    return jnp.pad(stacked, ((0, 8 - stacked.shape[0]), (0, (-stacked.shape[1]) % 128)))


def blocks_kernel(left, right, out):
    out[0] = jnp.dot(left[...], right[...], preferred_element_type=F32).astype(BF16)


def product_blocks(left, right, count):
    rows, depth = left.shape
    width = right.shape[1] // count
    return pl.pallas_call(
        blocks_kernel,
        grid=(count,),
        out_shape=jax.ShapeDtypeStruct((count, rows, width), BF16),
        in_specs=[
            pl.BlockSpec((rows, depth), lambda i: (0, 0)),
            pl.BlockSpec((depth, width), lambda i: (0, i)),
        ],
        out_specs=pl.BlockSpec((1, rows, width), lambda i: (i, 0, 0)),
        compiler_params=pltpu.CompilerParams(vmem_limit_bytes=48 << 20),
        cost_estimate=pl.CostEstimate(
            flops=2 * rows * depth * width * count,
            bytes_accessed=2 * (rows * depth + depth * width * count + rows * width * count),
            transcendentals=0,
        ),
        name="product_blocks",
    )(left, right)


QUERIES = 256


def both_heads(value):
    lane = lax.broadcasted_iota(jnp.int32, value.shape, 1)
    zero = jnp.zeros_like(value)
    return jnp.where(lane < HD, value, zero), jnp.where(lane < HD, zero, value)


def across(left, right):
    return lax.dot_general(left, right, (((1,), (1,)), ((), ())), preferred_element_type=F32)


def down(left, right):
    return lax.dot_general(left, right, (((0,), (0,)), ((), ())), preferred_element_type=F32)


def join_heads(pair):
    row = lax.broadcasted_iota(jnp.int32, pair[0].shape, 0)
    return jnp.where(row < HD, pair[0], pair[1])


def key_parts(block):
    return ([(0, block * QUERIES, False)] if block else []) + [
        (block * QUERIES, (block + 1) * QUERIES, True)
    ]


def masked_scores(keys, queries, diagonal):
    scores = across(keys, queries)
    if diagonal:
        key = lax.broadcasted_iota(jnp.int32, scores.shape, 0)
        query = lax.broadcasted_iota(jnp.int32, scores.shape, 1)
        scores = jnp.where(key <= query, scores, NEGATIVE)
    return scores


def attention_kernel(scale, q_ref, k_ref, v_ref, out_ref, logsum_ref):
    blocks = q_ref.shape[0] * q_ref.shape[2] // QUERIES
    k = k_ref[:, 0].reshape(-1, 2 * HD)
    v = v_ref[:, 0].reshape(-1, 2 * HD)
    for block in range(blocks):
        rows = slice(block * QUERIES, (block + 1) * QUERIES)
        queries = both_heads((q_ref[block, 0].astype(F32) * scale).astype(BF16))
        outs = []
        for head in range(2):
            parts = key_parts(block)
            scores = [masked_scores(k[a:b], queries[head], diagonal) for a, b, diagonal in parts]
            highest = functools.reduce(
                jnp.maximum, [jnp.max(part, axis=0, keepdims=True) for part in scores]
            )
            raised = [jnp.exp(part - highest) for part in scores]
            summed = sum(jnp.sum(part, axis=0, keepdims=True) for part in raised)
            total = sum(
                down(v[a:b], part.astype(BF16)) for (a, b, _), part in zip(parts, raised)
            )
            outs.append(total / summed)
            logsum_ref[0, 0, head : head + 1, rows] = highest + jnp.log(summed)
        out_ref[block, 0] = join_heads(outs).T.astype(BF16)


def attention(qkv, scale):
    blocks, clips, frames, width = qkv.shape
    pairs = width // (3 * 2 * HD)
    length = blocks * frames
    spec = lambda offset: pl.BlockSpec(
        (blocks, 1, frames, 2 * HD), lambda clip, pair: (0, clip, 0, offset + pair)
    )
    return pl.pallas_call(
        functools.partial(attention_kernel, scale),
        grid=(clips, pairs),
        out_shape=(
            jax.ShapeDtypeStruct((blocks, clips, frames, pairs * 2 * HD), BF16),
            jax.ShapeDtypeStruct((clips, pairs, 2, length), F32),
        ),
        in_specs=[spec(0), spec(pairs), spec(2 * pairs)],
        out_specs=(
            spec(0),
            pl.BlockSpec((1, 1, 2, length), lambda clip, pair: (clip, pair, 0, 0)),
        ),
        compiler_params=pltpu.CompilerParams(vmem_limit_bytes=48 << 20),
        cost_estimate=pl.CostEstimate(
            flops=clips * pairs * 2 * 4 * length * length * 2 * HD,
            bytes_accessed=4 * clips * pairs * length * 2 * HD * 2,
            transcendentals=clips * pairs * 2 * length * length,
        ),
        name="attention",
    )(qkv, qkv, qkv)


def attention_back_kernel(
    scale, q_ref, k_ref, v_ref, grad_ref, logsum_ref, out_ref, grad_keys, grad_values
):
    blocks = q_ref.shape[0] * q_ref.shape[2] // QUERIES
    frames = q_ref.shape[2]
    pair = pl.program_id(1)
    group = pl.num_programs(1) * 2 * HD
    k = k_ref[:, 0].reshape(-1, 2 * HD)
    v = v_ref[:, 0].reshape(-1, 2 * HD)

    def columns(kind):
        return pl.ds(pl.multiple_of(kind * group + pair * 2 * HD, 2 * HD), 2 * HD)

    for block in range(blocks):
        rows = slice(block * QUERIES, (block + 1) * QUERIES)
        queries = both_heads((q_ref[block, 0].astype(F32) * scale).astype(BF16))
        grads = both_heads(grad_ref[block, 0])
        parts = key_parts(block)
        query_grads = []
        held = [[], []]
        for head in range(2):
            logsum = logsum_ref[0, 0, head : head + 1, rows]
            weights, weighted = [], []
            for a, b, diagonal in parts:
                weight = jnp.exp(masked_scores(k[a:b], queries[head], diagonal) - logsum)
                weights.append(weight)
                weighted.append(weight * across(v[a:b], grads[head]))
            inner = sum(jnp.sum(part, axis=0, keepdims=True) for part in weighted)
            changes = [
                (term - weight * inner).astype(BF16) for term, weight in zip(weighted, weights)
            ]
            query_grads.append(sum(down(k[a:b], part) for (a, b, _), part in zip(parts, changes)))
            held[head] = [(weight.astype(BF16), change) for weight, change in zip(weights, changes)]
        out_ref[block, 0, :, columns(0)] = (join_heads(query_grads).T * scale).astype(BF16)
        for j, (a, b, diagonal) in enumerate(parts):
            value_term = sum(
                jnp.dot(held[head][j][0], grads[head], preferred_element_type=F32)
                for head in range(2)
            )
            key_term = sum(
                jnp.dot(held[head][j][1], queries[head], preferred_element_type=F32)
                for head in range(2)
            )
            if diagonal:
                grad_values[a:b] = value_term
                grad_keys[a:b] = key_term
            else:
                grad_values[a:b] += value_term
                grad_keys[a:b] += key_term
    out_ref[:, 0, :, columns(1)] = grad_keys[...].reshape(-1, frames, 2 * HD).astype(BF16)
    out_ref[:, 0, :, columns(2)] = grad_values[...].reshape(-1, frames, 2 * HD).astype(BF16)


def attention_back(qkv, grad, logsum, scale):
    blocks, clips, frames, width = qkv.shape
    pairs = width // (3 * 2 * HD)
    length = blocks * frames
    spec = lambda offset: pl.BlockSpec(
        (blocks, 1, frames, 2 * HD), lambda clip, pair: (0, clip, 0, offset + pair)
    )
    return pl.pallas_call(
        functools.partial(attention_back_kernel, scale),
        grid=(clips, pairs),
        out_shape=jax.ShapeDtypeStruct(qkv.shape, BF16),
        in_specs=[
            spec(0),
            spec(pairs),
            spec(2 * pairs),
            spec(0),
            pl.BlockSpec((1, 1, 2, length), lambda clip, pair: (clip, pair, 0, 0)),
        ],
        out_specs=pl.BlockSpec((blocks, 1, frames, width), lambda clip, pair: (0, clip, 0, 0)),
        scratch_shapes=[pltpu.VMEM((length, 2 * HD), F32), pltpu.VMEM((length, 2 * HD), F32)],
        compiler_params=pltpu.CompilerParams(vmem_limit_bytes=48 << 20),
        cost_estimate=pl.CostEstimate(
            flops=clips * pairs * 2 * 10 * length * length * 2 * HD,
            bytes_accessed=7 * clips * pairs * length * 2 * HD * 2,
            transcendentals=clips * pairs * 2 * length * length,
        ),
        name="attention_back",
    )(qkv, qkv, qkv, grad, logsum)


def spread(left, right, x_first):
    seq = lax.axis_index("seq")
    fsdp = lax.axis_index("fsdp")
    x, c = seq // 2, seq % 2
    z, y = fsdp // 2, fsdp % 2
    height, width = left.shape[1], right.shape[1]
    half, quarter = width // 2, width // 4
    rows = height // 8

    def add(a, b):
        return (a.astype(F32) + b.astype(F32)).astype(BF16)

    def columns(value, index, size):
        return lax.dynamic_slice_in_dim(value, index * size, size, value.ndim - 1)

    def of_y(value, index):
        return lax.dynamic_index_in_dim(value, index, 1, keepdims=False)

    def by_x(here, there):
        sent = add(columns(here, 1 - x, quarter), columns(there, 1 - x, quarter))
        kept = add(columns(here, x, quarter), columns(there, x, quarter))
        return lax.ppermute(sent, "seq", X_PAIRS), kept

    def by_y(here, there):
        sent = add(of_y(here, 1 - y), of_y(there, 1 - y))
        kept = add(of_y(here, y), of_y(there, y))
        return lax.ppermute(sent, "fsdp", Y_PAIRS), kept

    sent = product_left(left, columns(right, 1 - c, half)).astype(BF16)
    there = lax.ppermute(sent, "seq", CORE_PAIRS).reshape(4, 2, rows, half)
    here = product_left(left, columns(right, c, half)).astype(BF16).reshape(4, 2, rows, half)
    there, here = yield there, here
    for step in (by_x, by_y) if x_first else (by_y, by_x):
        there, here = yield step(here, there)

    def of_z(index):
        return lax.dynamic_index_in_dim(here, index, 0, keepdims=False).astype(
            F32
        ) + lax.dynamic_index_in_dim(there, index, 0, keepdims=False).astype(F32)

    parts = [
        lax.ppermute(of_z((z + k) % 4).astype(BF16), "fsdp", Z_SHIFTS[k - 1]) for k in (1, 2, 3)
    ]
    *parts, total = yield *parts, of_z(z)
    for piece in parts:
        total = total + piece.astype(F32)
    total = total.astype(BF16)
    total, other = yield total, lax.ppermute(total, "seq", X_PAIRS)
    pair = jnp.where(
        x == 0, jnp.concatenate([total, other], 1), jnp.concatenate([other, total], 1)
    )
    pair, other = yield pair, lax.ppermute(pair, "seq", CORE_PAIRS)
    result = jnp.where(
        c == 0, jnp.concatenate([pair, other], 1), jnp.concatenate([other, pair], 1)
    ).astype(F32)
    yield (result,)


class Sums:
    def __init__(self):
        self.steps = {}
        self.waiting = {}

    def add(self, name, left, right, x_first):
        self.steps[name] = spread(left, right, x_first)
        self.waiting[name] = next(self.steps[name])

    def advance(self, names, *anchors):
        names = [name for name in names if len(self.waiting[name]) > 1]
        values = [self.waiting[name] for name in names]
        anchors, values = lax.optimization_barrier((anchors, values))
        for name, value in zip(names, values):
            self.waiting[name] = self.steps[name].send(tuple(value))
        return anchors if len(anchors) > 1 else anchors[0]

    def finish(self):
        for name in self.steps:
            while len(self.waiting[name]) > 1:
                self.waiting[name] = self.steps[name].send(self.waiting[name])
        return {name: value[0] for name, value in self.waiting.items()}


def on_blocks(
    hidden_states,
    text_states,
    self_gain,
    self_bias,
    query_key_value,
    self_output,
    cross_gain,
    cross_bias,
    cross_query,
    cross_memory,
    cross_output,
    final_gain,
    final_bias,
    expand_weight,
    contract_weight,
    output_cotangent,
):
    clips, frames, width = hidden_states.shape
    rows = clips * frames
    groups = lax.axis_size("seq")
    fsdp_count = lax.axis_size("fsdp")
    scale = HD ** (-0.5)
    entries = rows * groups * fsdp_count * width
    group_width = width // groups

    def by_group(value):
        return value.reshape(-1, 3, groups, group_width).transpose(0, 2, 1, 3).reshape(value.shape)

    def by_kind(value):
        return value.reshape(-1, groups, 3, group_width).transpose(0, 2, 1, 3).reshape(value.shape)

    gains = (self_gain, self_bias, cross_gain, cross_bias, final_gain, final_bias)
    early = (by_group(query_key_value), self_output)
    (qkv_whole, self_output_whole), vectors = gather_weights(early, pack_vectors(gains), 1)
    qkv_whole, expand_weight = lax.optimization_barrier((qkv_whole, expand_weight))
    part = expand_weight.shape[0] // groups
    expand_whole = lax.all_gather(
        lax.dynamic_slice_in_dim(expand_weight, lax.axis_index("seq") * part, part, 0),
        ("fsdp", "seq"),
        axis=0,
        tiled=True,
    )
    vectors = vectors[:, :6, : width // fsdp_count]
    gains = [vectors[:, i].reshape(width) for i in range(6)]

    hidden = hidden_states.reshape(rows, width).astype(F32)
    normed_one, norm_one_back = jax.vjp(layer_norm, hidden, gains[0], gains[1])
    normed_one = normed_one.astype(BF16)
    projected = product_blocks(normed_one, qkv_whole, groups)
    regrouped = lax.all_to_all(projected, "seq", split_axis=0, concat_axis=0, tiled=True)
    regrouped = regrouped.reshape(groups, clips, frames, 3 * group_width)
    context_heads, logsum = attention(regrouped, scale)
    context_heads = context_heads.reshape(groups, rows, group_width)
    context = lax.all_to_all(context_heads, "seq", split_axis=0, concat_axis=0, tiled=True)
    late = (cross_query, cross_memory, cross_output, contract_weight)
    context, late = lax.optimization_barrier((context, late))
    late, _ = gather_weights(late, None, 2)
    cross_query_whole, cross_memory_whole, cross_output_whole, contract_whole = late
    context = context.transpose(1, 0, 2).reshape(rows, width)
    attended = product(context, self_output_whole)
    first = hidden + attended
    normed_two, norm_two_back = jax.vjp(layer_norm, first, gains[2], gains[3])
    normed_two = normed_two.astype(BF16)
    cross_q = product(normed_two, cross_query_whole).astype(BF16).reshape(clips, frames, H, HD)
    text_rows = text_states.reshape(clips * TEXT, width)
    memory = product(text_rows, cross_memory_whole).astype(BF16).reshape(clips, TEXT, 2, H, HD)
    cross_keys = memory[:, :, 0]
    cross_values = memory[:, :, 1]
    cross_scores = (
        jnp.einsum("cqhd,ckhd->chqk", cross_q, cross_keys, preferred_element_type=F32) * scale
    )
    highest = jnp.max(cross_scores, axis=-1, keepdims=True)
    raised = jnp.exp(cross_scores - highest)
    cross_weights = raised / jnp.sum(raised, axis=-1, keepdims=True)
    cross_rounded = cross_weights.astype(BF16)
    cross_context = jnp.einsum(
        "chqk,ckhd->cqhd", cross_rounded, cross_values, preferred_element_type=F32
    )
    cross_context = cross_context.astype(BF16).reshape(rows, width)
    crossed = product(cross_context, cross_output_whole)
    second = first + crossed
    normed_three, norm_three_back = jax.vjp(layer_norm, second, gains[4], gains[5])
    normed_three = normed_three.astype(BF16)
    preact = product(normed_three, expand_whole)
    activated, gelu_back = jax.vjp(gelu_exact, preact)
    activated = activated.astype(BF16)
    upstream = output_cotangent.reshape(rows, width).astype(F32)
    grad_mixed = output_cotangent.reshape(rows, width)
    sums = Sums()
    sums.add("contract", activated, grad_mixed, False)
    grad_activated = product_right(grad_mixed, contract_whole)
    grad_preact = gelu_back(grad_activated)[0].astype(BF16)
    sums.add("expand", normed_three, grad_preact, True)
    grad_preact, activated = sums.advance(["contract"], grad_preact, activated)
    mixed = product(activated, contract_whole)
    output = second + mixed
    squares = jnp.stack(
        [
            jnp.sum(output * output),
            jnp.sum(attended * attended),
            jnp.sum(crossed * crossed),
            jnp.sum(mixed * mixed),
        ]
    )
    output = output.astype(BF16)
    grad_preact, output, squares = sums.advance(["expand"], grad_preact, output, squares)
    grad_normed_three = product_right(grad_preact, expand_whole)
    grad_second, final_gain_term, final_bias_term = norm_three_back(grad_normed_three)
    grad_second = upstream + grad_second
    grad_crossed = grad_second.astype(BF16)
    sums.add("cross_output", cross_context, grad_crossed, False)
    grad_cross_context = (
        product_right(grad_crossed, cross_output_whole).astype(BF16).reshape(clips, frames, H, HD)
    )
    grad_cross_weights = jnp.einsum(
        "cqhd,ckhd->chqk", grad_cross_context, cross_values, preferred_element_type=F32
    )
    cross_inner = jnp.sum(cross_weights * grad_cross_weights, axis=-1, keepdims=True)
    grad_cross_scores = (cross_weights * (grad_cross_weights - cross_inner)).astype(BF16)
    grad_cross_q = (
        jnp.einsum("chqk,ckhd->cqhd", grad_cross_scores, cross_keys, preferred_element_type=F32)
        * scale
    )
    grad_cross_q = grad_cross_q.astype(BF16).reshape(rows, width)
    grad_cross_keys = (
        jnp.einsum("chqk,cqhd->ckhd", grad_cross_scores, cross_q, preferred_element_type=F32)
        * scale
    )
    grad_cross_values = jnp.einsum(
        "chqk,cqhd->ckhd", cross_rounded, grad_cross_context, preferred_element_type=F32
    )
    grad_memory = jnp.stack([grad_cross_keys, grad_cross_values], axis=2).reshape(
        clips * TEXT, 2 * width
    )
    sums.add("cross_query", normed_two, grad_cross_q, True)
    sums.add("cross_memory", text_rows, grad_memory.astype(BF16), False)
    grad_normed_two = product_right(grad_cross_q, cross_query_whole)
    grad_first, cross_gain_term, cross_bias_term = norm_two_back(grad_normed_two)
    grad_first = grad_second + grad_first
    grad_attended = grad_first.astype(BF16)
    sums.add("self_output", context, grad_attended, False)
    cross_sums = ["cross_output", "cross_query", "cross_memory", "self_output"]
    grad_context = product_right(grad_attended, self_output_whole).astype(BF16)
    grad_context = sums.advance(["contract", "expand"] + cross_sums, grad_context)
    grad_context = grad_context.reshape(rows, groups, group_width).transpose(1, 0, 2)
    grad_heads = lax.all_to_all(grad_context, "seq", split_axis=0, concat_axis=0, tiled=True)
    grad_heads = grad_heads.reshape(groups, clips, frames, group_width)
    grad_regrouped = attention_back(regrouped, grad_heads, logsum, scale)
    grad_regrouped = sums.advance(["contract", "expand"] + cross_sums, grad_regrouped)
    grad_regrouped = grad_regrouped.reshape(groups, rows, 3 * group_width)
    grad_projected = lax.all_to_all(grad_regrouped, "seq", split_axis=0, concat_axis=0, tiled=True)
    grad_projected = sums.advance(["contract", "expand"] + cross_sums, grad_projected)
    grad_projected = grad_projected.transpose(1, 0, 2).reshape(rows, 3 * width)
    sums.add("qkv", normed_one, grad_projected, True)
    grad_normed_one = product_right(grad_projected, qkv_whole)
    grad_hidden, gain_one_term, bias_one_term = norm_one_back(grad_normed_one)
    grad_hidden = grad_first + grad_hidden
    terms = (
        gain_one_term,
        bias_one_term,
        cross_gain_term,
        cross_bias_term,
        final_gain_term,
        final_bias_term,
    )
    totals = lax.psum(jnp.concatenate(terms + (squares,)), ("seq", "fsdp"))
    square_totals = totals[6 * width :]
    shard = width // fsdp_count
    vector_gradients = lax.dynamic_slice_in_dim(
        totals[: 6 * width].reshape(6, width), lax.axis_index("fsdp") * shard, shard, 1
    )
    layer_rms = jnp.sqrt(square_totals / entries)
    gradients = sums.finish()
    return (
        output.reshape(clips, frames, width),
        grad_hidden.reshape(clips, frames, width),
        vector_gradients[0],
        vector_gradients[1],
        by_kind(gradients["qkv"]),
        gradients["self_output"],
        vector_gradients[2],
        vector_gradients[3],
        gradients["cross_query"],
        gradients["cross_memory"],
        gradients["cross_output"],
        vector_gradients[4],
        vector_gradients[5],
        gradients["expand"],
        gradients["contract"],
        layer_rms,
    )


def solution(mesh):
    shape = dict(mesh.shape)
    blocks = shape["seq"] == 4 and shape["fsdp"] == 8
    return jax.shard_map(
        on_blocks if blocks else on_any_mesh,
        mesh=mesh,
        in_specs=(
            P("fsdp", "seq", None),
            P("fsdp", None, None),
            P("fsdp"),
            P("fsdp"),
            P("fsdp", None),
            P("fsdp", None),
            P("fsdp"),
            P("fsdp"),
            P("fsdp", None),
            P("fsdp", None),
            P("fsdp", None),
            P("fsdp"),
            P("fsdp"),
            P("fsdp", None),
            P("fsdp", None),
            P("fsdp", "seq", None),
        ),
        out_specs=(
            P("fsdp", "seq", None),
            P("fsdp", "seq", None),
            P("fsdp"),
            P("fsdp"),
            P("fsdp", None),
            P("fsdp", None),
            P("fsdp"),
            P("fsdp"),
            P("fsdp", None),
            P("fsdp", None),
            P("fsdp", None),
            P("fsdp"),
            P("fsdp"),
            P("fsdp", None),
            P("fsdp", None),
            P(),
        ),
        check_vma=False,
    )
```

```python
import functools

import jax
import jax.numpy as jnp
from jax import lax
from jax.experimental import pallas as pl
from jax.experimental.pallas import tpu as pltpu
from jax.sharding import PartitionSpec as P

H = 24
HD = 64
TEXT = 64

NEGATIVE = -1e30
BF16 = jnp.bfloat16
F32 = jnp.float32
MESH = pl.DeviceIdType.MESH


def layer_norm(values, gain, offset):
    center = values - jnp.mean(values, axis=-1, keepdims=True)
    spread = jnp.mean(center * center, axis=-1, keepdims=True)
    return center * lax.rsqrt(spread + 1e-05) * gain + offset


def gelu_exact(values):
    return jax.nn.gelu(values, approximate=False)


def product(left, right):
    return jnp.dot(left, right, preferred_element_type=jnp.float32)


def product_left(left, right):
    return lax.dot_general(
        left, right, (((0,), (0,)), ((), ())), preferred_element_type=jnp.float32
    )


def product_right(left, right):
    return lax.dot_general(
        left, right, (((1,), (1,)), ((), ())), preferred_element_type=jnp.float32
    )


def causal_forward(queries, keys, values, rows_block, scale):
    clips, length, heads_local, head_width = queries.shape
    count = length // rows_block
    columns = jnp.arange(length, dtype=jnp.int32)

    def one_block(start):
        block = lax.dynamic_slice_in_dim(queries, start, rows_block, 1)
        scores = (
            jnp.einsum("cqhd,ckhd->chqk", block, keys, preferred_element_type=jnp.float32) * scale
        )
        positions = start + jnp.arange(rows_block, dtype=jnp.int32)
        allowed = columns[None, :] <= positions[:, None]
        scores = jnp.where(allowed, scores, NEGATIVE)
        highest = jnp.max(scores, axis=-1, keepdims=True)
        raised = jnp.exp(scores - highest)
        summed = jnp.sum(raised, axis=-1, keepdims=True)
        weights = (raised / summed).astype(jnp.bfloat16)
        result = jnp.einsum("chqk,ckhd->cqhd", weights, values, preferred_element_type=jnp.float32)
        return (result.astype(jnp.bfloat16), (highest + jnp.log(summed))[..., 0])

    starts = jnp.arange(count, dtype=jnp.int32) * rows_block
    results, logsum = lax.map(one_block, starts)
    results = jnp.moveaxis(results, 0, 1).reshape(clips, length, heads_local * head_width)
    return (results, logsum)


def causal_backward(queries, keys, values, logsum, grad_heads, rows_block, scale):
    clips, length, heads_local, head_width = queries.shape
    count = length // rows_block
    columns = jnp.arange(length, dtype=jnp.int32)
    starts = jnp.arange(count, dtype=jnp.int32) * rows_block

    def one_block(carry, inputs):
        grad_keys, grad_values = carry
        start, block_logsum = inputs
        block = lax.dynamic_slice_in_dim(queries, start, rows_block, 1)
        block_grad = lax.dynamic_slice_in_dim(grad_heads, start, rows_block, 1)
        scores = (
            jnp.einsum("cqhd,ckhd->chqk", block, keys, preferred_element_type=jnp.float32) * scale
        )
        positions = start + jnp.arange(rows_block, dtype=jnp.int32)
        allowed = columns[None, :] <= positions[:, None]
        scores = jnp.where(allowed, scores, NEGATIVE)
        weights = jnp.exp(scores - block_logsum[..., None])
        rounded = weights.astype(jnp.bfloat16)
        grad_weights = jnp.einsum(
            "cqhd,ckhd->chqk", block_grad, values, preferred_element_type=jnp.float32
        )
        inner = jnp.sum(weights * grad_weights, axis=-1, keepdims=True)
        grad_scores = (weights * (grad_weights - inner)).astype(jnp.bfloat16)
        grad_query = (
            jnp.einsum("chqk,ckhd->cqhd", grad_scores, keys, preferred_element_type=jnp.float32)
            * scale
        )
        grad_keys = (
            grad_keys
            + jnp.einsum("chqk,cqhd->ckhd", grad_scores, block, preferred_element_type=jnp.float32)
            * scale
        )
        grad_values = grad_values + jnp.einsum(
            "chqk,cqhd->ckhd", rounded, block_grad, preferred_element_type=jnp.float32
        )
        return ((grad_keys, grad_values), grad_query.astype(jnp.bfloat16))

    zeros = jnp.zeros(queries.shape, jnp.float32)
    (grad_keys, grad_values), grad_queries = lax.scan(one_block, (zeros, zeros), (starts, logsum))
    local_width = heads_local * head_width
    grad_queries = jnp.moveaxis(grad_queries, 0, 1).reshape(clips, length, local_width)
    grad_keys = grad_keys.astype(jnp.bfloat16).reshape(clips, length, local_width)
    grad_values = grad_values.astype(jnp.bfloat16).reshape(clips, length, local_width)
    return jnp.stack([grad_queries, grad_keys, grad_values], axis=2)


def on_any_mesh(
    hidden_states,
    text_states,
    self_gain,
    self_bias,
    query_key_value,
    self_output,
    cross_gain,
    cross_bias,
    cross_query,
    cross_memory,
    cross_output,
    final_gain,
    final_bias,
    expand_weight,
    contract_weight,
    output_cotangent,
):
    clips, frames, width = hidden_states.shape
    rows = clips * frames
    groups = lax.axis_size("seq")
    fsdp_count = lax.axis_size("fsdp")
    heads_local = H // groups
    length = frames * groups
    rows_block = min(512, length)
    scale = HD ** (-0.5)
    entries = rows * groups * fsdp_count * width
    self_set = (
        lax.all_gather(self_gain, "fsdp", axis=0, tiled=True),
        lax.all_gather(self_bias, "fsdp", axis=0, tiled=True),
        lax.all_gather(query_key_value, "fsdp", axis=0, tiled=True),
        lax.all_gather(self_output, "fsdp", axis=0, tiled=True),
    )
    hidden = hidden_states.reshape(rows, width).astype(jnp.float32)
    normed_one, norm_one_back = jax.vjp(
        layer_norm, hidden, self_set[0].astype(jnp.float32), self_set[1].astype(jnp.float32)
    )
    normed_one = normed_one.astype(jnp.bfloat16)
    projected = (
        product(normed_one, self_set[2]).astype(jnp.bfloat16).reshape(clips, frames, 3, width)
    )
    regrouped = lax.all_to_all(projected, "seq", split_axis=3, concat_axis=1, tiled=True)
    regrouped = regrouped.reshape(clips, length, 3, heads_local, HD)
    queries = regrouped[:, :, 0]
    keys = regrouped[:, :, 1]
    values = regrouped[:, :, 2]
    context_heads, logsum = causal_forward(queries, keys, values, rows_block, scale)
    context = lax.all_to_all(context_heads, "seq", split_axis=1, concat_axis=2, tiled=True).reshape(
        rows, width
    )
    attended = product(context, self_set[3])
    first = hidden + attended
    rest_set = (
        lax.all_gather(cross_gain, "fsdp", axis=0, tiled=True),
        lax.all_gather(cross_bias, "fsdp", axis=0, tiled=True),
        lax.all_gather(cross_query, "fsdp", axis=0, tiled=True),
        lax.all_gather(cross_memory, "fsdp", axis=0, tiled=True),
        lax.all_gather(cross_output, "fsdp", axis=0, tiled=True),
        lax.all_gather(final_gain, "fsdp", axis=0, tiled=True),
        lax.all_gather(final_bias, "fsdp", axis=0, tiled=True),
        lax.all_gather(expand_weight, "fsdp", axis=0, tiled=True),
        lax.all_gather(contract_weight, "fsdp", axis=0, tiled=True),
    )
    normed_two, norm_two_back = jax.vjp(
        layer_norm, first, rest_set[0].astype(jnp.float32), rest_set[1].astype(jnp.float32)
    )
    normed_two = normed_two.astype(jnp.bfloat16)
    cross_q = product(normed_two, rest_set[2]).astype(jnp.bfloat16).reshape(clips, frames, H, HD)
    text_rows = text_states.reshape(clips * TEXT, width)
    memory = product(text_rows, rest_set[3]).astype(jnp.bfloat16).reshape(clips, TEXT, 2, H, HD)
    cross_keys = memory[:, :, 0]
    cross_values = memory[:, :, 1]
    cross_scores = (
        jnp.einsum("cqhd,ckhd->chqk", cross_q, cross_keys, preferred_element_type=jnp.float32)
        * scale
    )
    highest = jnp.max(cross_scores, axis=-1, keepdims=True)
    raised = jnp.exp(cross_scores - highest)
    cross_weights = raised / jnp.sum(raised, axis=-1, keepdims=True)
    cross_rounded = cross_weights.astype(jnp.bfloat16)
    cross_context = jnp.einsum(
        "chqk,ckhd->cqhd", cross_rounded, cross_values, preferred_element_type=jnp.float32
    )
    cross_context = cross_context.astype(jnp.bfloat16).reshape(rows, width)
    crossed = product(cross_context, rest_set[4])
    second = first + crossed
    normed_three, norm_three_back = jax.vjp(
        layer_norm, second, rest_set[5].astype(jnp.float32), rest_set[6].astype(jnp.float32)
    )
    normed_three = normed_three.astype(jnp.bfloat16)
    preact = product(normed_three, rest_set[7])
    activated, gelu_back = jax.vjp(gelu_exact, preact)
    activated = activated.astype(jnp.bfloat16)
    mixed = product(activated, rest_set[8])
    output = second + mixed
    squares = jnp.stack(
        [
            jnp.sum(output * output),
            jnp.sum(attended * attended),
            jnp.sum(crossed * crossed),
            jnp.sum(mixed * mixed),
        ]
    )
    square_totals = lax.psum(squares, ("seq", "fsdp"))
    back_rest = (
        lax.all_gather(cross_gain, "fsdp", axis=0, tiled=True),
        lax.all_gather(cross_bias, "fsdp", axis=0, tiled=True),
        lax.all_gather(cross_query, "fsdp", axis=0, tiled=True),
        lax.all_gather(cross_memory, "fsdp", axis=0, tiled=True),
        lax.all_gather(cross_output, "fsdp", axis=0, tiled=True),
        lax.all_gather(final_gain, "fsdp", axis=0, tiled=True),
        lax.all_gather(final_bias, "fsdp", axis=0, tiled=True),
        lax.all_gather(expand_weight, "fsdp", axis=0, tiled=True),
        lax.all_gather(contract_weight, "fsdp", axis=0, tiled=True),
    )
    upstream = output_cotangent.reshape(rows, width).astype(jnp.float32)
    grad_mixed = upstream.astype(jnp.bfloat16)
    contract_term = product_left(activated, grad_mixed)
    grad_activated = product_right(grad_mixed, back_rest[8])
    grad_preact = gelu_back(grad_activated)[0].astype(jnp.bfloat16)
    expand_term = product_left(normed_three, grad_preact)
    grad_normed_three = product_right(grad_preact, back_rest[7])
    grad_second, final_gain_term, final_bias_term = norm_three_back(grad_normed_three)
    grad_second = upstream + grad_second
    grad_crossed = grad_second.astype(jnp.bfloat16)
    cross_output_term = product_left(cross_context, grad_crossed)
    grad_cross_context = (
        product_right(grad_crossed, back_rest[4]).astype(jnp.bfloat16).reshape(clips, frames, H, HD)
    )
    grad_cross_weights = jnp.einsum(
        "cqhd,ckhd->chqk", grad_cross_context, cross_values, preferred_element_type=jnp.float32
    )
    cross_inner = jnp.sum(cross_weights * grad_cross_weights, axis=-1, keepdims=True)
    grad_cross_scores = (cross_weights * (grad_cross_weights - cross_inner)).astype(jnp.bfloat16)
    grad_cross_q = (
        jnp.einsum(
            "chqk,ckhd->cqhd", grad_cross_scores, cross_keys, preferred_element_type=jnp.float32
        )
        * scale
    )
    grad_cross_q = grad_cross_q.astype(jnp.bfloat16).reshape(rows, width)
    grad_cross_keys = (
        jnp.einsum(
            "chqk,cqhd->ckhd", grad_cross_scores, cross_q, preferred_element_type=jnp.float32
        )
        * scale
    )
    grad_cross_values = jnp.einsum(
        "chqk,cqhd->ckhd", cross_rounded, grad_cross_context, preferred_element_type=jnp.float32
    )
    grad_memory = jnp.stack([grad_cross_keys, grad_cross_values], axis=2).reshape(
        clips * TEXT, 2 * width
    )
    memory_term = lax.dot_general(
        text_rows.astype(jnp.float32),
        grad_memory,
        (((0,), (0,)), ((), ())),
        precision=lax.Precision.HIGHEST,
        preferred_element_type=jnp.float32,
    )
    query_term = product_left(normed_two, grad_cross_q)
    grad_normed_two = product_right(grad_cross_q, back_rest[2])
    grad_first, cross_gain_term, cross_bias_term = norm_two_back(grad_normed_two)
    grad_first = grad_second + grad_first
    rest_sums = (
        lax.psum_scatter(
            cross_gain_term.astype(jnp.bfloat16), "fsdp", scatter_dimension=0, tiled=True
        ).astype(jnp.float32),
        lax.psum_scatter(
            cross_bias_term.astype(jnp.bfloat16), "fsdp", scatter_dimension=0, tiled=True
        ).astype(jnp.float32),
        lax.psum_scatter(
            query_term.astype(jnp.bfloat16), "fsdp", scatter_dimension=0, tiled=True
        ).astype(jnp.float32),
        lax.psum_scatter(
            memory_term.astype(jnp.bfloat16), "fsdp", scatter_dimension=0, tiled=True
        ).astype(jnp.float32),
        lax.psum_scatter(
            cross_output_term.astype(jnp.bfloat16), "fsdp", scatter_dimension=0, tiled=True
        ).astype(jnp.float32),
        lax.psum_scatter(
            final_gain_term.astype(jnp.bfloat16), "fsdp", scatter_dimension=0, tiled=True
        ).astype(jnp.float32),
        lax.psum_scatter(
            final_bias_term.astype(jnp.bfloat16), "fsdp", scatter_dimension=0, tiled=True
        ).astype(jnp.float32),
        lax.psum_scatter(
            expand_term.astype(jnp.bfloat16), "fsdp", scatter_dimension=0, tiled=True
        ).astype(jnp.float32),
        lax.psum_scatter(
            contract_term.astype(jnp.bfloat16), "fsdp", scatter_dimension=0, tiled=True
        ).astype(jnp.float32),
    )
    back_self = (
        lax.all_gather(self_gain, "fsdp", axis=0, tiled=True),
        lax.all_gather(self_bias, "fsdp", axis=0, tiled=True),
        lax.all_gather(query_key_value, "fsdp", axis=0, tiled=True),
        lax.all_gather(self_output, "fsdp", axis=0, tiled=True),
    )
    grad_attended = grad_first.astype(jnp.bfloat16)
    self_output_term = product_left(context, grad_attended)
    grad_context = (
        product_right(grad_attended, back_self[3])
        .astype(jnp.bfloat16)
        .reshape(clips, frames, width)
    )
    grad_heads = lax.all_to_all(grad_context, "seq", split_axis=2, concat_axis=1, tiled=True)
    grad_heads = grad_heads.reshape(clips, length, heads_local, HD)
    grad_regrouped = causal_backward(queries, keys, values, logsum, grad_heads, rows_block, scale)
    grad_projected = lax.all_to_all(
        grad_regrouped, "seq", split_axis=1, concat_axis=3, tiled=True
    ).reshape(rows, 3 * width)
    qkv_term = product_left(normed_one, grad_projected)
    grad_normed_one = product_right(grad_projected, back_self[2])
    grad_hidden, gain_one_term, bias_one_term = norm_one_back(grad_normed_one)
    grad_hidden = grad_first + grad_hidden
    self_sums = (
        lax.psum_scatter(
            gain_one_term.astype(jnp.bfloat16), "fsdp", scatter_dimension=0, tiled=True
        ).astype(jnp.float32),
        lax.psum_scatter(
            bias_one_term.astype(jnp.bfloat16), "fsdp", scatter_dimension=0, tiled=True
        ).astype(jnp.float32),
        lax.psum_scatter(
            qkv_term.astype(jnp.bfloat16), "fsdp", scatter_dimension=0, tiled=True
        ).astype(jnp.float32),
        lax.psum_scatter(
            self_output_term.astype(jnp.bfloat16), "fsdp", scatter_dimension=0, tiled=True
        ).astype(jnp.float32),
    )
    finals = (
        lax.psum(self_sums[0].astype(jnp.bfloat16), "seq").astype(jnp.float32),
        lax.psum(self_sums[1].astype(jnp.bfloat16), "seq").astype(jnp.float32),
        lax.psum(self_sums[2].astype(jnp.bfloat16), "seq").astype(jnp.float32),
        lax.psum(self_sums[3].astype(jnp.bfloat16), "seq").astype(jnp.float32),
        lax.psum(rest_sums[0].astype(jnp.bfloat16), "seq").astype(jnp.float32),
        lax.psum(rest_sums[1].astype(jnp.bfloat16), "seq").astype(jnp.float32),
        lax.psum(rest_sums[2].astype(jnp.bfloat16), "seq").astype(jnp.float32),
        lax.psum(rest_sums[3].astype(jnp.bfloat16), "seq").astype(jnp.float32),
        lax.psum(rest_sums[4].astype(jnp.bfloat16), "seq").astype(jnp.float32),
        lax.psum(rest_sums[5].astype(jnp.bfloat16), "seq").astype(jnp.float32),
        lax.psum(rest_sums[6].astype(jnp.bfloat16), "seq").astype(jnp.float32),
        lax.psum(rest_sums[7].astype(jnp.bfloat16), "seq").astype(jnp.float32),
        lax.psum(rest_sums[8].astype(jnp.bfloat16), "seq").astype(jnp.float32),
    )
    layer_rms = jnp.sqrt(square_totals / entries)
    return (
        output.astype(jnp.bfloat16).reshape(clips, frames, width),
        grad_hidden.reshape(clips, frames, width),
        finals[0],
        finals[1],
        finals[2],
        finals[3],
        finals[4],
        finals[5],
        finals[6],
        finals[7],
        finals[8],
        finals[9],
        finals[10],
        finals[11],
        finals[12],
        layer_rms,
    )


CORE_PAIRS = [(0, 1), (1, 0), (2, 3), (3, 2)]
X_PAIRS = [(0, 2), (2, 0), (1, 3), (3, 1)]
Y_PAIRS = [(i, i ^ 1) for i in range(8)]
Z_SHIFTS = [[(i, (i + 2 * k) % 8) for i in range(8)] for k in (1, 2, 3)]


CHUNK = 768


def gather_kernel(plan, has_vectors, *refs):
    weights = len({entry[0] for entry in plan})
    inputs = refs[:weights]
    refs = refs[weights:]
    if has_vectors:
        vector_in, refs = refs[0], refs[1:]
    outputs = refs[:weights]
    refs = refs[weights:]
    if has_vectors:
        vector_out, refs = refs[0], refs[1:]
    zs_sem, zr_sem, ys_sem, yr_sem, xs_sem, xr_sem, cs_sem, cr_sem, own_sem, vs_sem, vr_sem = refs
    seq = lax.axis_index("seq")
    fsdp = lax.axis_index("fsdp")
    x, c = seq // 2, seq % 2
    z, y = fsdp // 2, fsdp % 2
    x_seq = 2 * (1 - x) + c
    c_seq = 2 * x + 1 - c
    y_fsdp = 2 * z + 1 - y

    def at_z(k):
        return 2 * ((z + k) % 4) + y

    barrier = pltpu.get_barrier_semaphore()
    partners = [(x_seq, fsdp), (c_seq, fsdp), (seq, y_fsdp)] + [(seq, at_z(k)) for k in (1, 2, 3)]
    if has_vectors:
        partners += [(seq, 2 * ((z + k) % 4) + 1 - y) for k in (1, 2, 3)]
    for partner in partners:
        pl.semaphore_signal(barrier, inc=1, device_id=partner, device_id_type=MESH)
    pl.semaphore_wait(barrier, len(partners))

    if has_vectors:
        vector_sends = []
        for k in range(1, 8):
            copy = pltpu.make_async_remote_copy(
                src_ref=vector_in,
                dst_ref=vector_out.at[fsdp],
                send_sem=vs_sem.at[k],
                recv_sem=vr_sem.at[k],
                device_id=(seq, (fsdp + k) % 8),
                device_id_type=MESH,
            )
            copy.start()
            vector_sends.append(copy)
        own = pltpu.make_async_copy(vector_in, vector_out.at[fsdp], vs_sem.at[0])
        own.start()

    def part(entry):
        weight, block, column, split = entry
        first = 2 * c + x if split else 2 * c
        count = 1 if split else 2
        return weight, block, pl.ds(column, CHUNK), pl.ds(first, count)

    def remote(region, send, recv, device):
        return pltpu.make_async_remote_copy(
            src_ref=region,
            dst_ref=region,
            send_sem=send,
            recv_sem=recv,
            device_id=device,
            device_id_type=MESH,
        )

    sends = []

    def send(copy):
        copy.start()
        sends.append(copy)

    def start_z(i):
        weight, block, columns, mine = part(plan[i])
        source = inputs[weight].at[block, mine, :, columns]
        target = outputs[weight].at[z, y, block, mine, :, columns]
        for k in (1, 2, 3):
            copy = pltpu.make_async_remote_copy(
                src_ref=source,
                dst_ref=target,
                send_sem=zs_sem.at[i, k],
                recv_sem=zr_sem.at[i, k],
                device_id=(seq, at_z(k)),
                device_id_type=MESH,
            )
            send(copy)
        pltpu.make_async_copy(source, target, own_sem.at[i]).start()

    def start_y(i):
        weight, block, columns, mine = part(plan[i])
        output = outputs[weight]
        for k in (1, 2, 3):
            region = output.at[(z + 4 - k) % 4, y, block, mine, :, columns]
            remote(region, zs_sem.at[i, k], zr_sem.at[i, k], (seq, at_z(k))).wait_recv()
        source = inputs[weight].at[block, mine, :, columns]
        target = output.at[z, y, block, mine, :, columns]
        pltpu.make_async_copy(source, target, own_sem.at[i]).wait()
        region = output.at[:, y, block, mine, :, columns]
        send(remote(region, ys_sem.at[i], yr_sem.at[i], (seq, y_fsdp)))

    def start_x(i):
        weight, block, columns, mine = part(plan[i])
        output = outputs[weight]
        region = output.at[:, 1 - y, block, mine, :, columns]
        remote(region, ys_sem.at[i], yr_sem.at[i], (seq, y_fsdp)).wait_recv()
        region = output.at[:, :, block, mine, :, columns]
        if plan[i][3]:
            send(remote(region, xs_sem.at[i], xr_sem.at[i], (x_seq, fsdp)))
        send(remote(region, cs_sem.at[i, 0], cr_sem.at[i, 0], (c_seq, fsdp)))

    def start_core(i):
        if plan[i][3]:
            weight, block, columns, _ = part(plan[i])
            region = outputs[weight].at[:, :, block, pl.ds(2 * c + 1 - x, 1), :, columns]
            remote(region, xs_sem.at[i], xr_sem.at[i], (x_seq, fsdp)).wait_recv()
            send(remote(region, cs_sem.at[i, 1], cr_sem.at[i, 1], (c_seq, fsdp)))

    def finish(i):
        weight, block, columns, _ = part(plan[i])
        other = 2 * (1 - c)
        output = outputs[weight]
        if plan[i][3]:
            for j, quarter in ((0, other + x), (1, other + 1 - x)):
                region = output.at[:, :, block, pl.ds(quarter, 1), :, columns]
                remote(region, cs_sem.at[i, j], cr_sem.at[i, j], (c_seq, fsdp)).wait_recv()
        else:
            region = output.at[:, :, block, pl.ds(other, 2), :, columns]
            remote(region, cs_sem.at[i, 0], cr_sem.at[i, 0], (c_seq, fsdp)).wait_recv()

    chunks = len(plan)
    ahead = 3
    for i in range(min(ahead, chunks)):
        start_z(i)
    for t in range(chunks + 2):
        if t + ahead < chunks:
            start_z(t + ahead)
        if t < chunks:
            start_y(t)
        if 0 <= t - 1 < chunks:
            start_x(t - 1)
        if 0 <= t - 2 < chunks:
            start_core(t - 2)
    for i in range(chunks):
        finish(i)
    for copy in sends:
        copy.wait_send()
    if has_vectors:
        own.wait()
        for k in range(1, 8):
            vector_sends[k - 1].wait_send()
            region = vector_out.at[(fsdp + 8 - k) % 8]
            remote(region, vs_sem.at[k], vr_sem.at[k], (seq, (fsdp + k) % 8)).wait_recv()


def gather_plan(shapes):
    places = [
        (weight, block, column)
        for weight, (rows, columns) in enumerate(shapes)
        for block in range(rows // 192)
        for column in range(0, columns, CHUNK)
    ]
    return tuple(place + ((len(places) - 1 - i) % 3 != 0,) for i, place in enumerate(places))


def gather_weights(shards, vectors, collective_id):
    shapes = [shard.shape for shard in shards]
    plan = gather_plan(shapes)
    chunks = len(plan)
    inputs = [shard.reshape(rows // 192, 4, 48, columns) for shard, (rows, columns) in zip(shards, shapes)]
    out_shapes = [
        jax.ShapeDtypeStruct((4, 2, rows // 192, 4, 48, columns), BF16) for rows, columns in shapes
    ]
    if vectors is not None:
        inputs.append(vectors)
        out_shapes.append(jax.ShapeDtypeStruct((8,) + vectors.shape, vectors.dtype))
    anywhere = pl.BlockSpec(memory_space=pl.ANY)
    dma = pltpu.SemaphoreType.DMA
    results = pl.pallas_call(
        functools.partial(gather_kernel, plan, vectors is not None),
        out_shape=out_shapes,
        in_specs=[anywhere] * len(inputs),
        out_specs=[anywhere] * len(out_shapes),
        scratch_shapes=[
            dma((chunks, 4)),
            dma((chunks, 4)),
            dma((chunks,)),
            dma((chunks,)),
            dma((chunks,)),
            dma((chunks,)),
            dma((chunks, 2)),
            dma((chunks, 2)),
            dma((chunks,)),
            dma((8,)),
            dma((8,)),
        ],
        compiler_params=pltpu.CompilerParams(collective_id=collective_id, has_side_effects=True),
        name="gather_weights",
    )(*inputs)
    whole = [result.reshape(8 * rows, columns) for result, (rows, columns) in zip(results, shapes)]
    return whole, results[-1]


def pack_vectors(vectors):
    stacked = jnp.stack([vector.astype(F32) for vector in vectors])
    return jnp.pad(stacked, ((0, 8 - stacked.shape[0]), (0, (-stacked.shape[1]) % 128)))


def blocks_kernel(left, right, out):
    out[0] = jnp.dot(left[...], right[...], preferred_element_type=F32).astype(BF16)


def product_blocks(left, right, count):
    rows, depth = left.shape
    width = right.shape[1] // count
    return pl.pallas_call(
        blocks_kernel,
        grid=(count,),
        out_shape=jax.ShapeDtypeStruct((count, rows, width), BF16),
        in_specs=[
            pl.BlockSpec((rows, depth), lambda i: (0, 0)),
            pl.BlockSpec((depth, width), lambda i: (0, i)),
        ],
        out_specs=pl.BlockSpec((1, rows, width), lambda i: (i, 0, 0)),
        compiler_params=pltpu.CompilerParams(vmem_limit_bytes=48 << 20),
        cost_estimate=pl.CostEstimate(
            flops=2 * rows * depth * width * count,
            bytes_accessed=2 * (rows * depth + depth * width * count + rows * width * count),
            transcendentals=0,
        ),
        name="product_blocks",
    )(left, right)


QUERIES = 256


def both_heads(value):
    lane = lax.broadcasted_iota(jnp.int32, value.shape, 1)
    zero = jnp.zeros_like(value)
    return jnp.where(lane < HD, value, zero), jnp.where(lane < HD, zero, value)


def across(left, right):
    return lax.dot_general(left, right, (((1,), (1,)), ((), ())), preferred_element_type=F32)


def down(left, right):
    return lax.dot_general(left, right, (((0,), (0,)), ((), ())), preferred_element_type=F32)


def join_heads(pair):
    row = lax.broadcasted_iota(jnp.int32, pair[0].shape, 0)
    return jnp.where(row < HD, pair[0], pair[1])


def key_parts(block):
    return ([(0, block * QUERIES, False)] if block else []) + [
        (block * QUERIES, (block + 1) * QUERIES, True)
    ]


def masked_scores(keys, queries, diagonal):
    scores = across(keys, queries)
    if diagonal:
        key = lax.broadcasted_iota(jnp.int32, scores.shape, 0)
        query = lax.broadcasted_iota(jnp.int32, scores.shape, 1)
        scores = jnp.where(key <= query, scores, NEGATIVE)
    return scores


def attention_kernel(scale, q_ref, k_ref, v_ref, out_ref, logsum_ref):
    blocks = q_ref.shape[0] * q_ref.shape[2] // QUERIES
    k = k_ref[:, 0].reshape(-1, 2 * HD)
    v = v_ref[:, 0].reshape(-1, 2 * HD)
    for block in range(blocks):
        rows = slice(block * QUERIES, (block + 1) * QUERIES)
        queries = both_heads((q_ref[block, 0].astype(F32) * scale).astype(BF16))
        outs = []
        for head in range(2):
            parts = key_parts(block)
            scores = [masked_scores(k[a:b], queries[head], diagonal) for a, b, diagonal in parts]
            highest = functools.reduce(
                jnp.maximum, [jnp.max(part, axis=0, keepdims=True) for part in scores]
            )
            raised = [jnp.exp(part - highest) for part in scores]
            summed = sum(jnp.sum(part, axis=0, keepdims=True) for part in raised)
            total = sum(
                down(v[a:b], part.astype(BF16)) for (a, b, _), part in zip(parts, raised)
            )
            outs.append(total / summed)
            logsum_ref[0, 0, head : head + 1, rows] = highest + jnp.log(summed)
        out_ref[block, 0] = join_heads(outs).T.astype(BF16)


def attention(qkv, scale):
    blocks, clips, frames, width = qkv.shape
    pairs = width // (3 * 2 * HD)
    length = blocks * frames
    spec = lambda offset: pl.BlockSpec(
        (blocks, 1, frames, 2 * HD), lambda clip, pair: (0, clip, 0, offset + pair)
    )
    return pl.pallas_call(
        functools.partial(attention_kernel, scale),
        grid=(clips, pairs),
        out_shape=(
            jax.ShapeDtypeStruct((blocks, clips, frames, pairs * 2 * HD), BF16),
            jax.ShapeDtypeStruct((clips, pairs, 2, length), F32),
        ),
        in_specs=[spec(0), spec(pairs), spec(2 * pairs)],
        out_specs=(
            spec(0),
            pl.BlockSpec((1, 1, 2, length), lambda clip, pair: (clip, pair, 0, 0)),
        ),
        compiler_params=pltpu.CompilerParams(vmem_limit_bytes=48 << 20),
        cost_estimate=pl.CostEstimate(
            flops=clips * pairs * 2 * 4 * length * length * 2 * HD,
            bytes_accessed=4 * clips * pairs * length * 2 * HD * 2,
            transcendentals=clips * pairs * 2 * length * length,
        ),
        name="attention",
    )(qkv, qkv, qkv)


def attention_back_kernel(
    scale, q_ref, k_ref, v_ref, grad_ref, logsum_ref, out_ref, grad_keys, grad_values
):
    blocks = q_ref.shape[0] * q_ref.shape[2] // QUERIES
    frames = q_ref.shape[2]
    pair = pl.program_id(1)
    group = pl.num_programs(1) * 2 * HD
    k = k_ref[:, 0].reshape(-1, 2 * HD)
    v = v_ref[:, 0].reshape(-1, 2 * HD)

    def columns(kind):
        return pl.ds(pl.multiple_of(kind * group + pair * 2 * HD, 2 * HD), 2 * HD)

    for block in range(blocks):
        rows = slice(block * QUERIES, (block + 1) * QUERIES)
        queries = both_heads((q_ref[block, 0].astype(F32) * scale).astype(BF16))
        grads = both_heads(grad_ref[block, 0])
        parts = key_parts(block)
        query_grads = []
        held = [[], []]
        for head in range(2):
            logsum = logsum_ref[0, 0, head : head + 1, rows]
            weights, weighted = [], []
            for a, b, diagonal in parts:
                weight = jnp.exp(masked_scores(k[a:b], queries[head], diagonal) - logsum)
                weights.append(weight)
                weighted.append(weight * across(v[a:b], grads[head]))
            inner = sum(jnp.sum(part, axis=0, keepdims=True) for part in weighted)
            changes = [
                (term - weight * inner).astype(BF16) for term, weight in zip(weighted, weights)
            ]
            query_grads.append(sum(down(k[a:b], part) for (a, b, _), part in zip(parts, changes)))
            held[head] = [(weight.astype(BF16), change) for weight, change in zip(weights, changes)]
        out_ref[block, 0, :, columns(0)] = (join_heads(query_grads).T * scale).astype(BF16)
        for j, (a, b, diagonal) in enumerate(parts):
            value_term = sum(
                jnp.dot(held[head][j][0], grads[head], preferred_element_type=F32)
                for head in range(2)
            )
            key_term = sum(
                jnp.dot(held[head][j][1], queries[head], preferred_element_type=F32)
                for head in range(2)
            )
            if diagonal:
                grad_values[a:b] = value_term
                grad_keys[a:b] = key_term
            else:
                grad_values[a:b] += value_term
                grad_keys[a:b] += key_term
    out_ref[:, 0, :, columns(1)] = grad_keys[...].reshape(-1, frames, 2 * HD).astype(BF16)
    out_ref[:, 0, :, columns(2)] = grad_values[...].reshape(-1, frames, 2 * HD).astype(BF16)


def attention_back(qkv, grad, logsum, scale):
    blocks, clips, frames, width = qkv.shape
    pairs = width // (3 * 2 * HD)
    length = blocks * frames
    spec = lambda offset: pl.BlockSpec(
        (blocks, 1, frames, 2 * HD), lambda clip, pair: (0, clip, 0, offset + pair)
    )
    return pl.pallas_call(
        functools.partial(attention_back_kernel, scale),
        grid=(clips, pairs),
        out_shape=jax.ShapeDtypeStruct(qkv.shape, BF16),
        in_specs=[
            spec(0),
            spec(pairs),
            spec(2 * pairs),
            spec(0),
            pl.BlockSpec((1, 1, 2, length), lambda clip, pair: (clip, pair, 0, 0)),
        ],
        out_specs=pl.BlockSpec((blocks, 1, frames, width), lambda clip, pair: (0, clip, 0, 0)),
        scratch_shapes=[pltpu.VMEM((length, 2 * HD), F32), pltpu.VMEM((length, 2 * HD), F32)],
        compiler_params=pltpu.CompilerParams(vmem_limit_bytes=48 << 20),
        cost_estimate=pl.CostEstimate(
            flops=clips * pairs * 2 * 10 * length * length * 2 * HD,
            bytes_accessed=7 * clips * pairs * length * 2 * HD * 2,
            transcendentals=clips * pairs * 2 * length * length,
        ),
        name="attention_back",
    )(qkv, qkv, qkv, grad, logsum)


PIECE = (192, 384)
LAGS = (0, 1, 3, 4, 5, 6, 7)


def sum_kernel(plan, weights, *refs):
    chunks = len(plan)
    tall = sum(entry[1] for entry in plan)
    lefts, rights = refs[:weights], refs[weights : 2 * weights]
    vector_in = refs[2 * weights]
    outputs = refs[2 * weights + 1 : 3 * weights + 1]
    vector_out = refs[3 * weights + 1]
    (
        mine,
        c_out,
        c_in,
        x_in,
        y_in,
        second_in,
        z_in,
        total,
        fx_in,
        fc_in,
        wide_stage,
        tall_stage,
        left_buf,
        right_buf,
        tall_buf,
        vector,
        vector_got,
        vector_z,
        c_sem,
        first_sem,
        second_sem,
        z_sem,
        fx_sem,
        fc_sem,
        stage_sem,
        load_sem,
        vector_sem,
    ) = refs[3 * weights + 2 :]
    seq = lax.axis_index("seq")
    fsdp = lax.axis_index("fsdp")
    x, c = seq // 2, seq % 2
    z, y = fsdp // 2, fsdp % 2
    x_device = (2 * (1 - x) + c, fsdp)
    c_device = (2 * x + 1 - c, fsdp)
    y_device = (seq, 2 * z + 1 - y)

    def z_device(k):
        return (seq, 2 * ((z + k) % 4) + y)

    barrier = pltpu.get_barrier_semaphore()
    partners = [x_device, c_device, y_device] + [z_device(k) for k in (1, 2, 3)]
    for partner in partners:
        pl.semaphore_signal(barrier, inc=1, device_id=partner, device_id_type=MESH)
    pl.semaphore_wait(barrier, len(partners))

    def remote(source, target, sems, device):
        return pltpu.make_async_remote_copy(
            src_ref=source,
            dst_ref=target,
            send_sem=sems.at[0],
            recv_sem=sems.at[1],
            device_id=device,
            device_id_type=MESH,
        )

    def x_first(i):
        return i % 2 == 0

    def loads(j):
        weight, is_tall, column = plan[j]
        slot = j % 2
        if is_tall:
            copies = [
                pltpu.make_async_copy(
                    rights[weight].at[:, pl.ds(column, 384)],
                    right_buf.at[slot, :, pl.ds(0, 384)],
                    load_sem.at[1, slot],
                )
            ]
            if j == 0:
                copies.append(pltpu.make_async_copy(lefts[weight], tall_buf, load_sem.at[2, 0]))
            return copies
        return [
            pltpu.make_async_copy(lefts[weight], left_buf.at[slot], load_sem.at[0, slot]),
            pltpu.make_async_copy(
                rights[weight].at[:, pl.ds(column, 1536)], right_buf.at[slot], load_sem.at[1, slot]
            ),
        ]

    def start_loads(i):
        for j in range(chunks):

            @pl.when(i == j)
            def _():
                for copy in loads(j):
                    copy.start()

    def wait_loads(i):
        for j in range(chunks):

            @pl.when(i == j)
            def _():
                for copy in loads(j):
                    copy.wait()

    def columns(block):
        return pl.ds(pl.multiple_of(block * 384, 128), 384)

    def multiply(i, half, target, slot):
        buffer = i % 2

        @pl.when(i >= tall)
        def _():
            right = right_buf.at[buffer, :, pl.ds(pl.multiple_of(half * 768, 128), 768)]

            @pl.loop(0, 4)
            def _(zz):
                out = down(left_buf[buffer, :, columns(zz)], right[...]).astype(BF16)
                for q in range(2):
                    for yy in range(2):
                        target[slot, q, zz, yy] = out[192 * yy : 192 * yy + 192, 384 * q : 384 * q + 384]

        @pl.when(i < tall)
        def _():
            right = right_buf.at[buffer, :, pl.ds(0, 384)]

            @pl.loop(0, 4)
            def _(zz):
                for yy in range(2):
                    left = tall_buf[:, columns((2 * zz + yy) * 2 + half)]
                    out = down(left, right[...]).astype(BF16)
                    for q in range(2):
                        target[slot, q, zz, yy] = out[192 * q : 192 * q + 192]

    def add_to(slot, q, zz, yy, other):
        here = mine[slot, q, zz, yy].astype(F32)
        mine[slot, q, zz, yy] = (here + other.astype(F32)).astype(BF16)

    def c_copy(i):
        return remote(c_out.at[i % 2], c_in.at[i % 2], c_sem.at[:, i % 2], c_device)

    def x_copy(i):
        slot = i // 2 % 2
        return remote(mine.at[i % 5, 1 - x], x_in.at[slot], first_sem.at[:, i % 4], x_device)

    def y_copy(i):
        slot = i // 2 % 2
        return remote(mine.at[i % 5, :, :, 1 - y], y_in.at[slot], first_sem.at[:, i % 4], y_device)

    def second_y_copy(i):
        slot = i % 4
        return remote(mine.at[i % 5, x, :, 1 - y], second_in.at[slot], second_sem.at[:, slot], y_device)

    def second_x_copy(i):
        slot = i % 4
        return remote(mine.at[i % 5, 1 - x, :, y], second_in.at[slot], second_sem.at[:, slot], x_device)

    def z_copy(i, k):
        slot = i % 4
        return remote(
            mine.at[i % 5, x, (z + k) % 4, y],
            z_in.at[slot, k - 1],
            z_sem.at[:, slot, k - 1],
            z_device(k),
        )

    def fx_copy(i):
        slot = i % 4
        return remote(total.at[slot], fx_in.at[slot], fx_sem.at[:, slot], x_device)

    def fc_copy(i, which):
        slot = i % 4
        source = fx_in.at[slot] if which else total.at[slot]
        return remote(source, fc_in.at[slot, which], fc_sem.at[:, slot, which], c_device)

    def begin(i):
        wait_loads(i)

        @pl.when(i >= 2)
        def _():
            c_copy(i - 2).wait_send()

        multiply(i, 1 - c, c_out, i % 2)
        c_copy(i).start()
        multiply(i, c, mine, i % 5)

    def first(i):
        slot = i % 5
        got = i % 2
        c_copy(i).wait_recv()

        @pl.when(x_first(i))
        def _():
            for q, last in ((1 - x, False), (x, True)):

                @pl.loop(0, 4)
                def _(zz):
                    for yy in range(2):
                        add_to(slot, q, zz, yy, c_in[got, q, zz, yy])

                if not last:
                    x_copy(i).start()

        @pl.when(jnp.logical_not(x_first(i)))
        def _():
            for yy, last in ((1 - y, False), (y, True)):

                @pl.loop(0, 4)
                def _(zz):
                    for q in range(2):
                        add_to(slot, q, zz, yy, c_in[got, q, zz, yy])

                if not last:
                    y_copy(i).start()

    def second(i):
        slot = i % 5
        got = i // 2 % 2

        @pl.when(x_first(i))
        def _():
            x_copy(i).wait()
            for yy, last in ((1 - y, False), (y, True)):

                @pl.loop(0, 4)
                def _(zz):
                    add_to(slot, x, zz, yy, x_in[got, zz, yy])

                if not last:
                    second_y_copy(i).start()

        @pl.when(jnp.logical_not(x_first(i)))
        def _():
            y_copy(i).wait()
            for q, last in ((1 - x, False), (x, True)):

                @pl.loop(0, 4)
                def _(zz):
                    add_to(slot, q, zz, y, y_in[got, q, zz])

                if not last:
                    second_x_copy(i).start()

    def third(i):
        slot = i % 4

        @pl.when(x_first(i))
        def _():
            second_y_copy(i).wait()

        @pl.when(jnp.logical_not(x_first(i)))
        def _():
            second_x_copy(i).wait()

        for k in (1, 2, 3):
            zz = (z + k) % 4
            add_to(i % 5, x, zz, y, second_in[slot, zz])
            z_copy(i, k).start()

    def put(i, quarter, value):
        slot = i % 2

        @pl.when(i >= tall)
        def _():
            wide_stage[slot, :, columns(quarter)] = value

        @pl.when(i < tall)
        def _():
            tall_stage[slot, pl.ds(pl.multiple_of(quarter * 192, 64), 192)] = value

    def fourth(i):
        slot = i % 4
        result = mine[i % 5, x, z, y].astype(F32) + second_in[slot, z].astype(F32)
        for k in (1, 2, 3):
            z_copy(i, k).wait()
            result = result + z_in[slot, k - 1].astype(F32)
        total[slot] = result.astype(BF16)
        fx_copy(i).start()
        fc_copy(i, 0).start()

    def fifth(i):
        fx_copy(i).wait()
        fc_copy(i, 1).start()

    def store(j):
        weight, is_tall, column = plan[j]
        slot = j % 2
        if is_tall:
            return pltpu.make_async_copy(
                tall_stage.at[slot], outputs[weight].at[:, pl.ds(column, 384)], stage_sem.at[0, slot]
            )
        return pltpu.make_async_copy(
            wide_stage.at[slot], outputs[weight].at[:, pl.ds(column, 1536)], stage_sem.at[1, slot]
        )

    def sixth(i):
        slot = i % 4
        for j in range(2, chunks):

            @pl.when(i == j)
            def _():
                store(j - 2).wait()

        fc_copy(i, 0).wait()
        fc_copy(i, 1).wait()
        put(i, 2 * c + x, total[slot])
        put(i, 2 * c + 1 - x, fx_in[slot])
        put(i, 2 * (1 - c) + x, fc_in[slot, 0])
        put(i, 2 * (1 - c) + 1 - x, fc_in[slot, 1])
        for j in range(chunks):

            @pl.when(i == j)
            def _():
                store(j).start()

    def vector_copy(leg):
        device = (c_device, x_device, y_device)[leg]
        return remote(vector.at[leg], vector_got.at[leg], vector_sem.at[:, leg], device)

    def vector_z_copy(k):
        return remote(vector_z.at[z], vector_z.at[z], vector_sem.at[:, 2 + k], z_device(k))

    def vector_arrival(k):
        source = (z + 4 - k) % 4
        return remote(vector_z.at[source], vector_z.at[source], vector_sem.at[:, 2 + k], z_device(k))

    def vector_step(t):
        @pl.when(t == 0)
        def _():
            pltpu.sync_copy(vector_in, vector.at[0])
            vector_copy(0).start()

        for leg in range(3):

            @pl.when(t == leg + 1)
            def _():
                vector_copy(leg).wait()
                both = vector[leg] + vector_got[leg]
                if leg < 2:
                    vector[leg + 1] = both
                    vector_copy(leg + 1).start()
                else:
                    vector_z[z] = both
                    for k in (1, 2, 3):
                        vector_z_copy(k).start()

        @pl.when(t == 4)
        def _():
            for k in (1, 2, 3):
                vector_z_copy(k).wait_send()
                vector_arrival(k).wait_recv()
            vector[0] = vector_z[0] + vector_z[1] + vector_z[2] + vector_z[3]
            pltpu.sync_copy(vector.at[0], vector_out)

    start_loads(0)

    @pl.loop(0, chunks + LAGS[-1])
    def _(t):
        @pl.when(t + 1 < chunks)
        def _():
            start_loads(t + 1)

        stages = (begin, first, second, third, fourth, fifth, sixth)
        for lag, run in zip(LAGS[::-1], stages[::-1]):
            i = t - lag

            @pl.when(jnp.logical_and(i >= 0, i < chunks))
            def _():
                run(i)

        vector_step(t)

    for j in (chunks - 2, chunks - 1):
        c_copy(j).wait_send()
        store(j).wait()


def sum_products(products, vectors):
    lefts = [left for left, _ in products]
    rights = [right for _, right in products]
    height, width = lefts[0].shape[1], rights[0].shape[1]
    plan = [(0, True, column) for column in range(0, width, 384)]
    for weight in range(1, len(products)):
        plan += [(weight, False, column) for column in range(0, rights[weight].shape[1], 1536)]
    out_shapes = [
        jax.ShapeDtypeStruct((left.shape[1] // 8, right.shape[1]), BF16) for left, right in products
    ]
    out_shapes.append(jax.ShapeDtypeStruct(vectors.shape, F32))
    depth = lefts[0].shape[0]
    anywhere = pl.BlockSpec(memory_space=pl.ANY)
    dma = pltpu.SemaphoreType.DMA
    block = lambda *lead: pltpu.VMEM(lead + PIECE, BF16)
    *sums, total = pl.pallas_call(
        functools.partial(sum_kernel, tuple(plan), len(products)),
        out_shape=out_shapes,
        in_specs=[anywhere] * (2 * len(products) + 1),
        out_specs=[anywhere] * len(out_shapes),
        scratch_shapes=[
            block(5, 2, 4, 2),
            block(2, 2, 4, 2),
            block(2, 2, 4, 2),
            block(2, 4, 2),
            block(2, 2, 4),
            block(4, 4),
            block(4, 3),
            block(4),
            block(4),
            block(4, 2),
            pltpu.VMEM((2, 192, 1536), BF16),
            pltpu.VMEM((2, 768, 384), BF16),
            pltpu.VMEM((2, depth, 1536), BF16),
            pltpu.VMEM((2, depth, 1536), BF16),
            pltpu.VMEM((depth, height), BF16),
            pltpu.VMEM((3,) + vectors.shape, F32),
            pltpu.VMEM((3,) + vectors.shape, F32),
            pltpu.VMEM((4,) + vectors.shape, F32),
            dma((2, 2)),
            dma((2, 4)),
            dma((2, 4)),
            dma((2, 4, 3)),
            dma((2, 4)),
            dma((2, 4, 2)),
            dma((2, 2)),
            dma((3, 2)),
            dma((2, 6)),
        ],
        compiler_params=pltpu.CompilerParams(
            collective_id=3, has_side_effects=True, vmem_limit_bytes=60 << 20
        ),
        name="sum_products",
    )(*lefts, *rights, vectors)
    return sums, total


def on_blocks(
    hidden_states,
    text_states,
    self_gain,
    self_bias,
    query_key_value,
    self_output,
    cross_gain,
    cross_bias,
    cross_query,
    cross_memory,
    cross_output,
    final_gain,
    final_bias,
    expand_weight,
    contract_weight,
    output_cotangent,
):
    clips, frames, width = hidden_states.shape
    rows = clips * frames
    groups = lax.axis_size("seq")
    fsdp_count = lax.axis_size("fsdp")
    scale = HD ** (-0.5)
    entries = rows * groups * fsdp_count * width
    group_width = width // groups

    def by_group(value):
        return value.reshape(-1, 3, groups, group_width).transpose(0, 2, 1, 3).reshape(value.shape)

    def by_kind(value):
        return value.reshape(-1, groups, 3, group_width).transpose(0, 2, 1, 3).reshape(value.shape)

    gains = (self_gain, self_bias, cross_gain, cross_bias, final_gain, final_bias)
    early = (by_group(query_key_value), self_output)
    (qkv_whole, self_output_whole), vectors = gather_weights(early, pack_vectors(gains), 1)
    qkv_whole, expand_weight = lax.optimization_barrier((qkv_whole, expand_weight))
    part = expand_weight.shape[0] // groups
    expand_whole = lax.all_gather(
        lax.dynamic_slice_in_dim(expand_weight, lax.axis_index("seq") * part, part, 0),
        ("fsdp", "seq"),
        axis=0,
        tiled=True,
    )
    vectors = vectors[:, :6, : width // fsdp_count]
    gains = [vectors[:, i].reshape(width) for i in range(6)]

    hidden = hidden_states.reshape(rows, width).astype(F32)
    normed_one, norm_one_back = jax.vjp(layer_norm, hidden, gains[0], gains[1])
    normed_one = normed_one.astype(BF16)
    projected = product_blocks(normed_one, qkv_whole, groups)
    regrouped = lax.all_to_all(projected, "seq", split_axis=0, concat_axis=0, tiled=True)
    regrouped = regrouped.reshape(groups, clips, frames, 3 * group_width)
    context_heads, logsum = attention(regrouped, scale)
    context_heads = context_heads.reshape(groups, rows, group_width)
    context = lax.all_to_all(context_heads, "seq", split_axis=0, concat_axis=0, tiled=True)
    late = (cross_query, cross_memory, cross_output, contract_weight)
    context, late = lax.optimization_barrier((context, late))
    late, _ = gather_weights(late, None, 2)
    cross_query_whole, cross_memory_whole, cross_output_whole, contract_whole = late
    context = context.transpose(1, 0, 2).reshape(rows, width)
    attended = product(context, self_output_whole)
    first = hidden + attended
    normed_two, norm_two_back = jax.vjp(layer_norm, first, gains[2], gains[3])
    normed_two = normed_two.astype(BF16)
    cross_q = product(normed_two, cross_query_whole).astype(BF16).reshape(clips, frames, H, HD)
    text_rows = text_states.reshape(clips * TEXT, width)
    memory = product(text_rows, cross_memory_whole).astype(BF16).reshape(clips, TEXT, 2, H, HD)
    cross_keys = memory[:, :, 0]
    cross_values = memory[:, :, 1]
    cross_scores = (
        jnp.einsum("cqhd,ckhd->chqk", cross_q, cross_keys, preferred_element_type=F32) * scale
    )
    highest = jnp.max(cross_scores, axis=-1, keepdims=True)
    raised = jnp.exp(cross_scores - highest)
    cross_weights = raised / jnp.sum(raised, axis=-1, keepdims=True)
    cross_rounded = cross_weights.astype(BF16)
    cross_context = jnp.einsum(
        "chqk,ckhd->cqhd", cross_rounded, cross_values, preferred_element_type=F32
    )
    cross_context = cross_context.astype(BF16).reshape(rows, width)
    crossed = product(cross_context, cross_output_whole)
    second = first + crossed
    normed_three, norm_three_back = jax.vjp(layer_norm, second, gains[4], gains[5])
    normed_three = normed_three.astype(BF16)
    preact = product(normed_three, expand_whole)
    activated, gelu_back = jax.vjp(gelu_exact, preact)
    activated = activated.astype(BF16)
    upstream = output_cotangent.reshape(rows, width).astype(F32)
    grad_mixed = output_cotangent.reshape(rows, width)
    grad_activated = product_right(grad_mixed, contract_whole)
    grad_preact = gelu_back(grad_activated)[0].astype(BF16)
    grad_normed_three = product_right(grad_preact, expand_whole)
    grad_second, final_gain_term, final_bias_term = norm_three_back(grad_normed_three)
    grad_second = upstream + grad_second
    grad_crossed = grad_second.astype(BF16)
    grad_cross_context = (
        product_right(grad_crossed, cross_output_whole).astype(BF16).reshape(clips, frames, H, HD)
    )
    grad_cross_weights = jnp.einsum(
        "cqhd,ckhd->chqk", grad_cross_context, cross_values, preferred_element_type=F32
    )
    cross_inner = jnp.sum(cross_weights * grad_cross_weights, axis=-1, keepdims=True)
    grad_cross_scores = (cross_weights * (grad_cross_weights - cross_inner)).astype(BF16)
    grad_cross_q = (
        jnp.einsum("chqk,ckhd->cqhd", grad_cross_scores, cross_keys, preferred_element_type=F32)
        * scale
    )
    grad_cross_q = grad_cross_q.astype(BF16).reshape(rows, width)
    grad_cross_keys = (
        jnp.einsum("chqk,cqhd->ckhd", grad_cross_scores, cross_q, preferred_element_type=F32)
        * scale
    )
    grad_cross_values = jnp.einsum(
        "chqk,cqhd->ckhd", cross_rounded, grad_cross_context, preferred_element_type=F32
    )
    grad_memory = jnp.stack([grad_cross_keys, grad_cross_values], axis=2).reshape(
        clips * TEXT, 2 * width
    )
    grad_normed_two = product_right(grad_cross_q, cross_query_whole)
    grad_first, cross_gain_term, cross_bias_term = norm_two_back(grad_normed_two)
    grad_first = grad_second + grad_first
    grad_attended = grad_first.astype(BF16)
    grad_context = product_right(grad_attended, self_output_whole).astype(BF16)
    grad_context = grad_context.reshape(rows, groups, group_width).transpose(1, 0, 2)
    grad_heads = lax.all_to_all(grad_context, "seq", split_axis=0, concat_axis=0, tiled=True)
    grad_heads = grad_heads.reshape(groups, clips, frames, group_width)
    grad_regrouped = attention_back(regrouped, grad_heads, logsum, scale)
    grad_regrouped, activated = lax.optimization_barrier((grad_regrouped, activated))
    grad_regrouped = grad_regrouped.reshape(groups, rows, 3 * group_width)
    grad_projected = lax.all_to_all(grad_regrouped, "seq", split_axis=0, concat_axis=0, tiled=True)
    mixed = product(activated, contract_whole)
    output = second + mixed
    squares = jnp.stack(
        [
            jnp.sum(output * output),
            jnp.sum(attended * attended),
            jnp.sum(crossed * crossed),
            jnp.sum(mixed * mixed),
        ]
    )
    output = output.astype(BF16)
    grad_projected, output, squares = lax.optimization_barrier((grad_projected, output, squares))
    grad_projected = grad_projected.transpose(1, 0, 2).reshape(rows, 3 * width)
    grad_normed_one = product_right(grad_projected, qkv_whole)
    grad_hidden, gain_one_term, bias_one_term = norm_one_back(grad_normed_one)
    grad_hidden = grad_first + grad_hidden
    terms = jnp.stack(
        [
            gain_one_term,
            bias_one_term,
            cross_gain_term,
            cross_bias_term,
            final_gain_term,
            final_bias_term,
            jnp.pad(squares, (0, width - 4)),
            jnp.zeros_like(gain_one_term),
        ]
    )
    deep = lambda value: jnp.pad(value, ((0, rows - value.shape[0]), (0, 0)))
    gradients, totals = sum_products(
        [
            (activated, grad_mixed),
            (normed_three, grad_preact),
            (cross_context, grad_crossed),
            (normed_two, grad_cross_q),
            (deep(text_rows), deep(grad_memory.astype(BF16))),
            (context, grad_attended),
            (normed_one, grad_projected),
        ],
        terms,
    )
    gradients = [gradient.astype(F32) for gradient in gradients]
    layer_rms = jnp.sqrt(totals[6, :4] / entries)
    shard = width // fsdp_count
    vector_gradients = lax.dynamic_slice_in_dim(
        totals, lax.axis_index("fsdp") * shard, shard, 1
    )
    return (
        output.reshape(clips, frames, width),
        grad_hidden.reshape(clips, frames, width),
        vector_gradients[0],
        vector_gradients[1],
        by_kind(gradients[6]),
        gradients[5],
        vector_gradients[2],
        vector_gradients[3],
        gradients[3],
        gradients[4],
        gradients[2],
        vector_gradients[4],
        vector_gradients[5],
        gradients[1],
        gradients[0],
        layer_rms,
    )


def solution(mesh):
    shape = dict(mesh.shape)
    blocks = shape["seq"] == 4 and shape["fsdp"] == 8
    return jax.shard_map(
        on_blocks if blocks else on_any_mesh,
        mesh=mesh,
        in_specs=(
            P("fsdp", "seq", None),
            P("fsdp", None, None),
            P("fsdp"),
            P("fsdp"),
            P("fsdp", None),
            P("fsdp", None),
            P("fsdp"),
            P("fsdp"),
            P("fsdp", None),
            P("fsdp", None),
            P("fsdp", None),
            P("fsdp"),
            P("fsdp"),
            P("fsdp", None),
            P("fsdp", None),
            P("fsdp", "seq", None),
        ),
        out_specs=(
            P("fsdp", "seq", None),
            P("fsdp", "seq", None),
            P("fsdp"),
            P("fsdp"),
            P("fsdp", None),
            P("fsdp", None),
            P("fsdp"),
            P("fsdp"),
            P("fsdp", None),
            P("fsdp", None),
            P("fsdp", None),
            P("fsdp"),
            P("fsdp"),
            P("fsdp", None),
            P("fsdp", None),
            P(),
        ),
        check_vma=False,
    )
```

```python
import functools

import jax
import jax.numpy as jnp
from jax import lax
from jax.experimental import pallas as pl
from jax.experimental.pallas import tpu as pltpu
from jax.sharding import PartitionSpec as P

H = 24
HD = 64
TEXT = 64

NEGATIVE = -1e30
BF16 = jnp.bfloat16
F32 = jnp.float32
MESH = pl.DeviceIdType.MESH


def layer_norm(values, gain, offset):
    center = values - jnp.mean(values, axis=-1, keepdims=True)
    spread = jnp.mean(center * center, axis=-1, keepdims=True)
    return center * lax.rsqrt(spread + 1e-05) * gain + offset


def gelu_exact(values):
    return jax.nn.gelu(values, approximate=False)


def product(left, right):
    return jnp.dot(left, right, preferred_element_type=jnp.float32)


def product_left(left, right):
    return lax.dot_general(
        left, right, (((0,), (0,)), ((), ())), preferred_element_type=jnp.float32
    )


def product_right(left, right):
    return lax.dot_general(
        left, right, (((1,), (1,)), ((), ())), preferred_element_type=jnp.float32
    )


def causal_forward(queries, keys, values, rows_block, scale):
    clips, length, heads_local, head_width = queries.shape
    count = length // rows_block
    columns = jnp.arange(length, dtype=jnp.int32)

    def one_block(start):
        block = lax.dynamic_slice_in_dim(queries, start, rows_block, 1)
        scores = (
            jnp.einsum("cqhd,ckhd->chqk", block, keys, preferred_element_type=jnp.float32) * scale
        )
        positions = start + jnp.arange(rows_block, dtype=jnp.int32)
        allowed = columns[None, :] <= positions[:, None]
        scores = jnp.where(allowed, scores, NEGATIVE)
        highest = jnp.max(scores, axis=-1, keepdims=True)
        raised = jnp.exp(scores - highest)
        summed = jnp.sum(raised, axis=-1, keepdims=True)
        weights = (raised / summed).astype(jnp.bfloat16)
        result = jnp.einsum("chqk,ckhd->cqhd", weights, values, preferred_element_type=jnp.float32)
        return (result.astype(jnp.bfloat16), (highest + jnp.log(summed))[..., 0])

    starts = jnp.arange(count, dtype=jnp.int32) * rows_block
    results, logsum = lax.map(one_block, starts)
    results = jnp.moveaxis(results, 0, 1).reshape(clips, length, heads_local * head_width)
    return (results, logsum)


def causal_backward(queries, keys, values, logsum, grad_heads, rows_block, scale):
    clips, length, heads_local, head_width = queries.shape
    count = length // rows_block
    columns = jnp.arange(length, dtype=jnp.int32)
    starts = jnp.arange(count, dtype=jnp.int32) * rows_block

    def one_block(carry, inputs):
        grad_keys, grad_values = carry
        start, block_logsum = inputs
        block = lax.dynamic_slice_in_dim(queries, start, rows_block, 1)
        block_grad = lax.dynamic_slice_in_dim(grad_heads, start, rows_block, 1)
        scores = (
            jnp.einsum("cqhd,ckhd->chqk", block, keys, preferred_element_type=jnp.float32) * scale
        )
        positions = start + jnp.arange(rows_block, dtype=jnp.int32)
        allowed = columns[None, :] <= positions[:, None]
        scores = jnp.where(allowed, scores, NEGATIVE)
        weights = jnp.exp(scores - block_logsum[..., None])
        rounded = weights.astype(jnp.bfloat16)
        grad_weights = jnp.einsum(
            "cqhd,ckhd->chqk", block_grad, values, preferred_element_type=jnp.float32
        )
        inner = jnp.sum(weights * grad_weights, axis=-1, keepdims=True)
        grad_scores = (weights * (grad_weights - inner)).astype(jnp.bfloat16)
        grad_query = (
            jnp.einsum("chqk,ckhd->cqhd", grad_scores, keys, preferred_element_type=jnp.float32)
            * scale
        )
        grad_keys = (
            grad_keys
            + jnp.einsum("chqk,cqhd->ckhd", grad_scores, block, preferred_element_type=jnp.float32)
            * scale
        )
        grad_values = grad_values + jnp.einsum(
            "chqk,cqhd->ckhd", rounded, block_grad, preferred_element_type=jnp.float32
        )
        return ((grad_keys, grad_values), grad_query.astype(jnp.bfloat16))

    zeros = jnp.zeros(queries.shape, jnp.float32)
    (grad_keys, grad_values), grad_queries = lax.scan(one_block, (zeros, zeros), (starts, logsum))
    local_width = heads_local * head_width
    grad_queries = jnp.moveaxis(grad_queries, 0, 1).reshape(clips, length, local_width)
    grad_keys = grad_keys.astype(jnp.bfloat16).reshape(clips, length, local_width)
    grad_values = grad_values.astype(jnp.bfloat16).reshape(clips, length, local_width)
    return jnp.stack([grad_queries, grad_keys, grad_values], axis=2)


def on_any_mesh(
    hidden_states,
    text_states,
    self_gain,
    self_bias,
    query_key_value,
    self_output,
    cross_gain,
    cross_bias,
    cross_query,
    cross_memory,
    cross_output,
    final_gain,
    final_bias,
    expand_weight,
    contract_weight,
    output_cotangent,
):
    clips, frames, width = hidden_states.shape
    rows = clips * frames
    groups = lax.axis_size("seq")
    fsdp_count = lax.axis_size("fsdp")
    heads_local = H // groups
    length = frames * groups
    rows_block = min(512, length)
    scale = HD ** (-0.5)
    entries = rows * groups * fsdp_count * width
    self_set = (
        lax.all_gather(self_gain, "fsdp", axis=0, tiled=True),
        lax.all_gather(self_bias, "fsdp", axis=0, tiled=True),
        lax.all_gather(query_key_value, "fsdp", axis=0, tiled=True),
        lax.all_gather(self_output, "fsdp", axis=0, tiled=True),
    )
    hidden = hidden_states.reshape(rows, width).astype(jnp.float32)
    normed_one, norm_one_back = jax.vjp(
        layer_norm, hidden, self_set[0].astype(jnp.float32), self_set[1].astype(jnp.float32)
    )
    normed_one = normed_one.astype(jnp.bfloat16)
    projected = (
        product(normed_one, self_set[2]).astype(jnp.bfloat16).reshape(clips, frames, 3, width)
    )
    regrouped = lax.all_to_all(projected, "seq", split_axis=3, concat_axis=1, tiled=True)
    regrouped = regrouped.reshape(clips, length, 3, heads_local, HD)
    queries = regrouped[:, :, 0]
    keys = regrouped[:, :, 1]
    values = regrouped[:, :, 2]
    context_heads, logsum = causal_forward(queries, keys, values, rows_block, scale)
    context = lax.all_to_all(context_heads, "seq", split_axis=1, concat_axis=2, tiled=True).reshape(
        rows, width
    )
    attended = product(context, self_set[3])
    first = hidden + attended
    rest_set = (
        lax.all_gather(cross_gain, "fsdp", axis=0, tiled=True),
        lax.all_gather(cross_bias, "fsdp", axis=0, tiled=True),
        lax.all_gather(cross_query, "fsdp", axis=0, tiled=True),
        lax.all_gather(cross_memory, "fsdp", axis=0, tiled=True),
        lax.all_gather(cross_output, "fsdp", axis=0, tiled=True),
        lax.all_gather(final_gain, "fsdp", axis=0, tiled=True),
        lax.all_gather(final_bias, "fsdp", axis=0, tiled=True),
        lax.all_gather(expand_weight, "fsdp", axis=0, tiled=True),
        lax.all_gather(contract_weight, "fsdp", axis=0, tiled=True),
    )
    normed_two, norm_two_back = jax.vjp(
        layer_norm, first, rest_set[0].astype(jnp.float32), rest_set[1].astype(jnp.float32)
    )
    normed_two = normed_two.astype(jnp.bfloat16)
    cross_q = product(normed_two, rest_set[2]).astype(jnp.bfloat16).reshape(clips, frames, H, HD)
    text_rows = text_states.reshape(clips * TEXT, width)
    memory = product(text_rows, rest_set[3]).astype(jnp.bfloat16).reshape(clips, TEXT, 2, H, HD)
    cross_keys = memory[:, :, 0]
    cross_values = memory[:, :, 1]
    cross_scores = (
        jnp.einsum("cqhd,ckhd->chqk", cross_q, cross_keys, preferred_element_type=jnp.float32)
        * scale
    )
    highest = jnp.max(cross_scores, axis=-1, keepdims=True)
    raised = jnp.exp(cross_scores - highest)
    cross_weights = raised / jnp.sum(raised, axis=-1, keepdims=True)
    cross_rounded = cross_weights.astype(jnp.bfloat16)
    cross_context = jnp.einsum(
        "chqk,ckhd->cqhd", cross_rounded, cross_values, preferred_element_type=jnp.float32
    )
    cross_context = cross_context.astype(jnp.bfloat16).reshape(rows, width)
    crossed = product(cross_context, rest_set[4])
    second = first + crossed
    normed_three, norm_three_back = jax.vjp(
        layer_norm, second, rest_set[5].astype(jnp.float32), rest_set[6].astype(jnp.float32)
    )
    normed_three = normed_three.astype(jnp.bfloat16)
    preact = product(normed_three, rest_set[7])
    activated, gelu_back = jax.vjp(gelu_exact, preact)
    activated = activated.astype(jnp.bfloat16)
    mixed = product(activated, rest_set[8])
    output = second + mixed
    squares = jnp.stack(
        [
            jnp.sum(output * output),
            jnp.sum(attended * attended),
            jnp.sum(crossed * crossed),
            jnp.sum(mixed * mixed),
        ]
    )
    square_totals = lax.psum(squares, ("seq", "fsdp"))
    back_rest = (
        lax.all_gather(cross_gain, "fsdp", axis=0, tiled=True),
        lax.all_gather(cross_bias, "fsdp", axis=0, tiled=True),
        lax.all_gather(cross_query, "fsdp", axis=0, tiled=True),
        lax.all_gather(cross_memory, "fsdp", axis=0, tiled=True),
        lax.all_gather(cross_output, "fsdp", axis=0, tiled=True),
        lax.all_gather(final_gain, "fsdp", axis=0, tiled=True),
        lax.all_gather(final_bias, "fsdp", axis=0, tiled=True),
        lax.all_gather(expand_weight, "fsdp", axis=0, tiled=True),
        lax.all_gather(contract_weight, "fsdp", axis=0, tiled=True),
    )
    upstream = output_cotangent.reshape(rows, width).astype(jnp.float32)
    grad_mixed = upstream.astype(jnp.bfloat16)
    contract_term = product_left(activated, grad_mixed)
    grad_activated = product_right(grad_mixed, back_rest[8])
    grad_preact = gelu_back(grad_activated)[0].astype(jnp.bfloat16)
    expand_term = product_left(normed_three, grad_preact)
    grad_normed_three = product_right(grad_preact, back_rest[7])
    grad_second, final_gain_term, final_bias_term = norm_three_back(grad_normed_three)
    grad_second = upstream + grad_second
    grad_crossed = grad_second.astype(jnp.bfloat16)
    cross_output_term = product_left(cross_context, grad_crossed)
    grad_cross_context = (
        product_right(grad_crossed, back_rest[4]).astype(jnp.bfloat16).reshape(clips, frames, H, HD)
    )
    grad_cross_weights = jnp.einsum(
        "cqhd,ckhd->chqk", grad_cross_context, cross_values, preferred_element_type=jnp.float32
    )
    cross_inner = jnp.sum(cross_weights * grad_cross_weights, axis=-1, keepdims=True)
    grad_cross_scores = (cross_weights * (grad_cross_weights - cross_inner)).astype(jnp.bfloat16)
    grad_cross_q = (
        jnp.einsum(
            "chqk,ckhd->cqhd", grad_cross_scores, cross_keys, preferred_element_type=jnp.float32
        )
        * scale
    )
    grad_cross_q = grad_cross_q.astype(jnp.bfloat16).reshape(rows, width)
    grad_cross_keys = (
        jnp.einsum(
            "chqk,cqhd->ckhd", grad_cross_scores, cross_q, preferred_element_type=jnp.float32
        )
        * scale
    )
    grad_cross_values = jnp.einsum(
        "chqk,cqhd->ckhd", cross_rounded, grad_cross_context, preferred_element_type=jnp.float32
    )
    grad_memory = jnp.stack([grad_cross_keys, grad_cross_values], axis=2).reshape(
        clips * TEXT, 2 * width
    )
    memory_term = lax.dot_general(
        text_rows.astype(jnp.float32),
        grad_memory,
        (((0,), (0,)), ((), ())),
        precision=lax.Precision.HIGHEST,
        preferred_element_type=jnp.float32,
    )
    query_term = product_left(normed_two, grad_cross_q)
    grad_normed_two = product_right(grad_cross_q, back_rest[2])
    grad_first, cross_gain_term, cross_bias_term = norm_two_back(grad_normed_two)
    grad_first = grad_second + grad_first
    rest_sums = (
        lax.psum_scatter(
            cross_gain_term.astype(jnp.bfloat16), "fsdp", scatter_dimension=0, tiled=True
        ).astype(jnp.float32),
        lax.psum_scatter(
            cross_bias_term.astype(jnp.bfloat16), "fsdp", scatter_dimension=0, tiled=True
        ).astype(jnp.float32),
        lax.psum_scatter(
            query_term.astype(jnp.bfloat16), "fsdp", scatter_dimension=0, tiled=True
        ).astype(jnp.float32),
        lax.psum_scatter(
            memory_term.astype(jnp.bfloat16), "fsdp", scatter_dimension=0, tiled=True
        ).astype(jnp.float32),
        lax.psum_scatter(
            cross_output_term.astype(jnp.bfloat16), "fsdp", scatter_dimension=0, tiled=True
        ).astype(jnp.float32),
        lax.psum_scatter(
            final_gain_term.astype(jnp.bfloat16), "fsdp", scatter_dimension=0, tiled=True
        ).astype(jnp.float32),
        lax.psum_scatter(
            final_bias_term.astype(jnp.bfloat16), "fsdp", scatter_dimension=0, tiled=True
        ).astype(jnp.float32),
        lax.psum_scatter(
            expand_term.astype(jnp.bfloat16), "fsdp", scatter_dimension=0, tiled=True
        ).astype(jnp.float32),
        lax.psum_scatter(
            contract_term.astype(jnp.bfloat16), "fsdp", scatter_dimension=0, tiled=True
        ).astype(jnp.float32),
    )
    back_self = (
        lax.all_gather(self_gain, "fsdp", axis=0, tiled=True),
        lax.all_gather(self_bias, "fsdp", axis=0, tiled=True),
        lax.all_gather(query_key_value, "fsdp", axis=0, tiled=True),
        lax.all_gather(self_output, "fsdp", axis=0, tiled=True),
    )
    grad_attended = grad_first.astype(jnp.bfloat16)
    self_output_term = product_left(context, grad_attended)
    grad_context = (
        product_right(grad_attended, back_self[3])
        .astype(jnp.bfloat16)
        .reshape(clips, frames, width)
    )
    grad_heads = lax.all_to_all(grad_context, "seq", split_axis=2, concat_axis=1, tiled=True)
    grad_heads = grad_heads.reshape(clips, length, heads_local, HD)
    grad_regrouped = causal_backward(queries, keys, values, logsum, grad_heads, rows_block, scale)
    grad_projected = lax.all_to_all(
        grad_regrouped, "seq", split_axis=1, concat_axis=3, tiled=True
    ).reshape(rows, 3 * width)
    qkv_term = product_left(normed_one, grad_projected)
    grad_normed_one = product_right(grad_projected, back_self[2])
    grad_hidden, gain_one_term, bias_one_term = norm_one_back(grad_normed_one)
    grad_hidden = grad_first + grad_hidden
    self_sums = (
        lax.psum_scatter(
            gain_one_term.astype(jnp.bfloat16), "fsdp", scatter_dimension=0, tiled=True
        ).astype(jnp.float32),
        lax.psum_scatter(
            bias_one_term.astype(jnp.bfloat16), "fsdp", scatter_dimension=0, tiled=True
        ).astype(jnp.float32),
        lax.psum_scatter(
            qkv_term.astype(jnp.bfloat16), "fsdp", scatter_dimension=0, tiled=True
        ).astype(jnp.float32),
        lax.psum_scatter(
            self_output_term.astype(jnp.bfloat16), "fsdp", scatter_dimension=0, tiled=True
        ).astype(jnp.float32),
    )
    finals = (
        lax.psum(self_sums[0].astype(jnp.bfloat16), "seq").astype(jnp.float32),
        lax.psum(self_sums[1].astype(jnp.bfloat16), "seq").astype(jnp.float32),
        lax.psum(self_sums[2].astype(jnp.bfloat16), "seq").astype(jnp.float32),
        lax.psum(self_sums[3].astype(jnp.bfloat16), "seq").astype(jnp.float32),
        lax.psum(rest_sums[0].astype(jnp.bfloat16), "seq").astype(jnp.float32),
        lax.psum(rest_sums[1].astype(jnp.bfloat16), "seq").astype(jnp.float32),
        lax.psum(rest_sums[2].astype(jnp.bfloat16), "seq").astype(jnp.float32),
        lax.psum(rest_sums[3].astype(jnp.bfloat16), "seq").astype(jnp.float32),
        lax.psum(rest_sums[4].astype(jnp.bfloat16), "seq").astype(jnp.float32),
        lax.psum(rest_sums[5].astype(jnp.bfloat16), "seq").astype(jnp.float32),
        lax.psum(rest_sums[6].astype(jnp.bfloat16), "seq").astype(jnp.float32),
        lax.psum(rest_sums[7].astype(jnp.bfloat16), "seq").astype(jnp.float32),
        lax.psum(rest_sums[8].astype(jnp.bfloat16), "seq").astype(jnp.float32),
    )
    layer_rms = jnp.sqrt(square_totals / entries)
    return (
        output.astype(jnp.bfloat16).reshape(clips, frames, width),
        grad_hidden.reshape(clips, frames, width),
        finals[0],
        finals[1],
        finals[2],
        finals[3],
        finals[4],
        finals[5],
        finals[6],
        finals[7],
        finals[8],
        finals[9],
        finals[10],
        finals[11],
        finals[12],
        layer_rms,
    )


CORE_PAIRS = [(0, 1), (1, 0), (2, 3), (3, 2)]
X_PAIRS = [(0, 2), (2, 0), (1, 3), (3, 1)]
Y_PAIRS = [(i, i ^ 1) for i in range(8)]
Z_SHIFTS = [[(i, (i + 2 * k) % 8) for i in range(8)] for k in (1, 2, 3)]


CHUNK = 768


def gather_kernel(plan, has_vectors, *refs):
    weights = len({entry[0] for entry in plan})
    inputs = refs[:weights]
    refs = refs[weights:]
    if has_vectors:
        vector_in, refs = refs[0], refs[1:]
    outputs = refs[:weights]
    refs = refs[weights:]
    if has_vectors:
        vector_out, refs = refs[0], refs[1:]
    zs_sem, zr_sem, ys_sem, yr_sem, xs_sem, xr_sem, cs_sem, cr_sem, own_sem, vs_sem, vr_sem = refs
    seq = lax.axis_index("seq")
    fsdp = lax.axis_index("fsdp")
    x, c = seq // 2, seq % 2
    z, y = fsdp // 2, fsdp % 2
    x_seq = 2 * (1 - x) + c
    c_seq = 2 * x + 1 - c
    y_fsdp = 2 * z + 1 - y

    def at_z(k):
        return 2 * ((z + k) % 4) + y

    barrier = pltpu.get_barrier_semaphore()
    partners = [(x_seq, fsdp), (c_seq, fsdp), (seq, y_fsdp)] + [(seq, at_z(k)) for k in (1, 2, 3)]
    if has_vectors:
        partners += [(seq, 2 * ((z + k) % 4) + 1 - y) for k in (1, 2, 3)]
    for partner in partners:
        pl.semaphore_signal(barrier, inc=1, device_id=partner, device_id_type=MESH)
    pl.semaphore_wait(barrier, len(partners))

    if has_vectors:
        vector_sends = []
        for k in range(1, 8):
            copy = pltpu.make_async_remote_copy(
                src_ref=vector_in,
                dst_ref=vector_out.at[fsdp],
                send_sem=vs_sem.at[k],
                recv_sem=vr_sem.at[k],
                device_id=(seq, (fsdp + k) % 8),
                device_id_type=MESH,
            )
            copy.start()
            vector_sends.append(copy)
        own = pltpu.make_async_copy(vector_in, vector_out.at[fsdp], vs_sem.at[0])
        own.start()

    def part(entry):
        weight, block, column, split = entry
        first = 2 * c + x if split else 2 * c
        count = 1 if split else 2
        return weight, block, pl.ds(column, CHUNK), pl.ds(first, count)

    def remote(region, send, recv, device):
        return pltpu.make_async_remote_copy(
            src_ref=region,
            dst_ref=region,
            send_sem=send,
            recv_sem=recv,
            device_id=device,
            device_id_type=MESH,
        )

    sends = []

    def send(copy):
        copy.start()
        sends.append(copy)

    def start_z(i):
        weight, block, columns, mine = part(plan[i])
        source = inputs[weight].at[block, mine, :, columns]
        target = outputs[weight].at[z, y, block, mine, :, columns]
        for k in (1, 2, 3):
            copy = pltpu.make_async_remote_copy(
                src_ref=source,
                dst_ref=target,
                send_sem=zs_sem.at[i, k],
                recv_sem=zr_sem.at[i, k],
                device_id=(seq, at_z(k)),
                device_id_type=MESH,
            )
            send(copy)
        pltpu.make_async_copy(source, target, own_sem.at[i]).start()

    def start_y(i):
        weight, block, columns, mine = part(plan[i])
        output = outputs[weight]
        for k in (1, 2, 3):
            region = output.at[(z + 4 - k) % 4, y, block, mine, :, columns]
            remote(region, zs_sem.at[i, k], zr_sem.at[i, k], (seq, at_z(k))).wait_recv()
        source = inputs[weight].at[block, mine, :, columns]
        target = output.at[z, y, block, mine, :, columns]
        pltpu.make_async_copy(source, target, own_sem.at[i]).wait()
        region = output.at[:, y, block, mine, :, columns]
        send(remote(region, ys_sem.at[i], yr_sem.at[i], (seq, y_fsdp)))

    def start_x(i):
        weight, block, columns, mine = part(plan[i])
        output = outputs[weight]
        region = output.at[:, 1 - y, block, mine, :, columns]
        remote(region, ys_sem.at[i], yr_sem.at[i], (seq, y_fsdp)).wait_recv()
        region = output.at[:, :, block, mine, :, columns]
        if plan[i][3]:
            send(remote(region, xs_sem.at[i], xr_sem.at[i], (x_seq, fsdp)))
        send(remote(region, cs_sem.at[i, 0], cr_sem.at[i, 0], (c_seq, fsdp)))

    def start_core(i):
        if plan[i][3]:
            weight, block, columns, _ = part(plan[i])
            region = outputs[weight].at[:, :, block, pl.ds(2 * c + 1 - x, 1), :, columns]
            remote(region, xs_sem.at[i], xr_sem.at[i], (x_seq, fsdp)).wait_recv()
            send(remote(region, cs_sem.at[i, 1], cr_sem.at[i, 1], (c_seq, fsdp)))

    def finish(i):
        weight, block, columns, _ = part(plan[i])
        other = 2 * (1 - c)
        output = outputs[weight]
        if plan[i][3]:
            for j, quarter in ((0, other + x), (1, other + 1 - x)):
                region = output.at[:, :, block, pl.ds(quarter, 1), :, columns]
                remote(region, cs_sem.at[i, j], cr_sem.at[i, j], (c_seq, fsdp)).wait_recv()
        else:
            region = output.at[:, :, block, pl.ds(other, 2), :, columns]
            remote(region, cs_sem.at[i, 0], cr_sem.at[i, 0], (c_seq, fsdp)).wait_recv()

    chunks = len(plan)
    ahead = 3
    for i in range(min(ahead, chunks)):
        start_z(i)
    for t in range(chunks + 2):
        if t + ahead < chunks:
            start_z(t + ahead)
        if t < chunks:
            start_y(t)
        if 0 <= t - 1 < chunks:
            start_x(t - 1)
        if 0 <= t - 2 < chunks:
            start_core(t - 2)
    for i in range(chunks):
        finish(i)
    for copy in sends:
        copy.wait_send()
    if has_vectors:
        own.wait()
        for k in range(1, 8):
            vector_sends[k - 1].wait_send()
            region = vector_out.at[(fsdp + 8 - k) % 8]
            remote(region, vs_sem.at[k], vr_sem.at[k], (seq, (fsdp + k) % 8)).wait_recv()


def gather_plan(shapes):
    places = [
        (weight, block, column)
        for weight, (rows, columns) in enumerate(shapes)
        for block in range(rows // 192)
        for column in range(0, columns, CHUNK)
    ]
    return tuple(place + ((len(places) - 1 - i) % 3 != 0,) for i, place in enumerate(places))


def gather_weights(shards, vectors, collective_id):
    shapes = [shard.shape for shard in shards]
    plan = gather_plan(shapes)
    chunks = len(plan)
    inputs = [shard.reshape(rows // 192, 4, 48, columns) for shard, (rows, columns) in zip(shards, shapes)]
    out_shapes = [
        jax.ShapeDtypeStruct((4, 2, rows // 192, 4, 48, columns), BF16) for rows, columns in shapes
    ]
    if vectors is not None:
        inputs.append(vectors)
        out_shapes.append(jax.ShapeDtypeStruct((8,) + vectors.shape, vectors.dtype))
    anywhere = pl.BlockSpec(memory_space=pl.ANY)
    dma = pltpu.SemaphoreType.DMA
    results = pl.pallas_call(
        functools.partial(gather_kernel, plan, vectors is not None),
        out_shape=out_shapes,
        in_specs=[anywhere] * len(inputs),
        out_specs=[anywhere] * len(out_shapes),
        scratch_shapes=[
            dma((chunks, 4)),
            dma((chunks, 4)),
            dma((chunks,)),
            dma((chunks,)),
            dma((chunks,)),
            dma((chunks,)),
            dma((chunks, 2)),
            dma((chunks, 2)),
            dma((chunks,)),
            dma((8,)),
            dma((8,)),
        ],
        compiler_params=pltpu.CompilerParams(collective_id=collective_id, has_side_effects=True),
        name="gather_weights",
    )(*inputs)
    whole = [result.reshape(8 * rows, columns) for result, (rows, columns) in zip(results, shapes)]
    return whole, results[-1]


def gather_quarters(shard):
    part = shard.shape[0] // lax.axis_size("seq")
    mine = lax.dynamic_slice_in_dim(shard, lax.axis_index("seq") * part, part, 0)
    return lax.all_gather(mine, ("fsdp", "seq"), axis=0, tiled=True)


def pack_vectors(vectors):
    stacked = jnp.stack([vector.astype(F32) for vector in vectors])
    return jnp.pad(stacked, ((0, 8 - stacked.shape[0]), (0, (-stacked.shape[1]) % 128)))


def blocks_kernel(left, *refs):
    *rights, out = refs
    width = rights[0].shape[1]
    for kind, right in enumerate(rights):
        out[0, :, kind * width : (kind + 1) * width] = jnp.dot(
            left[...], right[...], preferred_element_type=F32
        ).astype(BF16)


def product_blocks(left, right, kinds, groups):
    rows, depth = left.shape
    width = right.shape[1] // (kinds * groups)
    spec = lambda kind: pl.BlockSpec((depth, width), lambda i: (0, kind * groups + i))
    return pl.pallas_call(
        blocks_kernel,
        grid=(groups,),
        out_shape=jax.ShapeDtypeStruct((groups, rows, kinds * width), BF16),
        in_specs=[pl.BlockSpec((rows, depth), lambda i: (0, 0))] + [spec(k) for k in range(kinds)],
        out_specs=pl.BlockSpec((1, rows, kinds * width), lambda i: (i, 0, 0)),
        compiler_params=pltpu.CompilerParams(vmem_limit_bytes=48 << 20),
        cost_estimate=pl.CostEstimate(
            flops=2 * rows * right.size,
            bytes_accessed=2 * (rows * depth + right.size + rows * right.shape[1]),
            transcendentals=0,
        ),
        name="product_blocks",
    )(left, *[right] * kinds)


QUERIES = 256


def both_heads(value):
    lane = lax.broadcasted_iota(jnp.int32, value.shape, 1)
    zero = jnp.zeros_like(value)
    return jnp.where(lane < HD, value, zero), jnp.where(lane < HD, zero, value)


def across(left, right):
    return lax.dot_general(left, right, (((1,), (1,)), ((), ())), preferred_element_type=F32)


def down(left, right):
    return lax.dot_general(left, right, (((0,), (0,)), ((), ())), preferred_element_type=F32)


def join_heads(pair):
    row = lax.broadcasted_iota(jnp.int32, pair[0].shape, 0)
    return jnp.where(row < HD, pair[0], pair[1])


def key_parts(block):
    return ([(0, block * QUERIES, False)] if block else []) + [
        (block * QUERIES, (block + 1) * QUERIES, True)
    ]


def masked_scores(keys, queries, diagonal):
    scores = across(keys, queries)
    if diagonal:
        key = lax.broadcasted_iota(jnp.int32, scores.shape, 0)
        query = lax.broadcasted_iota(jnp.int32, scores.shape, 1)
        scores = jnp.where(key <= query, scores, NEGATIVE)
    return scores


def attention_kernel(scale, q_ref, k_ref, v_ref, out_ref, logsum_ref):
    blocks = q_ref.shape[0] * q_ref.shape[2] // QUERIES
    k = k_ref[:, 0].reshape(-1, 2 * HD)
    v = v_ref[:, 0].reshape(-1, 2 * HD)
    for block in range(blocks):
        rows = slice(block * QUERIES, (block + 1) * QUERIES)
        queries = both_heads((q_ref[block, 0].astype(F32) * scale).astype(BF16))
        outs = []
        for head in range(2):
            parts = key_parts(block)
            scores = [masked_scores(k[a:b], queries[head], diagonal) for a, b, diagonal in parts]
            highest = functools.reduce(
                jnp.maximum, [jnp.max(part, axis=0, keepdims=True) for part in scores]
            )
            raised = [jnp.exp(part - highest) for part in scores]
            summed = sum(jnp.sum(part, axis=0, keepdims=True) for part in raised)
            total = sum(
                down(v[a:b], part.astype(BF16)) for (a, b, _), part in zip(parts, raised)
            )
            outs.append(total / summed)
            logsum_ref[0, 0, head : head + 1, rows] = highest + jnp.log(summed)
        out_ref[block, 0] = join_heads(outs).T.astype(BF16)


def attention(qkv, scale):
    blocks, clips, frames, width = qkv.shape
    pairs = width // (3 * 2 * HD)
    length = blocks * frames
    spec = lambda offset: pl.BlockSpec(
        (blocks, 1, frames, 2 * HD), lambda clip, pair: (0, clip, 0, offset + pair)
    )
    return pl.pallas_call(
        functools.partial(attention_kernel, scale),
        grid=(clips, pairs),
        out_shape=(
            jax.ShapeDtypeStruct((blocks, clips, frames, pairs * 2 * HD), BF16),
            jax.ShapeDtypeStruct((clips, pairs, 2, length), F32),
        ),
        in_specs=[spec(0), spec(pairs), spec(2 * pairs)],
        out_specs=(
            spec(0),
            pl.BlockSpec((1, 1, 2, length), lambda clip, pair: (clip, pair, 0, 0)),
        ),
        compiler_params=pltpu.CompilerParams(vmem_limit_bytes=48 << 20),
        cost_estimate=pl.CostEstimate(
            flops=clips * pairs * 2 * 4 * length * length * 2 * HD,
            bytes_accessed=4 * clips * pairs * length * 2 * HD * 2,
            transcendentals=clips * pairs * 2 * length * length,
        ),
        name="attention",
    )(qkv, qkv, qkv)


def attention_back_kernel(
    scale, q_ref, k_ref, v_ref, grad_ref, logsum_ref, out_ref, grad_keys, grad_values
):
    blocks = q_ref.shape[0] * q_ref.shape[2] // QUERIES
    frames = q_ref.shape[2]
    pair = pl.program_id(1)
    group = pl.num_programs(1) * 2 * HD
    k = k_ref[:, 0].reshape(-1, 2 * HD)
    v = v_ref[:, 0].reshape(-1, 2 * HD)

    def columns(kind):
        return pl.ds(pl.multiple_of(kind * group + pair * 2 * HD, 2 * HD), 2 * HD)

    for block in range(blocks):
        rows = slice(block * QUERIES, (block + 1) * QUERIES)
        queries = both_heads((q_ref[block, 0].astype(F32) * scale).astype(BF16))
        grads = both_heads(grad_ref[block, 0])
        parts = key_parts(block)
        query_grads = []
        held = [[], []]
        for head in range(2):
            logsum = logsum_ref[0, 0, head : head + 1, rows]
            weights, weighted = [], []
            for a, b, diagonal in parts:
                weight = jnp.exp(masked_scores(k[a:b], queries[head], diagonal) - logsum)
                weights.append(weight)
                weighted.append(weight * across(v[a:b], grads[head]))
            inner = sum(jnp.sum(part, axis=0, keepdims=True) for part in weighted)
            changes = [
                (term - weight * inner).astype(BF16) for term, weight in zip(weighted, weights)
            ]
            query_grads.append(sum(down(k[a:b], part) for (a, b, _), part in zip(parts, changes)))
            held[head] = [(weight.astype(BF16), change) for weight, change in zip(weights, changes)]
        out_ref[block, 0, :, columns(0)] = (join_heads(query_grads).T * scale).astype(BF16)
        for j, (a, b, diagonal) in enumerate(parts):
            value_term = sum(
                jnp.dot(held[head][j][0], grads[head], preferred_element_type=F32)
                for head in range(2)
            )
            key_term = sum(
                jnp.dot(held[head][j][1], queries[head], preferred_element_type=F32)
                for head in range(2)
            )
            if diagonal:
                grad_values[a:b] = value_term
                grad_keys[a:b] = key_term
            else:
                grad_values[a:b] += value_term
                grad_keys[a:b] += key_term
    out_ref[:, 0, :, columns(1)] = grad_keys[...].reshape(-1, frames, 2 * HD).astype(BF16)
    out_ref[:, 0, :, columns(2)] = grad_values[...].reshape(-1, frames, 2 * HD).astype(BF16)


def attention_back(qkv, grad, logsum, scale):
    blocks, clips, frames, width = qkv.shape
    pairs = width // (3 * 2 * HD)
    length = blocks * frames
    spec = lambda offset: pl.BlockSpec(
        (blocks, 1, frames, 2 * HD), lambda clip, pair: (0, clip, 0, offset + pair)
    )
    return pl.pallas_call(
        functools.partial(attention_back_kernel, scale),
        grid=(clips, pairs),
        out_shape=jax.ShapeDtypeStruct(qkv.shape, BF16),
        in_specs=[
            spec(0),
            spec(pairs),
            spec(2 * pairs),
            spec(0),
            pl.BlockSpec((1, 1, 2, length), lambda clip, pair: (clip, pair, 0, 0)),
        ],
        out_specs=pl.BlockSpec((blocks, 1, frames, width), lambda clip, pair: (0, clip, 0, 0)),
        scratch_shapes=[pltpu.VMEM((length, 2 * HD), F32), pltpu.VMEM((length, 2 * HD), F32)],
        compiler_params=pltpu.CompilerParams(vmem_limit_bytes=48 << 20),
        cost_estimate=pl.CostEstimate(
            flops=clips * pairs * 2 * 10 * length * length * 2 * HD,
            bytes_accessed=7 * clips * pairs * length * 2 * HD * 2,
            transcendentals=clips * pairs * 2 * length * length,
        ),
        name="attention_back",
    )(qkv, qkv, qkv, grad, logsum)


def text_weights(scale, queries, keys):
    scores = across(keys, queries)
    raised = jnp.exp(scores - jnp.max(scores, axis=0, keepdims=True))
    return raised / jnp.sum(raised, axis=0, keepdims=True)


def pair_columns(pair):
    return slice(pair * 2 * HD, (pair + 1) * 2 * HD)


def text_attention_kernel(scale, q_ref, memory_ref, out_ref):
    pairs = q_ref.shape[1] // (2 * HD)
    for pair in range(pairs):
        queries = both_heads((q_ref[:, pair_columns(pair)].astype(F32) * scale).astype(BF16))
        k = memory_ref[:, pair_columns(pair)]
        v = memory_ref[:, pair_columns(pairs + pair)]
        outs = [down(v, text_weights(scale, part, k).astype(BF16)) for part in queries]
        out_ref[:, pair_columns(pair)] = join_heads(outs).T.astype(BF16)


def text_attention_back_kernel(scale, q_ref, memory_ref, grad_ref, q_out, memory_out):
    pairs = q_ref.shape[1] // (2 * HD)
    for pair in range(pairs):
        queries = both_heads((q_ref[:, pair_columns(pair)].astype(F32) * scale).astype(BF16))
        grads = both_heads(grad_ref[:, pair_columns(pair)])
        k = memory_ref[:, pair_columns(pair)]
        v = memory_ref[:, pair_columns(pairs + pair)]
        query_grads = []
        key_grad = value_grad = 0.0
        for head in range(2):
            weights = text_weights(scale, queries[head], k)
            weighted = weights * across(v, grads[head])
            inner = jnp.sum(weighted, axis=0, keepdims=True)
            change = (weighted - weights * inner).astype(BF16)
            query_grads.append(down(k, change))
            key_grad += jnp.dot(change, queries[head], preferred_element_type=F32)
            value_grad += jnp.dot(weights.astype(BF16), grads[head], preferred_element_type=F32)
        q_out[:, pair_columns(pair)] = (join_heads(query_grads).T * scale).astype(BF16)
        memory_out[:, pair_columns(pair)] = key_grad.astype(BF16)
        memory_out[:, pair_columns(pairs + pair)] = value_grad.astype(BF16)


def text_attention(clips, scale, queries, memory, grad=None):
    spec = lambda value: pl.BlockSpec(
        (value.shape[0] // clips, value.shape[1]), lambda clip: (clip, 0)
    )
    back = grad is not None
    operands = (queries, memory) + ((grad,) if back else ())
    results = (queries, memory) if back else (queries,)
    size = memory.shape[0] // clips * queries.size
    outs = pl.pallas_call(
        functools.partial(text_attention_back_kernel if back else text_attention_kernel, scale),
        grid=(clips,),
        out_shape=[jax.ShapeDtypeStruct(value.shape, BF16) for value in results],
        in_specs=[spec(value) for value in operands],
        out_specs=[spec(value) for value in results],
        compiler_params=pltpu.CompilerParams(vmem_limit_bytes=32 << 20),
        cost_estimate=pl.CostEstimate(
            flops=(20 if back else 8) * size,
            bytes_accessed=2 * sum(value.size for value in operands + results),
            transcendentals=size // HD,
        ),
        name="text_attention_back" if back else "text_attention",
    )(*operands)
    return outs if back else outs[0]


PIECE = (192, 384)
LAGS = (0, 1, 3, 4, 5, 6, 7)


def sum_kernel(plan, weights, *refs):
    chunks = len(plan)
    lefts, rights = refs[:weights], refs[weights : 2 * weights]
    vector_in = refs[2 * weights]
    outputs = refs[2 * weights + 1 : 3 * weights + 1]
    vector_out = refs[3 * weights + 1]
    (
        mine,
        c_out,
        c_in,
        x_in,
        y_in,
        second_in,
        z_in,
        total,
        fx_in,
        fc_in,
        stage,
        left_buf,
        right_buf,
        vector,
        vector_got,
        vector_z,
        c_sem,
        first_sem,
        second_sem,
        z_sem,
        fx_sem,
        fc_sem,
        stage_sem,
        load_sem,
        vector_sem,
    ) = refs[3 * weights + 2 :]
    seq = lax.axis_index("seq")
    fsdp = lax.axis_index("fsdp")
    x, c = seq // 2, seq % 2
    z, y = fsdp // 2, fsdp % 2
    x_device = (2 * (1 - x) + c, fsdp)
    c_device = (2 * x + 1 - c, fsdp)
    y_device = (seq, 2 * z + 1 - y)

    def z_device(k):
        return (seq, 2 * ((z + k) % 4) + y)

    barrier = pltpu.get_barrier_semaphore()
    partners = [x_device, c_device, y_device] + [z_device(k) for k in (1, 2, 3)]
    for partner in partners:
        pl.semaphore_signal(barrier, inc=1, device_id=partner, device_id_type=MESH)
    pl.semaphore_wait(barrier, len(partners))

    def remote(source, target, sems, device):
        return pltpu.make_async_remote_copy(
            src_ref=source,
            dst_ref=target,
            send_sem=sems.at[0],
            recv_sem=sems.at[1],
            device_id=device,
            device_id_type=MESH,
        )

    def x_first(i):
        return i % 2 == 0

    def loads(j):
        weight, column = plan[j]
        slot = j % 2
        return [
            pltpu.make_async_copy(lefts[weight], left_buf.at[slot], load_sem.at[0, slot]),
            pltpu.make_async_copy(
                rights[weight].at[:, pl.ds(column, 1536)], right_buf.at[slot], load_sem.at[1, slot]
            ),
        ]

    def start_loads(i):
        for j in range(chunks):

            @pl.when(i == j)
            def _():
                for copy in loads(j):
                    copy.start()

    def wait_loads(i):
        for j in range(chunks):

            @pl.when(i == j)
            def _():
                for copy in loads(j):
                    copy.wait()

    def columns(block):
        return pl.ds(pl.multiple_of(block * 384, 128), 384)

    def multiply(i, half, target, slot):
        buffer = i % 2
        right = right_buf.at[buffer, :, pl.ds(pl.multiple_of(half * 768, 128), 768)]

        @pl.loop(0, 4)
        def _(zz):
            out = down(left_buf[buffer, :, columns(zz)], right[...]).astype(BF16)
            for q in range(2):
                for yy in range(2):
                    target[slot, q, zz, yy] = out[192 * yy : 192 * yy + 192, 384 * q : 384 * q + 384]

    def add_to(slot, q, zz, yy, other):
        here = mine[slot, q, zz, yy].astype(F32)
        mine[slot, q, zz, yy] = (here + other.astype(F32)).astype(BF16)

    def c_copy(i):
        return remote(c_out.at[i % 2], c_in.at[i % 2], c_sem.at[:, i % 2], c_device)

    def x_copy(i):
        slot = i // 2 % 2
        return remote(mine.at[i % 5, 1 - x], x_in.at[slot], first_sem.at[:, i % 4], x_device)

    def y_copy(i):
        slot = i // 2 % 2
        return remote(mine.at[i % 5, :, :, 1 - y], y_in.at[slot], first_sem.at[:, i % 4], y_device)

    def second_y_copy(i):
        slot = i % 4
        return remote(mine.at[i % 5, x, :, 1 - y], second_in.at[slot], second_sem.at[:, slot], y_device)

    def second_x_copy(i):
        slot = i % 4
        return remote(mine.at[i % 5, 1 - x, :, y], second_in.at[slot], second_sem.at[:, slot], x_device)

    def z_copy(i, k):
        slot = i % 4
        return remote(
            mine.at[i % 5, x, (z + k) % 4, y],
            z_in.at[slot, k - 1],
            z_sem.at[:, slot, k - 1],
            z_device(k),
        )

    def fx_copy(i):
        slot = i % 4
        return remote(total.at[slot], fx_in.at[slot], fx_sem.at[:, slot], x_device)

    def fc_copy(i, which):
        slot = i % 4
        source = fx_in.at[slot] if which else total.at[slot]
        return remote(source, fc_in.at[slot, which], fc_sem.at[:, slot, which], c_device)

    def begin(i):
        wait_loads(i)

        @pl.when(i >= 2)
        def _():
            c_copy(i - 2).wait_send()

        multiply(i, 1 - c, c_out, i % 2)
        c_copy(i).start()
        multiply(i, c, mine, i % 5)

    def first(i):
        slot = i % 5
        got = i % 2
        c_copy(i).wait_recv()

        @pl.when(x_first(i))
        def _():
            for q, last in ((1 - x, False), (x, True)):

                @pl.loop(0, 4)
                def _(zz):
                    for yy in range(2):
                        add_to(slot, q, zz, yy, c_in[got, q, zz, yy])

                if not last:
                    x_copy(i).start()

        @pl.when(jnp.logical_not(x_first(i)))
        def _():
            for yy, last in ((1 - y, False), (y, True)):

                @pl.loop(0, 4)
                def _(zz):
                    for q in range(2):
                        add_to(slot, q, zz, yy, c_in[got, q, zz, yy])

                if not last:
                    y_copy(i).start()

    def second(i):
        slot = i % 5
        got = i // 2 % 2

        @pl.when(x_first(i))
        def _():
            x_copy(i).wait()
            for yy, last in ((1 - y, False), (y, True)):

                @pl.loop(0, 4)
                def _(zz):
                    add_to(slot, x, zz, yy, x_in[got, zz, yy])

                if not last:
                    second_y_copy(i).start()

        @pl.when(jnp.logical_not(x_first(i)))
        def _():
            y_copy(i).wait()
            for q, last in ((1 - x, False), (x, True)):

                @pl.loop(0, 4)
                def _(zz):
                    add_to(slot, q, zz, y, y_in[got, q, zz])

                if not last:
                    second_x_copy(i).start()

    def third(i):
        slot = i % 4

        @pl.when(x_first(i))
        def _():
            second_y_copy(i).wait()

        @pl.when(jnp.logical_not(x_first(i)))
        def _():
            second_x_copy(i).wait()

        for k in (1, 2, 3):
            zz = (z + k) % 4
            add_to(i % 5, x, zz, y, second_in[slot, zz])
            z_copy(i, k).start()

    def put(i, quarter, value):
        stage[i % 2, :, columns(quarter)] = value

    def fourth(i):
        slot = i % 4
        result = mine[i % 5, x, z, y].astype(F32) + second_in[slot, z].astype(F32)
        for k in (1, 2, 3):
            z_copy(i, k).wait()
            result = result + z_in[slot, k - 1].astype(F32)
        total[slot] = result.astype(BF16)
        fx_copy(i).start()
        fc_copy(i, 0).start()

    def fifth(i):
        fx_copy(i).wait()
        fc_copy(i, 1).start()

    def store(j):
        weight, column = plan[j]
        return pltpu.make_async_copy(
            stage.at[j % 2], outputs[weight].at[:, pl.ds(column, 1536)], stage_sem.at[j % 2]
        )

    def sixth(i):
        slot = i % 4
        for j in range(2, chunks):

            @pl.when(i == j)
            def _():
                store(j - 2).wait()

        fc_copy(i, 0).wait()
        fc_copy(i, 1).wait()
        put(i, 2 * c + x, total[slot])
        put(i, 2 * c + 1 - x, fx_in[slot])
        put(i, 2 * (1 - c) + x, fc_in[slot, 0])
        put(i, 2 * (1 - c) + 1 - x, fc_in[slot, 1])
        for j in range(chunks):

            @pl.when(i == j)
            def _():
                store(j).start()

    def vector_copy(leg):
        device = (c_device, x_device, y_device)[leg]
        return remote(vector.at[leg], vector_got.at[leg], vector_sem.at[:, leg], device)

    def vector_z_copy(k):
        return remote(vector_z.at[z], vector_z.at[z], vector_sem.at[:, 2 + k], z_device(k))

    def vector_arrival(k):
        source = (z + 4 - k) % 4
        return remote(vector_z.at[source], vector_z.at[source], vector_sem.at[:, 2 + k], z_device(k))

    def vector_step(t):
        @pl.when(t == 0)
        def _():
            pltpu.sync_copy(vector_in, vector.at[0])
            vector_copy(0).start()

        for leg in range(3):

            @pl.when(t == leg + 1)
            def _():
                vector_copy(leg).wait()
                both = vector[leg] + vector_got[leg]
                if leg < 2:
                    vector[leg + 1] = both
                    vector_copy(leg + 1).start()
                else:
                    vector_z[z] = both
                    for k in (1, 2, 3):
                        vector_z_copy(k).start()

        @pl.when(t == 4)
        def _():
            for k in (1, 2, 3):
                vector_z_copy(k).wait_send()
                vector_arrival(k).wait_recv()
            vector[0] = vector_z[0] + vector_z[1] + vector_z[2] + vector_z[3]
            pltpu.sync_copy(vector.at[0], vector_out)

    start_loads(0)

    @pl.loop(0, chunks + LAGS[-1])
    def _(t):
        @pl.when(t + 1 < chunks)
        def _():
            start_loads(t + 1)

        stages = (begin, first, second, third, fourth, fifth, sixth)
        for lag, run in zip(LAGS[::-1], stages[::-1]):
            i = t - lag

            @pl.when(jnp.logical_and(i >= 0, i < chunks))
            def _():
                run(i)

        vector_step(t)

    for j in (chunks - 2, chunks - 1):
        c_copy(j).wait_send()
        store(j).wait()


def sum_products(products, vectors):
    lefts = [left for left, _ in products]
    rights = [right for _, right in products]
    plan = [
        (weight, column)
        for weight, right in enumerate(rights)
        for column in range(0, right.shape[1], 1536)
    ]
    out_shapes = [
        jax.ShapeDtypeStruct((left.shape[1] // 8, right.shape[1]), BF16) for left, right in products
    ]
    out_shapes.append(jax.ShapeDtypeStruct(vectors.shape, F32))
    depth = lefts[0].shape[0]
    anywhere = pl.BlockSpec(memory_space=pl.ANY)
    dma = pltpu.SemaphoreType.DMA
    block = lambda *lead: pltpu.VMEM(lead + PIECE, BF16)
    *sums, total = pl.pallas_call(
        functools.partial(sum_kernel, tuple(plan), len(products)),
        out_shape=out_shapes,
        in_specs=[anywhere] * (2 * len(products) + 1),
        out_specs=[anywhere] * len(out_shapes),
        scratch_shapes=[
            block(5, 2, 4, 2),
            block(2, 2, 4, 2),
            block(2, 2, 4, 2),
            block(2, 4, 2),
            block(2, 2, 4),
            block(4, 4),
            block(4, 3),
            block(4),
            block(4),
            block(4, 2),
            pltpu.VMEM((2, 192, 1536), BF16),
            pltpu.VMEM((2, depth, 1536), BF16),
            pltpu.VMEM((2, depth, 1536), BF16),
            pltpu.VMEM((3,) + vectors.shape, F32),
            pltpu.VMEM((3,) + vectors.shape, F32),
            pltpu.VMEM((4,) + vectors.shape, F32),
            dma((2, 2)),
            dma((2, 4)),
            dma((2, 4)),
            dma((2, 4, 3)),
            dma((2, 4)),
            dma((2, 4, 2)),
            dma((2,)),
            dma((2, 2)),
            dma((2, 6)),
        ],
        compiler_params=pltpu.CompilerParams(
            collective_id=3, has_side_effects=True, vmem_limit_bytes=60 << 20
        ),
        name="sum_products",
    )(*lefts, *rights, vectors)
    return sums, total


def on_blocks(
    hidden_states,
    text_states,
    self_gain,
    self_bias,
    query_key_value,
    self_output,
    cross_gain,
    cross_bias,
    cross_query,
    cross_memory,
    cross_output,
    final_gain,
    final_bias,
    expand_weight,
    contract_weight,
    output_cotangent,
):
    clips, frames, width = hidden_states.shape
    rows = clips * frames
    groups = lax.axis_size("seq")
    fsdp_count = lax.axis_size("fsdp")
    scale = HD ** (-0.5)
    entries = rows * groups * fsdp_count * width
    group_width = width // groups

    gains = (self_gain, self_bias, cross_gain, cross_bias, final_gain, final_bias)
    early = (query_key_value, self_output)
    (qkv_whole, self_output_whole), vectors = gather_weights(early, pack_vectors(gains), 1)
    qkv_whole, expand_weight = lax.optimization_barrier((qkv_whole, expand_weight))
    expand_whole = gather_quarters(expand_weight)
    vectors = vectors[:, :6, : width // fsdp_count]
    gains = [vectors[:, i].reshape(width) for i in range(6)]

    hidden = hidden_states.reshape(rows, width).astype(F32)
    normed_one, norm_one_back = jax.vjp(layer_norm, hidden, gains[0], gains[1])
    normed_one = normed_one.astype(BF16)
    projected = product_blocks(normed_one, qkv_whole, 3, groups)
    regrouped = lax.all_to_all(projected, "seq", split_axis=0, concat_axis=0, tiled=True)
    regrouped = regrouped.reshape(groups, clips, frames, 3 * group_width)
    context_heads, logsum = attention(regrouped, scale)
    context_heads = context_heads.reshape(groups, rows, group_width)
    context = lax.all_to_all(context_heads, "seq", split_axis=0, concat_axis=0, tiled=True)
    late = (cross_query, cross_memory, cross_output)
    context, late, expand_whole, contract_weight = lax.optimization_barrier(
        (context, late, expand_whole, contract_weight)
    )
    contract_whole = gather_quarters(contract_weight)
    late, _ = gather_weights(late, None, 2)
    cross_query_whole, cross_memory_whole, cross_output_whole = late
    context = context.transpose(1, 0, 2).reshape(rows, width)
    attended = product(context, self_output_whole)
    first = hidden + attended
    normed_two, norm_two_back = jax.vjp(layer_norm, first, gains[2], gains[3])
    normed_two = normed_two.astype(BF16)
    cross_q = product(normed_two, cross_query_whole).astype(BF16)
    text_rows = text_states.reshape(clips * TEXT, width)
    memory = product(text_rows, cross_memory_whole).astype(BF16)
    cross_context = text_attention(clips, scale, cross_q, memory)
    crossed = product(cross_context, cross_output_whole)
    second = first + crossed
    normed_three, norm_three_back = jax.vjp(layer_norm, second, gains[4], gains[5])
    normed_three = normed_three.astype(BF16)
    preact = product(normed_three, expand_whole)
    below = 0.5 + 0.5 * lax.erf(preact * 0.5**0.5)
    density = jnp.exp(preact * preact * -0.5) * (0.5 / jnp.pi) ** 0.5
    activated = (preact * below).astype(BF16)
    slope = (below + preact * density).astype(BF16)
    upstream = output_cotangent.reshape(rows, width).astype(F32)
    grad_mixed = output_cotangent.reshape(rows, width)
    contract_term = product_left(activated, grad_mixed).astype(BF16)
    grad_mixed, contract_term, contract_whole = lax.optimization_barrier(
        (grad_mixed, contract_term, contract_whole)
    )
    contract_part = lax.psum_scatter(
        contract_term, ("fsdp", "seq"), scatter_dimension=0, tiled=True
    )
    contract_gradient = lax.all_gather(contract_part, "seq", axis=0, tiled=True)
    grad_activated = product_right(grad_mixed, contract_whole)
    grad_preact = (grad_activated * slope.astype(F32)).astype(BF16)
    grad_normed_three = product_right(grad_preact, expand_whole)
    grad_second, final_gain_term, final_bias_term = norm_three_back(grad_normed_three)
    grad_second = upstream + grad_second
    grad_crossed = grad_second.astype(BF16)
    grad_cross_context = product_right(grad_crossed, cross_output_whole).astype(BF16)
    grad_cross_q, grad_memory = text_attention(clips, scale, cross_q, memory, grad_cross_context)
    grad_normed_two = product_right(grad_cross_q, cross_query_whole)
    grad_first, cross_gain_term, cross_bias_term = norm_two_back(grad_normed_two)
    grad_first = grad_second + grad_first
    grad_attended = grad_first.astype(BF16)
    grad_context = product_right(grad_attended, self_output_whole).astype(BF16)
    grad_context = grad_context.reshape(rows, groups, group_width).transpose(1, 0, 2)
    grad_heads = lax.all_to_all(grad_context, "seq", split_axis=0, concat_axis=0, tiled=True)
    grad_heads = grad_heads.reshape(groups, clips, frames, group_width)
    grad_regrouped = attention_back(regrouped, grad_heads, logsum, scale)
    grad_regrouped, activated = lax.optimization_barrier((grad_regrouped, activated))
    grad_regrouped = grad_regrouped.reshape(groups, rows, 3 * group_width)
    grad_projected = lax.all_to_all(grad_regrouped, "seq", split_axis=0, concat_axis=0, tiled=True)
    mixed = product(activated, contract_whole)
    output = second + mixed
    squares = jnp.stack(
        [
            jnp.sum(output * output),
            jnp.sum(attended * attended),
            jnp.sum(crossed * crossed),
            jnp.sum(mixed * mixed),
        ]
    )
    output = output.astype(BF16)
    grad_projected, output, squares = lax.optimization_barrier((grad_projected, output, squares))
    grad_projected = jnp.concatenate(
        [
            grad_projected[group, :, kind * group_width : (kind + 1) * group_width]
            for kind in range(3)
            for group in range(groups)
        ],
        1,
    )
    grad_normed_one = product_right(grad_projected, qkv_whole)
    grad_hidden, gain_one_term, bias_one_term = norm_one_back(grad_normed_one)
    grad_hidden = grad_first + grad_hidden
    terms = jnp.stack(
        [
            gain_one_term,
            bias_one_term,
            cross_gain_term,
            cross_bias_term,
            final_gain_term,
            final_bias_term,
            jnp.pad(squares, (0, width - 4)),
            jnp.zeros_like(gain_one_term),
        ]
    )
    deep = lambda value: jnp.pad(value, ((0, rows - value.shape[0]), (0, 0)))
    gradients, totals = sum_products(
        [
            (normed_three, grad_preact),
            (cross_context, grad_crossed),
            (normed_two, grad_cross_q),
            (deep(text_rows), deep(grad_memory)),
            (context, grad_attended),
            (normed_one, grad_projected),
        ],
        terms,
    )
    gradients = [gradient.astype(F32) for gradient in gradients]
    contract_gradient = contract_gradient.astype(F32)
    layer_rms = jnp.sqrt(totals[6, :4] / entries)
    shard = width // fsdp_count
    vector_gradients = lax.dynamic_slice_in_dim(
        totals, lax.axis_index("fsdp") * shard, shard, 1
    )
    return (
        output.reshape(clips, frames, width),
        grad_hidden.reshape(clips, frames, width),
        vector_gradients[0],
        vector_gradients[1],
        gradients[5],
        gradients[4],
        vector_gradients[2],
        vector_gradients[3],
        gradients[2],
        gradients[3],
        gradients[1],
        vector_gradients[4],
        vector_gradients[5],
        gradients[0],
        contract_gradient,
        layer_rms,
    )


def solution(mesh):
    shape = dict(mesh.shape)
    blocks = shape["seq"] == 4 and shape["fsdp"] == 8
    return jax.shard_map(
        on_blocks if blocks else on_any_mesh,
        mesh=mesh,
        in_specs=(
            P("fsdp", "seq", None),
            P("fsdp", None, None),
            P("fsdp"),
            P("fsdp"),
            P("fsdp", None),
            P("fsdp", None),
            P("fsdp"),
            P("fsdp"),
            P("fsdp", None),
            P("fsdp", None),
            P("fsdp", None),
            P("fsdp"),
            P("fsdp"),
            P("fsdp", None),
            P("fsdp", None),
            P("fsdp", "seq", None),
        ),
        out_specs=(
            P("fsdp", "seq", None),
            P("fsdp", "seq", None),
            P("fsdp"),
            P("fsdp"),
            P("fsdp", None),
            P("fsdp", None),
            P("fsdp"),
            P("fsdp"),
            P("fsdp", None),
            P("fsdp", None),
            P("fsdp", None),
            P("fsdp"),
            P("fsdp"),
            P("fsdp", None),
            P("fsdp", None),
            P(),
        ),
        check_vma=False,
    )
```

```python
import functools

import jax
import jax.numpy as jnp
from jax import lax
from jax.experimental import pallas as pl
from jax.experimental.pallas import tpu as pltpu
from jax.sharding import PartitionSpec as P

H = 24
HD = 64
TEXT = 64

NEGATIVE = -1e30
BF16 = jnp.bfloat16
F32 = jnp.float32
MESH = pl.DeviceIdType.MESH


def layer_norm(values, gain, offset):
    center = values - jnp.mean(values, axis=-1, keepdims=True)
    spread = jnp.mean(center * center, axis=-1, keepdims=True)
    return center * lax.rsqrt(spread + 1e-05) * gain + offset


def gelu_exact(values):
    return jax.nn.gelu(values, approximate=False)


def product(left, right):
    return jnp.dot(left, right, preferred_element_type=jnp.float32)


def product_left(left, right):
    return lax.dot_general(
        left, right, (((0,), (0,)), ((), ())), preferred_element_type=jnp.float32
    )


def product_right(left, right):
    return lax.dot_general(
        left, right, (((1,), (1,)), ((), ())), preferred_element_type=jnp.float32
    )


def causal_forward(queries, keys, values, rows_block, scale):
    clips, length, heads_local, head_width = queries.shape
    count = length // rows_block
    columns = jnp.arange(length, dtype=jnp.int32)

    def one_block(start):
        block = lax.dynamic_slice_in_dim(queries, start, rows_block, 1)
        scores = (
            jnp.einsum("cqhd,ckhd->chqk", block, keys, preferred_element_type=jnp.float32) * scale
        )
        positions = start + jnp.arange(rows_block, dtype=jnp.int32)
        allowed = columns[None, :] <= positions[:, None]
        scores = jnp.where(allowed, scores, NEGATIVE)
        highest = jnp.max(scores, axis=-1, keepdims=True)
        raised = jnp.exp(scores - highest)
        summed = jnp.sum(raised, axis=-1, keepdims=True)
        weights = (raised / summed).astype(jnp.bfloat16)
        result = jnp.einsum("chqk,ckhd->cqhd", weights, values, preferred_element_type=jnp.float32)
        return (result.astype(jnp.bfloat16), (highest + jnp.log(summed))[..., 0])

    starts = jnp.arange(count, dtype=jnp.int32) * rows_block
    results, logsum = lax.map(one_block, starts)
    results = jnp.moveaxis(results, 0, 1).reshape(clips, length, heads_local * head_width)
    return (results, logsum)


def causal_backward(queries, keys, values, logsum, grad_heads, rows_block, scale):
    clips, length, heads_local, head_width = queries.shape
    count = length // rows_block
    columns = jnp.arange(length, dtype=jnp.int32)
    starts = jnp.arange(count, dtype=jnp.int32) * rows_block

    def one_block(carry, inputs):
        grad_keys, grad_values = carry
        start, block_logsum = inputs
        block = lax.dynamic_slice_in_dim(queries, start, rows_block, 1)
        block_grad = lax.dynamic_slice_in_dim(grad_heads, start, rows_block, 1)
        scores = (
            jnp.einsum("cqhd,ckhd->chqk", block, keys, preferred_element_type=jnp.float32) * scale
        )
        positions = start + jnp.arange(rows_block, dtype=jnp.int32)
        allowed = columns[None, :] <= positions[:, None]
        scores = jnp.where(allowed, scores, NEGATIVE)
        weights = jnp.exp(scores - block_logsum[..., None])
        rounded = weights.astype(jnp.bfloat16)
        grad_weights = jnp.einsum(
            "cqhd,ckhd->chqk", block_grad, values, preferred_element_type=jnp.float32
        )
        inner = jnp.sum(weights * grad_weights, axis=-1, keepdims=True)
        grad_scores = (weights * (grad_weights - inner)).astype(jnp.bfloat16)
        grad_query = (
            jnp.einsum("chqk,ckhd->cqhd", grad_scores, keys, preferred_element_type=jnp.float32)
            * scale
        )
        grad_keys = (
            grad_keys
            + jnp.einsum("chqk,cqhd->ckhd", grad_scores, block, preferred_element_type=jnp.float32)
            * scale
        )
        grad_values = grad_values + jnp.einsum(
            "chqk,cqhd->ckhd", rounded, block_grad, preferred_element_type=jnp.float32
        )
        return ((grad_keys, grad_values), grad_query.astype(jnp.bfloat16))

    zeros = jnp.zeros(queries.shape, jnp.float32)
    (grad_keys, grad_values), grad_queries = lax.scan(one_block, (zeros, zeros), (starts, logsum))
    local_width = heads_local * head_width
    grad_queries = jnp.moveaxis(grad_queries, 0, 1).reshape(clips, length, local_width)
    grad_keys = grad_keys.astype(jnp.bfloat16).reshape(clips, length, local_width)
    grad_values = grad_values.astype(jnp.bfloat16).reshape(clips, length, local_width)
    return jnp.stack([grad_queries, grad_keys, grad_values], axis=2)


def on_any_mesh(
    hidden_states,
    text_states,
    self_gain,
    self_bias,
    query_key_value,
    self_output,
    cross_gain,
    cross_bias,
    cross_query,
    cross_memory,
    cross_output,
    final_gain,
    final_bias,
    expand_weight,
    contract_weight,
    output_cotangent,
):
    clips, frames, width = hidden_states.shape
    rows = clips * frames
    groups = lax.axis_size("seq")
    fsdp_count = lax.axis_size("fsdp")
    heads_local = H // groups
    length = frames * groups
    rows_block = min(512, length)
    scale = HD ** (-0.5)
    entries = rows * groups * fsdp_count * width
    self_set = (
        lax.all_gather(self_gain, "fsdp", axis=0, tiled=True),
        lax.all_gather(self_bias, "fsdp", axis=0, tiled=True),
        lax.all_gather(query_key_value, "fsdp", axis=0, tiled=True),
        lax.all_gather(self_output, "fsdp", axis=0, tiled=True),
    )
    hidden = hidden_states.reshape(rows, width).astype(jnp.float32)
    normed_one, norm_one_back = jax.vjp(
        layer_norm, hidden, self_set[0].astype(jnp.float32), self_set[1].astype(jnp.float32)
    )
    normed_one = normed_one.astype(jnp.bfloat16)
    projected = (
        product(normed_one, self_set[2]).astype(jnp.bfloat16).reshape(clips, frames, 3, width)
    )
    regrouped = lax.all_to_all(projected, "seq", split_axis=3, concat_axis=1, tiled=True)
    regrouped = regrouped.reshape(clips, length, 3, heads_local, HD)
    queries = regrouped[:, :, 0]
    keys = regrouped[:, :, 1]
    values = regrouped[:, :, 2]
    context_heads, logsum = causal_forward(queries, keys, values, rows_block, scale)
    context = lax.all_to_all(context_heads, "seq", split_axis=1, concat_axis=2, tiled=True).reshape(
        rows, width
    )
    attended = product(context, self_set[3])
    first = hidden + attended
    rest_set = (
        lax.all_gather(cross_gain, "fsdp", axis=0, tiled=True),
        lax.all_gather(cross_bias, "fsdp", axis=0, tiled=True),
        lax.all_gather(cross_query, "fsdp", axis=0, tiled=True),
        lax.all_gather(cross_memory, "fsdp", axis=0, tiled=True),
        lax.all_gather(cross_output, "fsdp", axis=0, tiled=True),
        lax.all_gather(final_gain, "fsdp", axis=0, tiled=True),
        lax.all_gather(final_bias, "fsdp", axis=0, tiled=True),
        lax.all_gather(expand_weight, "fsdp", axis=0, tiled=True),
        lax.all_gather(contract_weight, "fsdp", axis=0, tiled=True),
    )
    normed_two, norm_two_back = jax.vjp(
        layer_norm, first, rest_set[0].astype(jnp.float32), rest_set[1].astype(jnp.float32)
    )
    normed_two = normed_two.astype(jnp.bfloat16)
    cross_q = product(normed_two, rest_set[2]).astype(jnp.bfloat16).reshape(clips, frames, H, HD)
    text_rows = text_states.reshape(clips * TEXT, width)
    memory = product(text_rows, rest_set[3]).astype(jnp.bfloat16).reshape(clips, TEXT, 2, H, HD)
    cross_keys = memory[:, :, 0]
    cross_values = memory[:, :, 1]
    cross_scores = (
        jnp.einsum("cqhd,ckhd->chqk", cross_q, cross_keys, preferred_element_type=jnp.float32)
        * scale
    )
    highest = jnp.max(cross_scores, axis=-1, keepdims=True)
    raised = jnp.exp(cross_scores - highest)
    cross_weights = raised / jnp.sum(raised, axis=-1, keepdims=True)
    cross_rounded = cross_weights.astype(jnp.bfloat16)
    cross_context = jnp.einsum(
        "chqk,ckhd->cqhd", cross_rounded, cross_values, preferred_element_type=jnp.float32
    )
    cross_context = cross_context.astype(jnp.bfloat16).reshape(rows, width)
    crossed = product(cross_context, rest_set[4])
    second = first + crossed
    normed_three, norm_three_back = jax.vjp(
        layer_norm, second, rest_set[5].astype(jnp.float32), rest_set[6].astype(jnp.float32)
    )
    normed_three = normed_three.astype(jnp.bfloat16)
    preact = product(normed_three, rest_set[7])
    activated, gelu_back = jax.vjp(gelu_exact, preact)
    activated = activated.astype(jnp.bfloat16)
    mixed = product(activated, rest_set[8])
    output = second + mixed
    squares = jnp.stack(
        [
            jnp.sum(output * output),
            jnp.sum(attended * attended),
            jnp.sum(crossed * crossed),
            jnp.sum(mixed * mixed),
        ]
    )
    square_totals = lax.psum(squares, ("seq", "fsdp"))
    back_rest = (
        lax.all_gather(cross_gain, "fsdp", axis=0, tiled=True),
        lax.all_gather(cross_bias, "fsdp", axis=0, tiled=True),
        lax.all_gather(cross_query, "fsdp", axis=0, tiled=True),
        lax.all_gather(cross_memory, "fsdp", axis=0, tiled=True),
        lax.all_gather(cross_output, "fsdp", axis=0, tiled=True),
        lax.all_gather(final_gain, "fsdp", axis=0, tiled=True),
        lax.all_gather(final_bias, "fsdp", axis=0, tiled=True),
        lax.all_gather(expand_weight, "fsdp", axis=0, tiled=True),
        lax.all_gather(contract_weight, "fsdp", axis=0, tiled=True),
    )
    upstream = output_cotangent.reshape(rows, width).astype(jnp.float32)
    grad_mixed = upstream.astype(jnp.bfloat16)
    contract_term = product_left(activated, grad_mixed)
    grad_activated = product_right(grad_mixed, back_rest[8])
    grad_preact = gelu_back(grad_activated)[0].astype(jnp.bfloat16)
    expand_term = product_left(normed_three, grad_preact)
    grad_normed_three = product_right(grad_preact, back_rest[7])
    grad_second, final_gain_term, final_bias_term = norm_three_back(grad_normed_three)
    grad_second = upstream + grad_second
    grad_crossed = grad_second.astype(jnp.bfloat16)
    cross_output_term = product_left(cross_context, grad_crossed)
    grad_cross_context = (
        product_right(grad_crossed, back_rest[4]).astype(jnp.bfloat16).reshape(clips, frames, H, HD)
    )
    grad_cross_weights = jnp.einsum(
        "cqhd,ckhd->chqk", grad_cross_context, cross_values, preferred_element_type=jnp.float32
    )
    cross_inner = jnp.sum(cross_weights * grad_cross_weights, axis=-1, keepdims=True)
    grad_cross_scores = (cross_weights * (grad_cross_weights - cross_inner)).astype(jnp.bfloat16)
    grad_cross_q = (
        jnp.einsum(
            "chqk,ckhd->cqhd", grad_cross_scores, cross_keys, preferred_element_type=jnp.float32
        )
        * scale
    )
    grad_cross_q = grad_cross_q.astype(jnp.bfloat16).reshape(rows, width)
    grad_cross_keys = (
        jnp.einsum(
            "chqk,cqhd->ckhd", grad_cross_scores, cross_q, preferred_element_type=jnp.float32
        )
        * scale
    )
    grad_cross_values = jnp.einsum(
        "chqk,cqhd->ckhd", cross_rounded, grad_cross_context, preferred_element_type=jnp.float32
    )
    grad_memory = jnp.stack([grad_cross_keys, grad_cross_values], axis=2).reshape(
        clips * TEXT, 2 * width
    )
    memory_term = lax.dot_general(
        text_rows.astype(jnp.float32),
        grad_memory,
        (((0,), (0,)), ((), ())),
        precision=lax.Precision.HIGHEST,
        preferred_element_type=jnp.float32,
    )
    query_term = product_left(normed_two, grad_cross_q)
    grad_normed_two = product_right(grad_cross_q, back_rest[2])
    grad_first, cross_gain_term, cross_bias_term = norm_two_back(grad_normed_two)
    grad_first = grad_second + grad_first
    rest_sums = (
        lax.psum_scatter(
            cross_gain_term.astype(jnp.bfloat16), "fsdp", scatter_dimension=0, tiled=True
        ).astype(jnp.float32),
        lax.psum_scatter(
            cross_bias_term.astype(jnp.bfloat16), "fsdp", scatter_dimension=0, tiled=True
        ).astype(jnp.float32),
        lax.psum_scatter(
            query_term.astype(jnp.bfloat16), "fsdp", scatter_dimension=0, tiled=True
        ).astype(jnp.float32),
        lax.psum_scatter(
            memory_term.astype(jnp.bfloat16), "fsdp", scatter_dimension=0, tiled=True
        ).astype(jnp.float32),
        lax.psum_scatter(
            cross_output_term.astype(jnp.bfloat16), "fsdp", scatter_dimension=0, tiled=True
        ).astype(jnp.float32),
        lax.psum_scatter(
            final_gain_term.astype(jnp.bfloat16), "fsdp", scatter_dimension=0, tiled=True
        ).astype(jnp.float32),
        lax.psum_scatter(
            final_bias_term.astype(jnp.bfloat16), "fsdp", scatter_dimension=0, tiled=True
        ).astype(jnp.float32),
        lax.psum_scatter(
            expand_term.astype(jnp.bfloat16), "fsdp", scatter_dimension=0, tiled=True
        ).astype(jnp.float32),
        lax.psum_scatter(
            contract_term.astype(jnp.bfloat16), "fsdp", scatter_dimension=0, tiled=True
        ).astype(jnp.float32),
    )
    back_self = (
        lax.all_gather(self_gain, "fsdp", axis=0, tiled=True),
        lax.all_gather(self_bias, "fsdp", axis=0, tiled=True),
        lax.all_gather(query_key_value, "fsdp", axis=0, tiled=True),
        lax.all_gather(self_output, "fsdp", axis=0, tiled=True),
    )
    grad_attended = grad_first.astype(jnp.bfloat16)
    self_output_term = product_left(context, grad_attended)
    grad_context = (
        product_right(grad_attended, back_self[3])
        .astype(jnp.bfloat16)
        .reshape(clips, frames, width)
    )
    grad_heads = lax.all_to_all(grad_context, "seq", split_axis=2, concat_axis=1, tiled=True)
    grad_heads = grad_heads.reshape(clips, length, heads_local, HD)
    grad_regrouped = causal_backward(queries, keys, values, logsum, grad_heads, rows_block, scale)
    grad_projected = lax.all_to_all(
        grad_regrouped, "seq", split_axis=1, concat_axis=3, tiled=True
    ).reshape(rows, 3 * width)
    qkv_term = product_left(normed_one, grad_projected)
    grad_normed_one = product_right(grad_projected, back_self[2])
    grad_hidden, gain_one_term, bias_one_term = norm_one_back(grad_normed_one)
    grad_hidden = grad_first + grad_hidden
    self_sums = (
        lax.psum_scatter(
            gain_one_term.astype(jnp.bfloat16), "fsdp", scatter_dimension=0, tiled=True
        ).astype(jnp.float32),
        lax.psum_scatter(
            bias_one_term.astype(jnp.bfloat16), "fsdp", scatter_dimension=0, tiled=True
        ).astype(jnp.float32),
        lax.psum_scatter(
            qkv_term.astype(jnp.bfloat16), "fsdp", scatter_dimension=0, tiled=True
        ).astype(jnp.float32),
        lax.psum_scatter(
            self_output_term.astype(jnp.bfloat16), "fsdp", scatter_dimension=0, tiled=True
        ).astype(jnp.float32),
    )
    finals = (
        lax.psum(self_sums[0].astype(jnp.bfloat16), "seq").astype(jnp.float32),
        lax.psum(self_sums[1].astype(jnp.bfloat16), "seq").astype(jnp.float32),
        lax.psum(self_sums[2].astype(jnp.bfloat16), "seq").astype(jnp.float32),
        lax.psum(self_sums[3].astype(jnp.bfloat16), "seq").astype(jnp.float32),
        lax.psum(rest_sums[0].astype(jnp.bfloat16), "seq").astype(jnp.float32),
        lax.psum(rest_sums[1].astype(jnp.bfloat16), "seq").astype(jnp.float32),
        lax.psum(rest_sums[2].astype(jnp.bfloat16), "seq").astype(jnp.float32),
        lax.psum(rest_sums[3].astype(jnp.bfloat16), "seq").astype(jnp.float32),
        lax.psum(rest_sums[4].astype(jnp.bfloat16), "seq").astype(jnp.float32),
        lax.psum(rest_sums[5].astype(jnp.bfloat16), "seq").astype(jnp.float32),
        lax.psum(rest_sums[6].astype(jnp.bfloat16), "seq").astype(jnp.float32),
        lax.psum(rest_sums[7].astype(jnp.bfloat16), "seq").astype(jnp.float32),
        lax.psum(rest_sums[8].astype(jnp.bfloat16), "seq").astype(jnp.float32),
    )
    layer_rms = jnp.sqrt(square_totals / entries)
    return (
        output.astype(jnp.bfloat16).reshape(clips, frames, width),
        grad_hidden.reshape(clips, frames, width),
        finals[0],
        finals[1],
        finals[2],
        finals[3],
        finals[4],
        finals[5],
        finals[6],
        finals[7],
        finals[8],
        finals[9],
        finals[10],
        finals[11],
        finals[12],
        layer_rms,
    )


CORE_PAIRS = [(0, 1), (1, 0), (2, 3), (3, 2)]
X_PAIRS = [(0, 2), (2, 0), (1, 3), (3, 1)]
Y_PAIRS = [(i, i ^ 1) for i in range(8)]
Z_SHIFTS = [[(i, (i + 2 * k) % 8) for i in range(8)] for k in (1, 2, 3)]


CHUNK = 384


def gather_kernel(plan, has_vectors, *refs):
    weights = len({entry[0] for entry in plan})
    inputs = refs[:weights]
    refs = refs[weights:]
    if has_vectors:
        vector_in, refs = refs[0], refs[1:]
    outputs = refs[:weights]
    refs = refs[weights:]
    if has_vectors:
        vector_out, refs = refs[0], refs[1:]
    zs_sem, zr_sem, ys_sem, yr_sem, xs_sem, xr_sem, cs_sem, cr_sem, own_sem, vs_sem, vr_sem = refs
    seq = lax.axis_index("seq")
    fsdp = lax.axis_index("fsdp")
    x, c = seq // 2, seq % 2
    z, y = fsdp // 2, fsdp % 2
    x_seq = 2 * (1 - x) + c
    c_seq = 2 * x + 1 - c
    y_fsdp = 2 * z + 1 - y

    def at_z(k):
        return 2 * ((z + k) % 4) + y

    barrier = pltpu.get_barrier_semaphore()
    partners = [(x_seq, fsdp), (c_seq, fsdp), (seq, y_fsdp)] + [(seq, at_z(k)) for k in (1, 2, 3)]
    if has_vectors:
        partners += [(seq, 2 * ((z + k) % 4) + 1 - y) for k in (1, 2, 3)]
    for partner in partners:
        pl.semaphore_signal(barrier, inc=1, device_id=partner, device_id_type=MESH)
    pl.semaphore_wait(barrier, len(partners))

    if has_vectors:
        vector_sends = []
        for k in range(1, 8):
            copy = pltpu.make_async_remote_copy(
                src_ref=vector_in,
                dst_ref=vector_out.at[fsdp],
                send_sem=vs_sem.at[k],
                recv_sem=vr_sem.at[k],
                device_id=(seq, (fsdp + k) % 8),
                device_id_type=MESH,
            )
            copy.start()
            vector_sends.append(copy)
        own = pltpu.make_async_copy(vector_in, vector_out.at[fsdp], vs_sem.at[0])
        own.start()

    def part(entry):
        weight, block, column, split = entry
        first = 2 * c + x if split else 2 * c
        count = 1 if split else 2
        return weight, block, pl.ds(column, CHUNK), pl.ds(first, count)

    def remote(region, send, recv, device):
        return pltpu.make_async_remote_copy(
            src_ref=region,
            dst_ref=region,
            send_sem=send,
            recv_sem=recv,
            device_id=device,
            device_id_type=MESH,
        )

    sends = []

    def send(copy):
        copy.start()
        sends.append(copy)

    def start_z(i):
        weight, block, columns, mine = part(plan[i])
        source = inputs[weight].at[block, mine, :, columns]
        target = outputs[weight].at[z, y, block, mine, :, columns]
        for k in (1, 2, 3):
            copy = pltpu.make_async_remote_copy(
                src_ref=source,
                dst_ref=target,
                send_sem=zs_sem.at[i, k],
                recv_sem=zr_sem.at[i, k],
                device_id=(seq, at_z(k)),
                device_id_type=MESH,
            )
            send(copy)
        pltpu.make_async_copy(source, target, own_sem.at[i]).start()

    def start_y(i):
        weight, block, columns, mine = part(plan[i])
        output = outputs[weight]
        for k in (1, 2, 3):
            region = output.at[(z + 4 - k) % 4, y, block, mine, :, columns]
            remote(region, zs_sem.at[i, k], zr_sem.at[i, k], (seq, at_z(k))).wait_recv()
        source = inputs[weight].at[block, mine, :, columns]
        target = output.at[z, y, block, mine, :, columns]
        pltpu.make_async_copy(source, target, own_sem.at[i]).wait()
        region = output.at[:, y, block, mine, :, columns]
        send(remote(region, ys_sem.at[i], yr_sem.at[i], (seq, y_fsdp)))

    def start_x(i):
        weight, block, columns, mine = part(plan[i])
        output = outputs[weight]
        region = output.at[:, 1 - y, block, mine, :, columns]
        remote(region, ys_sem.at[i], yr_sem.at[i], (seq, y_fsdp)).wait_recv()
        region = output.at[:, :, block, mine, :, columns]
        if plan[i][3]:
            send(remote(region, xs_sem.at[i], xr_sem.at[i], (x_seq, fsdp)))
        send(remote(region, cs_sem.at[i, 0], cr_sem.at[i, 0], (c_seq, fsdp)))

    def start_core(i):
        if plan[i][3]:
            weight, block, columns, _ = part(plan[i])
            region = outputs[weight].at[:, :, block, pl.ds(2 * c + 1 - x, 1), :, columns]
            remote(region, xs_sem.at[i], xr_sem.at[i], (x_seq, fsdp)).wait_recv()
            send(remote(region, cs_sem.at[i, 1], cr_sem.at[i, 1], (c_seq, fsdp)))

    def finish(i):
        weight, block, columns, _ = part(plan[i])
        other = 2 * (1 - c)
        output = outputs[weight]
        if plan[i][3]:
            for j, quarter in ((0, other + x), (1, other + 1 - x)):
                region = output.at[:, :, block, pl.ds(quarter, 1), :, columns]
                remote(region, cs_sem.at[i, j], cr_sem.at[i, j], (c_seq, fsdp)).wait_recv()
        else:
            region = output.at[:, :, block, pl.ds(other, 2), :, columns]
            remote(region, cs_sem.at[i, 0], cr_sem.at[i, 0], (c_seq, fsdp)).wait_recv()

    chunks = len(plan)
    ahead = 3
    for i in range(min(ahead, chunks)):
        start_z(i)
    for t in range(chunks + 2):
        if t + ahead < chunks:
            start_z(t + ahead)
        if t < chunks:
            start_y(t)
        if 0 <= t - 1 < chunks:
            start_x(t - 1)
        if 0 <= t - 2 < chunks:
            start_core(t - 2)
    for i in range(chunks):
        finish(i)
    for copy in sends:
        copy.wait_send()
    if has_vectors:
        own.wait()
        for k in range(1, 8):
            vector_sends[k - 1].wait_send()
            region = vector_out.at[(fsdp + 8 - k) % 8]
            remote(region, vs_sem.at[k], vr_sem.at[k], (seq, (fsdp + k) % 8)).wait_recv()


def gather_plan(shapes):
    places = [
        (weight, block, column)
        for weight, (rows, columns) in enumerate(shapes)
        for block in range(rows // 192)
        for column in range(0, columns, CHUNK)
    ]
    return tuple(place + ((len(places) - 1 - i) % 3 != 0,) for i, place in enumerate(places))


def gather_weights(shards, vectors, collective_id):
    shapes = [shard.shape for shard in shards]
    plan = gather_plan(shapes)
    chunks = len(plan)
    inputs = [shard.reshape(rows // 192, 4, 48, columns) for shard, (rows, columns) in zip(shards, shapes)]
    out_shapes = [
        jax.ShapeDtypeStruct((4, 2, rows // 192, 4, 48, columns), BF16) for rows, columns in shapes
    ]
    if vectors is not None:
        inputs.append(vectors)
        out_shapes.append(jax.ShapeDtypeStruct((8,) + vectors.shape, vectors.dtype))
    anywhere = pl.BlockSpec(memory_space=pl.ANY)
    dma = pltpu.SemaphoreType.DMA
    results = pl.pallas_call(
        functools.partial(gather_kernel, plan, vectors is not None),
        out_shape=out_shapes,
        in_specs=[anywhere] * len(inputs),
        out_specs=[anywhere] * len(out_shapes),
        scratch_shapes=[
            dma((chunks, 4)),
            dma((chunks, 4)),
            dma((chunks,)),
            dma((chunks,)),
            dma((chunks,)),
            dma((chunks,)),
            dma((chunks, 2)),
            dma((chunks, 2)),
            dma((chunks,)),
            dma((8,)),
            dma((8,)),
        ],
        compiler_params=pltpu.CompilerParams(collective_id=collective_id, has_side_effects=True),
        name="gather_weights",
    )(*inputs)
    whole = [result.reshape(8 * rows, columns) for result, (rows, columns) in zip(results, shapes)]
    return whole, results[-1]


def gather_quarters(shard):
    part = shard.shape[0] // lax.axis_size("seq")
    mine = lax.dynamic_slice_in_dim(shard, lax.axis_index("seq") * part, part, 0)
    return lax.all_gather(mine, ("fsdp", "seq"), axis=0, tiled=True)


def pack_vectors(vectors):
    stacked = jnp.stack([vector.astype(F32) for vector in vectors])
    return jnp.pad(stacked, ((0, 8 - stacked.shape[0]), (0, (-stacked.shape[1]) % 128)))


def blocks_kernel(left, *refs):
    *rights, out = refs
    width = rights[0].shape[1]
    for kind, right in enumerate(rights):
        out[0, :, kind * width : (kind + 1) * width] = jnp.dot(
            left[...], right[...], preferred_element_type=F32
        ).astype(BF16)


def product_blocks(left, right, kinds, groups):
    rows, depth = left.shape
    width = right.shape[1] // (kinds * groups)
    spec = lambda kind: pl.BlockSpec((depth, width), lambda i: (0, kind * groups + i))
    return pl.pallas_call(
        blocks_kernel,
        grid=(groups,),
        out_shape=jax.ShapeDtypeStruct((groups, rows, kinds * width), BF16),
        in_specs=[pl.BlockSpec((rows, depth), lambda i: (0, 0))] + [spec(k) for k in range(kinds)],
        out_specs=pl.BlockSpec((1, rows, kinds * width), lambda i: (i, 0, 0)),
        compiler_params=pltpu.CompilerParams(vmem_limit_bytes=48 << 20),
        cost_estimate=pl.CostEstimate(
            flops=2 * rows * right.size,
            bytes_accessed=2 * (rows * depth + right.size + rows * right.shape[1]),
            transcendentals=0,
        ),
        name="product_blocks",
    )(left, *[right] * kinds)


QUERIES = 256


def both_heads(value):
    lane = lax.broadcasted_iota(jnp.int32, value.shape, 1)
    zero = jnp.zeros_like(value)
    return jnp.where(lane < HD, value, zero), jnp.where(lane < HD, zero, value)


def across(left, right):
    return lax.dot_general(left, right, (((1,), (1,)), ((), ())), preferred_element_type=F32)


def down(left, right):
    return lax.dot_general(left, right, (((0,), (0,)), ((), ())), preferred_element_type=F32)


def join_heads(pair):
    row = lax.broadcasted_iota(jnp.int32, pair[0].shape, 0)
    return jnp.where(row < HD, pair[0], pair[1])


def key_parts(block):
    return ([(0, block * QUERIES, False)] if block else []) + [
        (block * QUERIES, (block + 1) * QUERIES, True)
    ]


def masked_scores(keys, queries, diagonal):
    scores = across(keys, queries)
    if diagonal:
        key = lax.broadcasted_iota(jnp.int32, scores.shape, 0)
        query = lax.broadcasted_iota(jnp.int32, scores.shape, 1)
        scores = jnp.where(key <= query, scores, NEGATIVE)
    return scores


def attention_kernel(scale, q_ref, k_ref, v_ref, out_ref, logsum_ref):
    blocks = q_ref.shape[0] * q_ref.shape[2] // QUERIES
    k = k_ref[:, 0].reshape(-1, 2 * HD)
    v = v_ref[:, 0].reshape(-1, 2 * HD)
    for block in range(blocks):
        rows = slice(block * QUERIES, (block + 1) * QUERIES)
        queries = both_heads((q_ref[block, 0].astype(F32) * scale).astype(BF16))
        outs = []
        for head in range(2):
            parts = key_parts(block)
            scores = [masked_scores(k[a:b], queries[head], diagonal) for a, b, diagonal in parts]
            highest = functools.reduce(
                jnp.maximum, [jnp.max(part, axis=0, keepdims=True) for part in scores]
            )
            raised = [jnp.exp(part - highest) for part in scores]
            summed = sum(jnp.sum(part, axis=0, keepdims=True) for part in raised)
            total = sum(
                down(v[a:b], part.astype(BF16)) for (a, b, _), part in zip(parts, raised)
            )
            outs.append(total / summed)
            logsum_ref[0, 0, head : head + 1, rows] = highest + jnp.log(summed)
        out_ref[block, 0] = join_heads(outs).T.astype(BF16)


def attention(qkv, scale):
    blocks, clips, frames, width = qkv.shape
    pairs = width // (3 * 2 * HD)
    length = blocks * frames
    spec = lambda offset: pl.BlockSpec(
        (blocks, 1, frames, 2 * HD), lambda clip, pair: (0, clip, 0, offset + pair)
    )
    return pl.pallas_call(
        functools.partial(attention_kernel, scale),
        grid=(clips, pairs),
        out_shape=(
            jax.ShapeDtypeStruct((blocks, clips, frames, pairs * 2 * HD), BF16),
            jax.ShapeDtypeStruct((clips, pairs, 2, length), F32),
        ),
        in_specs=[spec(0), spec(pairs), spec(2 * pairs)],
        out_specs=(
            spec(0),
            pl.BlockSpec((1, 1, 2, length), lambda clip, pair: (clip, pair, 0, 0)),
        ),
        compiler_params=pltpu.CompilerParams(vmem_limit_bytes=48 << 20),
        cost_estimate=pl.CostEstimate(
            flops=clips * pairs * 2 * 4 * length * length * 2 * HD,
            bytes_accessed=4 * clips * pairs * length * 2 * HD * 2,
            transcendentals=clips * pairs * 2 * length * length,
        ),
        name="attention",
    )(qkv, qkv, qkv)


def attention_back_kernel(
    scale, q_ref, k_ref, v_ref, grad_ref, logsum_ref, out_ref, grad_keys, grad_values
):
    blocks = q_ref.shape[0] * q_ref.shape[2] // QUERIES
    frames = q_ref.shape[2]
    pair = pl.program_id(1)
    group = pl.num_programs(1) * 2 * HD
    k = k_ref[:, 0].reshape(-1, 2 * HD)
    v = v_ref[:, 0].reshape(-1, 2 * HD)

    def columns(kind):
        return pl.ds(pl.multiple_of(kind * group + pair * 2 * HD, 2 * HD), 2 * HD)

    for block in range(blocks):
        rows = slice(block * QUERIES, (block + 1) * QUERIES)
        queries = both_heads((q_ref[block, 0].astype(F32) * scale).astype(BF16))
        grads = both_heads(grad_ref[block, 0])
        parts = key_parts(block)
        query_grads = []
        held = [[], []]
        for head in range(2):
            logsum = logsum_ref[0, 0, head : head + 1, rows]
            weights, weighted = [], []
            for a, b, diagonal in parts:
                weight = jnp.exp(masked_scores(k[a:b], queries[head], diagonal) - logsum)
                weights.append(weight)
                weighted.append(weight * across(v[a:b], grads[head]))
            inner = sum(jnp.sum(part, axis=0, keepdims=True) for part in weighted)
            changes = [
                (term - weight * inner).astype(BF16) for term, weight in zip(weighted, weights)
            ]
            query_grads.append(sum(down(k[a:b], part) for (a, b, _), part in zip(parts, changes)))
            held[head] = [(weight.astype(BF16), change) for weight, change in zip(weights, changes)]
        out_ref[block, 0, :, columns(0)] = (join_heads(query_grads).T * scale).astype(BF16)
        for j, (a, b, diagonal) in enumerate(parts):
            value_term = sum(
                jnp.dot(held[head][j][0], grads[head], preferred_element_type=F32)
                for head in range(2)
            )
            key_term = sum(
                jnp.dot(held[head][j][1], queries[head], preferred_element_type=F32)
                for head in range(2)
            )
            if diagonal:
                grad_values[a:b] = value_term
                grad_keys[a:b] = key_term
            else:
                grad_values[a:b] += value_term
                grad_keys[a:b] += key_term
    out_ref[:, 0, :, columns(1)] = grad_keys[...].reshape(-1, frames, 2 * HD).astype(BF16)
    out_ref[:, 0, :, columns(2)] = grad_values[...].reshape(-1, frames, 2 * HD).astype(BF16)


def attention_back(qkv, grad, logsum, scale):
    blocks, clips, frames, width = qkv.shape
    pairs = width // (3 * 2 * HD)
    length = blocks * frames
    spec = lambda offset: pl.BlockSpec(
        (blocks, 1, frames, 2 * HD), lambda clip, pair: (0, clip, 0, offset + pair)
    )
    return pl.pallas_call(
        functools.partial(attention_back_kernel, scale),
        grid=(clips, pairs),
        out_shape=jax.ShapeDtypeStruct(qkv.shape, BF16),
        in_specs=[
            spec(0),
            spec(pairs),
            spec(2 * pairs),
            spec(0),
            pl.BlockSpec((1, 1, 2, length), lambda clip, pair: (clip, pair, 0, 0)),
        ],
        out_specs=pl.BlockSpec((blocks, 1, frames, width), lambda clip, pair: (0, clip, 0, 0)),
        scratch_shapes=[pltpu.VMEM((length, 2 * HD), F32), pltpu.VMEM((length, 2 * HD), F32)],
        compiler_params=pltpu.CompilerParams(vmem_limit_bytes=48 << 20),
        cost_estimate=pl.CostEstimate(
            flops=clips * pairs * 2 * 10 * length * length * 2 * HD,
            bytes_accessed=7 * clips * pairs * length * 2 * HD * 2,
            transcendentals=clips * pairs * 2 * length * length,
        ),
        name="attention_back",
    )(qkv, qkv, qkv, grad, logsum)


def text_weights(scale, queries, keys):
    scores = across(keys, queries)
    raised = jnp.exp(scores - jnp.max(scores, axis=0, keepdims=True))
    return raised / jnp.sum(raised, axis=0, keepdims=True)


def pair_columns(pair):
    return slice(pair * 2 * HD, (pair + 1) * 2 * HD)


def text_attention_kernel(scale, q_ref, memory_ref, out_ref):
    pairs = q_ref.shape[1] // (2 * HD)
    for pair in range(pairs):
        queries = both_heads((q_ref[:, pair_columns(pair)].astype(F32) * scale).astype(BF16))
        k = memory_ref[:, pair_columns(pair)]
        v = memory_ref[:, pair_columns(pairs + pair)]
        outs = [down(v, text_weights(scale, part, k).astype(BF16)) for part in queries]
        out_ref[:, pair_columns(pair)] = join_heads(outs).T.astype(BF16)


def text_attention_back_kernel(scale, q_ref, memory_ref, grad_ref, q_out, memory_out):
    pairs = q_ref.shape[1] // (2 * HD)
    for pair in range(pairs):
        queries = both_heads((q_ref[:, pair_columns(pair)].astype(F32) * scale).astype(BF16))
        grads = both_heads(grad_ref[:, pair_columns(pair)])
        k = memory_ref[:, pair_columns(pair)]
        v = memory_ref[:, pair_columns(pairs + pair)]
        query_grads = []
        key_grad = value_grad = 0.0
        for head in range(2):
            weights = text_weights(scale, queries[head], k)
            weighted = weights * across(v, grads[head])
            inner = jnp.sum(weighted, axis=0, keepdims=True)
            change = (weighted - weights * inner).astype(BF16)
            query_grads.append(down(k, change))
            key_grad += jnp.dot(change, queries[head], preferred_element_type=F32)
            value_grad += jnp.dot(weights.astype(BF16), grads[head], preferred_element_type=F32)
        q_out[:, pair_columns(pair)] = (join_heads(query_grads).T * scale).astype(BF16)
        memory_out[:, pair_columns(pair)] = key_grad.astype(BF16)
        memory_out[:, pair_columns(pairs + pair)] = value_grad.astype(BF16)


def text_attention(clips, scale, queries, memory, grad=None):
    spec = lambda value: pl.BlockSpec(
        (value.shape[0] // clips, value.shape[1]), lambda clip: (clip, 0)
    )
    back = grad is not None
    operands = (queries, memory) + ((grad,) if back else ())
    results = (queries, memory) if back else (queries,)
    size = memory.shape[0] // clips * queries.size
    outs = pl.pallas_call(
        functools.partial(text_attention_back_kernel if back else text_attention_kernel, scale),
        grid=(clips,),
        out_shape=[jax.ShapeDtypeStruct(value.shape, BF16) for value in results],
        in_specs=[spec(value) for value in operands],
        out_specs=[spec(value) for value in results],
        compiler_params=pltpu.CompilerParams(vmem_limit_bytes=32 << 20),
        cost_estimate=pl.CostEstimate(
            flops=(20 if back else 8) * size,
            bytes_accessed=2 * sum(value.size for value in operands + results),
            transcendentals=size // HD,
        ),
        name="text_attention_back" if back else "text_attention",
    )(*operands)
    return outs if back else outs[0]


PIECE = (192, 384)
EARLY = 32
OVER_X = 1
STAGES = 7
SLOTS = 6


def sum_kernel(plan, weights, *refs):
    chunks = len(plan)
    late = chunks - 3
    lefts, rights = refs[:weights], refs[weights : 2 * weights - 1]
    refs = refs[2 * weights - 1 :]
    heads_in, projection, hidden_in, grad_in, gain_in, vector_in = refs[:6]
    outputs = refs[6 : 6 + weights]
    heads, hidden_out, vector_out = refs[6 + weights : 9 + weights]
    (
        mine,
        c_out,
        c_in,
        x_in,
        y_in,
        second_in,
        z_in,
        early_z_in,
        early_y_in,
        early_x_in,
        total,
        fx_in,
        fc_in,
        stage,
        left_buf,
        right_buf,
        weight_buf,
        normed_grad,
        hidden,
        grad,
        gain,
        vector,
        vector_got,
        vector_z,
        c_sem,
        x_sem,
        y_sem,
        second_x_sem,
        second_y_sem,
        z_sem,
        early_sem,
        fx_sem,
        fc_sem,
        stage_sem,
        load_sem,
        vector_sem,
        heads_sem,
        own_sem,
    ) = refs[9 + weights :]
    rights = rights + (heads,)
    seq = lax.axis_index("seq")
    fsdp = lax.axis_index("fsdp")
    x, c = seq // 2, seq % 2
    z, y = fsdp // 2, fsdp % 2
    x_device = (2 * (1 - x) + c, fsdp)
    c_device = (2 * x + 1 - c, fsdp)
    far_device = (3 - seq, fsdp)
    y_device = (seq, 2 * z + 1 - y)

    def z_device(k):
        return (seq, 2 * ((z + k) % 4) + y)

    barrier = pltpu.get_barrier_semaphore()
    partners = [x_device, c_device, far_device, y_device] + [z_device(k) for k in (1, 2, 3)]
    for partner in partners:
        pl.semaphore_signal(barrier, inc=1, device_id=partner, device_id_type=MESH)
    pl.semaphore_wait(barrier, len(partners))

    def remote(source, target, sems, device):
        return pltpu.make_async_remote_copy(
            src_ref=source,
            dst_ref=target,
            send_sem=sems.at[0],
            recv_sem=sems.at[1],
            device_id=device,
            device_id_type=MESH,
        )

    def columns(block):
        return pl.ds(pl.multiple_of(block * 384, 128), 384)

    neighbours = (x_device, c_device, far_device)

    def heads_send(which, kind):
        return remote(
            heads_in.at[neighbours[which][0], :, pl.ds(kind * 384, 384)],
            heads.at[:, columns(kind * 4 + seq)],
            heads_sem.at[:, which, kind],
            neighbours[which],
        )

    def heads_arrival(which, kind):
        region = heads.at[:, columns(kind * 4 + neighbours[which][0])]
        return remote(region, region, heads_sem.at[:, which, kind], neighbours[which])

    def heads_own(kind):
        return pltpu.make_async_copy(
            heads_in.at[seq, :, pl.ds(kind * 384, 384)],
            heads.at[:, columns(kind * 4 + seq)],
            own_sem.at[kind],
        )

    def whole(kind):
        return pltpu.make_async_copy(
            projection.at[:, pl.ds(kind * 1536, 1536)], weight_buf, own_sem.at[3]
        )

    operands = [
        pltpu.make_async_copy(hidden_in, hidden, own_sem.at[4]),
        pltpu.make_async_copy(grad_in, grad, own_sem.at[5]),
        pltpu.make_async_copy(gain_in, gain, own_sem.at[6]),
        pltpu.make_async_copy(vector_in, vector.at[0], own_sem.at[7]),
    ]

    def loads(j):
        weight, column = plan[j]
        slot = j % 2
        return [
            pltpu.make_async_copy(lefts[weight], left_buf.at[slot], load_sem.at[0, slot]),
            pltpu.make_async_copy(
                rights[weight].at[:, pl.ds(column, 1536)], right_buf.at[slot], load_sem.at[1, slot]
            ),
        ]

    def start_loads(i):
        for j in range(chunks):

            @pl.when(i == j)
            def _():
                if j >= late:
                    heads_own(j - late).wait()
                    for which in range(3):
                        heads_arrival(which, j - late).wait_recv()
                for copy in loads(j):
                    copy.start()

    def wait_loads(i):
        for j in range(chunks):

            @pl.when(i == j)
            def _():
                for copy in loads(j):
                    copy.wait()

    def multiply(i, half, target, slot):
        buffer = i % 2
        right = right_buf.at[buffer, :, pl.ds(pl.multiple_of(half * 768, 128), 768)]

        @pl.loop(0, 4)
        def _(zz):
            out = down(left_buf[buffer, :, columns(zz)], right[...]).astype(BF16)
            for q in range(2):
                for yy in range(2):
                    target[slot, q, zz, yy] = out[192 * yy : 192 * yy + 192, 384 * q : 384 * q + 384]

    def multiply_back(i):
        for kind in range(3):

            @pl.when(i == late + kind)
            def _():
                whole(kind).wait()

                @pl.loop(0, right_buf.shape[1] // 128)
                def _(block):
                    rows = pl.ds(pl.multiple_of(block * 128, 128), 128)
                    term = across(right_buf[i % 2, rows, :], weight_buf[...])
                    if kind:
                        normed_grad[rows, :] += term
                    else:
                        normed_grad[rows, :] = term

                if kind < 2:
                    whole(kind + 1).start()

    def norm_back():
        for copy in operands:
            copy.wait()

        def block(index, terms):
            rows = pl.ds(pl.multiple_of(index * 32, 32), 32)
            value = hidden[rows, :].astype(F32)
            center = value - jnp.mean(value, axis=1, keepdims=True)
            inverse = lax.rsqrt(jnp.mean(center * center, axis=1, keepdims=True) + 1e-05)
            normed = center * inverse
            change = normed_grad[rows, :]
            scaled = change * gain[0:1, :]
            first_mean = jnp.mean(scaled, axis=1, keepdims=True)
            second_mean = jnp.mean(scaled * normed, axis=1, keepdims=True)
            grad[rows, :] += inverse * (scaled - first_mean - normed * second_mean)
            gains, biases = terms
            return (
                gains + jnp.sum(change * normed, axis=0, keepdims=True),
                biases + jnp.sum(change, axis=0, keepdims=True),
            )

        zero = jnp.zeros((1, gain.shape[1]), F32)
        gains, biases = lax.fori_loop(0, hidden.shape[0] // 32, block, (zero, zero))
        vector[0, 0:1, :] = gains
        vector[0, 1:2, :] = biases

    def add_to(slot, q, zz, yy, rows, other):
        here = mine[slot, q, zz, yy, rows].astype(F32)
        mine[slot, q, zz, yy, rows] = (here + other.astype(F32)).astype(BF16)

    early_rows = pl.ds(0, EARLY)
    other_rows = pl.ds(EARLY, PIECE[0] - EARLY)

    def c_copy(i):
        return remote(c_out.at[i % 2], c_in.at[i % 2], c_sem.at[:, i % 2], c_device)

    def x_copy(i, count):
        region = pl.ds(0, count)
        return remote(
            mine.at[i % 5, 1 - x, region, :, other_rows],
            x_in.at[i % 4, region],
            x_sem.at[:, i % 4],
            x_device,
        )

    def y_copy(i, count):
        return remote(
            mine.at[i % 5, :, pl.ds(count, 4 - count), 1 - y, other_rows],
            y_in.at[i % 4, :, pl.ds(0, 4 - count)],
            y_sem.at[:, i % 4],
            y_device,
        )

    def second_y_copy(i, count):
        region = pl.ds(0, count)
        return remote(
            mine.at[i % 5, x, region, 1 - y, other_rows],
            second_in.at[i % 5, region],
            second_y_sem.at[:, i % 5],
            y_device,
        )

    def second_x_copy(i, count):
        region = pl.ds(count, 4 - count)
        return remote(
            mine.at[i % 5, 1 - x, region, y, other_rows],
            second_in.at[i % 5, region],
            second_x_sem.at[:, i % 5],
            x_device,
        )

    def z_copy(i, k):
        return remote(
            mine.at[i % 5, x, (z + k) % 4, y, other_rows],
            z_in.at[i % 4, k - 1],
            z_sem.at[:, i % 4, k - 1],
            z_device(k),
        )

    def early_z_copy(i, k):
        return remote(
            mine.at[i % 5, :, (z + k) % 4, :, early_rows],
            early_z_in.at[i % 4, k - 1],
            early_sem.at[:, i % 4, k - 1],
            z_device(k),
        )

    def early_y_copy(i):
        return remote(
            mine.at[i % 5, :, z, 1 - y, early_rows],
            early_y_in.at[i % 4],
            early_sem.at[:, i % 4, 3],
            y_device,
        )

    def early_x_copy(i):
        return remote(
            mine.at[i % 5, 1 - x, z, y, early_rows],
            early_x_in.at[i % 4],
            early_sem.at[:, i % 4, 4],
            x_device,
        )

    def fx_copy(i):
        slot = i % SLOTS
        return remote(total.at[slot], fx_in.at[slot], fx_sem.at[:, slot], x_device)

    def fc_copy(i, which):
        slot = i % SLOTS
        source = fx_in.at[slot] if which else total.at[slot]
        return remote(source, fc_in.at[slot, which], fc_sem.at[:, slot, which], c_device)

    def begin(i):
        wait_loads(i)

        @pl.when(i >= 2)
        def _():
            c_copy(i - 2).wait_send()

        multiply(i, 1 - c, c_out, i % 2)
        c_copy(i).start()
        multiply(i, c, mine, i % 5)
        multiply_back(i)

    def first(i):
        c_copy(i).wait_recv()

        def add_c(q, zz, yy, rows):
            add_to(i % 5, q, zz, yy, rows, c_in[i % 2, q, zz, yy, rows])

        for k in (1, 2, 3):
            for q in range(2):
                for yy in range(2):
                    add_c(q, (z + k) % 4, yy, early_rows)
            early_z_copy(i, k).start()

        def run(i, count):
            @pl.loop(0, count)
            def _(zz):
                for yy in range(2):
                    add_c(1 - x, zz, yy, other_rows)

            x_copy(i, count).start()

            @pl.loop(count, 4)
            def _(zz):
                for q in range(2):
                    add_c(q, zz, 1 - y, other_rows)

            y_copy(i, count).start()

            @pl.loop(0, count)
            def _(zz):
                for yy in range(2):
                    add_c(x, zz, yy, other_rows)

            @pl.loop(count, 4)
            def _(zz):
                for q in range(2):
                    add_c(q, zz, y, other_rows)

        run(i, OVER_X)
        for q in range(2):
            for yy in range(2):
                add_c(q, z, yy, early_rows)

    def second(i):
        own, slot = i % 5, i % 4

        def run(i, count):
            def add_x(yy):
                @pl.loop(0, count)
                def _(zz):
                    add_to(own, x, zz, yy, other_rows, x_in[slot, zz, yy])

            def add_y(q):
                @pl.loop(count, 4)
                def _(zz):
                    add_to(own, q, zz, y, other_rows, y_in[slot, q, zz - count])

            x_copy(i, count).wait()
            add_x(1 - y)
            second_y_copy(i, count).start()
            y_copy(i, count).wait()
            add_y(1 - x)
            second_x_copy(i, count).start()
            add_x(y)
            add_y(x)

        run(i, OVER_X)
        for k in (1, 2, 3):
            early_z_copy(i, k).wait()

        def add_early(q, yy):
            others = [early_z_in[slot, k, q, yy].astype(F32) for k in range(3)]
            add_to(own, q, z, yy, early_rows, others[0] + others[1] + others[2])

        for q in range(2):
            add_early(q, 1 - y)
        early_y_copy(i).start()
        for q in range(2):
            add_early(q, y)

    def third(i):
        own, slot = i % 5, i % 4

        def run(i, count):
            second_y_copy(i, count).wait()
            second_x_copy(i, count).wait()

        run(i, OVER_X)
        for k in (1, 2, 3):
            zz = (z + k) % 4
            add_to(own, x, zz, y, other_rows, second_in[own, zz])
            z_copy(i, k).start()
        early_y_copy(i).wait()
        add_to(own, 1 - x, z, y, early_rows, early_y_in[slot, 1 - x])
        early_x_copy(i).start()
        add_to(own, x, z, y, early_rows, early_y_in[slot, x])

    def fourth(i):
        own, slot = i % 5, i % 4
        result = mine[own, x, z, y, other_rows].astype(F32) + second_in[own, z].astype(F32)
        for k in (1, 2, 3):
            z_copy(i, k).wait()
            result = result + z_in[slot, k - 1].astype(F32)
        total[i % SLOTS, other_rows] = result.astype(BF16)
        early_x_copy(i).wait()
        result = mine[own, x, z, y, early_rows].astype(F32) + early_x_in[slot].astype(F32)
        total[i % SLOTS, early_rows] = result.astype(BF16)
        fx_copy(i).start()
        fc_copy(i, 0).start()

    def fifth(i):
        fx_copy(i).wait()
        fc_copy(i, 1).start()

    def store(j):
        weight, column = plan[j]
        return pltpu.make_async_copy(
            stage.at[j % 2], outputs[weight].at[:, pl.ds(column, 1536)], stage_sem.at[j % 2]
        )

    def sixth(i):
        slot = i % SLOTS
        for j in range(2, chunks):

            @pl.when(i == j)
            def _():
                store(j - 2).wait()

        def put(quarter, value):
            stage[i % 2, :, columns(quarter)] = value

        fc_copy(i, 0).wait()
        fc_copy(i, 1).wait()
        put(2 * c + x, total[slot])
        put(2 * c + 1 - x, fx_in[slot])
        put(2 * (1 - c) + x, fc_in[slot, 0])
        put(2 * (1 - c) + 1 - x, fc_in[slot, 1])
        for j in range(chunks):

            @pl.when(i == j)
            def _():
                store(j).start()

    def vector_copy(leg):
        device = (c_device, x_device, y_device)[leg]
        return remote(vector.at[leg], vector_got.at[leg], vector_sem.at[:, leg], device)

    def vector_z_copy(k):
        return remote(vector_z.at[z], vector_z.at[z], vector_sem.at[:, 2 + k], z_device(k))

    def vector_arrival(k):
        source = (z + 4 - k) % 4
        return remote(vector_z.at[source], vector_z.at[source], vector_sem.at[:, 2 + k], z_device(k))

    hidden_store = pltpu.make_async_copy(grad, hidden_out, own_sem.at[5])

    def vector_step(step):
        @pl.when(step == 0)
        def _():
            norm_back()
            hidden_store.start()
            vector_copy(0).start()

        for leg in range(3):

            @pl.when(step == leg + 1)
            def _():
                vector_copy(leg).wait()
                both = vector[leg] + vector_got[leg]
                if leg < 2:
                    vector[leg + 1] = both
                    vector_copy(leg + 1).start()
                else:
                    vector_z[z] = both
                    for k in (1, 2, 3):
                        vector_z_copy(k).start()

        @pl.when(step == 4)
        def _():
            for k in (1, 2, 3):
                vector_z_copy(k).wait_send()
                vector_arrival(k).wait_recv()
            vector[0] = vector_z[0] + vector_z[1] + vector_z[2] + vector_z[3]
            pltpu.sync_copy(vector.at[0], vector_out)

    start_loads(0)
    for kind in range(3):
        heads_own(kind).start()
        for which in range(3):
            heads_send(which, kind).start()
    whole(0).start()
    for copy in operands:
        copy.start()

    @pl.loop(0, chunks + STAGES - 1)
    def _(t):
        @pl.when(t + 1 < chunks)
        def _():
            start_loads(t + 1)

        for lag, run in ((1, first), (0, begin), (2, second), (3, third), (4, fourth), (5, fifth), (6, sixth)):
            i = t - lag

            @pl.when(jnp.logical_and(i >= 0, i < chunks))
            def _():
                run(i)

        vector_step(t - chunks)

    for j in (chunks - 2, chunks - 1):
        c_copy(j).wait_send()
        store(j).wait()
    for kind in range(3):
        for which in range(3):
            heads_send(which, kind).wait_send()
    hidden_store.wait()


def sum_products(lefts, rights, heads, projection, hidden, grad, gain, vectors):
    weights = len(lefts)
    widths = [right.shape[1] for right in rights] + [projection.shape[1]]
    plan = [
        (weight, column)
        for weight, width in enumerate(widths)
        for column in range(0, width, 1536)
    ]
    depth, width = hidden.shape
    out_shapes = [
        jax.ShapeDtypeStruct((left.shape[1] // 8, columns), BF16)
        for left, columns in zip(lefts, widths)
    ]
    out_shapes += [
        jax.ShapeDtypeStruct((depth, widths[-1]), BF16),
        jax.ShapeDtypeStruct(grad.shape, F32),
        jax.ShapeDtypeStruct(vectors.shape, F32),
    ]
    inputs = (*lefts, *rights, heads, projection, hidden, grad, gain, vectors)
    anywhere = pl.BlockSpec(memory_space=pl.ANY)
    dma = pltpu.SemaphoreType.DMA
    rest = PIECE[0] - EARLY
    block = lambda *lead, rows=PIECE[0]: pltpu.VMEM(lead + (rows, PIECE[1]), BF16)
    results = pl.pallas_call(
        functools.partial(sum_kernel, tuple(plan), weights),
        out_shape=out_shapes,
        in_specs=[anywhere] * len(inputs),
        out_specs=[anywhere] * len(out_shapes),
        scratch_shapes=[
            block(5, 2, 4, 2),
            block(2, 2, 4, 2),
            block(2, 2, 4, 2),
            block(4, OVER_X, 2, rows=rest),
            block(4, 2, 4 - OVER_X, rows=rest),
            block(5, 4, rows=rest),
            block(4, 3, rows=rest),
            block(4, 3, 2, 2, rows=EARLY),
            block(4, 2, rows=EARLY),
            block(4, rows=EARLY),
            block(SLOTS),
            block(SLOTS),
            block(SLOTS, 2),
            pltpu.VMEM((2, 192, 1536), BF16),
            pltpu.VMEM((2, depth, 1536), BF16),
            pltpu.VMEM((2, depth, 1536), BF16),
            pltpu.VMEM((width, 1536), BF16),
            pltpu.VMEM((depth, width), F32),
            pltpu.VMEM((depth, width), BF16),
            pltpu.VMEM((depth, width), F32),
            pltpu.VMEM(gain.shape, F32),
            pltpu.VMEM((3,) + vectors.shape, F32),
            pltpu.VMEM((3,) + vectors.shape, F32),
            pltpu.VMEM((4,) + vectors.shape, F32),
            dma((2, 2)),
            dma((2, 4)),
            dma((2, 4)),
            dma((2, 5)),
            dma((2, 5)),
            dma((2, 4, 3)),
            dma((2, 4, 5)),
            dma((2, SLOTS)),
            dma((2, SLOTS, 2)),
            dma((2,)),
            dma((2, 2)),
            dma((2, 6)),
            dma((2, 3, 3)),
            dma((8,)),
        ],
        compiler_params=pltpu.CompilerParams(
            collective_id=3, has_side_effects=True, vmem_limit_bytes=60 << 20
        ),
        name="sum_products",
    )(*inputs)
    return results[:weights], results[-2], results[-1]


def on_blocks(
    hidden_states,
    text_states,
    self_gain,
    self_bias,
    query_key_value,
    self_output,
    cross_gain,
    cross_bias,
    cross_query,
    cross_memory,
    cross_output,
    final_gain,
    final_bias,
    expand_weight,
    contract_weight,
    output_cotangent,
):
    clips, frames, width = hidden_states.shape
    rows = clips * frames
    groups = lax.axis_size("seq")
    fsdp_count = lax.axis_size("fsdp")
    scale = HD ** (-0.5)
    entries = rows * groups * fsdp_count * width
    group_width = width // groups

    gains = (self_gain, self_bias, cross_gain, cross_bias, final_gain, final_bias)
    early = (query_key_value, self_output)
    (qkv_whole, self_output_whole), vectors = gather_weights(early, pack_vectors(gains), 1)
    qkv_whole, expand_weight = lax.optimization_barrier((qkv_whole, expand_weight))
    expand_whole = gather_quarters(expand_weight)
    vectors = vectors[:, :6, : width // fsdp_count]
    gains = [vectors[:, i].reshape(width) for i in range(6)]

    hidden = hidden_states.reshape(rows, width).astype(F32)
    normed_one = layer_norm(hidden, gains[0], gains[1]).astype(BF16)
    projected = product_blocks(normed_one, qkv_whole, 3, groups)
    regrouped = lax.all_to_all(projected, "seq", split_axis=0, concat_axis=0, tiled=True)
    regrouped = regrouped.reshape(groups, clips, frames, 3 * group_width)
    context_heads, logsum = attention(regrouped, scale)
    context_heads = context_heads.reshape(groups, rows, group_width)
    context = lax.all_to_all(context_heads, "seq", split_axis=0, concat_axis=0, tiled=True)
    late = (cross_query, cross_memory, cross_output)
    context, late, expand_whole, contract_weight = lax.optimization_barrier(
        (context, late, expand_whole, contract_weight)
    )
    contract_whole = gather_quarters(contract_weight)
    late, _ = gather_weights(late, None, 2)
    cross_query_whole, cross_memory_whole, cross_output_whole = late
    context = context.transpose(1, 0, 2).reshape(rows, width)
    attended = product(context, self_output_whole)
    first = hidden + attended
    normed_two, norm_two_back = jax.vjp(layer_norm, first, gains[2], gains[3])
    normed_two = normed_two.astype(BF16)
    cross_q = product(normed_two, cross_query_whole).astype(BF16)
    text_rows = text_states.reshape(clips * TEXT, width)
    memory = product(text_rows, cross_memory_whole).astype(BF16)
    cross_context = text_attention(clips, scale, cross_q, memory)
    crossed = product(cross_context, cross_output_whole)
    second = first + crossed
    normed_three, norm_three_back = jax.vjp(layer_norm, second, gains[4], gains[5])
    normed_three = normed_three.astype(BF16)
    preact = product(normed_three, expand_whole)
    below = 0.5 + 0.5 * lax.erf(preact * 0.5**0.5)
    density = jnp.exp(preact * preact * -0.5) * (0.5 / jnp.pi) ** 0.5
    activated = (preact * below).astype(BF16)
    slope = (below + preact * density).astype(BF16)
    upstream = output_cotangent.reshape(rows, width).astype(F32)
    grad_mixed = output_cotangent.reshape(rows, width)
    contract_term = product_left(activated, grad_mixed).astype(BF16)
    grad_mixed, contract_term, contract_whole = lax.optimization_barrier(
        (grad_mixed, contract_term, contract_whole)
    )
    contract_part = lax.psum_scatter(
        contract_term, ("fsdp", "seq"), scatter_dimension=0, tiled=True
    )
    grad_activated = product_right(grad_mixed, contract_whole)
    grad_preact = (grad_activated * slope.astype(F32)).astype(BF16)
    grad_normed_three = product_right(grad_preact, expand_whole)
    grad_second, final_gain_term, final_bias_term = norm_three_back(grad_normed_three)
    grad_second = upstream + grad_second
    grad_crossed = grad_second.astype(BF16)
    grad_cross_context = product_right(grad_crossed, cross_output_whole).astype(BF16)
    grad_cross_q, grad_memory = text_attention(clips, scale, cross_q, memory, grad_cross_context)
    grad_normed_two = product_right(grad_cross_q, cross_query_whole)
    grad_first, cross_gain_term, cross_bias_term = norm_two_back(grad_normed_two)
    grad_first = grad_second + grad_first
    grad_attended = grad_first.astype(BF16)
    grad_context = product_right(grad_attended, self_output_whole).astype(BF16)
    grad_context = grad_context.reshape(rows, groups, group_width).transpose(1, 0, 2)
    grad_context, activated = lax.optimization_barrier((grad_context, activated))
    grad_heads = lax.all_to_all(grad_context, "seq", split_axis=0, concat_axis=0, tiled=True)
    mixed = product(activated, contract_whole)
    output = second + mixed
    squares = jnp.stack(
        [
            jnp.sum(output * output),
            jnp.sum(attended * attended),
            jnp.sum(crossed * crossed),
            jnp.sum(mixed * mixed),
        ]
    )
    output = output.astype(BF16)
    zeros = jnp.zeros_like(cross_gain_term)
    terms = jnp.stack(
        [
            zeros,
            zeros,
            cross_gain_term,
            cross_bias_term,
            final_gain_term,
            final_bias_term,
            jnp.pad(squares, (0, width - 4)),
            zeros,
        ]
    )
    deep = lambda value: jnp.pad(value, ((0, rows - value.shape[0]), (0, 0)))
    text_operands = (deep(text_rows), deep(grad_memory))
    grad_heads, output, terms, text_operands = lax.optimization_barrier(
        (grad_heads, output, terms, text_operands)
    )
    grad_heads = grad_heads.reshape(groups, clips, frames, group_width)
    grad_regrouped = attention_back(regrouped, grad_heads, logsum, scale)
    gradients, grad_hidden, totals = sum_products(
        [normed_three, cross_context, normed_two, text_operands[0], context, normed_one],
        [grad_preact, grad_crossed, grad_cross_q, text_operands[1], grad_attended],
        grad_regrouped.reshape(groups, rows, 3 * group_width),
        qkv_whole,
        hidden_states.reshape(rows, width),
        grad_first,
        jnp.broadcast_to(gains[0], (8, width)),
        terms,
    )
    gradients, contract_part = lax.optimization_barrier((gradients, contract_part))
    contract_gradient = lax.all_gather(contract_part, "seq", axis=0, tiled=True)
    gradients = [gradient.astype(F32) for gradient in gradients]
    contract_gradient = contract_gradient.astype(F32)
    layer_rms = jnp.sqrt(totals[6, :4] / entries)
    shard = width // fsdp_count
    vector_gradients = lax.dynamic_slice_in_dim(
        totals, lax.axis_index("fsdp") * shard, shard, 1
    )
    return (
        output.reshape(clips, frames, width),
        grad_hidden.reshape(clips, frames, width),
        vector_gradients[0],
        vector_gradients[1],
        gradients[5],
        gradients[4],
        vector_gradients[2],
        vector_gradients[3],
        gradients[2],
        gradients[3],
        gradients[1],
        vector_gradients[4],
        vector_gradients[5],
        gradients[0],
        contract_gradient,
        layer_rms,
    )


def solution(mesh):
    shape = dict(mesh.shape)
    blocks = shape["seq"] == 4 and shape["fsdp"] == 8
    return jax.shard_map(
        on_blocks if blocks else on_any_mesh,
        mesh=mesh,
        in_specs=(
            P("fsdp", "seq", None),
            P("fsdp", None, None),
            P("fsdp"),
            P("fsdp"),
            P("fsdp", None),
            P("fsdp", None),
            P("fsdp"),
            P("fsdp"),
            P("fsdp", None),
            P("fsdp", None),
            P("fsdp", None),
            P("fsdp"),
            P("fsdp"),
            P("fsdp", None),
            P("fsdp", None),
            P("fsdp", "seq", None),
        ),
        out_specs=(
            P("fsdp", "seq", None),
            P("fsdp", "seq", None),
            P("fsdp"),
            P("fsdp"),
            P("fsdp", None),
            P("fsdp", None),
            P("fsdp"),
            P("fsdp"),
            P("fsdp", None),
            P("fsdp", None),
            P("fsdp", None),
            P("fsdp"),
            P("fsdp"),
            P("fsdp", None),
            P("fsdp", None),
            P(),
        ),
        check_vma=False,
    )
```

```python
import functools

import jax
import jax.numpy as jnp
from jax import lax
from jax.experimental import pallas as pl
from jax.experimental.pallas import tpu as pltpu
from jax.sharding import PartitionSpec as P

H = 24
HD = 64
TEXT = 64

NEGATIVE = -1e30
BF16 = jnp.bfloat16
F32 = jnp.float32
MESH = pl.DeviceIdType.MESH


def layer_norm(values, gain, offset):
    center = values - jnp.mean(values, axis=-1, keepdims=True)
    spread = jnp.mean(center * center, axis=-1, keepdims=True)
    return center * lax.rsqrt(spread + 1e-05) * gain + offset


def gelu_exact(values):
    return jax.nn.gelu(values, approximate=False)


def product(left, right):
    return jnp.dot(left, right, preferred_element_type=jnp.float32)


def product_left(left, right):
    return lax.dot_general(
        left, right, (((0,), (0,)), ((), ())), preferred_element_type=jnp.float32
    )


def product_right(left, right):
    return lax.dot_general(
        left, right, (((1,), (1,)), ((), ())), preferred_element_type=jnp.float32
    )


def causal_forward(queries, keys, values, rows_block, scale):
    clips, length, heads_local, head_width = queries.shape
    count = length // rows_block
    columns = jnp.arange(length, dtype=jnp.int32)

    def one_block(start):
        block = lax.dynamic_slice_in_dim(queries, start, rows_block, 1)
        scores = (
            jnp.einsum("cqhd,ckhd->chqk", block, keys, preferred_element_type=jnp.float32) * scale
        )
        positions = start + jnp.arange(rows_block, dtype=jnp.int32)
        allowed = columns[None, :] <= positions[:, None]
        scores = jnp.where(allowed, scores, NEGATIVE)
        highest = jnp.max(scores, axis=-1, keepdims=True)
        raised = jnp.exp(scores - highest)
        summed = jnp.sum(raised, axis=-1, keepdims=True)
        weights = (raised / summed).astype(jnp.bfloat16)
        result = jnp.einsum("chqk,ckhd->cqhd", weights, values, preferred_element_type=jnp.float32)
        return (result.astype(jnp.bfloat16), (highest + jnp.log(summed))[..., 0])

    starts = jnp.arange(count, dtype=jnp.int32) * rows_block
    results, logsum = lax.map(one_block, starts)
    results = jnp.moveaxis(results, 0, 1).reshape(clips, length, heads_local * head_width)
    return (results, logsum)


def causal_backward(queries, keys, values, logsum, grad_heads, rows_block, scale):
    clips, length, heads_local, head_width = queries.shape
    count = length // rows_block
    columns = jnp.arange(length, dtype=jnp.int32)
    starts = jnp.arange(count, dtype=jnp.int32) * rows_block

    def one_block(carry, inputs):
        grad_keys, grad_values = carry
        start, block_logsum = inputs
        block = lax.dynamic_slice_in_dim(queries, start, rows_block, 1)
        block_grad = lax.dynamic_slice_in_dim(grad_heads, start, rows_block, 1)
        scores = (
            jnp.einsum("cqhd,ckhd->chqk", block, keys, preferred_element_type=jnp.float32) * scale
        )
        positions = start + jnp.arange(rows_block, dtype=jnp.int32)
        allowed = columns[None, :] <= positions[:, None]
        scores = jnp.where(allowed, scores, NEGATIVE)
        weights = jnp.exp(scores - block_logsum[..., None])
        rounded = weights.astype(jnp.bfloat16)
        grad_weights = jnp.einsum(
            "cqhd,ckhd->chqk", block_grad, values, preferred_element_type=jnp.float32
        )
        inner = jnp.sum(weights * grad_weights, axis=-1, keepdims=True)
        grad_scores = (weights * (grad_weights - inner)).astype(jnp.bfloat16)
        grad_query = (
            jnp.einsum("chqk,ckhd->cqhd", grad_scores, keys, preferred_element_type=jnp.float32)
            * scale
        )
        grad_keys = (
            grad_keys
            + jnp.einsum("chqk,cqhd->ckhd", grad_scores, block, preferred_element_type=jnp.float32)
            * scale
        )
        grad_values = grad_values + jnp.einsum(
            "chqk,cqhd->ckhd", rounded, block_grad, preferred_element_type=jnp.float32
        )
        return ((grad_keys, grad_values), grad_query.astype(jnp.bfloat16))

    zeros = jnp.zeros(queries.shape, jnp.float32)
    (grad_keys, grad_values), grad_queries = lax.scan(one_block, (zeros, zeros), (starts, logsum))
    local_width = heads_local * head_width
    grad_queries = jnp.moveaxis(grad_queries, 0, 1).reshape(clips, length, local_width)
    grad_keys = grad_keys.astype(jnp.bfloat16).reshape(clips, length, local_width)
    grad_values = grad_values.astype(jnp.bfloat16).reshape(clips, length, local_width)
    return jnp.stack([grad_queries, grad_keys, grad_values], axis=2)


def on_any_mesh(
    hidden_states,
    text_states,
    self_gain,
    self_bias,
    query_key_value,
    self_output,
    cross_gain,
    cross_bias,
    cross_query,
    cross_memory,
    cross_output,
    final_gain,
    final_bias,
    expand_weight,
    contract_weight,
    output_cotangent,
):
    clips, frames, width = hidden_states.shape
    rows = clips * frames
    groups = lax.axis_size("seq")
    fsdp_count = lax.axis_size("fsdp")
    heads_local = H // groups
    length = frames * groups
    rows_block = min(512, length)
    scale = HD ** (-0.5)
    entries = rows * groups * fsdp_count * width
    self_set = (
        lax.all_gather(self_gain, "fsdp", axis=0, tiled=True),
        lax.all_gather(self_bias, "fsdp", axis=0, tiled=True),
        lax.all_gather(query_key_value, "fsdp", axis=0, tiled=True),
        lax.all_gather(self_output, "fsdp", axis=0, tiled=True),
    )
    hidden = hidden_states.reshape(rows, width).astype(jnp.float32)
    normed_one, norm_one_back = jax.vjp(
        layer_norm, hidden, self_set[0].astype(jnp.float32), self_set[1].astype(jnp.float32)
    )
    normed_one = normed_one.astype(jnp.bfloat16)
    projected = (
        product(normed_one, self_set[2]).astype(jnp.bfloat16).reshape(clips, frames, 3, width)
    )
    regrouped = lax.all_to_all(projected, "seq", split_axis=3, concat_axis=1, tiled=True)
    regrouped = regrouped.reshape(clips, length, 3, heads_local, HD)
    queries = regrouped[:, :, 0]
    keys = regrouped[:, :, 1]
    values = regrouped[:, :, 2]
    context_heads, logsum = causal_forward(queries, keys, values, rows_block, scale)
    context = lax.all_to_all(context_heads, "seq", split_axis=1, concat_axis=2, tiled=True).reshape(
        rows, width
    )
    attended = product(context, self_set[3])
    first = hidden + attended
    rest_set = (
        lax.all_gather(cross_gain, "fsdp", axis=0, tiled=True),
        lax.all_gather(cross_bias, "fsdp", axis=0, tiled=True),
        lax.all_gather(cross_query, "fsdp", axis=0, tiled=True),
        lax.all_gather(cross_memory, "fsdp", axis=0, tiled=True),
        lax.all_gather(cross_output, "fsdp", axis=0, tiled=True),
        lax.all_gather(final_gain, "fsdp", axis=0, tiled=True),
        lax.all_gather(final_bias, "fsdp", axis=0, tiled=True),
        lax.all_gather(expand_weight, "fsdp", axis=0, tiled=True),
        lax.all_gather(contract_weight, "fsdp", axis=0, tiled=True),
    )
    normed_two, norm_two_back = jax.vjp(
        layer_norm, first, rest_set[0].astype(jnp.float32), rest_set[1].astype(jnp.float32)
    )
    normed_two = normed_two.astype(jnp.bfloat16)
    cross_q = product(normed_two, rest_set[2]).astype(jnp.bfloat16).reshape(clips, frames, H, HD)
    text_rows = text_states.reshape(clips * TEXT, width)
    memory = product(text_rows, rest_set[3]).astype(jnp.bfloat16).reshape(clips, TEXT, 2, H, HD)
    cross_keys = memory[:, :, 0]
    cross_values = memory[:, :, 1]
    cross_scores = (
        jnp.einsum("cqhd,ckhd->chqk", cross_q, cross_keys, preferred_element_type=jnp.float32)
        * scale
    )
    highest = jnp.max(cross_scores, axis=-1, keepdims=True)
    raised = jnp.exp(cross_scores - highest)
    cross_weights = raised / jnp.sum(raised, axis=-1, keepdims=True)
    cross_rounded = cross_weights.astype(jnp.bfloat16)
    cross_context = jnp.einsum(
        "chqk,ckhd->cqhd", cross_rounded, cross_values, preferred_element_type=jnp.float32
    )
    cross_context = cross_context.astype(jnp.bfloat16).reshape(rows, width)
    crossed = product(cross_context, rest_set[4])
    second = first + crossed
    normed_three, norm_three_back = jax.vjp(
        layer_norm, second, rest_set[5].astype(jnp.float32), rest_set[6].astype(jnp.float32)
    )
    normed_three = normed_three.astype(jnp.bfloat16)
    preact = product(normed_three, rest_set[7])
    activated, gelu_back = jax.vjp(gelu_exact, preact)
    activated = activated.astype(jnp.bfloat16)
    mixed = product(activated, rest_set[8])
    output = second + mixed
    squares = jnp.stack(
        [
            jnp.sum(output * output),
            jnp.sum(attended * attended),
            jnp.sum(crossed * crossed),
            jnp.sum(mixed * mixed),
        ]
    )
    square_totals = lax.psum(squares, ("seq", "fsdp"))
    back_rest = (
        lax.all_gather(cross_gain, "fsdp", axis=0, tiled=True),
        lax.all_gather(cross_bias, "fsdp", axis=0, tiled=True),
        lax.all_gather(cross_query, "fsdp", axis=0, tiled=True),
        lax.all_gather(cross_memory, "fsdp", axis=0, tiled=True),
        lax.all_gather(cross_output, "fsdp", axis=0, tiled=True),
        lax.all_gather(final_gain, "fsdp", axis=0, tiled=True),
        lax.all_gather(final_bias, "fsdp", axis=0, tiled=True),
        lax.all_gather(expand_weight, "fsdp", axis=0, tiled=True),
        lax.all_gather(contract_weight, "fsdp", axis=0, tiled=True),
    )
    upstream = output_cotangent.reshape(rows, width).astype(jnp.float32)
    grad_mixed = upstream.astype(jnp.bfloat16)
    contract_term = product_left(activated, grad_mixed)
    grad_activated = product_right(grad_mixed, back_rest[8])
    grad_preact = gelu_back(grad_activated)[0].astype(jnp.bfloat16)
    expand_term = product_left(normed_three, grad_preact)
    grad_normed_three = product_right(grad_preact, back_rest[7])
    grad_second, final_gain_term, final_bias_term = norm_three_back(grad_normed_three)
    grad_second = upstream + grad_second
    grad_crossed = grad_second.astype(jnp.bfloat16)
    cross_output_term = product_left(cross_context, grad_crossed)
    grad_cross_context = (
        product_right(grad_crossed, back_rest[4]).astype(jnp.bfloat16).reshape(clips, frames, H, HD)
    )
    grad_cross_weights = jnp.einsum(
        "cqhd,ckhd->chqk", grad_cross_context, cross_values, preferred_element_type=jnp.float32
    )
    cross_inner = jnp.sum(cross_weights * grad_cross_weights, axis=-1, keepdims=True)
    grad_cross_scores = (cross_weights * (grad_cross_weights - cross_inner)).astype(jnp.bfloat16)
    grad_cross_q = (
        jnp.einsum(
            "chqk,ckhd->cqhd", grad_cross_scores, cross_keys, preferred_element_type=jnp.float32
        )
        * scale
    )
    grad_cross_q = grad_cross_q.astype(jnp.bfloat16).reshape(rows, width)
    grad_cross_keys = (
        jnp.einsum(
            "chqk,cqhd->ckhd", grad_cross_scores, cross_q, preferred_element_type=jnp.float32
        )
        * scale
    )
    grad_cross_values = jnp.einsum(
        "chqk,cqhd->ckhd", cross_rounded, grad_cross_context, preferred_element_type=jnp.float32
    )
    grad_memory = jnp.stack([grad_cross_keys, grad_cross_values], axis=2).reshape(
        clips * TEXT, 2 * width
    )
    memory_term = lax.dot_general(
        text_rows.astype(jnp.float32),
        grad_memory,
        (((0,), (0,)), ((), ())),
        precision=lax.Precision.HIGHEST,
        preferred_element_type=jnp.float32,
    )
    query_term = product_left(normed_two, grad_cross_q)
    grad_normed_two = product_right(grad_cross_q, back_rest[2])
    grad_first, cross_gain_term, cross_bias_term = norm_two_back(grad_normed_two)
    grad_first = grad_second + grad_first
    rest_sums = (
        lax.psum_scatter(
            cross_gain_term.astype(jnp.bfloat16), "fsdp", scatter_dimension=0, tiled=True
        ).astype(jnp.float32),
        lax.psum_scatter(
            cross_bias_term.astype(jnp.bfloat16), "fsdp", scatter_dimension=0, tiled=True
        ).astype(jnp.float32),
        lax.psum_scatter(
            query_term.astype(jnp.bfloat16), "fsdp", scatter_dimension=0, tiled=True
        ).astype(jnp.float32),
        lax.psum_scatter(
            memory_term.astype(jnp.bfloat16), "fsdp", scatter_dimension=0, tiled=True
        ).astype(jnp.float32),
        lax.psum_scatter(
            cross_output_term.astype(jnp.bfloat16), "fsdp", scatter_dimension=0, tiled=True
        ).astype(jnp.float32),
        lax.psum_scatter(
            final_gain_term.astype(jnp.bfloat16), "fsdp", scatter_dimension=0, tiled=True
        ).astype(jnp.float32),
        lax.psum_scatter(
            final_bias_term.astype(jnp.bfloat16), "fsdp", scatter_dimension=0, tiled=True
        ).astype(jnp.float32),
        lax.psum_scatter(
            expand_term.astype(jnp.bfloat16), "fsdp", scatter_dimension=0, tiled=True
        ).astype(jnp.float32),
        lax.psum_scatter(
            contract_term.astype(jnp.bfloat16), "fsdp", scatter_dimension=0, tiled=True
        ).astype(jnp.float32),
    )
    back_self = (
        lax.all_gather(self_gain, "fsdp", axis=0, tiled=True),
        lax.all_gather(self_bias, "fsdp", axis=0, tiled=True),
        lax.all_gather(query_key_value, "fsdp", axis=0, tiled=True),
        lax.all_gather(self_output, "fsdp", axis=0, tiled=True),
    )
    grad_attended = grad_first.astype(jnp.bfloat16)
    self_output_term = product_left(context, grad_attended)
    grad_context = (
        product_right(grad_attended, back_self[3])
        .astype(jnp.bfloat16)
        .reshape(clips, frames, width)
    )
    grad_heads = lax.all_to_all(grad_context, "seq", split_axis=2, concat_axis=1, tiled=True)
    grad_heads = grad_heads.reshape(clips, length, heads_local, HD)
    grad_regrouped = causal_backward(queries, keys, values, logsum, grad_heads, rows_block, scale)
    grad_projected = lax.all_to_all(
        grad_regrouped, "seq", split_axis=1, concat_axis=3, tiled=True
    ).reshape(rows, 3 * width)
    qkv_term = product_left(normed_one, grad_projected)
    grad_normed_one = product_right(grad_projected, back_self[2])
    grad_hidden, gain_one_term, bias_one_term = norm_one_back(grad_normed_one)
    grad_hidden = grad_first + grad_hidden
    self_sums = (
        lax.psum_scatter(
            gain_one_term.astype(jnp.bfloat16), "fsdp", scatter_dimension=0, tiled=True
        ).astype(jnp.float32),
        lax.psum_scatter(
            bias_one_term.astype(jnp.bfloat16), "fsdp", scatter_dimension=0, tiled=True
        ).astype(jnp.float32),
        lax.psum_scatter(
            qkv_term.astype(jnp.bfloat16), "fsdp", scatter_dimension=0, tiled=True
        ).astype(jnp.float32),
        lax.psum_scatter(
            self_output_term.astype(jnp.bfloat16), "fsdp", scatter_dimension=0, tiled=True
        ).astype(jnp.float32),
    )
    finals = (
        lax.psum(self_sums[0].astype(jnp.bfloat16), "seq").astype(jnp.float32),
        lax.psum(self_sums[1].astype(jnp.bfloat16), "seq").astype(jnp.float32),
        lax.psum(self_sums[2].astype(jnp.bfloat16), "seq").astype(jnp.float32),
        lax.psum(self_sums[3].astype(jnp.bfloat16), "seq").astype(jnp.float32),
        lax.psum(rest_sums[0].astype(jnp.bfloat16), "seq").astype(jnp.float32),
        lax.psum(rest_sums[1].astype(jnp.bfloat16), "seq").astype(jnp.float32),
        lax.psum(rest_sums[2].astype(jnp.bfloat16), "seq").astype(jnp.float32),
        lax.psum(rest_sums[3].astype(jnp.bfloat16), "seq").astype(jnp.float32),
        lax.psum(rest_sums[4].astype(jnp.bfloat16), "seq").astype(jnp.float32),
        lax.psum(rest_sums[5].astype(jnp.bfloat16), "seq").astype(jnp.float32),
        lax.psum(rest_sums[6].astype(jnp.bfloat16), "seq").astype(jnp.float32),
        lax.psum(rest_sums[7].astype(jnp.bfloat16), "seq").astype(jnp.float32),
        lax.psum(rest_sums[8].astype(jnp.bfloat16), "seq").astype(jnp.float32),
    )
    layer_rms = jnp.sqrt(square_totals / entries)
    return (
        output.astype(jnp.bfloat16).reshape(clips, frames, width),
        grad_hidden.reshape(clips, frames, width),
        finals[0],
        finals[1],
        finals[2],
        finals[3],
        finals[4],
        finals[5],
        finals[6],
        finals[7],
        finals[8],
        finals[9],
        finals[10],
        finals[11],
        finals[12],
        layer_rms,
    )


QUERIES = 256


def both_heads(value):
    lane = lax.broadcasted_iota(jnp.int32, value.shape, 1)
    zero = jnp.zeros_like(value)
    return jnp.where(lane < HD, value, zero), jnp.where(lane < HD, zero, value)


def across(left, right):
    return lax.dot_general(left, right, (((1,), (1,)), ((), ())), preferred_element_type=F32)


def down(left, right):
    return lax.dot_general(left, right, (((0,), (0,)), ((), ())), preferred_element_type=F32)


def join_heads(pair):
    row = lax.broadcasted_iota(jnp.int32, pair[0].shape, 0)
    return jnp.where(row < HD, pair[0], pair[1])


def key_parts(block):
    return ([(0, block * QUERIES, False)] if block else []) + [
        (block * QUERIES, (block + 1) * QUERIES, True)
    ]


def masked_scores(keys, queries, diagonal):
    scores = across(keys, queries)
    if diagonal:
        key = lax.broadcasted_iota(jnp.int32, scores.shape, 0)
        query = lax.broadcasted_iota(jnp.int32, scores.shape, 1)
        scores = jnp.where(key <= query, scores, NEGATIVE)
    return scores


def attention_kernel(scale, q_ref, k_ref, v_ref, out_ref, logsum_ref):
    blocks = q_ref.shape[0] * q_ref.shape[2] // QUERIES
    k = k_ref[:, 0].reshape(-1, 2 * HD)
    v = v_ref[:, 0].reshape(-1, 2 * HD)
    for block in range(blocks):
        rows = slice(block * QUERIES, (block + 1) * QUERIES)
        queries = both_heads((q_ref[block, 0].astype(F32) * scale).astype(BF16))
        outs = []
        for head in range(2):
            parts = key_parts(block)
            scores = [masked_scores(k[a:b], queries[head], diagonal) for a, b, diagonal in parts]
            highest = functools.reduce(
                jnp.maximum, [jnp.max(part, axis=0, keepdims=True) for part in scores]
            )
            raised = [jnp.exp(part - highest) for part in scores]
            summed = sum(jnp.sum(part, axis=0, keepdims=True) for part in raised)
            total = sum(
                down(v[a:b], part.astype(BF16)) for (a, b, _), part in zip(parts, raised)
            )
            outs.append(total / summed)
            logsum_ref[0, 0, head : head + 1, rows] = highest + jnp.log(summed)
        out_ref[block, 0] = join_heads(outs).T.astype(BF16)


def attention_back_kernel(
    scale, q_ref, k_ref, v_ref, grad_ref, logsum_ref, out_ref, grad_keys, grad_values
):
    blocks = q_ref.shape[0] * q_ref.shape[2] // QUERIES
    frames = q_ref.shape[2]
    pair = pl.program_id(1)
    group = pl.num_programs(1) * 2 * HD
    k = k_ref[:, 0].reshape(-1, 2 * HD)
    v = v_ref[:, 0].reshape(-1, 2 * HD)

    def columns(kind):
        return pl.ds(pl.multiple_of(kind * group + pair * 2 * HD, 2 * HD), 2 * HD)

    for block in range(blocks):
        rows = slice(block * QUERIES, (block + 1) * QUERIES)
        queries = both_heads((q_ref[block, 0].astype(F32) * scale).astype(BF16))
        grads = both_heads(grad_ref[block, 0])
        parts = key_parts(block)
        query_grads = []
        held = [[], []]
        for head in range(2):
            logsum = logsum_ref[0, 0, head : head + 1, rows]
            weights, weighted = [], []
            for a, b, diagonal in parts:
                weight = jnp.exp(masked_scores(k[a:b], queries[head], diagonal) - logsum)
                weights.append(weight)
                weighted.append(weight * across(v[a:b], grads[head]))
            inner = sum(jnp.sum(part, axis=0, keepdims=True) for part in weighted)
            changes = [
                (term - weight * inner).astype(BF16) for term, weight in zip(weighted, weights)
            ]
            query_grads.append(sum(down(k[a:b], part) for (a, b, _), part in zip(parts, changes)))
            held[head] = [(weight.astype(BF16), change) for weight, change in zip(weights, changes)]
        out_ref[block, 0, :, columns(0)] = (join_heads(query_grads).T * scale).astype(BF16)
        for j, (a, b, diagonal) in enumerate(parts):
            value_term = sum(
                jnp.dot(held[head][j][0], grads[head], preferred_element_type=F32)
                for head in range(2)
            )
            key_term = sum(
                jnp.dot(held[head][j][1], queries[head], preferred_element_type=F32)
                for head in range(2)
            )
            if diagonal:
                grad_values[a:b] = value_term
                grad_keys[a:b] = key_term
            else:
                grad_values[a:b] += value_term
                grad_keys[a:b] += key_term
    out_ref[:, 0, :, columns(1)] = grad_keys[...].reshape(-1, frames, 2 * HD).astype(BF16)
    out_ref[:, 0, :, columns(2)] = grad_values[...].reshape(-1, frames, 2 * HD).astype(BF16)


def attention_back(qkv, grad, logsum, scale):
    blocks, clips, frames, width = qkv.shape
    pairs = width // (3 * 2 * HD)
    length = blocks * frames
    spec = lambda offset: pl.BlockSpec(
        (blocks, 1, frames, 2 * HD), lambda clip, pair: (0, clip, 0, offset + pair)
    )
    return pl.pallas_call(
        functools.partial(attention_back_kernel, scale),
        grid=(clips, pairs),
        out_shape=jax.ShapeDtypeStruct(qkv.shape, BF16),
        in_specs=[
            spec(0),
            spec(pairs),
            spec(2 * pairs),
            spec(0),
            pl.BlockSpec((1, 1, 2, length), lambda clip, pair: (clip, pair, 0, 0)),
        ],
        out_specs=pl.BlockSpec((blocks, 1, frames, width), lambda clip, pair: (0, clip, 0, 0)),
        scratch_shapes=[pltpu.VMEM((length, 2 * HD), F32), pltpu.VMEM((length, 2 * HD), F32)],
        compiler_params=pltpu.CompilerParams(vmem_limit_bytes=48 << 20),
        cost_estimate=pl.CostEstimate(
            flops=clips * pairs * 2 * 10 * length * length * 2 * HD,
            bytes_accessed=7 * clips * pairs * length * 2 * HD * 2,
            transcendentals=clips * pairs * 2 * length * length,
        ),
        name="attention_back",
    )(qkv, qkv, qkv, grad, logsum)


def forward_kernel(plan, weights, scale, *refs):
    inputs = refs[:weights]
    vector_in, hidden_in = refs[weights : weights + 2]
    refs = refs[weights + 2 :]
    outputs = refs[:weights]
    vector_out, normed_out, heads, logsum_out, context = refs[weights : weights + 5]
    (
        vector_land,
        vector,
        hidden,
        normed,
        weight_buf,
        product_buf,
        q_buf,
        k_buf,
        v_buf,
        context_buf,
        logsum_buf,
        z_send,
        z_recv,
        y_sem,
        x_sem,
        c_sem,
        own_sem,
        vector_sem,
        load_sem,
        product_send,
        product_recv,
        block_sem,
        context_sem,
        context_own,
    ) = refs[weights + 5 :]
    seq = lax.axis_index("seq")
    fsdp = lax.axis_index("fsdp")
    x, c = seq // 2, seq % 2
    z, y = fsdp // 2, fsdp % 2
    x_seq = 2 * (1 - x) + c
    c_seq = 2 * x + 1 - c
    neighbours = (x_seq, c_seq, 3 - seq)
    y_fsdp = 2 * z + 1 - y
    chunks = len(plan)
    clips, pairs = logsum_buf.shape[:2]
    frames = hidden.shape[0] // clips

    def at_z(k):
        return (seq, 2 * ((z + k) % 4) + y)

    barrier = pltpu.get_barrier_semaphore()
    partners = [(other, fsdp) for other in neighbours] + [(seq, (fsdp + k) % 8) for k in range(1, 8)]
    for partner in partners:
        pl.semaphore_signal(barrier, inc=1, device_id=partner, device_id_type=MESH)
    pl.semaphore_wait(barrier, len(partners))

    def remote(source, target, send, recv, device):
        return pltpu.make_async_remote_copy(
            src_ref=source,
            dst_ref=target,
            send_sem=send,
            recv_sem=recv,
            device_id=device,
            device_id_type=MESH,
        )

    def over(region, sems, device):
        return remote(region, region, sems.at[0], sems.at[1], device)

    sends = []

    def send(copy):
        copy.start()
        sends.append(copy)

    def vector_copy(k):
        return remote(
            vector_in,
            vector_land.at[fsdp],
            vector_sem.at[0, k],
            vector_sem.at[1, k],
            (seq, (fsdp + k) % 8),
        )

    def vector_arrival(k):
        region = vector_land.at[(fsdp + 8 - k) % 8]
        return over(region, vector_sem.at[:, k], (seq, (fsdp + k) % 8))

    own_vector = pltpu.make_async_copy(vector_in, vector_land.at[fsdp], vector_sem.at[0, 0])
    hidden_load = pltpu.make_async_copy(hidden_in, hidden, vector_sem.at[1, 0])
    normed_store = pltpu.make_async_copy(normed, normed_out, vector_sem.at[1, 0])
    vector_store = pltpu.make_async_copy(vector, vector_out, vector_sem.at[0, 0])

    def norm():
        own_vector.wait()
        for k in range(1, 8):
            vector_arrival(k).wait_recv()
        hidden_load.wait()
        vector[...] = sum(vector_land[f] for f in range(8))
        vector_store.start()

        @pl.loop(0, hidden.shape[0] // 32)
        def _(block):
            rows = pl.ds(pl.multiple_of(block * 32, 32), 32)
            value = hidden[rows, :].astype(F32)
            center = value - jnp.mean(value, axis=1, keepdims=True)
            inverse = lax.rsqrt(jnp.mean(center * center, axis=1, keepdims=True) + 1e-05)
            normed[rows, :] = (center * inverse * vector[0:1, :] + vector[1:2, :]).astype(BF16)

        normed_store.start()

    def part(entry):
        weight, block, column, width, split = entry
        first = 2 * c + x if split else 2 * c
        return weight, block, pl.ds(column, width), pl.ds(first, 1 if split else 2)

    def start_z(i):
        weight, block, columns, mine = part(plan[i])
        source = inputs[weight].at[block, mine, :, columns]
        target = outputs[weight].at[z, y, block, mine, :, columns]
        for k in (1, 2, 3):
            send(remote(source, target, z_send.at[i, k - 1], z_recv.at[i, k - 1], at_z(k)))
        pltpu.make_async_copy(source, target, own_sem.at[i]).start()

    def start_y(i):
        weight, block, columns, mine = part(plan[i])
        output = outputs[weight]
        for k in (1, 2, 3):
            region = output.at[(z + 4 - k) % 4, y, block, mine, :, columns]
            remote(region, region, z_send.at[i, k - 1], z_recv.at[i, k - 1], at_z(k)).wait_recv()
        source = inputs[weight].at[block, mine, :, columns]
        target = output.at[z, y, block, mine, :, columns]
        pltpu.make_async_copy(source, target, own_sem.at[i]).wait()
        region = output.at[:, y, block, mine, :, columns]
        send(over(region, y_sem.at[:, i], (seq, y_fsdp)))

    def start_x(i):
        weight, block, columns, mine = part(plan[i])
        output = outputs[weight]
        region = output.at[:, 1 - y, block, mine, :, columns]
        over(region, y_sem.at[:, i], (seq, y_fsdp)).wait_recv()
        region = output.at[:, :, block, mine, :, columns]
        if plan[i][4]:
            send(over(region, x_sem.at[:, i], (x_seq, fsdp)))
        send(over(region, c_sem.at[:, i, 0], (c_seq, fsdp)))

    def start_core(i):
        if plan[i][4]:
            weight, block, columns, _ = part(plan[i])
            region = outputs[weight].at[:, :, block, pl.ds(2 * c + 1 - x, 1), :, columns]
            over(region, x_sem.at[:, i], (x_seq, fsdp)).wait_recv()
            send(over(region, c_sem.at[:, i, 1], (c_seq, fsdp)))

    def finish(i):
        weight, block, columns, _ = part(plan[i])
        other = 2 * (1 - c)
        output = outputs[weight]
        if plan[i][4]:
            for j, quarter in ((0, other + x), (1, other + 1 - x)):
                region = output.at[:, :, block, pl.ds(quarter, 1), :, columns]
                over(region, c_sem.at[:, i, j], (c_seq, fsdp)).wait_recv()
        else:
            region = output.at[:, :, block, pl.ds(other, 2), :, columns]
            over(region, c_sem.at[:, i, 0], (c_seq, fsdp)).wait_recv()

    def weight_load(i):
        region = outputs[0].at[:, :, 0, :, :, pl.ds(384 * i, 384)]
        return pltpu.make_async_copy(region, weight_buf.at[i % 2], load_sem.at[i % 2])

    def product_copy(i):
        kind, group = i // 4, i % 4
        target = heads.at[seq, :, pl.ds(384 * kind, 384)]
        away = remote(
            product_buf.at[i % 2],
            target,
            product_send.at[i],
            product_recv.at[kind, seq],
            (group, fsdp),
        )
        here = pltpu.make_async_copy(product_buf.at[i % 2], target, product_send.at[i])
        return group, away, here

    def start_product(i):
        group, away, here = product_copy(i)

        @pl.when(seq != group)
        def _():
            away.start()

        @pl.when(seq == group)
        def _():
            here.start()

    def wait_product(i):
        group, away, here = product_copy(i)

        @pl.when(seq != group)
        def _():
            away.wait_send()

        @pl.when(seq == group)
        def _():
            here.wait()

    def project(i):
        weight_load(i).wait()
        if i >= 2:
            wait_product(i - 2)
        right = weight_buf[i % 2].reshape(-1, 384)

        @pl.loop(0, normed.shape[0] // 256)
        def _(block):
            rows = pl.ds(pl.multiple_of(block * 256, 256), 256)
            out = jnp.dot(normed[rows, :], right, preferred_element_type=F32)
            product_buf[i % 2, rows, :] = out.astype(BF16)

        start_product(i)

    def wait_heads():
        for i in (10, 11):
            wait_product(i)
        for kind in range(3):
            for other in neighbours:
                region = heads.at[other, :, pl.ds(384 * kind, 384)]
                remote(
                    region, region, product_send.at[0], product_recv.at[kind, other], (other, fsdp)
                ).wait_recv()

    def block_loads(step):
        clip, pair = step // pairs, step % pairs
        return [
            pltpu.make_async_copy(
                heads.at[:, pl.ds(clip * frames, frames), pl.ds(384 * kind + 128 * pair, 128)],
                buffer.at[step % 2, :, 0],
                block_sem.at[kind, step % 2],
            )
            for kind, buffer in enumerate((q_buf, k_buf, v_buf))
        ]

    def start_blocks(step):
        for copy in block_loads(step):
            copy.start()

    def context_region(step, group):
        clip, pair = step // pairs, step % pairs
        column = pl.multiple_of(group * 384 + pair * 128, 128)
        return context.at[pl.ds(clip * frames, frames), pl.ds(column, 128)]

    def context_copy(step, which):
        other = neighbours[which]
        return remote(
            context_buf.at[step % 2, other, 0],
            context_region(step, seq),
            context_sem.at[0, step, which],
            context_sem.at[1, step, which],
            (other, fsdp),
        )

    def context_here(step):
        return pltpu.make_async_copy(
            context_buf.at[step % 2, seq, 0], context_region(step, seq), context_own.at[step]
        )

    def context_sent(step):
        for which in range(3):
            context_copy(step, which).wait_send()
        context_here(step).wait()

    def attend(step):
        for copy in block_loads(step):
            copy.wait()
        if step + 1 < clips * pairs:
            start_blocks(step + 1)
        if step >= 2:
            context_sent(step - 2)
        slot = step % 2
        attention_kernel(
            scale,
            q_buf.at[slot],
            k_buf.at[slot],
            v_buf.at[slot],
            context_buf.at[slot],
            logsum_buf.at[step // pairs, step % pairs],
        )
        for which in range(3):
            context_copy(step, which).start()
        context_here(step).start()

    steps = clips * pairs
    projections = 12
    attention_start = projections + 7
    beside = {2: [norm]}
    for i in range(projections):
        beside.setdefault(i + 4, []).extend(
            [functools.partial(finish, i), lambda i=i: weight_load(i).start()]
        )
        beside.setdefault(i + 5, []).insert(0, functools.partial(project, i))
    beside.setdefault(attention_start, []).extend([wait_heads, lambda: start_blocks(0)])
    for step in range(steps):
        beside.setdefault(attention_start + 1 + 2 * step, []).append(functools.partial(attend, step))

    hidden_load.start()
    own_vector.start()
    for k in range(1, 8):
        send(vector_copy(k))
    ahead = 3
    for i in range(ahead):
        start_z(i)
    for t in range(chunks + 2):
        if t + ahead < chunks:
            start_z(t + ahead)
        if t < chunks:
            start_y(t)
        if 0 <= t - 1 < chunks:
            start_x(t - 1)
        if 0 <= t - 2 < chunks:
            start_core(t - 2)
        for run in beside.pop(t, []):
            run()
    for i in range(projections, chunks):
        finish(i)
    for copy in sends:
        copy.wait_send()
    normed_store.wait()
    vector_store.wait()
    for step in (steps - 2, steps - 1):
        context_sent(step)
    for step in range(steps):
        for which in range(3):
            region = context_region(step, neighbours[which])
            over(region, context_sem.at[:, step, which], (neighbours[which], fsdp)).wait_recv()
    pltpu.sync_copy(logsum_buf, logsum_out)


def forward_plan(shapes):
    places = []
    for weight, (rows, columns) in enumerate(shapes):
        blocks = rows // 192
        for block in range(blocks):
            last = weight == len(shapes) - 1 and block == blocks - 1
            width = 384 if weight == 0 or last else 768
            places += [(weight, block, column, width) for column in range(0, columns, width)]
    return tuple(
        place + ((len(places) - 1 - i) * 5 % 9 >= 4,) for i, place in enumerate(places)
    )


def forward(shards, vectors, hidden, clips, scale):
    shapes = [shard.shape for shard in shards]
    plan = forward_plan(shapes)
    chunks, weights = len(plan), len(shards)
    rows, width = hidden.shape
    frames, group = rows // clips, width // 4
    pairs = group // (2 * HD)
    inputs = [shard.reshape(depth // 192, 4, 48, columns) for shard, (depth, columns) in zip(shards, shapes)]
    inputs += [vectors, hidden]
    out_shapes = [
        jax.ShapeDtypeStruct((4, 2, depth // 192, 4, 48, columns), BF16) for depth, columns in shapes
    ]
    logsum_shape = (clips, pairs, 1, 1, 2, 4 * frames)
    out_shapes += [
        jax.ShapeDtypeStruct(vectors.shape, F32),
        jax.ShapeDtypeStruct(hidden.shape, BF16),
        jax.ShapeDtypeStruct((4, rows, 3 * group), BF16),
        jax.ShapeDtypeStruct(logsum_shape, F32),
        jax.ShapeDtypeStruct(hidden.shape, BF16),
    ]
    anywhere = pl.BlockSpec(memory_space=pl.ANY)
    dma = pltpu.SemaphoreType.DMA
    pair_block = pltpu.VMEM((2, 4, 1, frames, 2 * HD), BF16)
    results = pl.pallas_call(
        functools.partial(forward_kernel, plan, weights, scale),
        out_shape=out_shapes,
        in_specs=[anywhere] * len(inputs),
        out_specs=[anywhere] * len(out_shapes),
        scratch_shapes=[
            pltpu.VMEM((8,) + vectors.shape, F32),
            pltpu.VMEM(vectors.shape, F32),
            pltpu.VMEM(hidden.shape, BF16),
            pltpu.VMEM(hidden.shape, BF16),
            pltpu.VMEM((2, 4, 2, 4, 48, 384), BF16),
            pltpu.VMEM((2, rows, 384), BF16),
            pair_block,
            pair_block,
            pair_block,
            pair_block,
            pltpu.VMEM(logsum_shape, F32),
            dma((chunks, 3)),
            dma((chunks, 3)),
            dma((2, chunks)),
            dma((2, chunks)),
            dma((2, chunks, 2)),
            dma((chunks,)),
            dma((2, 8)),
            dma((2,)),
            dma((12,)),
            dma((3, 4)),
            dma((3, 2)),
            dma((2, clips * pairs, 3)),
            dma((clips * pairs,)),
        ],
        compiler_params=pltpu.CompilerParams(
            collective_id=1, has_side_effects=True, vmem_limit_bytes=48 << 20
        ),
        name="forward",
    )(*inputs)
    wholes = [
        result.reshape(8 * depth, columns) for result, (depth, columns) in zip(results, shapes)
    ]
    vector, normed, heads, logsum, context = results[weights:]
    return wholes, vector, normed, heads, logsum.reshape(clips, pairs, 2, 4 * frames), context


def place_vectors(vectors):
    stacked = jnp.stack([vector.astype(F32) for vector in vectors])
    count, shard = stacked.shape
    whole = jnp.zeros((8, 8 * shard), F32)
    return lax.dynamic_update_slice(whole, stacked, (0, lax.axis_index("fsdp") * shard))


def text_weights(scale, queries, keys):
    scores = across(keys, queries)
    raised = jnp.exp(scores - jnp.max(scores, axis=0, keepdims=True))
    return raised / jnp.sum(raised, axis=0, keepdims=True)


def pair_columns(pair):
    return slice(pair * 2 * HD, (pair + 1) * 2 * HD)


def text_attention_kernel(scale, q_ref, memory_ref, out_ref):
    pairs = q_ref.shape[1] // (2 * HD)
    for pair in range(pairs):
        queries = both_heads((q_ref[:, pair_columns(pair)].astype(F32) * scale).astype(BF16))
        k = memory_ref[:, pair_columns(pair)]
        v = memory_ref[:, pair_columns(pairs + pair)]
        outs = [down(v, text_weights(scale, part, k).astype(BF16)) for part in queries]
        out_ref[:, pair_columns(pair)] = join_heads(outs).T.astype(BF16)


def text_attention_back_kernel(scale, q_ref, memory_ref, grad_ref, q_out, memory_out):
    pairs = q_ref.shape[1] // (2 * HD)
    for pair in range(pairs):
        queries = both_heads((q_ref[:, pair_columns(pair)].astype(F32) * scale).astype(BF16))
        grads = both_heads(grad_ref[:, pair_columns(pair)])
        k = memory_ref[:, pair_columns(pair)]
        v = memory_ref[:, pair_columns(pairs + pair)]
        query_grads = []
        key_grad = value_grad = 0.0
        for head in range(2):
            weights = text_weights(scale, queries[head], k)
            weighted = weights * across(v, grads[head])
            inner = jnp.sum(weighted, axis=0, keepdims=True)
            change = (weighted - weights * inner).astype(BF16)
            query_grads.append(down(k, change))
            key_grad += jnp.dot(change, queries[head], preferred_element_type=F32)
            value_grad += jnp.dot(weights.astype(BF16), grads[head], preferred_element_type=F32)
        q_out[:, pair_columns(pair)] = (join_heads(query_grads).T * scale).astype(BF16)
        memory_out[:, pair_columns(pair)] = key_grad.astype(BF16)
        memory_out[:, pair_columns(pairs + pair)] = value_grad.astype(BF16)


def text_attention(clips, scale, queries, memory, grad=None):
    spec = lambda value: pl.BlockSpec(
        (value.shape[0] // clips, value.shape[1]), lambda clip: (clip, 0)
    )
    back = grad is not None
    operands = (queries, memory) + ((grad,) if back else ())
    results = (queries, memory) if back else (queries,)
    size = memory.shape[0] // clips * queries.size
    outs = pl.pallas_call(
        functools.partial(text_attention_back_kernel if back else text_attention_kernel, scale),
        grid=(clips,),
        out_shape=[jax.ShapeDtypeStruct(value.shape, BF16) for value in results],
        in_specs=[spec(value) for value in operands],
        out_specs=[spec(value) for value in results],
        compiler_params=pltpu.CompilerParams(vmem_limit_bytes=32 << 20),
        cost_estimate=pl.CostEstimate(
            flops=(20 if back else 8) * size,
            bytes_accessed=2 * sum(value.size for value in operands + results),
            transcendentals=size // HD,
        ),
        name="text_attention_back" if back else "text_attention",
    )(*operands)
    return outs if back else outs[0]


PIECE = (192, 384)
EARLY = 32
OVER_X = 1
STAGES = 7
SLOTS = 6


def sum_kernel(plan, weights, *refs):
    chunks = len(plan)
    late = chunks - 3
    lefts, rights = refs[:weights], refs[weights : 2 * weights - 1]
    refs = refs[2 * weights - 1 :]
    heads_in, projection, hidden_in, grad_in, gain_in, vector_in = refs[:6]
    outputs = refs[6 : 6 + weights]
    heads, hidden_out, vector_out = refs[6 + weights : 9 + weights]
    (
        mine,
        c_out,
        c_in,
        x_in,
        y_in,
        second_in,
        z_in,
        early_z_in,
        early_y_in,
        early_x_in,
        total,
        fx_in,
        fc_in,
        stage,
        left_buf,
        right_buf,
        weight_buf,
        normed_grad,
        hidden,
        grad,
        gain,
        vector,
        vector_got,
        vector_z,
        c_sem,
        x_sem,
        y_sem,
        second_x_sem,
        second_y_sem,
        z_sem,
        early_sem,
        fx_sem,
        fc_sem,
        stage_sem,
        load_sem,
        vector_sem,
        heads_sem,
        own_sem,
    ) = refs[9 + weights :]
    rights = rights + (heads,)
    seq = lax.axis_index("seq")
    fsdp = lax.axis_index("fsdp")
    x, c = seq // 2, seq % 2
    z, y = fsdp // 2, fsdp % 2
    x_device = (2 * (1 - x) + c, fsdp)
    c_device = (2 * x + 1 - c, fsdp)
    far_device = (3 - seq, fsdp)
    y_device = (seq, 2 * z + 1 - y)

    def z_device(k):
        return (seq, 2 * ((z + k) % 4) + y)

    barrier = pltpu.get_barrier_semaphore()
    partners = [x_device, c_device, far_device, y_device] + [z_device(k) for k in (1, 2, 3)]
    for partner in partners:
        pl.semaphore_signal(barrier, inc=1, device_id=partner, device_id_type=MESH)
    pl.semaphore_wait(barrier, len(partners))

    def remote(source, target, sems, device):
        return pltpu.make_async_remote_copy(
            src_ref=source,
            dst_ref=target,
            send_sem=sems.at[0],
            recv_sem=sems.at[1],
            device_id=device,
            device_id_type=MESH,
        )

    def columns(block):
        return pl.ds(pl.multiple_of(block * 384, 128), 384)

    neighbours = (x_device, c_device, far_device)

    def heads_send(which, kind):
        return remote(
            heads_in.at[neighbours[which][0], :, pl.ds(kind * 384, 384)],
            heads.at[:, columns(kind * 4 + seq)],
            heads_sem.at[:, which, kind],
            neighbours[which],
        )

    def heads_arrival(which, kind):
        region = heads.at[:, columns(kind * 4 + neighbours[which][0])]
        return remote(region, region, heads_sem.at[:, which, kind], neighbours[which])

    def heads_own(kind):
        return pltpu.make_async_copy(
            heads_in.at[seq, :, pl.ds(kind * 384, 384)],
            heads.at[:, columns(kind * 4 + seq)],
            own_sem.at[kind],
        )

    def whole(kind):
        return pltpu.make_async_copy(
            projection.at[:, pl.ds(kind * 1536, 1536)], weight_buf, own_sem.at[3]
        )

    operands = [
        pltpu.make_async_copy(hidden_in, hidden, own_sem.at[4]),
        pltpu.make_async_copy(grad_in, grad, own_sem.at[5]),
        pltpu.make_async_copy(gain_in, gain, own_sem.at[6]),
        pltpu.make_async_copy(vector_in, vector.at[0], own_sem.at[7]),
    ]

    def loads(j):
        weight, column = plan[j]
        slot = j % 2
        return [
            pltpu.make_async_copy(lefts[weight], left_buf.at[slot], load_sem.at[0, slot]),
            pltpu.make_async_copy(
                rights[weight].at[:, pl.ds(column, 1536)], right_buf.at[slot], load_sem.at[1, slot]
            ),
        ]

    def start_loads(i):
        for j in range(chunks):

            @pl.when(i == j)
            def _():
                if j >= late:
                    heads_own(j - late).wait()
                    for which in range(3):
                        heads_arrival(which, j - late).wait_recv()
                for copy in loads(j):
                    copy.start()

    def wait_loads(i):
        for j in range(chunks):

            @pl.when(i == j)
            def _():
                for copy in loads(j):
                    copy.wait()

    def multiply(i, half, target, slot):
        buffer = i % 2
        right = right_buf.at[buffer, :, pl.ds(pl.multiple_of(half * 768, 128), 768)]

        @pl.loop(0, 4)
        def _(zz):
            out = down(left_buf[buffer, :, columns(zz)], right[...]).astype(BF16)
            for q in range(2):
                for yy in range(2):
                    target[slot, q, zz, yy] = out[192 * yy : 192 * yy + 192, 384 * q : 384 * q + 384]

    def multiply_back(i):
        for kind in range(3):

            @pl.when(i == late + kind)
            def _():
                whole(kind).wait()

                @pl.loop(0, right_buf.shape[1] // 128)
                def _(block):
                    rows = pl.ds(pl.multiple_of(block * 128, 128), 128)
                    term = across(right_buf[i % 2, rows, :], weight_buf[...])
                    if kind:
                        normed_grad[rows, :] += term
                    else:
                        normed_grad[rows, :] = term

                if kind < 2:
                    whole(kind + 1).start()

    def norm_back():
        for copy in operands:
            copy.wait()

        def block(index, terms):
            rows = pl.ds(pl.multiple_of(index * 32, 32), 32)
            value = hidden[rows, :].astype(F32)
            center = value - jnp.mean(value, axis=1, keepdims=True)
            inverse = lax.rsqrt(jnp.mean(center * center, axis=1, keepdims=True) + 1e-05)
            normed = center * inverse
            change = normed_grad[rows, :]
            scaled = change * gain[0:1, :]
            first_mean = jnp.mean(scaled, axis=1, keepdims=True)
            second_mean = jnp.mean(scaled * normed, axis=1, keepdims=True)
            grad[rows, :] += inverse * (scaled - first_mean - normed * second_mean)
            gains, biases = terms
            return (
                gains + jnp.sum(change * normed, axis=0, keepdims=True),
                biases + jnp.sum(change, axis=0, keepdims=True),
            )

        zero = jnp.zeros((1, gain.shape[1]), F32)
        gains, biases = lax.fori_loop(0, hidden.shape[0] // 32, block, (zero, zero))
        vector[0, 0:1, :] = gains
        vector[0, 1:2, :] = biases

    def add_to(slot, q, zz, yy, rows, other):
        here = mine[slot, q, zz, yy, rows].astype(F32)
        mine[slot, q, zz, yy, rows] = (here + other.astype(F32)).astype(BF16)

    early_rows = pl.ds(0, EARLY)
    other_rows = pl.ds(EARLY, PIECE[0] - EARLY)

    def c_copy(i):
        return remote(c_out.at[i % 2], c_in.at[i % 2], c_sem.at[:, i % 2], c_device)

    def x_copy(i, count):
        region = pl.ds(0, count)
        return remote(
            mine.at[i % 5, 1 - x, region, :, other_rows],
            x_in.at[i % 4, region],
            x_sem.at[:, i % 4],
            x_device,
        )

    def y_copy(i, count):
        return remote(
            mine.at[i % 5, :, pl.ds(count, 4 - count), 1 - y, other_rows],
            y_in.at[i % 4, :, pl.ds(0, 4 - count)],
            y_sem.at[:, i % 4],
            y_device,
        )

    def second_y_copy(i, count):
        region = pl.ds(0, count)
        return remote(
            mine.at[i % 5, x, region, 1 - y, other_rows],
            second_in.at[i % 5, region],
            second_y_sem.at[:, i % 5],
            y_device,
        )

    def second_x_copy(i, count):
        region = pl.ds(count, 4 - count)
        return remote(
            mine.at[i % 5, 1 - x, region, y, other_rows],
            second_in.at[i % 5, region],
            second_x_sem.at[:, i % 5],
            x_device,
        )

    def z_copy(i, k):
        return remote(
            mine.at[i % 5, x, (z + k) % 4, y, other_rows],
            z_in.at[i % 4, k - 1],
            z_sem.at[:, i % 4, k - 1],
            z_device(k),
        )

    def early_z_copy(i, k):
        return remote(
            mine.at[i % 5, :, (z + k) % 4, :, early_rows],
            early_z_in.at[i % 4, k - 1],
            early_sem.at[:, i % 4, k - 1],
            z_device(k),
        )

    def early_y_copy(i):
        return remote(
            mine.at[i % 5, :, z, 1 - y, early_rows],
            early_y_in.at[i % 4],
            early_sem.at[:, i % 4, 3],
            y_device,
        )

    def early_x_copy(i):
        return remote(
            mine.at[i % 5, 1 - x, z, y, early_rows],
            early_x_in.at[i % 4],
            early_sem.at[:, i % 4, 4],
            x_device,
        )

    def fx_copy(i):
        slot = i % SLOTS
        return remote(total.at[slot], fx_in.at[slot], fx_sem.at[:, slot], x_device)

    def fc_copy(i, which):
        slot = i % SLOTS
        source = fx_in.at[slot] if which else total.at[slot]
        return remote(source, fc_in.at[slot, which], fc_sem.at[:, slot, which], c_device)

    def begin(i):
        wait_loads(i)

        @pl.when(i >= 2)
        def _():
            c_copy(i - 2).wait_send()

        multiply(i, 1 - c, c_out, i % 2)
        c_copy(i).start()
        multiply(i, c, mine, i % 5)
        multiply_back(i)

    def first(i):
        c_copy(i).wait_recv()

        def add_c(q, zz, yy, rows):
            add_to(i % 5, q, zz, yy, rows, c_in[i % 2, q, zz, yy, rows])

        for k in (1, 2, 3):
            for q in range(2):
                for yy in range(2):
                    add_c(q, (z + k) % 4, yy, early_rows)
            early_z_copy(i, k).start()

        def run(i, count):
            @pl.loop(0, count)
            def _(zz):
                for yy in range(2):
                    add_c(1 - x, zz, yy, other_rows)

            x_copy(i, count).start()

            @pl.loop(count, 4)
            def _(zz):
                for q in range(2):
                    add_c(q, zz, 1 - y, other_rows)

            y_copy(i, count).start()

            @pl.loop(0, count)
            def _(zz):
                for yy in range(2):
                    add_c(x, zz, yy, other_rows)

            @pl.loop(count, 4)
            def _(zz):
                for q in range(2):
                    add_c(q, zz, y, other_rows)

        run(i, OVER_X)
        for q in range(2):
            for yy in range(2):
                add_c(q, z, yy, early_rows)

    def second(i):
        own, slot = i % 5, i % 4

        def run(i, count):
            def add_x(yy):
                @pl.loop(0, count)
                def _(zz):
                    add_to(own, x, zz, yy, other_rows, x_in[slot, zz, yy])

            def add_y(q):
                @pl.loop(count, 4)
                def _(zz):
                    add_to(own, q, zz, y, other_rows, y_in[slot, q, zz - count])

            x_copy(i, count).wait()
            add_x(1 - y)
            second_y_copy(i, count).start()
            y_copy(i, count).wait()
            add_y(1 - x)
            second_x_copy(i, count).start()
            add_x(y)
            add_y(x)

        run(i, OVER_X)
        for k in (1, 2, 3):
            early_z_copy(i, k).wait()

        def add_early(q, yy):
            others = [early_z_in[slot, k, q, yy].astype(F32) for k in range(3)]
            add_to(own, q, z, yy, early_rows, others[0] + others[1] + others[2])

        for q in range(2):
            add_early(q, 1 - y)
        early_y_copy(i).start()
        for q in range(2):
            add_early(q, y)

    def third(i):
        own, slot = i % 5, i % 4

        def run(i, count):
            second_y_copy(i, count).wait()
            second_x_copy(i, count).wait()

        run(i, OVER_X)
        for k in (1, 2, 3):
            zz = (z + k) % 4
            add_to(own, x, zz, y, other_rows, second_in[own, zz])
            z_copy(i, k).start()
        early_y_copy(i).wait()
        add_to(own, 1 - x, z, y, early_rows, early_y_in[slot, 1 - x])
        early_x_copy(i).start()
        add_to(own, x, z, y, early_rows, early_y_in[slot, x])

    def fourth(i):
        own, slot = i % 5, i % 4
        result = mine[own, x, z, y, other_rows].astype(F32) + second_in[own, z].astype(F32)
        for k in (1, 2, 3):
            z_copy(i, k).wait()
            result = result + z_in[slot, k - 1].astype(F32)
        total[i % SLOTS, other_rows] = result.astype(BF16)
        early_x_copy(i).wait()
        result = mine[own, x, z, y, early_rows].astype(F32) + early_x_in[slot].astype(F32)
        total[i % SLOTS, early_rows] = result.astype(BF16)
        fx_copy(i).start()
        fc_copy(i, 0).start()

    def fifth(i):
        fx_copy(i).wait()
        fc_copy(i, 1).start()

    def store(j):
        weight, column = plan[j]
        return pltpu.make_async_copy(
            stage.at[j % 2], outputs[weight].at[:, pl.ds(column, 1536)], stage_sem.at[j % 2]
        )

    def sixth(i):
        slot = i % SLOTS
        for j in range(2, chunks):

            @pl.when(i == j)
            def _():
                store(j - 2).wait()

        def put(quarter, value):
            stage[i % 2, :, columns(quarter)] = value

        fc_copy(i, 0).wait()
        fc_copy(i, 1).wait()
        put(2 * c + x, total[slot])
        put(2 * c + 1 - x, fx_in[slot])
        put(2 * (1 - c) + x, fc_in[slot, 0])
        put(2 * (1 - c) + 1 - x, fc_in[slot, 1])
        for j in range(chunks):

            @pl.when(i == j)
            def _():
                store(j).start()

    def vector_copy(leg):
        device = (c_device, x_device, y_device)[leg]
        return remote(vector.at[leg], vector_got.at[leg], vector_sem.at[:, leg], device)

    def vector_z_copy(k):
        return remote(vector_z.at[z], vector_z.at[z], vector_sem.at[:, 2 + k], z_device(k))

    def vector_arrival(k):
        source = (z + 4 - k) % 4
        return remote(vector_z.at[source], vector_z.at[source], vector_sem.at[:, 2 + k], z_device(k))

    hidden_store = pltpu.make_async_copy(grad, hidden_out, own_sem.at[5])

    def vector_step(step):
        @pl.when(step == 0)
        def _():
            norm_back()
            hidden_store.start()
            vector_copy(0).start()

        for leg in range(3):

            @pl.when(step == leg + 1)
            def _():
                vector_copy(leg).wait()
                both = vector[leg] + vector_got[leg]
                if leg < 2:
                    vector[leg + 1] = both
                    vector_copy(leg + 1).start()
                else:
                    vector_z[z] = both
                    for k in (1, 2, 3):
                        vector_z_copy(k).start()

        @pl.when(step == 4)
        def _():
            for k in (1, 2, 3):
                vector_z_copy(k).wait_send()
                vector_arrival(k).wait_recv()
            vector[0] = vector_z[0] + vector_z[1] + vector_z[2] + vector_z[3]
            pltpu.sync_copy(vector.at[0], vector_out)

    start_loads(0)
    for kind in range(3):
        heads_own(kind).start()
        for which in range(3):
            heads_send(which, kind).start()
    whole(0).start()
    for copy in operands:
        copy.start()

    @pl.loop(0, chunks + STAGES - 1)
    def _(t):
        @pl.when(t + 1 < chunks)
        def _():
            start_loads(t + 1)

        for lag, run in ((1, first), (0, begin), (2, second), (3, third), (4, fourth), (5, fifth), (6, sixth)):
            i = t - lag

            @pl.when(jnp.logical_and(i >= 0, i < chunks))
            def _():
                run(i)

        vector_step(t - chunks)

    for j in (chunks - 2, chunks - 1):
        c_copy(j).wait_send()
        store(j).wait()
    for kind in range(3):
        for which in range(3):
            heads_send(which, kind).wait_send()
    hidden_store.wait()


def sum_products(lefts, rights, heads, projection, hidden, grad, gain, vectors):
    weights = len(lefts)
    widths = [right.shape[1] for right in rights] + [projection.shape[1]]
    plan = [
        (weight, column)
        for weight, width in enumerate(widths)
        for column in range(0, width, 1536)
    ]
    depth, width = hidden.shape
    out_shapes = [
        jax.ShapeDtypeStruct((left.shape[1] // 8, columns), BF16)
        for left, columns in zip(lefts, widths)
    ]
    out_shapes += [
        jax.ShapeDtypeStruct((depth, widths[-1]), BF16),
        jax.ShapeDtypeStruct(grad.shape, F32),
        jax.ShapeDtypeStruct(vectors.shape, F32),
    ]
    inputs = (*lefts, *rights, heads, projection, hidden, grad, gain, vectors)
    anywhere = pl.BlockSpec(memory_space=pl.ANY)
    dma = pltpu.SemaphoreType.DMA
    rest = PIECE[0] - EARLY
    block = lambda *lead, rows=PIECE[0]: pltpu.VMEM(lead + (rows, PIECE[1]), BF16)
    results = pl.pallas_call(
        functools.partial(sum_kernel, tuple(plan), weights),
        out_shape=out_shapes,
        in_specs=[anywhere] * len(inputs),
        out_specs=[anywhere] * len(out_shapes),
        scratch_shapes=[
            block(5, 2, 4, 2),
            block(2, 2, 4, 2),
            block(2, 2, 4, 2),
            block(4, OVER_X, 2, rows=rest),
            block(4, 2, 4 - OVER_X, rows=rest),
            block(5, 4, rows=rest),
            block(4, 3, rows=rest),
            block(4, 3, 2, 2, rows=EARLY),
            block(4, 2, rows=EARLY),
            block(4, rows=EARLY),
            block(SLOTS),
            block(SLOTS),
            block(SLOTS, 2),
            pltpu.VMEM((2, 192, 1536), BF16),
            pltpu.VMEM((2, depth, 1536), BF16),
            pltpu.VMEM((2, depth, 1536), BF16),
            pltpu.VMEM((width, 1536), BF16),
            pltpu.VMEM((depth, width), F32),
            pltpu.VMEM((depth, width), BF16),
            pltpu.VMEM((depth, width), F32),
            pltpu.VMEM(gain.shape, F32),
            pltpu.VMEM((3,) + vectors.shape, F32),
            pltpu.VMEM((3,) + vectors.shape, F32),
            pltpu.VMEM((4,) + vectors.shape, F32),
            dma((2, 2)),
            dma((2, 4)),
            dma((2, 4)),
            dma((2, 5)),
            dma((2, 5)),
            dma((2, 4, 3)),
            dma((2, 4, 5)),
            dma((2, SLOTS)),
            dma((2, SLOTS, 2)),
            dma((2,)),
            dma((2, 2)),
            dma((2, 6)),
            dma((2, 3, 3)),
            dma((8,)),
        ],
        compiler_params=pltpu.CompilerParams(
            collective_id=3, has_side_effects=True, vmem_limit_bytes=60 << 20
        ),
        name="sum_products",
    )(*inputs)
    return results[:weights], results[-2], results[-1]


def on_blocks(
    hidden_states,
    text_states,
    self_gain,
    self_bias,
    query_key_value,
    self_output,
    cross_gain,
    cross_bias,
    cross_query,
    cross_memory,
    cross_output,
    final_gain,
    final_bias,
    expand_weight,
    contract_weight,
    output_cotangent,
):
    clips, frames, width = hidden_states.shape
    rows = clips * frames
    groups = lax.axis_size("seq")
    fsdp_count = lax.axis_size("fsdp")
    scale = HD ** (-0.5)
    entries = rows * groups * fsdp_count * width
    group_width = width // groups

    gains = (self_gain, self_bias, cross_gain, cross_bias, final_gain, final_bias)
    wholes, gains, normed_one, regrouped, logsum, context = forward(
        (
            query_key_value,
            self_output,
            cross_query,
            cross_memory,
            cross_output,
            expand_weight,
            contract_weight,
        ),
        place_vectors(gains),
        hidden_states.reshape(rows, width),
        clips,
        scale,
    )
    (
        qkv_whole,
        self_output_whole,
        cross_query_whole,
        cross_memory_whole,
        cross_output_whole,
        expand_whole,
        contract_whole,
    ) = wholes
    regrouped = regrouped.reshape(groups, clips, frames, 3 * group_width)
    hidden = hidden_states.reshape(rows, width).astype(F32)
    attended = product(context, self_output_whole)
    first = hidden + attended
    normed_two, norm_two_back = jax.vjp(layer_norm, first, gains[2], gains[3])
    normed_two = normed_two.astype(BF16)
    cross_q = product(normed_two, cross_query_whole).astype(BF16)
    text_rows = text_states.reshape(clips * TEXT, width)
    memory = product(text_rows, cross_memory_whole).astype(BF16)
    cross_context = text_attention(clips, scale, cross_q, memory)
    crossed = product(cross_context, cross_output_whole)
    second = first + crossed
    normed_three, norm_three_back = jax.vjp(layer_norm, second, gains[4], gains[5])
    normed_three = normed_three.astype(BF16)
    preact = product(normed_three, expand_whole)
    below = 0.5 + 0.5 * lax.erf(preact * 0.5**0.5)
    density = jnp.exp(preact * preact * -0.5) * (0.5 / jnp.pi) ** 0.5
    activated = (preact * below).astype(BF16)
    slope = (below + preact * density).astype(BF16)
    upstream = output_cotangent.reshape(rows, width).astype(F32)
    grad_mixed = output_cotangent.reshape(rows, width)
    contract_term = product_left(activated, grad_mixed).astype(BF16)
    grad_mixed, contract_term, contract_whole = lax.optimization_barrier(
        (grad_mixed, contract_term, contract_whole)
    )
    contract_part = lax.psum_scatter(
        contract_term, ("fsdp", "seq"), scatter_dimension=0, tiled=True
    )
    grad_activated = product_right(grad_mixed, contract_whole)
    grad_preact = (grad_activated * slope.astype(F32)).astype(BF16)
    grad_normed_three = product_right(grad_preact, expand_whole)
    grad_second, final_gain_term, final_bias_term = norm_three_back(grad_normed_three)
    grad_second = upstream + grad_second
    grad_crossed = grad_second.astype(BF16)
    grad_cross_context = product_right(grad_crossed, cross_output_whole).astype(BF16)
    grad_cross_q, grad_memory = text_attention(clips, scale, cross_q, memory, grad_cross_context)
    grad_normed_two = product_right(grad_cross_q, cross_query_whole)
    grad_first, cross_gain_term, cross_bias_term = norm_two_back(grad_normed_two)
    grad_first = grad_second + grad_first
    grad_attended = grad_first.astype(BF16)
    grad_context = product_right(grad_attended, self_output_whole).astype(BF16)
    grad_context = grad_context.reshape(rows, groups, group_width).transpose(1, 0, 2)
    grad_context, activated = lax.optimization_barrier((grad_context, activated))
    grad_heads = lax.all_to_all(grad_context, "seq", split_axis=0, concat_axis=0, tiled=True)
    mixed = product(activated, contract_whole)
    output = second + mixed
    squares = jnp.stack(
        [
            jnp.sum(output * output),
            jnp.sum(attended * attended),
            jnp.sum(crossed * crossed),
            jnp.sum(mixed * mixed),
        ]
    )
    output = output.astype(BF16)
    zeros = jnp.zeros_like(cross_gain_term)
    terms = jnp.stack(
        [
            zeros,
            zeros,
            cross_gain_term,
            cross_bias_term,
            final_gain_term,
            final_bias_term,
            jnp.pad(squares, (0, width - 4)),
            zeros,
        ]
    )
    deep = lambda value: jnp.pad(value, ((0, rows - value.shape[0]), (0, 0)))
    text_operands = (deep(text_rows), deep(grad_memory))
    grad_heads, output, terms, text_operands = lax.optimization_barrier(
        (grad_heads, output, terms, text_operands)
    )
    grad_heads = grad_heads.reshape(groups, clips, frames, group_width)
    grad_regrouped = attention_back(regrouped, grad_heads, logsum, scale)
    gradients, grad_hidden, totals = sum_products(
        [normed_three, cross_context, normed_two, text_operands[0], context, normed_one],
        [grad_preact, grad_crossed, grad_cross_q, text_operands[1], grad_attended],
        grad_regrouped.reshape(groups, rows, 3 * group_width),
        qkv_whole,
        hidden_states.reshape(rows, width),
        grad_first,
        jnp.broadcast_to(gains[0], (8, width)),
        terms,
    )
    gradients, contract_part = lax.optimization_barrier((gradients, contract_part))
    contract_gradient = lax.all_gather(contract_part, "seq", axis=0, tiled=True)
    gradients = [gradient.astype(F32) for gradient in gradients]
    contract_gradient = contract_gradient.astype(F32)
    layer_rms = jnp.sqrt(totals[6, :4] / entries)
    shard = width // fsdp_count
    vector_gradients = lax.dynamic_slice_in_dim(
        totals, lax.axis_index("fsdp") * shard, shard, 1
    )
    return (
        output.reshape(clips, frames, width),
        grad_hidden.reshape(clips, frames, width),
        vector_gradients[0],
        vector_gradients[1],
        gradients[5],
        gradients[4],
        vector_gradients[2],
        vector_gradients[3],
        gradients[2],
        gradients[3],
        gradients[1],
        vector_gradients[4],
        vector_gradients[5],
        gradients[0],
        contract_gradient,
        layer_rms,
    )


def solution(mesh):
    shape = dict(mesh.shape)
    blocks = shape["seq"] == 4 and shape["fsdp"] == 8
    return jax.shard_map(
        on_blocks if blocks else on_any_mesh,
        mesh=mesh,
        in_specs=(
            P("fsdp", "seq", None),
            P("fsdp", None, None),
            P("fsdp"),
            P("fsdp"),
            P("fsdp", None),
            P("fsdp", None),
            P("fsdp"),
            P("fsdp"),
            P("fsdp", None),
            P("fsdp", None),
            P("fsdp", None),
            P("fsdp"),
            P("fsdp"),
            P("fsdp", None),
            P("fsdp", None),
            P("fsdp", "seq", None),
        ),
        out_specs=(
            P("fsdp", "seq", None),
            P("fsdp", "seq", None),
            P("fsdp"),
            P("fsdp"),
            P("fsdp", None),
            P("fsdp", None),
            P("fsdp"),
            P("fsdp"),
            P("fsdp", None),
            P("fsdp", None),
            P("fsdp", None),
            P("fsdp"),
            P("fsdp"),
            P("fsdp", None),
            P("fsdp", None),
            P(),
        ),
        check_vma=False,
    )
```

```python
import functools

import jax
import jax.numpy as jnp
from jax import lax
from jax.experimental import pallas as pl
from jax.experimental.pallas import tpu as pltpu
from jax.sharding import PartitionSpec as P

H = 24
HD = 64
TEXT = 64

NEGATIVE = -1e30
BF16 = jnp.bfloat16
F32 = jnp.float32
MESH = pl.DeviceIdType.MESH


def layer_norm(values, gain, offset):
    center = values - jnp.mean(values, axis=-1, keepdims=True)
    spread = jnp.mean(center * center, axis=-1, keepdims=True)
    return center * lax.rsqrt(spread + 1e-05) * gain + offset


def gelu_exact(values):
    return jax.nn.gelu(values, approximate=False)


def product(left, right):
    return jnp.dot(left, right, preferred_element_type=jnp.float32)


def product_left(left, right):
    return lax.dot_general(
        left, right, (((0,), (0,)), ((), ())), preferred_element_type=jnp.float32
    )


def product_right(left, right):
    return lax.dot_general(
        left, right, (((1,), (1,)), ((), ())), preferred_element_type=jnp.float32
    )


def causal_forward(queries, keys, values, rows_block, scale):
    clips, length, heads_local, head_width = queries.shape
    count = length // rows_block
    columns = jnp.arange(length, dtype=jnp.int32)

    def one_block(start):
        block = lax.dynamic_slice_in_dim(queries, start, rows_block, 1)
        scores = (
            jnp.einsum("cqhd,ckhd->chqk", block, keys, preferred_element_type=jnp.float32) * scale
        )
        positions = start + jnp.arange(rows_block, dtype=jnp.int32)
        allowed = columns[None, :] <= positions[:, None]
        scores = jnp.where(allowed, scores, NEGATIVE)
        highest = jnp.max(scores, axis=-1, keepdims=True)
        raised = jnp.exp(scores - highest)
        summed = jnp.sum(raised, axis=-1, keepdims=True)
        weights = (raised / summed).astype(jnp.bfloat16)
        result = jnp.einsum("chqk,ckhd->cqhd", weights, values, preferred_element_type=jnp.float32)
        return (result.astype(jnp.bfloat16), (highest + jnp.log(summed))[..., 0])

    starts = jnp.arange(count, dtype=jnp.int32) * rows_block
    results, logsum = lax.map(one_block, starts)
    results = jnp.moveaxis(results, 0, 1).reshape(clips, length, heads_local * head_width)
    return (results, logsum)


def causal_backward(queries, keys, values, logsum, grad_heads, rows_block, scale):
    clips, length, heads_local, head_width = queries.shape
    count = length // rows_block
    columns = jnp.arange(length, dtype=jnp.int32)
    starts = jnp.arange(count, dtype=jnp.int32) * rows_block

    def one_block(carry, inputs):
        grad_keys, grad_values = carry
        start, block_logsum = inputs
        block = lax.dynamic_slice_in_dim(queries, start, rows_block, 1)
        block_grad = lax.dynamic_slice_in_dim(grad_heads, start, rows_block, 1)
        scores = (
            jnp.einsum("cqhd,ckhd->chqk", block, keys, preferred_element_type=jnp.float32) * scale
        )
        positions = start + jnp.arange(rows_block, dtype=jnp.int32)
        allowed = columns[None, :] <= positions[:, None]
        scores = jnp.where(allowed, scores, NEGATIVE)
        weights = jnp.exp(scores - block_logsum[..., None])
        rounded = weights.astype(jnp.bfloat16)
        grad_weights = jnp.einsum(
            "cqhd,ckhd->chqk", block_grad, values, preferred_element_type=jnp.float32
        )
        inner = jnp.sum(weights * grad_weights, axis=-1, keepdims=True)
        grad_scores = (weights * (grad_weights - inner)).astype(jnp.bfloat16)
        grad_query = (
            jnp.einsum("chqk,ckhd->cqhd", grad_scores, keys, preferred_element_type=jnp.float32)
            * scale
        )
        grad_keys = (
            grad_keys
            + jnp.einsum("chqk,cqhd->ckhd", grad_scores, block, preferred_element_type=jnp.float32)
            * scale
        )
        grad_values = grad_values + jnp.einsum(
            "chqk,cqhd->ckhd", rounded, block_grad, preferred_element_type=jnp.float32
        )
        return ((grad_keys, grad_values), grad_query.astype(jnp.bfloat16))

    zeros = jnp.zeros(queries.shape, jnp.float32)
    (grad_keys, grad_values), grad_queries = lax.scan(one_block, (zeros, zeros), (starts, logsum))
    local_width = heads_local * head_width
    grad_queries = jnp.moveaxis(grad_queries, 0, 1).reshape(clips, length, local_width)
    grad_keys = grad_keys.astype(jnp.bfloat16).reshape(clips, length, local_width)
    grad_values = grad_values.astype(jnp.bfloat16).reshape(clips, length, local_width)
    return jnp.stack([grad_queries, grad_keys, grad_values], axis=2)


def on_any_mesh(
    hidden_states,
    text_states,
    self_gain,
    self_bias,
    query_key_value,
    self_output,
    cross_gain,
    cross_bias,
    cross_query,
    cross_memory,
    cross_output,
    final_gain,
    final_bias,
    expand_weight,
    contract_weight,
    output_cotangent,
):
    clips, frames, width = hidden_states.shape
    rows = clips * frames
    groups = lax.axis_size("seq")
    fsdp_count = lax.axis_size("fsdp")
    heads_local = H // groups
    length = frames * groups
    rows_block = min(512, length)
    scale = HD ** (-0.5)
    entries = rows * groups * fsdp_count * width
    self_set = (
        lax.all_gather(self_gain, "fsdp", axis=0, tiled=True),
        lax.all_gather(self_bias, "fsdp", axis=0, tiled=True),
        lax.all_gather(query_key_value, "fsdp", axis=0, tiled=True),
        lax.all_gather(self_output, "fsdp", axis=0, tiled=True),
    )
    hidden = hidden_states.reshape(rows, width).astype(jnp.float32)
    normed_one, norm_one_back = jax.vjp(
        layer_norm, hidden, self_set[0].astype(jnp.float32), self_set[1].astype(jnp.float32)
    )
    normed_one = normed_one.astype(jnp.bfloat16)
    projected = (
        product(normed_one, self_set[2]).astype(jnp.bfloat16).reshape(clips, frames, 3, width)
    )
    regrouped = lax.all_to_all(projected, "seq", split_axis=3, concat_axis=1, tiled=True)
    regrouped = regrouped.reshape(clips, length, 3, heads_local, HD)
    queries = regrouped[:, :, 0]
    keys = regrouped[:, :, 1]
    values = regrouped[:, :, 2]
    context_heads, logsum = causal_forward(queries, keys, values, rows_block, scale)
    context = lax.all_to_all(context_heads, "seq", split_axis=1, concat_axis=2, tiled=True).reshape(
        rows, width
    )
    attended = product(context, self_set[3])
    first = hidden + attended
    rest_set = (
        lax.all_gather(cross_gain, "fsdp", axis=0, tiled=True),
        lax.all_gather(cross_bias, "fsdp", axis=0, tiled=True),
        lax.all_gather(cross_query, "fsdp", axis=0, tiled=True),
        lax.all_gather(cross_memory, "fsdp", axis=0, tiled=True),
        lax.all_gather(cross_output, "fsdp", axis=0, tiled=True),
        lax.all_gather(final_gain, "fsdp", axis=0, tiled=True),
        lax.all_gather(final_bias, "fsdp", axis=0, tiled=True),
        lax.all_gather(expand_weight, "fsdp", axis=0, tiled=True),
        lax.all_gather(contract_weight, "fsdp", axis=0, tiled=True),
    )
    normed_two, norm_two_back = jax.vjp(
        layer_norm, first, rest_set[0].astype(jnp.float32), rest_set[1].astype(jnp.float32)
    )
    normed_two = normed_two.astype(jnp.bfloat16)
    cross_q = product(normed_two, rest_set[2]).astype(jnp.bfloat16).reshape(clips, frames, H, HD)
    text_rows = text_states.reshape(clips * TEXT, width)
    memory = product(text_rows, rest_set[3]).astype(jnp.bfloat16).reshape(clips, TEXT, 2, H, HD)
    cross_keys = memory[:, :, 0]
    cross_values = memory[:, :, 1]
    cross_scores = (
        jnp.einsum("cqhd,ckhd->chqk", cross_q, cross_keys, preferred_element_type=jnp.float32)
        * scale
    )
    highest = jnp.max(cross_scores, axis=-1, keepdims=True)
    raised = jnp.exp(cross_scores - highest)
    cross_weights = raised / jnp.sum(raised, axis=-1, keepdims=True)
    cross_rounded = cross_weights.astype(jnp.bfloat16)
    cross_context = jnp.einsum(
        "chqk,ckhd->cqhd", cross_rounded, cross_values, preferred_element_type=jnp.float32
    )
    cross_context = cross_context.astype(jnp.bfloat16).reshape(rows, width)
    crossed = product(cross_context, rest_set[4])
    second = first + crossed
    normed_three, norm_three_back = jax.vjp(
        layer_norm, second, rest_set[5].astype(jnp.float32), rest_set[6].astype(jnp.float32)
    )
    normed_three = normed_three.astype(jnp.bfloat16)
    preact = product(normed_three, rest_set[7])
    activated, gelu_back = jax.vjp(gelu_exact, preact)
    activated = activated.astype(jnp.bfloat16)
    mixed = product(activated, rest_set[8])
    output = second + mixed
    squares = jnp.stack(
        [
            jnp.sum(output * output),
            jnp.sum(attended * attended),
            jnp.sum(crossed * crossed),
            jnp.sum(mixed * mixed),
        ]
    )
    square_totals = lax.psum(squares, ("seq", "fsdp"))
    back_rest = (
        lax.all_gather(cross_gain, "fsdp", axis=0, tiled=True),
        lax.all_gather(cross_bias, "fsdp", axis=0, tiled=True),
        lax.all_gather(cross_query, "fsdp", axis=0, tiled=True),
        lax.all_gather(cross_memory, "fsdp", axis=0, tiled=True),
        lax.all_gather(cross_output, "fsdp", axis=0, tiled=True),
        lax.all_gather(final_gain, "fsdp", axis=0, tiled=True),
        lax.all_gather(final_bias, "fsdp", axis=0, tiled=True),
        lax.all_gather(expand_weight, "fsdp", axis=0, tiled=True),
        lax.all_gather(contract_weight, "fsdp", axis=0, tiled=True),
    )
    upstream = output_cotangent.reshape(rows, width).astype(jnp.float32)
    grad_mixed = upstream.astype(jnp.bfloat16)
    contract_term = product_left(activated, grad_mixed)
    grad_activated = product_right(grad_mixed, back_rest[8])
    grad_preact = gelu_back(grad_activated)[0].astype(jnp.bfloat16)
    expand_term = product_left(normed_three, grad_preact)
    grad_normed_three = product_right(grad_preact, back_rest[7])
    grad_second, final_gain_term, final_bias_term = norm_three_back(grad_normed_three)
    grad_second = upstream + grad_second
    grad_crossed = grad_second.astype(jnp.bfloat16)
    cross_output_term = product_left(cross_context, grad_crossed)
    grad_cross_context = (
        product_right(grad_crossed, back_rest[4]).astype(jnp.bfloat16).reshape(clips, frames, H, HD)
    )
    grad_cross_weights = jnp.einsum(
        "cqhd,ckhd->chqk", grad_cross_context, cross_values, preferred_element_type=jnp.float32
    )
    cross_inner = jnp.sum(cross_weights * grad_cross_weights, axis=-1, keepdims=True)
    grad_cross_scores = (cross_weights * (grad_cross_weights - cross_inner)).astype(jnp.bfloat16)
    grad_cross_q = (
        jnp.einsum(
            "chqk,ckhd->cqhd", grad_cross_scores, cross_keys, preferred_element_type=jnp.float32
        )
        * scale
    )
    grad_cross_q = grad_cross_q.astype(jnp.bfloat16).reshape(rows, width)
    grad_cross_keys = (
        jnp.einsum(
            "chqk,cqhd->ckhd", grad_cross_scores, cross_q, preferred_element_type=jnp.float32
        )
        * scale
    )
    grad_cross_values = jnp.einsum(
        "chqk,cqhd->ckhd", cross_rounded, grad_cross_context, preferred_element_type=jnp.float32
    )
    grad_memory = jnp.stack([grad_cross_keys, grad_cross_values], axis=2).reshape(
        clips * TEXT, 2 * width
    )
    memory_term = lax.dot_general(
        text_rows.astype(jnp.float32),
        grad_memory,
        (((0,), (0,)), ((), ())),
        precision=lax.Precision.HIGHEST,
        preferred_element_type=jnp.float32,
    )
    query_term = product_left(normed_two, grad_cross_q)
    grad_normed_two = product_right(grad_cross_q, back_rest[2])
    grad_first, cross_gain_term, cross_bias_term = norm_two_back(grad_normed_two)
    grad_first = grad_second + grad_first
    rest_sums = (
        lax.psum_scatter(
            cross_gain_term.astype(jnp.bfloat16), "fsdp", scatter_dimension=0, tiled=True
        ).astype(jnp.float32),
        lax.psum_scatter(
            cross_bias_term.astype(jnp.bfloat16), "fsdp", scatter_dimension=0, tiled=True
        ).astype(jnp.float32),
        lax.psum_scatter(
            query_term.astype(jnp.bfloat16), "fsdp", scatter_dimension=0, tiled=True
        ).astype(jnp.float32),
        lax.psum_scatter(
            memory_term.astype(jnp.bfloat16), "fsdp", scatter_dimension=0, tiled=True
        ).astype(jnp.float32),
        lax.psum_scatter(
            cross_output_term.astype(jnp.bfloat16), "fsdp", scatter_dimension=0, tiled=True
        ).astype(jnp.float32),
        lax.psum_scatter(
            final_gain_term.astype(jnp.bfloat16), "fsdp", scatter_dimension=0, tiled=True
        ).astype(jnp.float32),
        lax.psum_scatter(
            final_bias_term.astype(jnp.bfloat16), "fsdp", scatter_dimension=0, tiled=True
        ).astype(jnp.float32),
        lax.psum_scatter(
            expand_term.astype(jnp.bfloat16), "fsdp", scatter_dimension=0, tiled=True
        ).astype(jnp.float32),
        lax.psum_scatter(
            contract_term.astype(jnp.bfloat16), "fsdp", scatter_dimension=0, tiled=True
        ).astype(jnp.float32),
    )
    back_self = (
        lax.all_gather(self_gain, "fsdp", axis=0, tiled=True),
        lax.all_gather(self_bias, "fsdp", axis=0, tiled=True),
        lax.all_gather(query_key_value, "fsdp", axis=0, tiled=True),
        lax.all_gather(self_output, "fsdp", axis=0, tiled=True),
    )
    grad_attended = grad_first.astype(jnp.bfloat16)
    self_output_term = product_left(context, grad_attended)
    grad_context = (
        product_right(grad_attended, back_self[3])
        .astype(jnp.bfloat16)
        .reshape(clips, frames, width)
    )
    grad_heads = lax.all_to_all(grad_context, "seq", split_axis=2, concat_axis=1, tiled=True)
    grad_heads = grad_heads.reshape(clips, length, heads_local, HD)
    grad_regrouped = causal_backward(queries, keys, values, logsum, grad_heads, rows_block, scale)
    grad_projected = lax.all_to_all(
        grad_regrouped, "seq", split_axis=1, concat_axis=3, tiled=True
    ).reshape(rows, 3 * width)
    qkv_term = product_left(normed_one, grad_projected)
    grad_normed_one = product_right(grad_projected, back_self[2])
    grad_hidden, gain_one_term, bias_one_term = norm_one_back(grad_normed_one)
    grad_hidden = grad_first + grad_hidden
    self_sums = (
        lax.psum_scatter(
            gain_one_term.astype(jnp.bfloat16), "fsdp", scatter_dimension=0, tiled=True
        ).astype(jnp.float32),
        lax.psum_scatter(
            bias_one_term.astype(jnp.bfloat16), "fsdp", scatter_dimension=0, tiled=True
        ).astype(jnp.float32),
        lax.psum_scatter(
            qkv_term.astype(jnp.bfloat16), "fsdp", scatter_dimension=0, tiled=True
        ).astype(jnp.float32),
        lax.psum_scatter(
            self_output_term.astype(jnp.bfloat16), "fsdp", scatter_dimension=0, tiled=True
        ).astype(jnp.float32),
    )
    finals = (
        lax.psum(self_sums[0].astype(jnp.bfloat16), "seq").astype(jnp.float32),
        lax.psum(self_sums[1].astype(jnp.bfloat16), "seq").astype(jnp.float32),
        lax.psum(self_sums[2].astype(jnp.bfloat16), "seq").astype(jnp.float32),
        lax.psum(self_sums[3].astype(jnp.bfloat16), "seq").astype(jnp.float32),
        lax.psum(rest_sums[0].astype(jnp.bfloat16), "seq").astype(jnp.float32),
        lax.psum(rest_sums[1].astype(jnp.bfloat16), "seq").astype(jnp.float32),
        lax.psum(rest_sums[2].astype(jnp.bfloat16), "seq").astype(jnp.float32),
        lax.psum(rest_sums[3].astype(jnp.bfloat16), "seq").astype(jnp.float32),
        lax.psum(rest_sums[4].astype(jnp.bfloat16), "seq").astype(jnp.float32),
        lax.psum(rest_sums[5].astype(jnp.bfloat16), "seq").astype(jnp.float32),
        lax.psum(rest_sums[6].astype(jnp.bfloat16), "seq").astype(jnp.float32),
        lax.psum(rest_sums[7].astype(jnp.bfloat16), "seq").astype(jnp.float32),
        lax.psum(rest_sums[8].astype(jnp.bfloat16), "seq").astype(jnp.float32),
    )
    layer_rms = jnp.sqrt(square_totals / entries)
    return (
        output.astype(jnp.bfloat16).reshape(clips, frames, width),
        grad_hidden.reshape(clips, frames, width),
        finals[0],
        finals[1],
        finals[2],
        finals[3],
        finals[4],
        finals[5],
        finals[6],
        finals[7],
        finals[8],
        finals[9],
        finals[10],
        finals[11],
        finals[12],
        layer_rms,
    )


QUERIES = 256


def both_heads(value):
    lane = lax.broadcasted_iota(jnp.int32, value.shape, 1)
    zero = jnp.zeros_like(value)
    return jnp.where(lane < HD, value, zero), jnp.where(lane < HD, zero, value)


def across(left, right):
    return lax.dot_general(left, right, (((1,), (1,)), ((), ())), preferred_element_type=F32)


def down(left, right):
    return lax.dot_general(left, right, (((0,), (0,)), ((), ())), preferred_element_type=F32)


def join_heads(pair):
    row = lax.broadcasted_iota(jnp.int32, pair[0].shape, 0)
    return jnp.where(row < HD, pair[0], pair[1])


def key_parts(block):
    return ([(0, block * QUERIES, False)] if block else []) + [
        (block * QUERIES, (block + 1) * QUERIES, True)
    ]


def masked_scores(keys, queries, diagonal):
    scores = across(keys, queries)
    if diagonal:
        key = lax.broadcasted_iota(jnp.int32, scores.shape, 0)
        query = lax.broadcasted_iota(jnp.int32, scores.shape, 1)
        scores = jnp.where(key <= query, scores, NEGATIVE)
    return scores


def attention_kernel(scale, q_ref, k_ref, v_ref, out_ref, logsum_ref):
    blocks = q_ref.shape[0] * q_ref.shape[2] // QUERIES
    k = k_ref[:, 0].reshape(-1, 2 * HD)
    v = v_ref[:, 0].reshape(-1, 2 * HD)
    for block in range(blocks):
        rows = slice(block * QUERIES, (block + 1) * QUERIES)
        queries = both_heads((q_ref[block, 0].astype(F32) * scale).astype(BF16))
        outs = []
        for head in range(2):
            parts = key_parts(block)
            scores = [masked_scores(k[a:b], queries[head], diagonal) for a, b, diagonal in parts]
            highest = functools.reduce(
                jnp.maximum, [jnp.max(part, axis=0, keepdims=True) for part in scores]
            )
            raised = [jnp.exp(part - highest) for part in scores]
            summed = sum(jnp.sum(part, axis=0, keepdims=True) for part in raised)
            total = sum(
                down(v[a:b], part.astype(BF16)) for (a, b, _), part in zip(parts, raised)
            )
            outs.append(total / summed)
            logsum_ref[0, 0, head : head + 1, rows] = highest + jnp.log(summed)
        out_ref[block, 0] = join_heads(outs).T.astype(BF16)


def attention_back_kernel(
    scale, q_ref, k_ref, v_ref, grad_ref, logsum_ref, out_ref, grad_keys, grad_values
):
    blocks = q_ref.shape[0] * q_ref.shape[2] // QUERIES
    frames = q_ref.shape[2]
    k = k_ref[:, 0].reshape(-1, 2 * HD)
    v = v_ref[:, 0].reshape(-1, 2 * HD)

    def columns(kind):
        return pl.ds(kind * 2 * HD, 2 * HD)

    for block in range(blocks):
        rows = slice(block * QUERIES, (block + 1) * QUERIES)
        queries = both_heads((q_ref[block, 0].astype(F32) * scale).astype(BF16))
        grads = both_heads(grad_ref[block, 0])
        parts = key_parts(block)
        query_grads = []
        held = [[], []]
        for head in range(2):
            logsum = logsum_ref[0, 0, head : head + 1, rows]
            weights, weighted = [], []
            for a, b, diagonal in parts:
                weight = jnp.exp(masked_scores(k[a:b], queries[head], diagonal) - logsum)
                weights.append(weight)
                weighted.append(weight * across(v[a:b], grads[head]))
            inner = sum(jnp.sum(part, axis=0, keepdims=True) for part in weighted)
            changes = [
                (term - weight * inner).astype(BF16) for term, weight in zip(weighted, weights)
            ]
            query_grads.append(sum(down(k[a:b], part) for (a, b, _), part in zip(parts, changes)))
            held[head] = [(weight.astype(BF16), change) for weight, change in zip(weights, changes)]
        out_ref[block, 0, :, columns(0)] = (join_heads(query_grads).T * scale).astype(BF16)
        for j, (a, b, diagonal) in enumerate(parts):
            value_term = sum(
                jnp.dot(held[head][j][0], grads[head], preferred_element_type=F32)
                for head in range(2)
            )
            key_term = sum(
                jnp.dot(held[head][j][1], queries[head], preferred_element_type=F32)
                for head in range(2)
            )
            if diagonal:
                grad_values[a:b] = value_term
                grad_keys[a:b] = key_term
            else:
                grad_values[a:b] += value_term
                grad_keys[a:b] += key_term
    out_ref[:, 0, :, columns(1)] = grad_keys[...].reshape(-1, frames, 2 * HD).astype(BF16)
    out_ref[:, 0, :, columns(2)] = grad_values[...].reshape(-1, frames, 2 * HD).astype(BF16)


X_LAG = 2
CORE_LAG = 4


def forward_kernel(plan, weights, scale, *refs):
    inputs = refs[:weights]
    vector_in, hidden_in = refs[weights : weights + 2]
    refs = refs[weights + 2 :]
    outputs = refs[:weights]
    vector_out, normed_out, heads, logsum_out, context = refs[weights : weights + 5]
    (
        vector_land,
        vector,
        hidden,
        normed,
        weight_buf,
        product_buf,
        q_buf,
        k_buf,
        v_buf,
        context_buf,
        logsum_buf,
        z_send,
        z_recv,
        y_sem,
        x_sem,
        c_sem,
        own_sem,
        vector_sem,
        load_sem,
        product_send,
        product_recv,
        block_sem,
        context_sem,
        context_own,
    ) = refs[weights + 5 :]
    seq = lax.axis_index("seq")
    fsdp = lax.axis_index("fsdp")
    x, c = seq // 2, seq % 2
    z, y = fsdp // 2, fsdp % 2
    x_seq = 2 * (1 - x) + c
    c_seq = 2 * x + 1 - c
    neighbours = (x_seq, c_seq, 3 - seq)
    y_fsdp = 2 * z + 1 - y
    chunks = len(plan)
    clips, pairs = logsum_buf.shape[:2]
    frames = hidden.shape[0] // clips

    def at_z(k):
        return (seq, 2 * ((z + k) % 4) + y)

    barrier = pltpu.get_barrier_semaphore()
    partners = [(other, fsdp) for other in neighbours] + [(seq, (fsdp + k) % 8) for k in range(1, 8)]
    for partner in partners:
        pl.semaphore_signal(barrier, inc=1, device_id=partner, device_id_type=MESH)
    pl.semaphore_wait(barrier, len(partners))

    def remote(source, target, send, recv, device):
        return pltpu.make_async_remote_copy(
            src_ref=source,
            dst_ref=target,
            send_sem=send,
            recv_sem=recv,
            device_id=device,
            device_id_type=MESH,
        )

    def over(region, sems, device):
        return remote(region, region, sems.at[0], sems.at[1], device)

    sends = []

    def send(copy):
        copy.start()
        sends.append(copy)

    def vector_copy(k):
        return remote(
            vector_in,
            vector_land.at[fsdp],
            vector_sem.at[0, k],
            vector_sem.at[1, k],
            (seq, (fsdp + k) % 8),
        )

    def vector_arrival(k):
        region = vector_land.at[(fsdp + 8 - k) % 8]
        return over(region, vector_sem.at[:, k], (seq, (fsdp + k) % 8))

    own_vector = pltpu.make_async_copy(vector_in, vector_land.at[fsdp], vector_sem.at[0, 0])
    hidden_load = pltpu.make_async_copy(hidden_in, hidden, vector_sem.at[1, 0])
    normed_store = pltpu.make_async_copy(normed, normed_out, vector_sem.at[1, 0])
    vector_store = pltpu.make_async_copy(vector, vector_out, vector_sem.at[0, 0])

    def norm():
        own_vector.wait()
        for k in range(1, 8):
            vector_arrival(k).wait_recv()
        hidden_load.wait()
        vector[...] = sum(vector_land[f] for f in range(8))
        vector_store.start()

        @pl.loop(0, hidden.shape[0] // 32)
        def _(block):
            rows = pl.ds(pl.multiple_of(block * 32, 32), 32)
            value = hidden[rows, :].astype(F32)
            center = value - jnp.mean(value, axis=1, keepdims=True)
            inverse = lax.rsqrt(jnp.mean(center * center, axis=1, keepdims=True) + 1e-05)
            normed[rows, :] = (center * inverse * vector[0:1, :] + vector[1:2, :]).astype(BF16)

        normed_store.start()

    def part(entry):
        weight, block, column, width, split = entry
        first = 2 * c + x if split else 2 * c
        return weight, block, pl.ds(column, width), pl.ds(first, 1 if split else 2)

    def own_copy(i):
        weight, block, columns, _ = part(plan[i])
        both = pl.ds(2 * c, 2)
        return pltpu.make_async_copy(
            inputs[weight].at[block, both, :, columns],
            outputs[weight].at[z, y, block, both, :, columns],
            own_sem.at[i],
        )

    def start_z(i):
        weight, block, columns, mine = part(plan[i])
        source = inputs[weight].at[block, mine, :, columns]
        target = outputs[weight].at[z, y, block, mine, :, columns]
        for k in (1, 2, 3):
            send(remote(source, target, z_send.at[i, k - 1], z_recv.at[i, k - 1], at_z(k)))
        own_copy(i).start()

    def start_y(i):
        weight, block, columns, mine = part(plan[i])
        output = outputs[weight]
        for k in (1, 2, 3):
            region = output.at[(z + 4 - k) % 4, y, block, mine, :, columns]
            remote(region, region, z_send.at[i, k - 1], z_recv.at[i, k - 1], at_z(k)).wait_recv()
        own_copy(i).wait()
        region = output.at[:, y, block, mine, :, columns]
        send(over(region, y_sem.at[:, i], (seq, y_fsdp)))

    def x_copies(i, quarter):
        weight, block, columns, _ = part(plan[i])
        rest = (block, pl.ds(quarter, 1), slice(None), columns)
        regions = [outputs[weight].at[(slice(None), 1 - y) + rest]]
        regions += [outputs[weight].at[((z + k) % 4, y) + rest] for k in (1, 2, 3)]
        return [
            over(region, x_sem.at[:, i, j], (x_seq, fsdp)) for j, region in enumerate(regions)
        ]

    def start_x(i):
        weight, block, columns, mine = part(plan[i])
        output = outputs[weight]
        region = output.at[:, 1 - y, block, mine, :, columns]
        over(region, y_sem.at[:, i], (seq, y_fsdp)).wait_recv()
        if plan[i][4]:
            for copy in x_copies(i, 2 * c + x):
                send(copy)
        region = output.at[:, :, block, mine, :, columns]
        send(over(region, c_sem.at[:, i, 0], (c_seq, fsdp)))

    def start_core(i):
        if plan[i][4]:
            weight, block, columns, _ = part(plan[i])
            for copy in x_copies(i, 2 * c + 1 - x):
                copy.wait_recv()
            region = outputs[weight].at[:, :, block, pl.ds(2 * c + 1 - x, 1), :, columns]
            send(over(region, c_sem.at[:, i, 1], (c_seq, fsdp)))

    def finish(i):
        weight, block, columns, _ = part(plan[i])
        other = 2 * (1 - c)
        output = outputs[weight]
        if plan[i][4]:
            for j, quarter in ((0, other + x), (1, other + 1 - x)):
                region = output.at[:, :, block, pl.ds(quarter, 1), :, columns]
                over(region, c_sem.at[:, i, j], (c_seq, fsdp)).wait_recv()
        else:
            region = output.at[:, :, block, pl.ds(other, 2), :, columns]
            over(region, c_sem.at[:, i, 0], (c_seq, fsdp)).wait_recv()

    def weight_load(i):
        region = outputs[0].at[:, :, 0, :, :, pl.ds(384 * i, 384)]
        return pltpu.make_async_copy(region, weight_buf.at[i % 2], load_sem.at[i % 2])

    def product_copy(i):
        kind, group = i // 4, i % 4
        target = heads.at[seq, :, pl.ds(384 * kind, 384)]
        away = remote(
            product_buf.at[i % 2],
            target,
            product_send.at[i],
            product_recv.at[kind, seq],
            (group, fsdp),
        )
        here = pltpu.make_async_copy(product_buf.at[i % 2], target, product_send.at[i])
        return group, away, here

    def start_product(i):
        group, away, here = product_copy(i)

        @pl.when(seq != group)
        def _():
            away.start()

        @pl.when(seq == group)
        def _():
            here.start()

    def wait_product(i):
        group, away, here = product_copy(i)

        @pl.when(seq != group)
        def _():
            away.wait_send()

        @pl.when(seq == group)
        def _():
            here.wait()

    def project(i):
        weight_load(i).wait()
        if i >= 2:
            wait_product(i - 2)
        right = weight_buf[i % 2].reshape(-1, 384)

        @pl.loop(0, normed.shape[0] // 256)
        def _(block):
            rows = pl.ds(pl.multiple_of(block * 256, 256), 256)
            out = jnp.dot(normed[rows, :], right, preferred_element_type=F32)
            product_buf[i % 2, rows, :] = out.astype(BF16)

        start_product(i)

    def wait_heads():
        for i in (10, 11):
            wait_product(i)
        for kind in range(3):
            for other in neighbours:
                region = heads.at[other, :, pl.ds(384 * kind, 384)]
                remote(
                    region, region, product_send.at[0], product_recv.at[kind, other], (other, fsdp)
                ).wait_recv()

    def block_loads(step):
        clip, pair = step // pairs, step % pairs
        return [
            pltpu.make_async_copy(
                heads.at[:, pl.ds(clip * frames, frames), pl.ds(384 * kind + 128 * pair, 128)],
                buffer.at[step % 2, :, 0],
                block_sem.at[kind, step % 2],
            )
            for kind, buffer in enumerate((q_buf, k_buf, v_buf))
        ]

    def start_blocks(step):
        for copy in block_loads(step):
            copy.start()

    def context_region(step, group):
        clip, pair = step // pairs, step % pairs
        column = pl.multiple_of(group * 384 + pair * 128, 128)
        return context.at[pl.ds(clip * frames, frames), pl.ds(column, 128)]

    def context_copy(step, which):
        other = neighbours[which]
        return remote(
            context_buf.at[step % 2, other, 0],
            context_region(step, seq),
            context_sem.at[0, step, which],
            context_sem.at[1, step, which],
            (other, fsdp),
        )

    def context_here(step):
        return pltpu.make_async_copy(
            context_buf.at[step % 2, seq, 0], context_region(step, seq), context_own.at[step]
        )

    def context_sent(step):
        for which in range(3):
            context_copy(step, which).wait_send()
        context_here(step).wait()

    def attend(step):
        for copy in block_loads(step):
            copy.wait()
        if step + 1 < clips * pairs:
            start_blocks(step + 1)
        if step >= 2:
            context_sent(step - 2)
        slot = step % 2
        attention_kernel(
            scale,
            q_buf.at[slot],
            k_buf.at[slot],
            v_buf.at[slot],
            context_buf.at[slot],
            logsum_buf.at[step // pairs, step % pairs],
        )
        for which in range(3):
            context_copy(step, which).start()
        context_here(step).start()

    steps = clips * pairs
    projections = 12
    attention_start = projections + CORE_LAG + 5
    beside = {2: [norm]}
    for i in range(projections):
        beside.setdefault(i + CORE_LAG + 2, []).extend(
            [functools.partial(finish, i), lambda i=i: weight_load(i).start()]
        )
        beside.setdefault(i + CORE_LAG + 3, []).insert(0, functools.partial(project, i))
    beside.setdefault(attention_start, []).extend([wait_heads, lambda: start_blocks(0)])
    for step in range(steps):
        beside.setdefault(attention_start + 1 + 2 * step, []).append(functools.partial(attend, step))

    hidden_load.start()
    own_vector.start()
    for k in range(1, 8):
        send(vector_copy(k))
    ahead = 3
    for i in range(ahead):
        start_z(i)
    for t in range(chunks + CORE_LAG):
        if t + ahead < chunks:
            start_z(t + ahead)
        if t < chunks:
            start_y(t)
        if 0 <= t - X_LAG < chunks:
            start_x(t - X_LAG)
        if 0 <= t - CORE_LAG < chunks:
            start_core(t - CORE_LAG)
        for run in beside.pop(t, []):
            run()
    for i in range(projections, chunks):
        finish(i)
    for copy in sends:
        copy.wait_send()
    normed_store.wait()
    vector_store.wait()
    for step in (steps - 2, steps - 1):
        context_sent(step)
    for step in range(steps):
        for which in range(3):
            region = context_region(step, neighbours[which])
            over(region, context_sem.at[:, step, which], (neighbours[which], fsdp)).wait_recv()
    pltpu.sync_copy(logsum_buf, logsum_out)


def forward_plan(shapes):
    places = []
    for weight, (rows, columns) in enumerate(shapes):
        blocks = rows // 192
        for block in range(blocks):
            last = weight == len(shapes) - 1 and block == blocks - 1
            width = 384 if weight == 0 or last else 768
            places += [(weight, block, column, width) for column in range(0, columns, width)]
    return tuple(
        place + ((len(places) - 1 - i) * 3 % 5 >= 2,) for i, place in enumerate(places)
    )


def forward(shards, vectors, hidden, clips, scale):
    shapes = [shard.shape for shard in shards]
    plan = forward_plan(shapes)
    chunks, weights = len(plan), len(shards)
    rows, width = hidden.shape
    frames, group = rows // clips, width // 4
    pairs = group // (2 * HD)
    inputs = [shard.reshape(depth // 192, 4, 48, columns) for shard, (depth, columns) in zip(shards, shapes)]
    inputs += [vectors, hidden]
    out_shapes = [
        jax.ShapeDtypeStruct((4, 2, depth // 192, 4, 48, columns), BF16) for depth, columns in shapes
    ]
    logsum_shape = (clips, pairs, 1, 1, 2, 4 * frames)
    out_shapes += [
        jax.ShapeDtypeStruct(vectors.shape, F32),
        jax.ShapeDtypeStruct(hidden.shape, BF16),
        jax.ShapeDtypeStruct((4, rows, 3 * group), BF16),
        jax.ShapeDtypeStruct(logsum_shape, F32),
        jax.ShapeDtypeStruct(hidden.shape, BF16),
    ]
    anywhere = pl.BlockSpec(memory_space=pl.ANY)
    dma = pltpu.SemaphoreType.DMA
    pair_block = pltpu.VMEM((2, 4, 1, frames, 2 * HD), BF16)
    results = pl.pallas_call(
        functools.partial(forward_kernel, plan, weights, scale),
        out_shape=out_shapes,
        in_specs=[anywhere] * len(inputs),
        out_specs=[anywhere] * len(out_shapes),
        scratch_shapes=[
            pltpu.VMEM((8,) + vectors.shape, F32),
            pltpu.VMEM(vectors.shape, F32),
            pltpu.VMEM(hidden.shape, BF16),
            pltpu.VMEM(hidden.shape, BF16),
            pltpu.VMEM((2, 4, 2, 4, 48, 384), BF16),
            pltpu.VMEM((2, rows, 384), BF16),
            pair_block,
            pair_block,
            pair_block,
            pair_block,
            pltpu.VMEM(logsum_shape, F32),
            dma((chunks, 3)),
            dma((chunks, 3)),
            dma((2, chunks)),
            dma((2, chunks, 4)),
            dma((2, chunks, 2)),
            dma((chunks,)),
            dma((2, 8)),
            dma((2,)),
            dma((12,)),
            dma((3, 4)),
            dma((3, 2)),
            dma((2, clips * pairs, 3)),
            dma((clips * pairs,)),
        ],
        compiler_params=pltpu.CompilerParams(
            collective_id=1, has_side_effects=True, vmem_limit_bytes=48 << 20
        ),
        name="forward",
    )(*inputs)
    wholes = [
        result.reshape(8 * depth, columns) for result, (depth, columns) in zip(results, shapes)
    ]
    vector, normed, heads, logsum, context = results[weights:]
    return wholes, vector, normed, heads, logsum, context


def place_vectors(vectors):
    stacked = jnp.stack([vector.astype(F32) for vector in vectors])
    count, shard = stacked.shape
    whole = jnp.zeros((8, 8 * shard), F32)
    return lax.dynamic_update_slice(whole, stacked, (0, lax.axis_index("fsdp") * shard))


def text_weights(scale, queries, keys):
    scores = across(keys, queries)
    raised = jnp.exp(scores - jnp.max(scores, axis=0, keepdims=True))
    return raised / jnp.sum(raised, axis=0, keepdims=True)


def pair_columns(pair):
    return slice(pair * 2 * HD, (pair + 1) * 2 * HD)


def text_attention_kernel(scale, q_ref, memory_ref, out_ref):
    pairs = q_ref.shape[1] // (2 * HD)
    for pair in range(pairs):
        queries = both_heads((q_ref[:, pair_columns(pair)].astype(F32) * scale).astype(BF16))
        k = memory_ref[:, pair_columns(pair)]
        v = memory_ref[:, pair_columns(pairs + pair)]
        outs = [down(v, text_weights(scale, part, k).astype(BF16)) for part in queries]
        out_ref[:, pair_columns(pair)] = join_heads(outs).T.astype(BF16)


def text_attention_back_kernel(scale, q_ref, memory_ref, grad_ref, q_out, memory_out):
    pairs = q_ref.shape[1] // (2 * HD)
    for pair in range(pairs):
        queries = both_heads((q_ref[:, pair_columns(pair)].astype(F32) * scale).astype(BF16))
        grads = both_heads(grad_ref[:, pair_columns(pair)])
        k = memory_ref[:, pair_columns(pair)]
        v = memory_ref[:, pair_columns(pairs + pair)]
        query_grads = []
        key_grad = value_grad = 0.0
        for head in range(2):
            weights = text_weights(scale, queries[head], k)
            weighted = weights * across(v, grads[head])
            inner = jnp.sum(weighted, axis=0, keepdims=True)
            change = (weighted - weights * inner).astype(BF16)
            query_grads.append(down(k, change))
            key_grad += jnp.dot(change, queries[head], preferred_element_type=F32)
            value_grad += jnp.dot(weights.astype(BF16), grads[head], preferred_element_type=F32)
        q_out[:, pair_columns(pair)] = (join_heads(query_grads).T * scale).astype(BF16)
        memory_out[:, pair_columns(pair)] = key_grad.astype(BF16)
        memory_out[:, pair_columns(pairs + pair)] = value_grad.astype(BF16)


def text_attention(clips, scale, queries, memory, grad=None):
    spec = lambda value: pl.BlockSpec(
        (value.shape[0] // clips, value.shape[1]), lambda clip: (clip, 0)
    )
    back = grad is not None
    operands = (queries, memory) + ((grad,) if back else ())
    results = (queries, memory) if back else (queries,)
    size = memory.shape[0] // clips * queries.size
    outs = pl.pallas_call(
        functools.partial(text_attention_back_kernel if back else text_attention_kernel, scale),
        grid=(clips,),
        out_shape=[jax.ShapeDtypeStruct(value.shape, BF16) for value in results],
        in_specs=[spec(value) for value in operands],
        out_specs=[spec(value) for value in results],
        compiler_params=pltpu.CompilerParams(vmem_limit_bytes=32 << 20),
        cost_estimate=pl.CostEstimate(
            flops=(20 if back else 8) * size,
            bytes_accessed=2 * sum(value.size for value in operands + results),
            transcendentals=size // HD,
        ),
        name="text_attention_back" if back else "text_attention",
    )(*operands)
    return outs if back else outs[0]


PIECE = (192, 384)
EARLY = 32
AFTER_LAG = 0
OVER_X = 1
STAGES = 7
SLOTS = 6


def sum_kernel(plan, weights, scale, *refs):
    chunks = len(plan)
    late = chunks - 3
    lefts, rights = refs[:weights], refs[weights : 2 * weights - 1]
    refs = refs[2 * weights - 1 :]
    regrouped, context_grad, logsum_in, projection, hidden_in, grad_in, gain_in, vector_in = refs[:8]
    outputs = refs[8 : 8 + weights]
    heads, hidden_out, vector_out = refs[8 + weights : 11 + weights]
    (
        mine,
        c_out,
        c_in,
        x_in,
        y_in,
        second_in,
        z_in,
        early_z_in,
        early_y_in,
        early_x_in,
        total,
        fx_in,
        fc_in,
        stage,
        left_buf,
        right_buf,
        weight_buf,
        normed_grad,
        hidden,
        grad,
        gain,
        q_buf,
        k_buf,
        v_buf,
        context_buf,
        logsum,
        heads_buf,
        key_grads,
        value_grads,
        vector,
        vector_got,
        vector_z,
        c_sem,
        x_sem,
        y_sem,
        second_x_sem,
        second_y_sem,
        z_sem,
        early_sem,
        fx_sem,
        fc_sem,
        stage_sem,
        load_sem,
        vector_sem,
        heads_sem,
        heads_own_sem,
        block_sem,
        own_sem,
    ) = refs[11 + weights :]
    rights = rights + (heads,)
    seq = lax.axis_index("seq")
    fsdp = lax.axis_index("fsdp")
    x, c = seq // 2, seq % 2
    z, y = fsdp // 2, fsdp % 2
    x_device = (2 * (1 - x) + c, fsdp)
    c_device = (2 * x + 1 - c, fsdp)
    far_device = (3 - seq, fsdp)
    y_device = (seq, 2 * z + 1 - y)

    def z_device(k):
        return (seq, 2 * ((z + k) % 4) + y)

    barrier = pltpu.get_barrier_semaphore()
    partners = [x_device, c_device, far_device, y_device] + [z_device(k) for k in (1, 2, 3)]
    for partner in partners:
        pl.semaphore_signal(barrier, inc=1, device_id=partner, device_id_type=MESH)
    pl.semaphore_wait(barrier, len(partners))

    def remote(source, target, sems, device):
        return pltpu.make_async_remote_copy(
            src_ref=source,
            dst_ref=target,
            send_sem=sems.at[0],
            recv_sem=sems.at[1],
            device_id=device,
            device_id_type=MESH,
        )

    def columns(block):
        return pl.ds(pl.multiple_of(block * 384, 128), 384)

    neighbours = (x_device, c_device, far_device)
    clips, pairs = logsum.shape[:2]
    frames = context_grad.shape[1] // clips
    steps = clips * pairs

    def block_loads(step):
        rows = pl.ds(pl.multiple_of(step // pairs * frames, frames), frames)
        first = step % pairs * 2 * HD
        places = [(regrouped, q_buf, 0), (regrouped, k_buf, 384), (regrouped, v_buf, 768)]
        places.append((context_grad, context_buf, 0))
        return [
            pltpu.make_async_copy(
                source.at[:, rows, pl.ds(pl.multiple_of(column + first, 128), 128)],
                buffer.at[:, 0],
                block_sem.at[j],
            )
            for j, (source, buffer, column) in enumerate(places)
        ]

    def heads_region(step, kind, group):
        rows = pl.ds(pl.multiple_of(step // pairs * frames, frames), frames)
        column = (kind * 4 + group) * 384 + step % pairs * 2 * HD
        return heads.at[rows, pl.ds(pl.multiple_of(column, 128), 128)]

    def heads_send(step, which, kind):
        other = neighbours[which]
        return remote(
            heads_buf.at[other[0], 0, :, pl.ds(kind * 128, 128)],
            heads_region(step, kind, seq),
            heads_sem.at[:, step, which, kind],
            other,
        )

    def heads_arrival(step, which, kind):
        region = heads_region(step, kind, neighbours[which][0])
        return remote(region, region, heads_sem.at[:, step, which, kind], neighbours[which])

    def heads_own(step, kind):
        return pltpu.make_async_copy(
            heads_buf.at[seq, 0, :, pl.ds(kind * 128, 128)],
            heads_region(step, kind, seq),
            heads_own_sem.at[step, kind],
        )

    logsum_load = pltpu.make_async_copy(logsum_in, logsum, block_sem.at[4])

    def attention_step(t):
        @pl.when(t == 0)
        def _():
            logsum_load.wait()

        @pl.when(jnp.logical_and(t >= 1, t <= steps))
        def _():
            for kind in range(3):
                heads_own(t - 1, kind).wait()
                for which in range(3):
                    heads_send(t - 1, which, kind).wait_send()

        @pl.when(t < steps)
        def _():
            for copy in block_loads(t):
                copy.wait()
            attention_back_kernel(
                scale,
                q_buf,
                k_buf,
                v_buf,
                context_buf,
                logsum.at[t // pairs, t % pairs],
                heads_buf,
                key_grads,
                value_grads,
            )
            for kind in range(3):
                for which in range(3):
                    heads_send(t, which, kind).start()
                heads_own(t, kind).start()

        @pl.when(t + 1 < steps)
        def _():
            for copy in block_loads(t + 1):
                copy.start()

    def whole(kind):
        return pltpu.make_async_copy(
            projection.at[:, pl.ds(kind * 1536, 1536)], weight_buf, own_sem.at[3]
        )

    operands = [
        pltpu.make_async_copy(hidden_in, hidden, own_sem.at[4]),
        pltpu.make_async_copy(grad_in, grad, own_sem.at[5]),
        pltpu.make_async_copy(gain_in, gain, own_sem.at[6]),
        pltpu.make_async_copy(vector_in, vector.at[0], own_sem.at[7]),
    ]

    def loads(j):
        weight, column = plan[j]
        slot = j % 2
        return [
            pltpu.make_async_copy(lefts[weight], left_buf.at[slot], load_sem.at[0, slot]),
            pltpu.make_async_copy(
                rights[weight].at[:, pl.ds(column, 1536)], right_buf.at[slot], load_sem.at[1, slot]
            ),
        ]

    def start_loads(i):
        for j in range(chunks):

            @pl.when(i == j)
            def _():
                if j >= late:
                    for step in range(steps):
                        for which in range(3):
                            heads_arrival(step, which, j - late).wait_recv()
                for copy in loads(j):
                    copy.start()

    def wait_loads(i):
        for j in range(chunks):

            @pl.when(i == j)
            def _():
                for copy in loads(j):
                    copy.wait()

    def multiply(i, half, target, slot):
        buffer = i % 2
        right = right_buf.at[buffer, :, pl.ds(pl.multiple_of(half * 768, 128), 768)]

        @pl.loop(0, 4)
        def _(zz):
            out = down(left_buf[buffer, :, columns(zz)], right[...]).astype(BF16)
            for q in range(2):
                for yy in range(2):
                    target[slot, q, zz, yy] = out[192 * yy : 192 * yy + 192, 384 * q : 384 * q + 384]

    def multiply_back(i):
        for kind in range(3):

            @pl.when(i == late + kind)
            def _():
                whole(kind).wait()

                @pl.loop(0, right_buf.shape[1] // 128)
                def _(block):
                    rows = pl.ds(pl.multiple_of(block * 128, 128), 128)
                    term = across(right_buf[i % 2, rows, :], weight_buf[...])
                    if kind:
                        normed_grad[rows, :] += term
                    else:
                        normed_grad[rows, :] = term

                if kind < 2:
                    whole(kind + 1).start()

    def norm_back():
        for copy in operands:
            copy.wait()

        def block(index, terms):
            rows = pl.ds(pl.multiple_of(index * 32, 32), 32)
            value = hidden[rows, :].astype(F32)
            center = value - jnp.mean(value, axis=1, keepdims=True)
            inverse = lax.rsqrt(jnp.mean(center * center, axis=1, keepdims=True) + 1e-05)
            normed = center * inverse
            change = normed_grad[rows, :]
            scaled = change * gain[0:1, :]
            first_mean = jnp.mean(scaled, axis=1, keepdims=True)
            second_mean = jnp.mean(scaled * normed, axis=1, keepdims=True)
            grad[rows, :] += inverse * (scaled - first_mean - normed * second_mean)
            gains, biases = terms
            return (
                gains + jnp.sum(change * normed, axis=0, keepdims=True),
                biases + jnp.sum(change, axis=0, keepdims=True),
            )

        zero = jnp.zeros((1, gain.shape[1]), F32)
        gains, biases = lax.fori_loop(0, hidden.shape[0] // 32, block, (zero, zero))
        vector[0, 0:1, :] = gains
        vector[0, 1:2, :] = biases

    def add_to(slot, q, zz, yy, rows, other):
        here = mine[slot, q, zz, yy, rows].astype(F32)
        mine[slot, q, zz, yy, rows] = (here + other.astype(F32)).astype(BF16)

    early_rows = pl.ds(0, EARLY)
    other_rows = pl.ds(EARLY, PIECE[0] - EARLY)

    def c_copy(i):
        return remote(c_out.at[i % 2], c_in.at[i % 2], c_sem.at[:, i % 2], c_device)

    def x_copy(i, count):
        region = pl.ds(0, count)
        return remote(
            mine.at[i % 5, 1 - x, region, :, other_rows],
            x_in.at[i % 4, region],
            x_sem.at[:, i % 4],
            x_device,
        )

    def y_copy(i, count):
        return remote(
            mine.at[i % 5, :, pl.ds(count, 4 - count), 1 - y, other_rows],
            y_in.at[i % 4, :, pl.ds(0, 4 - count)],
            y_sem.at[:, i % 4],
            y_device,
        )

    def second_y_copy(i, count):
        region = pl.ds(0, count)
        return remote(
            mine.at[i % 5, x, region, 1 - y, other_rows],
            second_in.at[i % 5, region],
            second_y_sem.at[:, i % 5],
            y_device,
        )

    def second_x_copy(i, count):
        region = pl.ds(count, 4 - count)
        return remote(
            mine.at[i % 5, 1 - x, region, y, other_rows],
            second_in.at[i % 5, region],
            second_x_sem.at[:, i % 5],
            x_device,
        )

    def z_copy(i, k):
        return remote(
            mine.at[i % 5, x, (z + k) % 4, y, other_rows],
            z_in.at[i % 4, k - 1],
            z_sem.at[:, i % 4, k - 1],
            z_device(k),
        )

    def early_z_copy(i, k):
        return remote(
            mine.at[i % 5, :, (z + k) % 4, :, early_rows],
            early_z_in.at[i % 4, k - 1],
            early_sem.at[:, i % 4, k - 1],
            z_device(k),
        )

    def early_y_copy(i):
        return remote(
            mine.at[i % 5, :, z, 1 - y, early_rows],
            early_y_in.at[i % 4],
            early_sem.at[:, i % 4, 3],
            y_device,
        )

    def early_x_copy(i):
        return remote(
            mine.at[i % 5, 1 - x, z, y, early_rows],
            early_x_in.at[i % 4],
            early_sem.at[:, i % 4, 4],
            x_device,
        )

    def fx_copy(i):
        slot = i % SLOTS
        return remote(total.at[slot], fx_in.at[slot], fx_sem.at[:, slot], x_device)

    def fc_copy(i, which):
        slot = i % SLOTS
        source = fx_in.at[slot] if which else total.at[slot]
        return remote(source, fc_in.at[slot, which], fc_sem.at[:, slot, which], c_device)

    def begin(i):
        wait_loads(i)

        @pl.when(i >= 2)
        def _():
            c_copy(i - 2).wait_send()

        multiply(i, 1 - c, c_out, i % 2)
        c_copy(i).start()
        multiply(i, c, mine, i % 5)
        multiply_back(i)

    def first(i):
        c_copy(i).wait_recv()

        def add_c(q, zz, yy, rows):
            add_to(i % 5, q, zz, yy, rows, c_in[i % 2, q, zz, yy, rows])

        for k in (1, 2, 3):
            for q in range(2):
                for yy in range(2):
                    add_c(q, (z + k) % 4, yy, early_rows)
            early_z_copy(i, k).start()

        def run(i, count):
            @pl.loop(0, count)
            def _(zz):
                for yy in range(2):
                    add_c(1 - x, zz, yy, other_rows)

            x_copy(i, count).start()

            @pl.loop(count, 4)
            def _(zz):
                for q in range(2):
                    add_c(q, zz, 1 - y, other_rows)

            y_copy(i, count).start()

            @pl.loop(0, count)
            def _(zz):
                for yy in range(2):
                    add_c(x, zz, yy, other_rows)

            @pl.loop(count, 4)
            def _(zz):
                for q in range(2):
                    add_c(q, zz, y, other_rows)

        run(i, OVER_X)
        for q in range(2):
            for yy in range(2):
                add_c(q, z, yy, early_rows)

    def second(i):
        own, slot = i % 5, i % 4

        def run(i, count):
            def add_x(yy):
                @pl.loop(0, count)
                def _(zz):
                    add_to(own, x, zz, yy, other_rows, x_in[slot, zz, yy])

            def add_y(q):
                @pl.loop(count, 4)
                def _(zz):
                    add_to(own, q, zz, y, other_rows, y_in[slot, q, zz - count])

            x_copy(i, count).wait()
            add_x(1 - y)
            second_y_copy(i, count).start()
            y_copy(i, count).wait()
            add_y(1 - x)
            second_x_copy(i, count).start()
            add_x(y)
            add_y(x)

        run(i, OVER_X)
        for k in (1, 2, 3):
            early_z_copy(i, k).wait()

        def add_early(q, yy):
            others = [early_z_in[slot, k, q, yy].astype(F32) for k in range(3)]
            add_to(own, q, z, yy, early_rows, others[0] + others[1] + others[2])

        for q in range(2):
            add_early(q, 1 - y)
        early_y_copy(i).start()
        for q in range(2):
            add_early(q, y)

    def third(i):
        own, slot = i % 5, i % 4

        def run(i, count):
            second_y_copy(i, count).wait()
            second_x_copy(i, count).wait()

        run(i, OVER_X)
        for k in (1, 2, 3):
            zz = (z + k) % 4
            add_to(own, x, zz, y, other_rows, second_in[own, zz])
            z_copy(i, k).start()
        early_y_copy(i).wait()
        add_to(own, 1 - x, z, y, early_rows, early_y_in[slot, 1 - x])
        early_x_copy(i).start()
        add_to(own, x, z, y, early_rows, early_y_in[slot, x])

    def fourth(i):
        own, slot = i % 5, i % 4
        result = mine[own, x, z, y, other_rows].astype(F32) + second_in[own, z].astype(F32)
        for k in (1, 2, 3):
            z_copy(i, k).wait()
            result = result + z_in[slot, k - 1].astype(F32)
        total[i % SLOTS, other_rows] = result.astype(BF16)
        early_x_copy(i).wait()
        result = mine[own, x, z, y, early_rows].astype(F32) + early_x_in[slot].astype(F32)
        total[i % SLOTS, early_rows] = result.astype(BF16)
        fx_copy(i).start()
        fc_copy(i, 0).start()

    def fifth(i):
        fx_copy(i).wait()
        fc_copy(i, 1).start()

    def store(j):
        weight, column = plan[j]
        return pltpu.make_async_copy(
            stage.at[j % 2], outputs[weight].at[:, pl.ds(column, 1536)], stage_sem.at[j % 2]
        )

    def sixth(i):
        slot = i % SLOTS
        for j in range(2, chunks):

            @pl.when(i == j)
            def _():
                store(j - 2).wait()

        def put(quarter, value):
            stage[i % 2, :, columns(quarter)] = value

        fc_copy(i, 0).wait()
        fc_copy(i, 1).wait()
        put(2 * c + x, total[slot])
        put(2 * c + 1 - x, fx_in[slot])
        put(2 * (1 - c) + x, fc_in[slot, 0])
        put(2 * (1 - c) + 1 - x, fc_in[slot, 1])
        for j in range(chunks):

            @pl.when(i == j)
            def _():
                store(j).start()

    def vector_copy(leg):
        device = (c_device, x_device, y_device)[leg]
        return remote(vector.at[leg], vector_got.at[leg], vector_sem.at[:, leg], device)

    def vector_z_copy(k):
        return remote(vector_z.at[z], vector_z.at[z], vector_sem.at[:, 2 + k], z_device(k))

    def vector_arrival(k):
        source = (z + 4 - k) % 4
        return remote(vector_z.at[source], vector_z.at[source], vector_sem.at[:, 2 + k], z_device(k))

    hidden_store = pltpu.make_async_copy(grad, hidden_out, own_sem.at[5])

    def vector_step(step):
        @pl.when(step == 0)
        def _():
            norm_back()
            hidden_store.start()
            vector_copy(0).start()

        for leg in range(3):

            @pl.when(step == leg + 1)
            def _():
                vector_copy(leg).wait()
                both = vector[leg] + vector_got[leg]
                if leg < 2:
                    vector[leg + 1] = both
                    vector_copy(leg + 1).start()
                else:
                    vector_z[z] = both
                    for k in (1, 2, 3):
                        vector_z_copy(k).start()

        @pl.when(step == 4)
        def _():
            for k in (1, 2, 3):
                vector_z_copy(k).wait_send()
                vector_arrival(k).wait_recv()
            vector[0] = vector_z[0] + vector_z[1] + vector_z[2] + vector_z[3]
            pltpu.sync_copy(vector.at[0], vector_out)

    start_loads(0)
    for copy in block_loads(0):
        copy.start()
    logsum_load.start()
    whole(0).start()
    for copy in operands:
        copy.start()

    @pl.loop(0, chunks + STAGES - 1)
    def _(t):
        @pl.when(t + 1 < chunks)
        def _():
            start_loads(t + 1)

        for lag, run in ((1, first), (0, begin), (2, second), (3, third), (4, fourth), (5, fifth), (6, sixth)):
            i = t - lag

            @pl.when(jnp.logical_and(i >= 0, i < chunks))
            def _():
                run(i)

            if lag == AFTER_LAG:
                attention_step(t)

        vector_step(t - chunks)

    for j in (chunks - 2, chunks - 1):
        c_copy(j).wait_send()
        store(j).wait()
    hidden_store.wait()


def sum_products(
    lefts, rights, regrouped, context_grad, logsum, projection, hidden, grad, gain, vectors, scale
):
    weights = len(lefts)
    widths = [right.shape[1] for right in rights] + [projection.shape[1]]
    plan = [
        (weight, column)
        for weight, width in enumerate(widths)
        for column in range(0, width, 1536)
    ]
    depth, width = hidden.shape
    out_shapes = [
        jax.ShapeDtypeStruct((left.shape[1] // 8, columns), BF16)
        for left, columns in zip(lefts, widths)
    ]
    out_shapes += [
        jax.ShapeDtypeStruct((depth, widths[-1]), BF16),
        jax.ShapeDtypeStruct(grad.shape, F32),
        jax.ShapeDtypeStruct(vectors.shape, F32),
    ]
    inputs = (
        *lefts,
        *rights,
        regrouped,
        context_grad,
        logsum,
        projection,
        hidden,
        grad,
        gain,
        vectors,
    )
    clips, pairs, *_, length = logsum.shape
    frames = depth // clips
    pair_block = pltpu.VMEM((4, 1, frames, 2 * HD), BF16)
    pair_grads = pltpu.VMEM((length, 2 * HD), F32)
    anywhere = pl.BlockSpec(memory_space=pl.ANY)
    dma = pltpu.SemaphoreType.DMA
    rest = PIECE[0] - EARLY
    block = lambda *lead, rows=PIECE[0]: pltpu.VMEM(lead + (rows, PIECE[1]), BF16)
    results = pl.pallas_call(
        functools.partial(sum_kernel, tuple(plan), weights, scale),
        out_shape=out_shapes,
        in_specs=[anywhere] * len(inputs),
        out_specs=[anywhere] * len(out_shapes),
        scratch_shapes=[
            block(5, 2, 4, 2),
            block(2, 2, 4, 2),
            block(2, 2, 4, 2),
            block(4, OVER_X, 2, rows=rest),
            block(4, 2, 4 - OVER_X, rows=rest),
            block(5, 4, rows=rest),
            block(4, 3, rows=rest),
            block(4, 3, 2, 2, rows=EARLY),
            block(4, 2, rows=EARLY),
            block(4, rows=EARLY),
            block(SLOTS),
            block(SLOTS),
            block(SLOTS, 2),
            pltpu.VMEM((2, 192, 1536), BF16),
            pltpu.VMEM((2, depth, 1536), BF16),
            pltpu.VMEM((2, depth, 1536), BF16),
            pltpu.VMEM((width, 1536), BF16),
            pltpu.VMEM((depth, width), F32),
            pltpu.VMEM((depth, width), BF16),
            pltpu.VMEM((depth, width), F32),
            pltpu.VMEM(gain.shape, F32),
            pair_block,
            pair_block,
            pair_block,
            pair_block,
            pltpu.VMEM(logsum.shape, F32),
            pltpu.VMEM((4, 1, frames, 3 * 2 * HD), BF16),
            pair_grads,
            pair_grads,
            pltpu.VMEM((3,) + vectors.shape, F32),
            pltpu.VMEM((3,) + vectors.shape, F32),
            pltpu.VMEM((4,) + vectors.shape, F32),
            dma((2, 2)),
            dma((2, 4)),
            dma((2, 4)),
            dma((2, 5)),
            dma((2, 5)),
            dma((2, 4, 3)),
            dma((2, 4, 5)),
            dma((2, SLOTS)),
            dma((2, SLOTS, 2)),
            dma((2,)),
            dma((2, 2)),
            dma((2, 6)),
            dma((2, clips * pairs, 3, 3)),
            dma((clips * pairs, 3)),
            dma((5,)),
            dma((8,)),
        ],
        compiler_params=pltpu.CompilerParams(
            collective_id=3, has_side_effects=True, vmem_limit_bytes=60 << 20
        ),
        name="sum_products",
    )(*inputs)
    return results[:weights], results[-2], results[-1]


def on_blocks(
    hidden_states,
    text_states,
    self_gain,
    self_bias,
    query_key_value,
    self_output,
    cross_gain,
    cross_bias,
    cross_query,
    cross_memory,
    cross_output,
    final_gain,
    final_bias,
    expand_weight,
    contract_weight,
    output_cotangent,
):
    clips, frames, width = hidden_states.shape
    rows = clips * frames
    groups = lax.axis_size("seq")
    fsdp_count = lax.axis_size("fsdp")
    scale = HD ** (-0.5)
    entries = rows * groups * fsdp_count * width
    group_width = width // groups

    gains = (self_gain, self_bias, cross_gain, cross_bias, final_gain, final_bias)
    wholes, gains, normed_one, regrouped, logsum, context = forward(
        (
            query_key_value,
            self_output,
            cross_query,
            cross_memory,
            cross_output,
            expand_weight,
            contract_weight,
        ),
        place_vectors(gains),
        hidden_states.reshape(rows, width),
        clips,
        scale,
    )
    (
        qkv_whole,
        self_output_whole,
        cross_query_whole,
        cross_memory_whole,
        cross_output_whole,
        expand_whole,
        contract_whole,
    ) = wholes
    hidden = hidden_states.reshape(rows, width).astype(F32)
    attended = product(context, self_output_whole)
    first = hidden + attended
    normed_two, norm_two_back = jax.vjp(layer_norm, first, gains[2], gains[3])
    normed_two = normed_two.astype(BF16)
    cross_q = product(normed_two, cross_query_whole).astype(BF16)
    text_rows = text_states.reshape(clips * TEXT, width)
    memory = product(text_rows, cross_memory_whole).astype(BF16)
    cross_context = text_attention(clips, scale, cross_q, memory)
    crossed = product(cross_context, cross_output_whole)
    second = first + crossed
    normed_three, norm_three_back = jax.vjp(layer_norm, second, gains[4], gains[5])
    normed_three = normed_three.astype(BF16)
    preact = product(normed_three, expand_whole)
    below = 0.5 + 0.5 * lax.erf(preact * 0.5**0.5)
    density = jnp.exp(preact * preact * -0.5) * (0.5 / jnp.pi) ** 0.5
    activated = (preact * below).astype(BF16)
    slope = (below + preact * density).astype(BF16)
    upstream = output_cotangent.reshape(rows, width).astype(F32)
    grad_mixed = output_cotangent.reshape(rows, width)
    contract_term = product_left(activated, grad_mixed).astype(BF16)
    grad_mixed, contract_term, contract_whole = lax.optimization_barrier(
        (grad_mixed, contract_term, contract_whole)
    )
    contract_part = lax.psum_scatter(
        contract_term, ("fsdp", "seq"), scatter_dimension=0, tiled=True
    )
    grad_activated = product_right(grad_mixed, contract_whole)
    grad_preact = (grad_activated * slope.astype(F32)).astype(BF16)
    grad_normed_three = product_right(grad_preact, expand_whole)
    grad_second, final_gain_term, final_bias_term = norm_three_back(grad_normed_three)
    grad_second = upstream + grad_second
    grad_crossed = grad_second.astype(BF16)
    grad_cross_context = product_right(grad_crossed, cross_output_whole).astype(BF16)
    grad_cross_q, grad_memory = text_attention(clips, scale, cross_q, memory, grad_cross_context)
    grad_normed_two = product_right(grad_cross_q, cross_query_whole)
    grad_first, cross_gain_term, cross_bias_term = norm_two_back(grad_normed_two)
    grad_first = grad_second + grad_first
    grad_attended = grad_first.astype(BF16)
    grad_context = product_right(grad_attended, self_output_whole).astype(BF16)
    grad_context = grad_context.reshape(rows, groups, group_width).transpose(1, 0, 2)
    grad_context, activated = lax.optimization_barrier((grad_context, activated))
    grad_heads = lax.all_to_all(grad_context, "seq", split_axis=0, concat_axis=0, tiled=True)
    mixed = product(activated, contract_whole)
    output = second + mixed
    squares = jnp.stack(
        [
            jnp.sum(output * output),
            jnp.sum(attended * attended),
            jnp.sum(crossed * crossed),
            jnp.sum(mixed * mixed),
        ]
    )
    output = output.astype(BF16)
    zeros = jnp.zeros_like(cross_gain_term)
    terms = jnp.stack(
        [
            zeros,
            zeros,
            cross_gain_term,
            cross_bias_term,
            final_gain_term,
            final_bias_term,
            jnp.pad(squares, (0, width - 4)),
            zeros,
        ]
    )
    deep = lambda value: jnp.pad(value, ((0, rows - value.shape[0]), (0, 0)))
    text_operands = (deep(text_rows), deep(grad_memory))
    grad_heads, output, terms, text_operands = lax.optimization_barrier(
        (grad_heads, output, terms, text_operands)
    )
    gradients, grad_hidden, totals = sum_products(
        [normed_three, cross_context, normed_two, text_operands[0], context, normed_one],
        [grad_preact, grad_crossed, grad_cross_q, text_operands[1], grad_attended],
        regrouped,
        grad_heads,
        logsum,
        qkv_whole,
        hidden_states.reshape(rows, width),
        grad_first,
        jnp.broadcast_to(gains[0], (8, width)),
        terms,
        scale,
    )
    gradients, contract_part = lax.optimization_barrier((gradients, contract_part))
    contract_gradient = lax.all_gather(contract_part, "seq", axis=0, tiled=True)
    gradients = [gradient.astype(F32) for gradient in gradients]
    contract_gradient = contract_gradient.astype(F32)
    layer_rms = jnp.sqrt(totals[6, :4] / entries)
    shard = width // fsdp_count
    vector_gradients = lax.dynamic_slice_in_dim(
        totals, lax.axis_index("fsdp") * shard, shard, 1
    )
    return (
        output.reshape(clips, frames, width),
        grad_hidden.reshape(clips, frames, width),
        vector_gradients[0],
        vector_gradients[1],
        gradients[5],
        gradients[4],
        vector_gradients[2],
        vector_gradients[3],
        gradients[2],
        gradients[3],
        gradients[1],
        vector_gradients[4],
        vector_gradients[5],
        gradients[0],
        contract_gradient,
        layer_rms,
    )


def solution(mesh):
    shape = dict(mesh.shape)
    blocks = shape["seq"] == 4 and shape["fsdp"] == 8
    return jax.shard_map(
        on_blocks if blocks else on_any_mesh,
        mesh=mesh,
        in_specs=(
            P("fsdp", "seq", None),
            P("fsdp", None, None),
            P("fsdp"),
            P("fsdp"),
            P("fsdp", None),
            P("fsdp", None),
            P("fsdp"),
            P("fsdp"),
            P("fsdp", None),
            P("fsdp", None),
            P("fsdp", None),
            P("fsdp"),
            P("fsdp"),
            P("fsdp", None),
            P("fsdp", None),
            P("fsdp", "seq", None),
        ),
        out_specs=(
            P("fsdp", "seq", None),
            P("fsdp", "seq", None),
            P("fsdp"),
            P("fsdp"),
            P("fsdp", None),
            P("fsdp", None),
            P("fsdp"),
            P("fsdp"),
            P("fsdp", None),
            P("fsdp", None),
            P("fsdp", None),
            P("fsdp"),
            P("fsdp"),
            P("fsdp", None),
            P("fsdp", None),
            P(),
        ),
        check_vma=False,
    )
```

```python
import functools

import jax
import jax.numpy as jnp
from jax import lax
from jax.experimental import pallas as pl
from jax.experimental.pallas import tpu as pltpu
from jax.sharding import PartitionSpec as P

H = 24
HD = 64
TEXT = 64

NEGATIVE = -1e30
BF16 = jnp.bfloat16
F32 = jnp.float32
MESH = pl.DeviceIdType.MESH


def layer_norm(values, gain, offset):
    center = values - jnp.mean(values, axis=-1, keepdims=True)
    spread = jnp.mean(center * center, axis=-1, keepdims=True)
    return center * lax.rsqrt(spread + 1e-05) * gain + offset


def gelu_exact(values):
    return jax.nn.gelu(values, approximate=False)


def product(left, right):
    return jnp.dot(left, right, preferred_element_type=jnp.float32)


def product_left(left, right):
    return lax.dot_general(
        left, right, (((0,), (0,)), ((), ())), preferred_element_type=jnp.float32
    )


def product_right(left, right):
    return lax.dot_general(
        left, right, (((1,), (1,)), ((), ())), preferred_element_type=jnp.float32
    )


def causal_forward(queries, keys, values, rows_block, scale):
    clips, length, heads_local, head_width = queries.shape
    count = length // rows_block
    columns = jnp.arange(length, dtype=jnp.int32)

    def one_block(start):
        block = lax.dynamic_slice_in_dim(queries, start, rows_block, 1)
        scores = (
            jnp.einsum("cqhd,ckhd->chqk", block, keys, preferred_element_type=jnp.float32) * scale
        )
        positions = start + jnp.arange(rows_block, dtype=jnp.int32)
        allowed = columns[None, :] <= positions[:, None]
        scores = jnp.where(allowed, scores, NEGATIVE)
        highest = jnp.max(scores, axis=-1, keepdims=True)
        raised = jnp.exp(scores - highest)
        summed = jnp.sum(raised, axis=-1, keepdims=True)
        weights = (raised / summed).astype(jnp.bfloat16)
        result = jnp.einsum("chqk,ckhd->cqhd", weights, values, preferred_element_type=jnp.float32)
        return (result.astype(jnp.bfloat16), (highest + jnp.log(summed))[..., 0])

    starts = jnp.arange(count, dtype=jnp.int32) * rows_block
    results, logsum = lax.map(one_block, starts)
    results = jnp.moveaxis(results, 0, 1).reshape(clips, length, heads_local * head_width)
    return (results, logsum)


def causal_backward(queries, keys, values, logsum, grad_heads, rows_block, scale):
    clips, length, heads_local, head_width = queries.shape
    count = length // rows_block
    columns = jnp.arange(length, dtype=jnp.int32)
    starts = jnp.arange(count, dtype=jnp.int32) * rows_block

    def one_block(carry, inputs):
        grad_keys, grad_values = carry
        start, block_logsum = inputs
        block = lax.dynamic_slice_in_dim(queries, start, rows_block, 1)
        block_grad = lax.dynamic_slice_in_dim(grad_heads, start, rows_block, 1)
        scores = (
            jnp.einsum("cqhd,ckhd->chqk", block, keys, preferred_element_type=jnp.float32) * scale
        )
        positions = start + jnp.arange(rows_block, dtype=jnp.int32)
        allowed = columns[None, :] <= positions[:, None]
        scores = jnp.where(allowed, scores, NEGATIVE)
        weights = jnp.exp(scores - block_logsum[..., None])
        rounded = weights.astype(jnp.bfloat16)
        grad_weights = jnp.einsum(
            "cqhd,ckhd->chqk", block_grad, values, preferred_element_type=jnp.float32
        )
        inner = jnp.sum(weights * grad_weights, axis=-1, keepdims=True)
        grad_scores = (weights * (grad_weights - inner)).astype(jnp.bfloat16)
        grad_query = (
            jnp.einsum("chqk,ckhd->cqhd", grad_scores, keys, preferred_element_type=jnp.float32)
            * scale
        )
        grad_keys = (
            grad_keys
            + jnp.einsum("chqk,cqhd->ckhd", grad_scores, block, preferred_element_type=jnp.float32)
            * scale
        )
        grad_values = grad_values + jnp.einsum(
            "chqk,cqhd->ckhd", rounded, block_grad, preferred_element_type=jnp.float32
        )
        return ((grad_keys, grad_values), grad_query.astype(jnp.bfloat16))

    zeros = jnp.zeros(queries.shape, jnp.float32)
    (grad_keys, grad_values), grad_queries = lax.scan(one_block, (zeros, zeros), (starts, logsum))
    local_width = heads_local * head_width
    grad_queries = jnp.moveaxis(grad_queries, 0, 1).reshape(clips, length, local_width)
    grad_keys = grad_keys.astype(jnp.bfloat16).reshape(clips, length, local_width)
    grad_values = grad_values.astype(jnp.bfloat16).reshape(clips, length, local_width)
    return jnp.stack([grad_queries, grad_keys, grad_values], axis=2)


def on_any_mesh(
    hidden_states,
    text_states,
    self_gain,
    self_bias,
    query_key_value,
    self_output,
    cross_gain,
    cross_bias,
    cross_query,
    cross_memory,
    cross_output,
    final_gain,
    final_bias,
    expand_weight,
    contract_weight,
    output_cotangent,
):
    clips, frames, width = hidden_states.shape
    rows = clips * frames
    groups = lax.axis_size("seq")
    fsdp_count = lax.axis_size("fsdp")
    heads_local = H // groups
    length = frames * groups
    rows_block = min(512, length)
    scale = HD ** (-0.5)
    entries = rows * groups * fsdp_count * width
    self_set = (
        lax.all_gather(self_gain, "fsdp", axis=0, tiled=True),
        lax.all_gather(self_bias, "fsdp", axis=0, tiled=True),
        lax.all_gather(query_key_value, "fsdp", axis=0, tiled=True),
        lax.all_gather(self_output, "fsdp", axis=0, tiled=True),
    )
    hidden = hidden_states.reshape(rows, width).astype(jnp.float32)
    normed_one, norm_one_back = jax.vjp(
        layer_norm, hidden, self_set[0].astype(jnp.float32), self_set[1].astype(jnp.float32)
    )
    normed_one = normed_one.astype(jnp.bfloat16)
    projected = (
        product(normed_one, self_set[2]).astype(jnp.bfloat16).reshape(clips, frames, 3, width)
    )
    regrouped = lax.all_to_all(projected, "seq", split_axis=3, concat_axis=1, tiled=True)
    regrouped = regrouped.reshape(clips, length, 3, heads_local, HD)
    queries = regrouped[:, :, 0]
    keys = regrouped[:, :, 1]
    values = regrouped[:, :, 2]
    context_heads, logsum = causal_forward(queries, keys, values, rows_block, scale)
    context = lax.all_to_all(context_heads, "seq", split_axis=1, concat_axis=2, tiled=True).reshape(
        rows, width
    )
    attended = product(context, self_set[3])
    first = hidden + attended
    rest_set = (
        lax.all_gather(cross_gain, "fsdp", axis=0, tiled=True),
        lax.all_gather(cross_bias, "fsdp", axis=0, tiled=True),
        lax.all_gather(cross_query, "fsdp", axis=0, tiled=True),
        lax.all_gather(cross_memory, "fsdp", axis=0, tiled=True),
        lax.all_gather(cross_output, "fsdp", axis=0, tiled=True),
        lax.all_gather(final_gain, "fsdp", axis=0, tiled=True),
        lax.all_gather(final_bias, "fsdp", axis=0, tiled=True),
        lax.all_gather(expand_weight, "fsdp", axis=0, tiled=True),
        lax.all_gather(contract_weight, "fsdp", axis=0, tiled=True),
    )
    normed_two, norm_two_back = jax.vjp(
        layer_norm, first, rest_set[0].astype(jnp.float32), rest_set[1].astype(jnp.float32)
    )
    normed_two = normed_two.astype(jnp.bfloat16)
    cross_q = product(normed_two, rest_set[2]).astype(jnp.bfloat16).reshape(clips, frames, H, HD)
    text_rows = text_states.reshape(clips * TEXT, width)
    memory = product(text_rows, rest_set[3]).astype(jnp.bfloat16).reshape(clips, TEXT, 2, H, HD)
    cross_keys = memory[:, :, 0]
    cross_values = memory[:, :, 1]
    cross_scores = (
        jnp.einsum("cqhd,ckhd->chqk", cross_q, cross_keys, preferred_element_type=jnp.float32)
        * scale
    )
    highest = jnp.max(cross_scores, axis=-1, keepdims=True)
    raised = jnp.exp(cross_scores - highest)
    cross_weights = raised / jnp.sum(raised, axis=-1, keepdims=True)
    cross_rounded = cross_weights.astype(jnp.bfloat16)
    cross_context = jnp.einsum(
        "chqk,ckhd->cqhd", cross_rounded, cross_values, preferred_element_type=jnp.float32
    )
    cross_context = cross_context.astype(jnp.bfloat16).reshape(rows, width)
    crossed = product(cross_context, rest_set[4])
    second = first + crossed
    normed_three, norm_three_back = jax.vjp(
        layer_norm, second, rest_set[5].astype(jnp.float32), rest_set[6].astype(jnp.float32)
    )
    normed_three = normed_three.astype(jnp.bfloat16)
    preact = product(normed_three, rest_set[7])
    activated, gelu_back = jax.vjp(gelu_exact, preact)
    activated = activated.astype(jnp.bfloat16)
    mixed = product(activated, rest_set[8])
    output = second + mixed
    squares = jnp.stack(
        [
            jnp.sum(output * output),
            jnp.sum(attended * attended),
            jnp.sum(crossed * crossed),
            jnp.sum(mixed * mixed),
        ]
    )
    square_totals = lax.psum(squares, ("seq", "fsdp"))
    back_rest = (
        lax.all_gather(cross_gain, "fsdp", axis=0, tiled=True),
        lax.all_gather(cross_bias, "fsdp", axis=0, tiled=True),
        lax.all_gather(cross_query, "fsdp", axis=0, tiled=True),
        lax.all_gather(cross_memory, "fsdp", axis=0, tiled=True),
        lax.all_gather(cross_output, "fsdp", axis=0, tiled=True),
        lax.all_gather(final_gain, "fsdp", axis=0, tiled=True),
        lax.all_gather(final_bias, "fsdp", axis=0, tiled=True),
        lax.all_gather(expand_weight, "fsdp", axis=0, tiled=True),
        lax.all_gather(contract_weight, "fsdp", axis=0, tiled=True),
    )
    upstream = output_cotangent.reshape(rows, width).astype(jnp.float32)
    grad_mixed = upstream.astype(jnp.bfloat16)
    contract_term = product_left(activated, grad_mixed)
    grad_activated = product_right(grad_mixed, back_rest[8])
    grad_preact = gelu_back(grad_activated)[0].astype(jnp.bfloat16)
    expand_term = product_left(normed_three, grad_preact)
    grad_normed_three = product_right(grad_preact, back_rest[7])
    grad_second, final_gain_term, final_bias_term = norm_three_back(grad_normed_three)
    grad_second = upstream + grad_second
    grad_crossed = grad_second.astype(jnp.bfloat16)
    cross_output_term = product_left(cross_context, grad_crossed)
    grad_cross_context = (
        product_right(grad_crossed, back_rest[4]).astype(jnp.bfloat16).reshape(clips, frames, H, HD)
    )
    grad_cross_weights = jnp.einsum(
        "cqhd,ckhd->chqk", grad_cross_context, cross_values, preferred_element_type=jnp.float32
    )
    cross_inner = jnp.sum(cross_weights * grad_cross_weights, axis=-1, keepdims=True)
    grad_cross_scores = (cross_weights * (grad_cross_weights - cross_inner)).astype(jnp.bfloat16)
    grad_cross_q = (
        jnp.einsum(
            "chqk,ckhd->cqhd", grad_cross_scores, cross_keys, preferred_element_type=jnp.float32
        )
        * scale
    )
    grad_cross_q = grad_cross_q.astype(jnp.bfloat16).reshape(rows, width)
    grad_cross_keys = (
        jnp.einsum(
            "chqk,cqhd->ckhd", grad_cross_scores, cross_q, preferred_element_type=jnp.float32
        )
        * scale
    )
    grad_cross_values = jnp.einsum(
        "chqk,cqhd->ckhd", cross_rounded, grad_cross_context, preferred_element_type=jnp.float32
    )
    grad_memory = jnp.stack([grad_cross_keys, grad_cross_values], axis=2).reshape(
        clips * TEXT, 2 * width
    )
    memory_term = lax.dot_general(
        text_rows.astype(jnp.float32),
        grad_memory,
        (((0,), (0,)), ((), ())),
        precision=lax.Precision.HIGHEST,
        preferred_element_type=jnp.float32,
    )
    query_term = product_left(normed_two, grad_cross_q)
    grad_normed_two = product_right(grad_cross_q, back_rest[2])
    grad_first, cross_gain_term, cross_bias_term = norm_two_back(grad_normed_two)
    grad_first = grad_second + grad_first
    rest_sums = (
        lax.psum_scatter(
            cross_gain_term.astype(jnp.bfloat16), "fsdp", scatter_dimension=0, tiled=True
        ).astype(jnp.float32),
        lax.psum_scatter(
            cross_bias_term.astype(jnp.bfloat16), "fsdp", scatter_dimension=0, tiled=True
        ).astype(jnp.float32),
        lax.psum_scatter(
            query_term.astype(jnp.bfloat16), "fsdp", scatter_dimension=0, tiled=True
        ).astype(jnp.float32),
        lax.psum_scatter(
            memory_term.astype(jnp.bfloat16), "fsdp", scatter_dimension=0, tiled=True
        ).astype(jnp.float32),
        lax.psum_scatter(
            cross_output_term.astype(jnp.bfloat16), "fsdp", scatter_dimension=0, tiled=True
        ).astype(jnp.float32),
        lax.psum_scatter(
            final_gain_term.astype(jnp.bfloat16), "fsdp", scatter_dimension=0, tiled=True
        ).astype(jnp.float32),
        lax.psum_scatter(
            final_bias_term.astype(jnp.bfloat16), "fsdp", scatter_dimension=0, tiled=True
        ).astype(jnp.float32),
        lax.psum_scatter(
            expand_term.astype(jnp.bfloat16), "fsdp", scatter_dimension=0, tiled=True
        ).astype(jnp.float32),
        lax.psum_scatter(
            contract_term.astype(jnp.bfloat16), "fsdp", scatter_dimension=0, tiled=True
        ).astype(jnp.float32),
    )
    back_self = (
        lax.all_gather(self_gain, "fsdp", axis=0, tiled=True),
        lax.all_gather(self_bias, "fsdp", axis=0, tiled=True),
        lax.all_gather(query_key_value, "fsdp", axis=0, tiled=True),
        lax.all_gather(self_output, "fsdp", axis=0, tiled=True),
    )
    grad_attended = grad_first.astype(jnp.bfloat16)
    self_output_term = product_left(context, grad_attended)
    grad_context = (
        product_right(grad_attended, back_self[3])
        .astype(jnp.bfloat16)
        .reshape(clips, frames, width)
    )
    grad_heads = lax.all_to_all(grad_context, "seq", split_axis=2, concat_axis=1, tiled=True)
    grad_heads = grad_heads.reshape(clips, length, heads_local, HD)
    grad_regrouped = causal_backward(queries, keys, values, logsum, grad_heads, rows_block, scale)
    grad_projected = lax.all_to_all(
        grad_regrouped, "seq", split_axis=1, concat_axis=3, tiled=True
    ).reshape(rows, 3 * width)
    qkv_term = product_left(normed_one, grad_projected)
    grad_normed_one = product_right(grad_projected, back_self[2])
    grad_hidden, gain_one_term, bias_one_term = norm_one_back(grad_normed_one)
    grad_hidden = grad_first + grad_hidden
    self_sums = (
        lax.psum_scatter(
            gain_one_term.astype(jnp.bfloat16), "fsdp", scatter_dimension=0, tiled=True
        ).astype(jnp.float32),
        lax.psum_scatter(
            bias_one_term.astype(jnp.bfloat16), "fsdp", scatter_dimension=0, tiled=True
        ).astype(jnp.float32),
        lax.psum_scatter(
            qkv_term.astype(jnp.bfloat16), "fsdp", scatter_dimension=0, tiled=True
        ).astype(jnp.float32),
        lax.psum_scatter(
            self_output_term.astype(jnp.bfloat16), "fsdp", scatter_dimension=0, tiled=True
        ).astype(jnp.float32),
    )
    finals = (
        lax.psum(self_sums[0].astype(jnp.bfloat16), "seq").astype(jnp.float32),
        lax.psum(self_sums[1].astype(jnp.bfloat16), "seq").astype(jnp.float32),
        lax.psum(self_sums[2].astype(jnp.bfloat16), "seq").astype(jnp.float32),
        lax.psum(self_sums[3].astype(jnp.bfloat16), "seq").astype(jnp.float32),
        lax.psum(rest_sums[0].astype(jnp.bfloat16), "seq").astype(jnp.float32),
        lax.psum(rest_sums[1].astype(jnp.bfloat16), "seq").astype(jnp.float32),
        lax.psum(rest_sums[2].astype(jnp.bfloat16), "seq").astype(jnp.float32),
        lax.psum(rest_sums[3].astype(jnp.bfloat16), "seq").astype(jnp.float32),
        lax.psum(rest_sums[4].astype(jnp.bfloat16), "seq").astype(jnp.float32),
        lax.psum(rest_sums[5].astype(jnp.bfloat16), "seq").astype(jnp.float32),
        lax.psum(rest_sums[6].astype(jnp.bfloat16), "seq").astype(jnp.float32),
        lax.psum(rest_sums[7].astype(jnp.bfloat16), "seq").astype(jnp.float32),
        lax.psum(rest_sums[8].astype(jnp.bfloat16), "seq").astype(jnp.float32),
    )
    layer_rms = jnp.sqrt(square_totals / entries)
    return (
        output.astype(jnp.bfloat16).reshape(clips, frames, width),
        grad_hidden.reshape(clips, frames, width),
        finals[0],
        finals[1],
        finals[2],
        finals[3],
        finals[4],
        finals[5],
        finals[6],
        finals[7],
        finals[8],
        finals[9],
        finals[10],
        finals[11],
        finals[12],
        layer_rms,
    )


QUERIES = 256


def both_heads(value):
    lane = lax.broadcasted_iota(jnp.int32, value.shape, 1)
    zero = jnp.zeros_like(value)
    return jnp.where(lane < HD, value, zero), jnp.where(lane < HD, zero, value)


def across(left, right):
    return lax.dot_general(left, right, (((1,), (1,)), ((), ())), preferred_element_type=F32)


def down(left, right):
    return lax.dot_general(left, right, (((0,), (0,)), ((), ())), preferred_element_type=F32)


def join_heads(pair):
    row = lax.broadcasted_iota(jnp.int32, pair[0].shape, 0)
    return jnp.where(row < HD, pair[0], pair[1])


def key_parts(block):
    return ([(0, block * QUERIES, False)] if block else []) + [
        (block * QUERIES, (block + 1) * QUERIES, True)
    ]


def masked_scores(keys, queries, diagonal):
    scores = across(keys, queries)
    if diagonal:
        key = lax.broadcasted_iota(jnp.int32, scores.shape, 0)
        query = lax.broadcasted_iota(jnp.int32, scores.shape, 1)
        scores = jnp.where(key <= query, scores, NEGATIVE)
    return scores


def attention_kernel(scale, q_ref, k_ref, v_ref, out_ref, logsum_ref):
    blocks = q_ref.shape[0] * q_ref.shape[2] // QUERIES
    k = k_ref[:, 0].reshape(-1, 2 * HD)
    v = v_ref[:, 0].reshape(-1, 2 * HD)
    for block in range(blocks):
        rows = slice(block * QUERIES, (block + 1) * QUERIES)
        queries = both_heads((q_ref[block, 0].astype(F32) * scale).astype(BF16))
        outs = []
        for head in range(2):
            parts = key_parts(block)
            scores = [masked_scores(k[a:b], queries[head], diagonal) for a, b, diagonal in parts]
            highest = functools.reduce(
                jnp.maximum, [jnp.max(part, axis=0, keepdims=True) for part in scores]
            )
            raised = [jnp.exp(part - highest) for part in scores]
            summed = sum(jnp.sum(part, axis=0, keepdims=True) for part in raised)
            total = sum(
                down(v[a:b], part.astype(BF16)) for (a, b, _), part in zip(parts, raised)
            )
            outs.append(total / summed)
            logsum_ref[0, 0, head : head + 1, rows] = highest + jnp.log(summed)
        out_ref[block, 0] = join_heads(outs).T.astype(BF16)


def attention_back_kernel(
    scale, q_ref, k_ref, v_ref, grad_ref, logsum_ref, out_ref, grad_keys, grad_values
):
    blocks = q_ref.shape[0] * q_ref.shape[2] // QUERIES
    frames = q_ref.shape[2]
    k = k_ref[:, 0].reshape(-1, 2 * HD)
    v = v_ref[:, 0].reshape(-1, 2 * HD)

    def columns(kind):
        return pl.ds(kind * 2 * HD, 2 * HD)

    for block in range(blocks):
        rows = slice(block * QUERIES, (block + 1) * QUERIES)
        queries = both_heads((q_ref[block, 0].astype(F32) * scale).astype(BF16))
        grads = both_heads(grad_ref[block, 0])
        parts = key_parts(block)
        query_grads = []
        held = [[], []]
        for head in range(2):
            logsum = logsum_ref[0, 0, head : head + 1, rows]
            weights, weighted = [], []
            for a, b, diagonal in parts:
                weight = jnp.exp(masked_scores(k[a:b], queries[head], diagonal) - logsum)
                weights.append(weight)
                weighted.append(weight * across(v[a:b], grads[head]))
            inner = sum(jnp.sum(part, axis=0, keepdims=True) for part in weighted)
            changes = [
                (term - weight * inner).astype(BF16) for term, weight in zip(weighted, weights)
            ]
            query_grads.append(sum(down(k[a:b], part) for (a, b, _), part in zip(parts, changes)))
            held[head] = [(weight.astype(BF16), change) for weight, change in zip(weights, changes)]
        out_ref[block, 0, :, columns(0)] = (join_heads(query_grads).T * scale).astype(BF16)
        for j, (a, b, diagonal) in enumerate(parts):
            value_term = sum(
                jnp.dot(held[head][j][0], grads[head], preferred_element_type=F32)
                for head in range(2)
            )
            key_term = sum(
                jnp.dot(held[head][j][1], queries[head], preferred_element_type=F32)
                for head in range(2)
            )
            if diagonal:
                grad_values[a:b] = value_term
                grad_keys[a:b] = key_term
            else:
                grad_values[a:b] += value_term
                grad_keys[a:b] += key_term
    out_ref[:, 0, :, columns(1)] = grad_keys[...].reshape(-1, frames, 2 * HD).astype(BF16)
    out_ref[:, 0, :, columns(2)] = grad_values[...].reshape(-1, frames, 2 * HD).astype(BF16)


X_LAG = 2
CORE_LAG = 4


def forward_kernel(plan, weights, scale, *refs):
    inputs = refs[:weights]
    vector_in, hidden_in = refs[weights : weights + 2]
    refs = refs[weights + 2 :]
    outputs = refs[:weights]
    vector_out, normed_out, heads, logsum_out, context = refs[weights : weights + 5]
    (
        vector_land,
        vector,
        hidden,
        normed,
        weight_buf,
        product_buf,
        q_buf,
        k_buf,
        v_buf,
        context_buf,
        logsum_buf,
        z_send,
        z_recv,
        y_sem,
        x_sem,
        c_sem,
        own_sem,
        vector_sem,
        load_sem,
        product_send,
        product_recv,
        block_sem,
        context_sem,
        context_own,
    ) = refs[weights + 5 :]
    seq = lax.axis_index("seq")
    fsdp = lax.axis_index("fsdp")
    x, c = seq // 2, seq % 2
    z, y = fsdp // 2, fsdp % 2
    x_seq = 2 * (1 - x) + c
    c_seq = 2 * x + 1 - c
    neighbours = (x_seq, c_seq, 3 - seq)
    y_fsdp = 2 * z + 1 - y
    chunks = len(plan)
    clips, pairs = logsum_buf.shape[:2]
    frames = hidden.shape[0] // clips

    def at_z(k):
        return (seq, 2 * ((z + k) % 4) + y)

    barrier = pltpu.get_barrier_semaphore()
    partners = [(other, fsdp) for other in neighbours] + [(seq, (fsdp + k) % 8) for k in range(1, 8)]
    for partner in partners:
        pl.semaphore_signal(barrier, inc=1, device_id=partner, device_id_type=MESH)
    pl.semaphore_wait(barrier, len(partners))

    def remote(source, target, send, recv, device):
        return pltpu.make_async_remote_copy(
            src_ref=source,
            dst_ref=target,
            send_sem=send,
            recv_sem=recv,
            device_id=device,
            device_id_type=MESH,
        )

    def over(region, sems, device):
        return remote(region, region, sems.at[0], sems.at[1], device)

    sends = []

    def send(copy):
        copy.start()
        sends.append(copy)

    def vector_copy(k):
        return remote(
            vector_in,
            vector_land.at[fsdp],
            vector_sem.at[0, k],
            vector_sem.at[1, k],
            (seq, (fsdp + k) % 8),
        )

    def vector_arrival(k):
        region = vector_land.at[(fsdp + 8 - k) % 8]
        return over(region, vector_sem.at[:, k], (seq, (fsdp + k) % 8))

    own_vector = pltpu.make_async_copy(vector_in, vector_land.at[fsdp], vector_sem.at[0, 0])
    hidden_load = pltpu.make_async_copy(hidden_in, hidden, vector_sem.at[1, 0])
    normed_store = pltpu.make_async_copy(normed, normed_out, vector_sem.at[1, 0])
    vector_store = pltpu.make_async_copy(vector, vector_out, vector_sem.at[0, 0])

    def norm():
        own_vector.wait()
        for k in range(1, 8):
            vector_arrival(k).wait_recv()
        hidden_load.wait()
        vector[...] = sum(vector_land[f] for f in range(8))
        vector_store.start()

        @pl.loop(0, hidden.shape[0] // 32)
        def _(block):
            rows = pl.ds(pl.multiple_of(block * 32, 32), 32)
            value = hidden[rows, :].astype(F32)
            center = value - jnp.mean(value, axis=1, keepdims=True)
            inverse = lax.rsqrt(jnp.mean(center * center, axis=1, keepdims=True) + 1e-05)
            normed[rows, :] = (center * inverse * vector[0:1, :] + vector[1:2, :]).astype(BF16)

        normed_store.start()

    def part(entry):
        weight, block, column, width, split = entry
        first = 2 * c + x if split else 2 * c
        return weight, block, pl.ds(column, width), pl.ds(first, 1 if split else 2)

    def own_copy(i):
        weight, block, columns, _ = part(plan[i])
        both = pl.ds(2 * c, 2)
        return pltpu.make_async_copy(
            inputs[weight].at[block, both, :, columns],
            outputs[weight].at[z, y, block, both, :, columns],
            own_sem.at[i],
        )

    def start_z(i):
        weight, block, columns, mine = part(plan[i])
        source = inputs[weight].at[block, mine, :, columns]
        target = outputs[weight].at[z, y, block, mine, :, columns]
        for k in (1, 2, 3):
            send(remote(source, target, z_send.at[i, k - 1], z_recv.at[i, k - 1], at_z(k)))
        own_copy(i).start()

    def start_y(i):
        weight, block, columns, mine = part(plan[i])
        output = outputs[weight]
        for k in (1, 2, 3):
            region = output.at[(z + 4 - k) % 4, y, block, mine, :, columns]
            remote(region, region, z_send.at[i, k - 1], z_recv.at[i, k - 1], at_z(k)).wait_recv()
        own_copy(i).wait()
        region = output.at[:, y, block, mine, :, columns]
        send(over(region, y_sem.at[:, i], (seq, y_fsdp)))

    def x_copies(i, quarter):
        weight, block, columns, _ = part(plan[i])
        rest = (block, pl.ds(quarter, 1), slice(None), columns)
        regions = [outputs[weight].at[(slice(None), 1 - y) + rest]]
        regions += [outputs[weight].at[((z + k) % 4, y) + rest] for k in (1, 2, 3)]
        return [
            over(region, x_sem.at[:, i, j], (x_seq, fsdp)) for j, region in enumerate(regions)
        ]

    def start_x(i):
        weight, block, columns, mine = part(plan[i])
        output = outputs[weight]
        region = output.at[:, 1 - y, block, mine, :, columns]
        over(region, y_sem.at[:, i], (seq, y_fsdp)).wait_recv()
        if plan[i][4]:
            for copy in x_copies(i, 2 * c + x):
                send(copy)
        region = output.at[:, :, block, mine, :, columns]
        send(over(region, c_sem.at[:, i, 0], (c_seq, fsdp)))

    def start_core(i):
        if plan[i][4]:
            weight, block, columns, _ = part(plan[i])
            for copy in x_copies(i, 2 * c + 1 - x):
                copy.wait_recv()
            region = outputs[weight].at[:, :, block, pl.ds(2 * c + 1 - x, 1), :, columns]
            send(over(region, c_sem.at[:, i, 1], (c_seq, fsdp)))

    def finish(i):
        weight, block, columns, _ = part(plan[i])
        other = 2 * (1 - c)
        output = outputs[weight]
        if plan[i][4]:
            for j, quarter in ((0, other + x), (1, other + 1 - x)):
                region = output.at[:, :, block, pl.ds(quarter, 1), :, columns]
                over(region, c_sem.at[:, i, j], (c_seq, fsdp)).wait_recv()
        else:
            region = output.at[:, :, block, pl.ds(other, 2), :, columns]
            over(region, c_sem.at[:, i, 0], (c_seq, fsdp)).wait_recv()

    def weight_load(i):
        region = outputs[0].at[:, :, 0, :, :, pl.ds(384 * i, 384)]
        return pltpu.make_async_copy(region, weight_buf.at[i % 2], load_sem.at[i % 2])

    def product_copy(i):
        kind, group = i // 4, i % 4
        target = heads.at[seq, :, pl.ds(384 * kind, 384)]
        away = remote(
            product_buf.at[i % 2],
            target,
            product_send.at[i],
            product_recv.at[kind, seq],
            (group, fsdp),
        )
        here = pltpu.make_async_copy(product_buf.at[i % 2], target, product_send.at[i])
        return group, away, here

    def start_product(i):
        group, away, here = product_copy(i)

        @pl.when(seq != group)
        def _():
            away.start()

        @pl.when(seq == group)
        def _():
            here.start()

    def wait_product(i):
        group, away, here = product_copy(i)

        @pl.when(seq != group)
        def _():
            away.wait_send()

        @pl.when(seq == group)
        def _():
            here.wait()

    def project(i):
        weight_load(i).wait()
        if i >= 2:
            wait_product(i - 2)
        right = weight_buf[i % 2].reshape(-1, 384)

        @pl.loop(0, normed.shape[0] // 256)
        def _(block):
            rows = pl.ds(pl.multiple_of(block * 256, 256), 256)
            out = jnp.dot(normed[rows, :], right, preferred_element_type=F32)
            product_buf[i % 2, rows, :] = out.astype(BF16)

        start_product(i)

    def wait_heads():
        for i in (10, 11):
            wait_product(i)
        for kind in range(3):
            for other in neighbours:
                region = heads.at[other, :, pl.ds(384 * kind, 384)]
                remote(
                    region, region, product_send.at[0], product_recv.at[kind, other], (other, fsdp)
                ).wait_recv()

    def block_loads(step):
        clip, pair = step // pairs, step % pairs
        return [
            pltpu.make_async_copy(
                heads.at[:, pl.ds(clip * frames, frames), pl.ds(384 * kind + 128 * pair, 128)],
                buffer.at[step % 2, :, 0],
                block_sem.at[kind, step % 2],
            )
            for kind, buffer in enumerate((q_buf, k_buf, v_buf))
        ]

    def start_blocks(step):
        for copy in block_loads(step):
            copy.start()

    def context_region(step, group):
        clip, pair = step // pairs, step % pairs
        column = pl.multiple_of(group * 384 + pair * 128, 128)
        return context.at[pl.ds(clip * frames, frames), pl.ds(column, 128)]

    def context_copy(step, which):
        other = neighbours[which]
        return remote(
            context_buf.at[step % 2, other, 0],
            context_region(step, seq),
            context_sem.at[0, step, which],
            context_sem.at[1, step, which],
            (other, fsdp),
        )

    def context_here(step):
        return pltpu.make_async_copy(
            context_buf.at[step % 2, seq, 0], context_region(step, seq), context_own.at[step]
        )

    def context_sent(step):
        for which in range(3):
            context_copy(step, which).wait_send()
        context_here(step).wait()

    def attend(step):
        for copy in block_loads(step):
            copy.wait()
        if step + 1 < clips * pairs:
            start_blocks(step + 1)
        if step >= 2:
            context_sent(step - 2)
        slot = step % 2
        attention_kernel(
            scale,
            q_buf.at[slot],
            k_buf.at[slot],
            v_buf.at[slot],
            context_buf.at[slot],
            logsum_buf.at[step // pairs, step % pairs],
        )
        for which in range(3):
            context_copy(step, which).start()
        context_here(step).start()

    steps = clips * pairs
    projections = 12
    attention_start = projections + CORE_LAG + 5
    beside = {2: [norm]}
    for i in range(projections):
        beside.setdefault(i + CORE_LAG + 2, []).extend(
            [functools.partial(finish, i), lambda i=i: weight_load(i).start()]
        )
        beside.setdefault(i + CORE_LAG + 3, []).insert(0, functools.partial(project, i))
    beside.setdefault(attention_start, []).extend([wait_heads, lambda: start_blocks(0)])
    for step in range(steps):
        beside.setdefault(attention_start + 1 + 2 * step, []).append(functools.partial(attend, step))

    hidden_load.start()
    own_vector.start()
    for k in range(1, 8):
        send(vector_copy(k))
    ahead = 3
    for i in range(ahead):
        start_z(i)
    for t in range(chunks + CORE_LAG):
        if t + ahead < chunks:
            start_z(t + ahead)
        if t < chunks:
            start_y(t)
        if 0 <= t - X_LAG < chunks:
            start_x(t - X_LAG)
        if 0 <= t - CORE_LAG < chunks:
            start_core(t - CORE_LAG)
        for run in beside.pop(t, []):
            run()
    for i in range(projections, chunks):
        finish(i)
    for copy in sends:
        copy.wait_send()
    normed_store.wait()
    vector_store.wait()
    for step in (steps - 2, steps - 1):
        context_sent(step)
    for step in range(steps):
        for which in range(3):
            region = context_region(step, neighbours[which])
            over(region, context_sem.at[:, step, which], (neighbours[which], fsdp)).wait_recv()
    pltpu.sync_copy(logsum_buf, logsum_out)


def forward_plan(shapes):
    places = []
    for weight, (rows, columns) in enumerate(shapes):
        blocks = rows // 192
        for block in range(blocks):
            last = weight == len(shapes) - 1 and block == blocks - 1
            width = 384 if weight == 0 or last else 768
            places += [(weight, block, column, width) for column in range(0, columns, width)]
    return tuple(
        place + ((len(places) - 1 - i) * 3 % 5 >= 2,) for i, place in enumerate(places)
    )


def forward(shards, vectors, hidden, clips, scale):
    shapes = [shard.shape for shard in shards]
    plan = forward_plan(shapes)
    chunks, weights = len(plan), len(shards)
    rows, width = hidden.shape
    frames, group = rows // clips, width // 4
    pairs = group // (2 * HD)
    inputs = [shard.reshape(depth // 192, 4, 48, columns) for shard, (depth, columns) in zip(shards, shapes)]
    inputs += [vectors, hidden]
    out_shapes = [
        jax.ShapeDtypeStruct((4, 2, depth // 192, 4, 48, columns), BF16) for depth, columns in shapes
    ]
    logsum_shape = (clips, pairs, 1, 1, 2, 4 * frames)
    out_shapes += [
        jax.ShapeDtypeStruct(vectors.shape, F32),
        jax.ShapeDtypeStruct(hidden.shape, BF16),
        jax.ShapeDtypeStruct((4, rows, 3 * group), BF16),
        jax.ShapeDtypeStruct(logsum_shape, F32),
        jax.ShapeDtypeStruct(hidden.shape, BF16),
    ]
    anywhere = pl.BlockSpec(memory_space=pl.ANY)
    dma = pltpu.SemaphoreType.DMA
    pair_block = pltpu.VMEM((2, 4, 1, frames, 2 * HD), BF16)
    results = pl.pallas_call(
        functools.partial(forward_kernel, plan, weights, scale),
        out_shape=out_shapes,
        in_specs=[anywhere] * len(inputs),
        out_specs=[anywhere] * len(out_shapes),
        scratch_shapes=[
            pltpu.VMEM((8,) + vectors.shape, F32),
            pltpu.VMEM(vectors.shape, F32),
            pltpu.VMEM(hidden.shape, BF16),
            pltpu.VMEM(hidden.shape, BF16),
            pltpu.VMEM((2, 4, 2, 4, 48, 384), BF16),
            pltpu.VMEM((2, rows, 384), BF16),
            pair_block,
            pair_block,
            pair_block,
            pair_block,
            pltpu.VMEM(logsum_shape, F32),
            dma((chunks, 3)),
            dma((chunks, 3)),
            dma((2, chunks)),
            dma((2, chunks, 4)),
            dma((2, chunks, 2)),
            dma((chunks,)),
            dma((2, 8)),
            dma((2,)),
            dma((12,)),
            dma((3, 4)),
            dma((3, 2)),
            dma((2, clips * pairs, 3)),
            dma((clips * pairs,)),
        ],
        compiler_params=pltpu.CompilerParams(
            collective_id=1, has_side_effects=True, vmem_limit_bytes=60 << 20
        ),
        name="forward",
    )(*inputs)
    wholes = [
        result.reshape(8 * depth, columns) for result, (depth, columns) in zip(results, shapes)
    ]
    vector, normed, heads, logsum, context = results[weights:]
    return wholes, vector, normed, heads, logsum, context


def place_vectors(vectors):
    stacked = jnp.stack([vector.astype(F32) for vector in vectors])
    count, shard = stacked.shape
    whole = jnp.zeros((8, 8 * shard), F32)
    return lax.dynamic_update_slice(whole, stacked, (0, lax.axis_index("fsdp") * shard))


def text_weights(queries, keys):
    scores = across(keys, queries)
    raised = jnp.exp(scores - jnp.max(scores, axis=0, keepdims=True))
    return raised / jnp.sum(raised, axis=0, keepdims=True)


def pair_columns(pair):
    return slice(pair * 2 * HD, (pair + 1) * 2 * HD)


def text_attention_kernel(scale, q_ref, memory_ref, out_ref):
    pairs = q_ref.shape[1] // (2 * HD)
    for pair in range(pairs):
        queries = both_heads((q_ref[:, pair_columns(pair)].astype(F32) * scale).astype(BF16))
        k = memory_ref[:, pair_columns(pair)]
        v = memory_ref[:, pair_columns(pairs + pair)]
        outs = [down(v, text_weights(part, k).astype(BF16)) for part in queries]
        out_ref[:, pair_columns(pair)] = join_heads(outs).T.astype(BF16)


def head_rows(value):
    return jnp.concatenate(both_heads(value), 0)


def join_rows(value):
    rows = value.shape[1] // 2
    return join_heads((value[:, :rows], value[:, rows:])).T


def text_attention_back_kernel(scale, q_ref, memory_ref, grad_ref, q_out, memory_out):
    pairs = q_ref.shape[1] // (2 * HD)
    for pair in range(pairs):
        queries = head_rows((q_ref[:, pair_columns(pair)].astype(F32) * scale).astype(BF16))
        grads = head_rows(grad_ref[:, pair_columns(pair)])
        k = memory_ref[:, pair_columns(pair)]
        v = memory_ref[:, pair_columns(pairs + pair)]
        weights = text_weights(queries, k)
        weighted = weights * across(v, grads)
        inner = jnp.sum(weighted, axis=0, keepdims=True)
        change = (weighted - weights * inner).astype(BF16)
        key_grad = jnp.dot(change, queries, preferred_element_type=F32)
        value_grad = jnp.dot(weights.astype(BF16), grads, preferred_element_type=F32)
        q_out[:, pair_columns(pair)] = (join_rows(down(k, change)) * scale).astype(BF16)
        memory_out[:, pair_columns(pair)] = key_grad.astype(BF16)
        memory_out[:, pair_columns(pairs + pair)] = value_grad.astype(BF16)


def text_attention(clips, scale, queries, memory, grad=None):
    spec = lambda value: pl.BlockSpec(
        (value.shape[0] // clips, value.shape[1]), lambda clip: (clip, 0)
    )
    back = grad is not None
    operands = (queries, memory) + ((grad,) if back else ())
    results = (queries, memory) if back else (queries,)
    size = memory.shape[0] // clips * queries.size
    outs = pl.pallas_call(
        functools.partial(text_attention_back_kernel if back else text_attention_kernel, scale),
        grid=(clips,),
        out_shape=[jax.ShapeDtypeStruct(value.shape, BF16) for value in results],
        in_specs=[spec(value) for value in operands],
        out_specs=[spec(value) for value in results],
        compiler_params=pltpu.CompilerParams(vmem_limit_bytes=32 << 20),
        cost_estimate=pl.CostEstimate(
            flops=(20 if back else 8) * size,
            bytes_accessed=2 * sum(value.size for value in operands + results),
            transcendentals=size // HD,
        ),
        name="text_attention_back" if back else "text_attention",
    )(*operands)
    return outs if back else outs[0]


PIECE = (192, 384)
EARLY = 32
AFTER_LAG = 0
OVER_X = 1
STAGES = 7
SLOTS = 6


def sum_kernel(plan, weights, scale, *refs):
    chunks = len(plan)
    late = chunks - 3
    lefts, rights = refs[:weights], refs[weights : 2 * weights - 1]
    refs = refs[2 * weights - 1 :]
    regrouped, context_grad, logsum_in, projection, hidden_in, grad_in, gain_in, vector_in = refs[:8]
    outputs = refs[8 : 8 + weights]
    heads, hidden_out, vector_out = refs[8 + weights : 11 + weights]
    (
        mine,
        c_out,
        c_in,
        x_in,
        y_in,
        second_in,
        z_in,
        early_z_in,
        early_y_in,
        early_x_in,
        total,
        fx_in,
        fc_in,
        stage,
        left_buf,
        right_buf,
        weight_buf,
        normed_grad,
        hidden,
        grad,
        gain,
        q_buf,
        k_buf,
        v_buf,
        context_buf,
        logsum,
        heads_buf,
        key_grads,
        value_grads,
        vector,
        vector_got,
        vector_z,
        c_sem,
        x_sem,
        y_sem,
        second_x_sem,
        second_y_sem,
        z_sem,
        early_sem,
        fx_sem,
        fc_sem,
        stage_sem,
        load_sem,
        vector_sem,
        heads_sem,
        heads_own_sem,
        block_sem,
        own_sem,
    ) = refs[11 + weights :]
    rights = rights + (heads,)
    seq = lax.axis_index("seq")
    fsdp = lax.axis_index("fsdp")
    x, c = seq // 2, seq % 2
    z, y = fsdp // 2, fsdp % 2
    x_device = (2 * (1 - x) + c, fsdp)
    c_device = (2 * x + 1 - c, fsdp)
    far_device = (3 - seq, fsdp)
    y_device = (seq, 2 * z + 1 - y)

    def z_device(k):
        return (seq, 2 * ((z + k) % 4) + y)

    barrier = pltpu.get_barrier_semaphore()
    partners = [x_device, c_device, far_device, y_device] + [z_device(k) for k in (1, 2, 3)]
    for partner in partners:
        pl.semaphore_signal(barrier, inc=1, device_id=partner, device_id_type=MESH)
    pl.semaphore_wait(barrier, len(partners))

    def remote(source, target, sems, device):
        return pltpu.make_async_remote_copy(
            src_ref=source,
            dst_ref=target,
            send_sem=sems.at[0],
            recv_sem=sems.at[1],
            device_id=device,
            device_id_type=MESH,
        )

    def columns(block):
        return pl.ds(pl.multiple_of(block * 384, 128), 384)

    neighbours = (x_device, c_device, far_device)
    clips, pairs = logsum.shape[:2]
    frames = context_grad.shape[1] // clips
    steps = clips * pairs

    def block_loads(step):
        rows = pl.ds(pl.multiple_of(step // pairs * frames, frames), frames)
        first = step % pairs * 2 * HD
        places = [(regrouped, q_buf, 0), (regrouped, k_buf, 384), (regrouped, v_buf, 768)]
        places.append((context_grad, context_buf, 0))
        return [
            pltpu.make_async_copy(
                source.at[:, rows, pl.ds(pl.multiple_of(column + first, 128), 128)],
                buffer.at[:, 0],
                block_sem.at[j],
            )
            for j, (source, buffer, column) in enumerate(places)
        ]

    def heads_region(step, kind, group):
        rows = pl.ds(pl.multiple_of(step // pairs * frames, frames), frames)
        column = (kind * 4 + group) * 384 + step % pairs * 2 * HD
        return heads.at[rows, pl.ds(pl.multiple_of(column, 128), 128)]

    def heads_send(step, which, kind):
        other = neighbours[which]
        return remote(
            heads_buf.at[other[0], 0, :, pl.ds(kind * 128, 128)],
            heads_region(step, kind, seq),
            heads_sem.at[:, step, which, kind],
            other,
        )

    def heads_arrival(step, which, kind):
        region = heads_region(step, kind, neighbours[which][0])
        return remote(region, region, heads_sem.at[:, step, which, kind], neighbours[which])

    def heads_own(step, kind):
        return pltpu.make_async_copy(
            heads_buf.at[seq, 0, :, pl.ds(kind * 128, 128)],
            heads_region(step, kind, seq),
            heads_own_sem.at[step, kind],
        )

    logsum_load = pltpu.make_async_copy(logsum_in, logsum, block_sem.at[4])

    def attention_step(t):
        @pl.when(t == 0)
        def _():
            logsum_load.wait()

        @pl.when(jnp.logical_and(t >= 1, t <= steps))
        def _():
            for kind in range(3):
                heads_own(t - 1, kind).wait()
                for which in range(3):
                    heads_send(t - 1, which, kind).wait_send()

        @pl.when(t < steps)
        def _():
            for copy in block_loads(t):
                copy.wait()
            attention_back_kernel(
                scale,
                q_buf,
                k_buf,
                v_buf,
                context_buf,
                logsum.at[t // pairs, t % pairs],
                heads_buf,
                key_grads,
                value_grads,
            )
            for kind in range(3):
                for which in range(3):
                    heads_send(t, which, kind).start()
                heads_own(t, kind).start()

        @pl.when(t + 1 < steps)
        def _():
            for copy in block_loads(t + 1):
                copy.start()

    def whole(kind):
        return pltpu.make_async_copy(
            projection.at[:, pl.ds(kind * 1536, 1536)], weight_buf, own_sem.at[3]
        )

    operands = [
        pltpu.make_async_copy(hidden_in, hidden, own_sem.at[4]),
        pltpu.make_async_copy(grad_in, grad, own_sem.at[5]),
        pltpu.make_async_copy(gain_in, gain, own_sem.at[6]),
        pltpu.make_async_copy(vector_in, vector.at[0], own_sem.at[7]),
    ]

    def loads(j):
        weight, column = plan[j]
        slot = j % 2
        return [
            pltpu.make_async_copy(lefts[weight], left_buf.at[slot], load_sem.at[0, slot]),
            pltpu.make_async_copy(
                rights[weight].at[:, pl.ds(column, 1536)], right_buf.at[slot], load_sem.at[1, slot]
            ),
        ]

    def start_loads(i):
        for j in range(chunks):

            @pl.when(i == j)
            def _():
                if j >= late:
                    for step in range(steps):
                        for which in range(3):
                            heads_arrival(step, which, j - late).wait_recv()
                for copy in loads(j):
                    copy.start()

    def wait_loads(i):
        for j in range(chunks):

            @pl.when(i == j)
            def _():
                for copy in loads(j):
                    copy.wait()

    def multiply(i, half, target, slot):
        buffer = i % 2
        right = right_buf.at[buffer, :, pl.ds(pl.multiple_of(half * 768, 128), 768)]

        @pl.loop(0, 4)
        def _(zz):
            out = down(left_buf[buffer, :, columns(zz)], right[...]).astype(BF16)
            for q in range(2):
                for yy in range(2):
                    target[slot, q, zz, yy] = out[192 * yy : 192 * yy + 192, 384 * q : 384 * q + 384]

    def multiply_back(i):
        for kind in range(3):

            @pl.when(i == late + kind)
            def _():
                whole(kind).wait()

                @pl.loop(0, right_buf.shape[1] // 128)
                def _(block):
                    rows = pl.ds(pl.multiple_of(block * 128, 128), 128)
                    term = across(right_buf[i % 2, rows, :], weight_buf[...])
                    if kind:
                        normed_grad[rows, :] += term
                    else:
                        normed_grad[rows, :] = term

                if kind < 2:
                    whole(kind + 1).start()

    def norm_back():
        for copy in operands:
            copy.wait()

        def block(index, terms):
            rows = pl.ds(pl.multiple_of(index * 32, 32), 32)
            value = hidden[rows, :].astype(F32)
            center = value - jnp.mean(value, axis=1, keepdims=True)
            inverse = lax.rsqrt(jnp.mean(center * center, axis=1, keepdims=True) + 1e-05)
            normed = center * inverse
            change = normed_grad[rows, :]
            scaled = change * gain[0:1, :]
            first_mean = jnp.mean(scaled, axis=1, keepdims=True)
            second_mean = jnp.mean(scaled * normed, axis=1, keepdims=True)
            grad[rows, :] += inverse * (scaled - first_mean - normed * second_mean)
            gains, biases = terms
            return (
                gains + jnp.sum(change * normed, axis=0, keepdims=True),
                biases + jnp.sum(change, axis=0, keepdims=True),
            )

        zero = jnp.zeros((1, gain.shape[1]), F32)
        gains, biases = lax.fori_loop(0, hidden.shape[0] // 32, block, (zero, zero))
        vector[0, 0:1, :] = gains
        vector[0, 1:2, :] = biases

    def add_to(slot, q, zz, yy, rows, other):
        here = mine[slot, q, zz, yy, rows].astype(F32)
        mine[slot, q, zz, yy, rows] = (here + other.astype(F32)).astype(BF16)

    early_rows = pl.ds(0, EARLY)
    other_rows = pl.ds(EARLY, PIECE[0] - EARLY)

    def c_copy(i):
        return remote(c_out.at[i % 2], c_in.at[i % 2], c_sem.at[:, i % 2], c_device)

    def x_copy(i, count):
        region = pl.ds(0, count)
        return remote(
            mine.at[i % 5, 1 - x, region, :, other_rows],
            x_in.at[i % 4, region],
            x_sem.at[:, i % 4],
            x_device,
        )

    def y_copy(i, count):
        return remote(
            mine.at[i % 5, :, pl.ds(count, 4 - count), 1 - y, other_rows],
            y_in.at[i % 4, :, pl.ds(0, 4 - count)],
            y_sem.at[:, i % 4],
            y_device,
        )

    def second_y_copy(i, count):
        region = pl.ds(0, count)
        return remote(
            mine.at[i % 5, x, region, 1 - y, other_rows],
            second_in.at[i % 5, region],
            second_y_sem.at[:, i % 5],
            y_device,
        )

    def second_x_copy(i, count):
        region = pl.ds(count, 4 - count)
        return remote(
            mine.at[i % 5, 1 - x, region, y, other_rows],
            second_in.at[i % 5, region],
            second_x_sem.at[:, i % 5],
            x_device,
        )

    def z_copy(i, k):
        return remote(
            mine.at[i % 5, x, (z + k) % 4, y, other_rows],
            z_in.at[i % 4, k - 1],
            z_sem.at[:, i % 4, k - 1],
            z_device(k),
        )

    def early_z_copy(i, k):
        return remote(
            mine.at[i % 5, :, (z + k) % 4, :, early_rows],
            early_z_in.at[i % 4, k - 1],
            early_sem.at[:, i % 4, k - 1],
            z_device(k),
        )

    def early_y_copy(i):
        return remote(
            mine.at[i % 5, :, z, 1 - y, early_rows],
            early_y_in.at[i % 4],
            early_sem.at[:, i % 4, 3],
            y_device,
        )

    def early_x_copy(i):
        return remote(
            mine.at[i % 5, 1 - x, z, y, early_rows],
            early_x_in.at[i % 4],
            early_sem.at[:, i % 4, 4],
            x_device,
        )

    def fx_copy(i):
        slot = i % SLOTS
        return remote(total.at[slot], fx_in.at[slot], fx_sem.at[:, slot], x_device)

    def fc_copy(i, which):
        slot = i % SLOTS
        source = fx_in.at[slot] if which else total.at[slot]
        return remote(source, fc_in.at[slot, which], fc_sem.at[:, slot, which], c_device)

    def begin(i):
        wait_loads(i)

        @pl.when(i >= 2)
        def _():
            c_copy(i - 2).wait_send()

        multiply(i, 1 - c, c_out, i % 2)
        c_copy(i).start()
        multiply(i, c, mine, i % 5)
        multiply_back(i)

    def first(i):
        c_copy(i).wait_recv()

        def add_c(q, zz, yy, rows):
            add_to(i % 5, q, zz, yy, rows, c_in[i % 2, q, zz, yy, rows])

        for k in (1, 2, 3):
            for q in range(2):
                for yy in range(2):
                    add_c(q, (z + k) % 4, yy, early_rows)
            early_z_copy(i, k).start()

        def run(i, count):
            @pl.loop(0, count)
            def _(zz):
                for yy in range(2):
                    add_c(1 - x, zz, yy, other_rows)

            x_copy(i, count).start()

            @pl.loop(count, 4)
            def _(zz):
                for q in range(2):
                    add_c(q, zz, 1 - y, other_rows)

            y_copy(i, count).start()

            @pl.loop(0, count)
            def _(zz):
                for yy in range(2):
                    add_c(x, zz, yy, other_rows)

            @pl.loop(count, 4)
            def _(zz):
                for q in range(2):
                    add_c(q, zz, y, other_rows)

        run(i, OVER_X)
        for q in range(2):
            for yy in range(2):
                add_c(q, z, yy, early_rows)

    def second(i):
        own, slot = i % 5, i % 4

        def run(i, count):
            def add_x(yy):
                @pl.loop(0, count)
                def _(zz):
                    add_to(own, x, zz, yy, other_rows, x_in[slot, zz, yy])

            def add_y(q):
                @pl.loop(count, 4)
                def _(zz):
                    add_to(own, q, zz, y, other_rows, y_in[slot, q, zz - count])

            x_copy(i, count).wait()
            add_x(1 - y)
            second_y_copy(i, count).start()
            y_copy(i, count).wait()
            add_y(1 - x)
            second_x_copy(i, count).start()
            add_x(y)
            add_y(x)

        run(i, OVER_X)
        for k in (1, 2, 3):
            early_z_copy(i, k).wait()

        def add_early(q, yy):
            others = [early_z_in[slot, k, q, yy].astype(F32) for k in range(3)]
            add_to(own, q, z, yy, early_rows, others[0] + others[1] + others[2])

        for q in range(2):
            add_early(q, 1 - y)
        early_y_copy(i).start()
        for q in range(2):
            add_early(q, y)

    def third(i):
        own, slot = i % 5, i % 4

        def run(i, count):
            second_y_copy(i, count).wait()
            second_x_copy(i, count).wait()

        run(i, OVER_X)
        for k in (1, 2, 3):
            zz = (z + k) % 4
            add_to(own, x, zz, y, other_rows, second_in[own, zz])
            z_copy(i, k).start()
        early_y_copy(i).wait()
        add_to(own, 1 - x, z, y, early_rows, early_y_in[slot, 1 - x])
        early_x_copy(i).start()
        add_to(own, x, z, y, early_rows, early_y_in[slot, x])

    def fourth(i):
        own, slot = i % 5, i % 4
        result = mine[own, x, z, y, other_rows].astype(F32) + second_in[own, z].astype(F32)
        for k in (1, 2, 3):
            z_copy(i, k).wait()
            result = result + z_in[slot, k - 1].astype(F32)
        total[i % SLOTS, other_rows] = result.astype(BF16)
        early_x_copy(i).wait()
        result = mine[own, x, z, y, early_rows].astype(F32) + early_x_in[slot].astype(F32)
        total[i % SLOTS, early_rows] = result.astype(BF16)
        fx_copy(i).start()
        fc_copy(i, 0).start()

    def fifth(i):
        fx_copy(i).wait()
        fc_copy(i, 1).start()

    def store(j):
        weight, column = plan[j]
        return pltpu.make_async_copy(
            stage.at[j % 2], outputs[weight].at[:, pl.ds(column, 1536)], stage_sem.at[j % 2]
        )

    def sixth(i):
        slot = i % SLOTS
        for j in range(2, chunks):

            @pl.when(i == j)
            def _():
                store(j - 2).wait()

        def put(quarter, value):
            stage[i % 2, :, columns(quarter)] = value

        fc_copy(i, 0).wait()
        fc_copy(i, 1).wait()
        put(2 * c + x, total[slot])
        put(2 * c + 1 - x, fx_in[slot])
        put(2 * (1 - c) + x, fc_in[slot, 0])
        put(2 * (1 - c) + 1 - x, fc_in[slot, 1])
        for j in range(chunks):

            @pl.when(i == j)
            def _():
                store(j).start()

    def vector_copy(leg):
        device = (c_device, x_device, y_device)[leg]
        return remote(vector.at[leg], vector_got.at[leg], vector_sem.at[:, leg], device)

    def vector_z_copy(k):
        return remote(vector_z.at[z], vector_z.at[z], vector_sem.at[:, 2 + k], z_device(k))

    def vector_arrival(k):
        source = (z + 4 - k) % 4
        return remote(vector_z.at[source], vector_z.at[source], vector_sem.at[:, 2 + k], z_device(k))

    hidden_store = pltpu.make_async_copy(grad, hidden_out, own_sem.at[5])

    def vector_step(step):
        @pl.when(step == 0)
        def _():
            norm_back()
            hidden_store.start()
            vector_copy(0).start()

        for leg in range(3):

            @pl.when(step == leg + 1)
            def _():
                vector_copy(leg).wait()
                both = vector[leg] + vector_got[leg]
                if leg < 2:
                    vector[leg + 1] = both
                    vector_copy(leg + 1).start()
                else:
                    vector_z[z] = both
                    for k in (1, 2, 3):
                        vector_z_copy(k).start()

        @pl.when(step == 4)
        def _():
            for k in (1, 2, 3):
                vector_z_copy(k).wait_send()
                vector_arrival(k).wait_recv()
            vector[0] = vector_z[0] + vector_z[1] + vector_z[2] + vector_z[3]
            pltpu.sync_copy(vector.at[0], vector_out)

    start_loads(0)
    for copy in block_loads(0):
        copy.start()
    logsum_load.start()
    whole(0).start()
    for copy in operands:
        copy.start()

    @pl.loop(0, chunks + STAGES - 1)
    def _(t):
        @pl.when(t + 1 < chunks)
        def _():
            start_loads(t + 1)

        for lag, run in ((1, first), (0, begin), (2, second), (3, third), (4, fourth), (5, fifth), (6, sixth)):
            i = t - lag

            @pl.when(jnp.logical_and(i >= 0, i < chunks))
            def _():
                run(i)

            if lag == AFTER_LAG:
                attention_step(t)

        vector_step(t - chunks)

    for j in (chunks - 2, chunks - 1):
        c_copy(j).wait_send()
        store(j).wait()
    hidden_store.wait()


def sum_products(
    lefts, rights, regrouped, context_grad, logsum, projection, hidden, grad, gain, vectors, scale
):
    weights = len(lefts)
    widths = [right.shape[1] for right in rights] + [projection.shape[1]]
    plan = [
        (weight, column)
        for weight, width in enumerate(widths)
        for column in range(0, width, 1536)
    ]
    depth, width = hidden.shape
    out_shapes = [
        jax.ShapeDtypeStruct((left.shape[1] // 8, columns), BF16)
        for left, columns in zip(lefts, widths)
    ]
    out_shapes += [
        jax.ShapeDtypeStruct((depth, widths[-1]), BF16),
        jax.ShapeDtypeStruct(grad.shape, F32),
        jax.ShapeDtypeStruct(vectors.shape, F32),
    ]
    inputs = (
        *lefts,
        *rights,
        regrouped,
        context_grad,
        logsum,
        projection,
        hidden,
        grad,
        gain,
        vectors,
    )
    clips, pairs, *_, length = logsum.shape
    frames = depth // clips
    pair_block = pltpu.VMEM((4, 1, frames, 2 * HD), BF16)
    pair_grads = pltpu.VMEM((length, 2 * HD), F32)
    anywhere = pl.BlockSpec(memory_space=pl.ANY)
    dma = pltpu.SemaphoreType.DMA
    rest = PIECE[0] - EARLY
    block = lambda *lead, rows=PIECE[0]: pltpu.VMEM(lead + (rows, PIECE[1]), BF16)
    results = pl.pallas_call(
        functools.partial(sum_kernel, tuple(plan), weights, scale),
        out_shape=out_shapes,
        in_specs=[anywhere] * len(inputs),
        out_specs=[anywhere] * len(out_shapes),
        scratch_shapes=[
            block(5, 2, 4, 2),
            block(2, 2, 4, 2),
            block(2, 2, 4, 2),
            block(4, OVER_X, 2, rows=rest),
            block(4, 2, 4 - OVER_X, rows=rest),
            block(5, 4, rows=rest),
            block(4, 3, rows=rest),
            block(4, 3, 2, 2, rows=EARLY),
            block(4, 2, rows=EARLY),
            block(4, rows=EARLY),
            block(SLOTS),
            block(SLOTS),
            block(SLOTS, 2),
            pltpu.VMEM((2, 192, 1536), BF16),
            pltpu.VMEM((2, depth, 1536), BF16),
            pltpu.VMEM((2, depth, 1536), BF16),
            pltpu.VMEM((width, 1536), BF16),
            pltpu.VMEM((depth, width), F32),
            pltpu.VMEM((depth, width), BF16),
            pltpu.VMEM((depth, width), F32),
            pltpu.VMEM(gain.shape, F32),
            pair_block,
            pair_block,
            pair_block,
            pair_block,
            pltpu.VMEM(logsum.shape, F32),
            pltpu.VMEM((4, 1, frames, 3 * 2 * HD), BF16),
            pair_grads,
            pair_grads,
            pltpu.VMEM((3,) + vectors.shape, F32),
            pltpu.VMEM((3,) + vectors.shape, F32),
            pltpu.VMEM((4,) + vectors.shape, F32),
            dma((2, 2)),
            dma((2, 4)),
            dma((2, 4)),
            dma((2, 5)),
            dma((2, 5)),
            dma((2, 4, 3)),
            dma((2, 4, 5)),
            dma((2, SLOTS)),
            dma((2, SLOTS, 2)),
            dma((2,)),
            dma((2, 2)),
            dma((2, 6)),
            dma((2, clips * pairs, 3, 3)),
            dma((clips * pairs, 3)),
            dma((5,)),
            dma((8,)),
        ],
        compiler_params=pltpu.CompilerParams(
            collective_id=3, has_side_effects=True, vmem_limit_bytes=60 << 20
        ),
        name="sum_products",
    )(*inputs)
    return results[:weights], results[-2], results[-1]


def on_blocks(
    hidden_states,
    text_states,
    self_gain,
    self_bias,
    query_key_value,
    self_output,
    cross_gain,
    cross_bias,
    cross_query,
    cross_memory,
    cross_output,
    final_gain,
    final_bias,
    expand_weight,
    contract_weight,
    output_cotangent,
):
    clips, frames, width = hidden_states.shape
    rows = clips * frames
    groups = lax.axis_size("seq")
    fsdp_count = lax.axis_size("fsdp")
    scale = HD ** (-0.5)
    entries = rows * groups * fsdp_count * width
    group_width = width // groups

    gains = (self_gain, self_bias, cross_gain, cross_bias, final_gain, final_bias)
    wholes, gains, normed_one, regrouped, logsum, context = forward(
        (
            query_key_value,
            self_output,
            cross_query,
            cross_memory,
            cross_output,
            expand_weight,
            contract_weight,
        ),
        place_vectors(gains),
        hidden_states.reshape(rows, width),
        clips,
        scale,
    )
    (
        qkv_whole,
        self_output_whole,
        cross_query_whole,
        cross_memory_whole,
        cross_output_whole,
        expand_whole,
        contract_whole,
    ) = wholes
    hidden = hidden_states.reshape(rows, width).astype(F32)
    attended = product(context, self_output_whole)
    first = hidden + attended
    normed_two, norm_two_back = jax.vjp(layer_norm, first, gains[2], gains[3])
    normed_two = normed_two.astype(BF16)
    cross_q = product(normed_two, cross_query_whole).astype(BF16)
    text_rows = text_states.reshape(clips * TEXT, width)
    memory = product(text_rows, cross_memory_whole).astype(BF16)
    cross_context = text_attention(clips, scale, cross_q, memory)
    crossed = product(cross_context, cross_output_whole)
    second = first + crossed
    normed_three, norm_three_back = jax.vjp(layer_norm, second, gains[4], gains[5])
    normed_three = normed_three.astype(BF16)
    preact = product(normed_three, expand_whole)
    below = 0.5 + 0.5 * lax.erf(preact * 0.5**0.5)
    density = jnp.exp(preact * preact * -0.5) * (0.5 / jnp.pi) ** 0.5
    activated = (preact * below).astype(BF16)
    slope = (below + preact * density).astype(BF16)
    upstream = output_cotangent.reshape(rows, width).astype(F32)
    grad_mixed = output_cotangent.reshape(rows, width)
    contract_term = product_left(activated, grad_mixed).astype(BF16)
    grad_mixed, contract_term, contract_whole = lax.optimization_barrier(
        (grad_mixed, contract_term, contract_whole)
    )
    contract_part = lax.psum_scatter(
        contract_term, ("fsdp", "seq"), scatter_dimension=0, tiled=True
    )
    grad_activated = product_right(grad_mixed, contract_whole)
    grad_preact = (grad_activated * slope.astype(F32)).astype(BF16)
    grad_normed_three = product_right(grad_preact, expand_whole)
    grad_second, final_gain_term, final_bias_term = norm_three_back(grad_normed_three)
    grad_second = upstream + grad_second
    grad_crossed = grad_second.astype(BF16)
    grad_cross_context = product_right(grad_crossed, cross_output_whole).astype(BF16)
    grad_cross_q, grad_memory = text_attention(clips, scale, cross_q, memory, grad_cross_context)
    grad_normed_two = product_right(grad_cross_q, cross_query_whole)
    grad_first, cross_gain_term, cross_bias_term = norm_two_back(grad_normed_two)
    grad_first = grad_second + grad_first
    grad_attended = grad_first.astype(BF16)
    grad_context = product_right(grad_attended, self_output_whole).astype(BF16)
    grad_context = grad_context.reshape(rows, groups, group_width).transpose(1, 0, 2)
    grad_context, activated = lax.optimization_barrier((grad_context, activated))
    grad_heads = lax.all_to_all(grad_context, "seq", split_axis=0, concat_axis=0, tiled=True)
    mixed = product(activated, contract_whole)
    output = second + mixed
    squares = jnp.stack(
        [
            jnp.sum(output * output),
            jnp.sum(attended * attended),
            jnp.sum(crossed * crossed),
            jnp.sum(mixed * mixed),
        ]
    )
    output = output.astype(BF16)
    zeros = jnp.zeros_like(cross_gain_term)
    terms = jnp.stack(
        [
            zeros,
            zeros,
            cross_gain_term,
            cross_bias_term,
            final_gain_term,
            final_bias_term,
            jnp.pad(squares, (0, width - 4)),
            zeros,
        ]
    )
    deep = lambda value: jnp.pad(value, ((0, rows - value.shape[0]), (0, 0)))
    text_operands = (deep(text_rows), deep(grad_memory))
    grad_heads, output, terms, text_operands = lax.optimization_barrier(
        (grad_heads, output, terms, text_operands)
    )
    gradients, grad_hidden, totals = sum_products(
        [normed_three, cross_context, normed_two, text_operands[0], context, normed_one],
        [grad_preact, grad_crossed, grad_cross_q, text_operands[1], grad_attended],
        regrouped,
        grad_heads,
        logsum,
        qkv_whole,
        hidden_states.reshape(rows, width),
        grad_first,
        jnp.broadcast_to(gains[0], (8, width)),
        terms,
        scale,
    )
    gradients, contract_part = lax.optimization_barrier((gradients, contract_part))
    contract_gradient = lax.all_gather(contract_part, "seq", axis=0, tiled=True)
    gradients = [gradient.astype(F32) for gradient in gradients]
    contract_gradient = contract_gradient.astype(F32)
    layer_rms = jnp.sqrt(totals[6, :4] / entries)
    shard = width // fsdp_count
    vector_gradients = lax.dynamic_slice_in_dim(
        totals, lax.axis_index("fsdp") * shard, shard, 1
    )
    return (
        output.reshape(clips, frames, width),
        grad_hidden.reshape(clips, frames, width),
        vector_gradients[0],
        vector_gradients[1],
        gradients[5],
        gradients[4],
        vector_gradients[2],
        vector_gradients[3],
        gradients[2],
        gradients[3],
        gradients[1],
        vector_gradients[4],
        vector_gradients[5],
        gradients[0],
        contract_gradient,
        layer_rms,
    )


def solution(mesh):
    shape = dict(mesh.shape)
    blocks = shape["seq"] == 4 and shape["fsdp"] == 8
    return jax.shard_map(
        on_blocks if blocks else on_any_mesh,
        mesh=mesh,
        in_specs=(
            P("fsdp", "seq", None),
            P("fsdp", None, None),
            P("fsdp"),
            P("fsdp"),
            P("fsdp", None),
            P("fsdp", None),
            P("fsdp"),
            P("fsdp"),
            P("fsdp", None),
            P("fsdp", None),
            P("fsdp", None),
            P("fsdp"),
            P("fsdp"),
            P("fsdp", None),
            P("fsdp", None),
            P("fsdp", "seq", None),
        ),
        out_specs=(
            P("fsdp", "seq", None),
            P("fsdp", "seq", None),
            P("fsdp"),
            P("fsdp"),
            P("fsdp", None),
            P("fsdp", None),
            P("fsdp"),
            P("fsdp"),
            P("fsdp", None),
            P("fsdp", None),
            P("fsdp", None),
            P("fsdp"),
            P("fsdp"),
            P("fsdp", None),
            P("fsdp", None),
            P(),
        ),
        check_vma=False,
    )
```

```python
import functools

import jax
import jax.numpy as jnp
from jax import lax
from jax.experimental import pallas as pl
from jax.experimental.pallas import tpu as pltpu
from jax.sharding import PartitionSpec as P

H = 24
HD = 64
TEXT = 64

NEGATIVE = -1e30
BF16 = jnp.bfloat16
F32 = jnp.float32
MESH = pl.DeviceIdType.MESH


def layer_norm(values, gain, offset):
    center = values - jnp.mean(values, axis=-1, keepdims=True)
    spread = jnp.mean(center * center, axis=-1, keepdims=True)
    return center * lax.rsqrt(spread + 1e-05) * gain + offset


def gelu_exact(values):
    return jax.nn.gelu(values, approximate=False)


def product(left, right):
    return jnp.dot(left, right, preferred_element_type=jnp.float32)


def product_left(left, right):
    return lax.dot_general(
        left, right, (((0,), (0,)), ((), ())), preferred_element_type=jnp.float32
    )


def product_right(left, right):
    return lax.dot_general(
        left, right, (((1,), (1,)), ((), ())), preferred_element_type=jnp.float32
    )


def causal_forward(queries, keys, values, rows_block, scale):
    clips, length, heads_local, head_width = queries.shape
    count = length // rows_block
    columns = jnp.arange(length, dtype=jnp.int32)

    def one_block(start):
        block = lax.dynamic_slice_in_dim(queries, start, rows_block, 1)
        scores = (
            jnp.einsum("cqhd,ckhd->chqk", block, keys, preferred_element_type=jnp.float32) * scale
        )
        positions = start + jnp.arange(rows_block, dtype=jnp.int32)
        allowed = columns[None, :] <= positions[:, None]
        scores = jnp.where(allowed, scores, NEGATIVE)
        highest = jnp.max(scores, axis=-1, keepdims=True)
        raised = jnp.exp(scores - highest)
        summed = jnp.sum(raised, axis=-1, keepdims=True)
        weights = (raised / summed).astype(jnp.bfloat16)
        result = jnp.einsum("chqk,ckhd->cqhd", weights, values, preferred_element_type=jnp.float32)
        return (result.astype(jnp.bfloat16), (highest + jnp.log(summed))[..., 0])

    starts = jnp.arange(count, dtype=jnp.int32) * rows_block
    results, logsum = lax.map(one_block, starts)
    results = jnp.moveaxis(results, 0, 1).reshape(clips, length, heads_local * head_width)
    return (results, logsum)


def causal_backward(queries, keys, values, logsum, grad_heads, rows_block, scale):
    clips, length, heads_local, head_width = queries.shape
    count = length // rows_block
    columns = jnp.arange(length, dtype=jnp.int32)
    starts = jnp.arange(count, dtype=jnp.int32) * rows_block

    def one_block(carry, inputs):
        grad_keys, grad_values = carry
        start, block_logsum = inputs
        block = lax.dynamic_slice_in_dim(queries, start, rows_block, 1)
        block_grad = lax.dynamic_slice_in_dim(grad_heads, start, rows_block, 1)
        scores = (
            jnp.einsum("cqhd,ckhd->chqk", block, keys, preferred_element_type=jnp.float32) * scale
        )
        positions = start + jnp.arange(rows_block, dtype=jnp.int32)
        allowed = columns[None, :] <= positions[:, None]
        scores = jnp.where(allowed, scores, NEGATIVE)
        weights = jnp.exp(scores - block_logsum[..., None])
        rounded = weights.astype(jnp.bfloat16)
        grad_weights = jnp.einsum(
            "cqhd,ckhd->chqk", block_grad, values, preferred_element_type=jnp.float32
        )
        inner = jnp.sum(weights * grad_weights, axis=-1, keepdims=True)
        grad_scores = (weights * (grad_weights - inner)).astype(jnp.bfloat16)
        grad_query = (
            jnp.einsum("chqk,ckhd->cqhd", grad_scores, keys, preferred_element_type=jnp.float32)
            * scale
        )
        grad_keys = (
            grad_keys
            + jnp.einsum("chqk,cqhd->ckhd", grad_scores, block, preferred_element_type=jnp.float32)
            * scale
        )
        grad_values = grad_values + jnp.einsum(
            "chqk,cqhd->ckhd", rounded, block_grad, preferred_element_type=jnp.float32
        )
        return ((grad_keys, grad_values), grad_query.astype(jnp.bfloat16))

    zeros = jnp.zeros(queries.shape, jnp.float32)
    (grad_keys, grad_values), grad_queries = lax.scan(one_block, (zeros, zeros), (starts, logsum))
    local_width = heads_local * head_width
    grad_queries = jnp.moveaxis(grad_queries, 0, 1).reshape(clips, length, local_width)
    grad_keys = grad_keys.astype(jnp.bfloat16).reshape(clips, length, local_width)
    grad_values = grad_values.astype(jnp.bfloat16).reshape(clips, length, local_width)
    return jnp.stack([grad_queries, grad_keys, grad_values], axis=2)


def on_any_mesh(
    hidden_states,
    text_states,
    self_gain,
    self_bias,
    query_key_value,
    self_output,
    cross_gain,
    cross_bias,
    cross_query,
    cross_memory,
    cross_output,
    final_gain,
    final_bias,
    expand_weight,
    contract_weight,
    output_cotangent,
):
    clips, frames, width = hidden_states.shape
    rows = clips * frames
    groups = lax.axis_size("seq")
    fsdp_count = lax.axis_size("fsdp")
    heads_local = H // groups
    length = frames * groups
    rows_block = min(512, length)
    scale = HD ** (-0.5)
    entries = rows * groups * fsdp_count * width
    self_set = (
        lax.all_gather(self_gain, "fsdp", axis=0, tiled=True),
        lax.all_gather(self_bias, "fsdp", axis=0, tiled=True),
        lax.all_gather(query_key_value, "fsdp", axis=0, tiled=True),
        lax.all_gather(self_output, "fsdp", axis=0, tiled=True),
    )
    hidden = hidden_states.reshape(rows, width).astype(jnp.float32)
    normed_one, norm_one_back = jax.vjp(
        layer_norm, hidden, self_set[0].astype(jnp.float32), self_set[1].astype(jnp.float32)
    )
    normed_one = normed_one.astype(jnp.bfloat16)
    projected = (
        product(normed_one, self_set[2]).astype(jnp.bfloat16).reshape(clips, frames, 3, width)
    )
    regrouped = lax.all_to_all(projected, "seq", split_axis=3, concat_axis=1, tiled=True)
    regrouped = regrouped.reshape(clips, length, 3, heads_local, HD)
    queries = regrouped[:, :, 0]
    keys = regrouped[:, :, 1]
    values = regrouped[:, :, 2]
    context_heads, logsum = causal_forward(queries, keys, values, rows_block, scale)
    context = lax.all_to_all(context_heads, "seq", split_axis=1, concat_axis=2, tiled=True).reshape(
        rows, width
    )
    attended = product(context, self_set[3])
    first = hidden + attended
    rest_set = (
        lax.all_gather(cross_gain, "fsdp", axis=0, tiled=True),
        lax.all_gather(cross_bias, "fsdp", axis=0, tiled=True),
        lax.all_gather(cross_query, "fsdp", axis=0, tiled=True),
        lax.all_gather(cross_memory, "fsdp", axis=0, tiled=True),
        lax.all_gather(cross_output, "fsdp", axis=0, tiled=True),
        lax.all_gather(final_gain, "fsdp", axis=0, tiled=True),
        lax.all_gather(final_bias, "fsdp", axis=0, tiled=True),
        lax.all_gather(expand_weight, "fsdp", axis=0, tiled=True),
        lax.all_gather(contract_weight, "fsdp", axis=0, tiled=True),
    )
    normed_two, norm_two_back = jax.vjp(
        layer_norm, first, rest_set[0].astype(jnp.float32), rest_set[1].astype(jnp.float32)
    )
    normed_two = normed_two.astype(jnp.bfloat16)
    cross_q = product(normed_two, rest_set[2]).astype(jnp.bfloat16).reshape(clips, frames, H, HD)
    text_rows = text_states.reshape(clips * TEXT, width)
    memory = product(text_rows, rest_set[3]).astype(jnp.bfloat16).reshape(clips, TEXT, 2, H, HD)
    cross_keys = memory[:, :, 0]
    cross_values = memory[:, :, 1]
    cross_scores = (
        jnp.einsum("cqhd,ckhd->chqk", cross_q, cross_keys, preferred_element_type=jnp.float32)
        * scale
    )
    highest = jnp.max(cross_scores, axis=-1, keepdims=True)
    raised = jnp.exp(cross_scores - highest)
    cross_weights = raised / jnp.sum(raised, axis=-1, keepdims=True)
    cross_rounded = cross_weights.astype(jnp.bfloat16)
    cross_context = jnp.einsum(
        "chqk,ckhd->cqhd", cross_rounded, cross_values, preferred_element_type=jnp.float32
    )
    cross_context = cross_context.astype(jnp.bfloat16).reshape(rows, width)
    crossed = product(cross_context, rest_set[4])
    second = first + crossed
    normed_three, norm_three_back = jax.vjp(
        layer_norm, second, rest_set[5].astype(jnp.float32), rest_set[6].astype(jnp.float32)
    )
    normed_three = normed_three.astype(jnp.bfloat16)
    preact = product(normed_three, rest_set[7])
    activated, gelu_back = jax.vjp(gelu_exact, preact)
    activated = activated.astype(jnp.bfloat16)
    mixed = product(activated, rest_set[8])
    output = second + mixed
    squares = jnp.stack(
        [
            jnp.sum(output * output),
            jnp.sum(attended * attended),
            jnp.sum(crossed * crossed),
            jnp.sum(mixed * mixed),
        ]
    )
    square_totals = lax.psum(squares, ("seq", "fsdp"))
    back_rest = (
        lax.all_gather(cross_gain, "fsdp", axis=0, tiled=True),
        lax.all_gather(cross_bias, "fsdp", axis=0, tiled=True),
        lax.all_gather(cross_query, "fsdp", axis=0, tiled=True),
        lax.all_gather(cross_memory, "fsdp", axis=0, tiled=True),
        lax.all_gather(cross_output, "fsdp", axis=0, tiled=True),
        lax.all_gather(final_gain, "fsdp", axis=0, tiled=True),
        lax.all_gather(final_bias, "fsdp", axis=0, tiled=True),
        lax.all_gather(expand_weight, "fsdp", axis=0, tiled=True),
        lax.all_gather(contract_weight, "fsdp", axis=0, tiled=True),
    )
    upstream = output_cotangent.reshape(rows, width).astype(jnp.float32)
    grad_mixed = upstream.astype(jnp.bfloat16)
    contract_term = product_left(activated, grad_mixed)
    grad_activated = product_right(grad_mixed, back_rest[8])
    grad_preact = gelu_back(grad_activated)[0].astype(jnp.bfloat16)
    expand_term = product_left(normed_three, grad_preact)
    grad_normed_three = product_right(grad_preact, back_rest[7])
    grad_second, final_gain_term, final_bias_term = norm_three_back(grad_normed_three)
    grad_second = upstream + grad_second
    grad_crossed = grad_second.astype(jnp.bfloat16)
    cross_output_term = product_left(cross_context, grad_crossed)
    grad_cross_context = (
        product_right(grad_crossed, back_rest[4]).astype(jnp.bfloat16).reshape(clips, frames, H, HD)
    )
    grad_cross_weights = jnp.einsum(
        "cqhd,ckhd->chqk", grad_cross_context, cross_values, preferred_element_type=jnp.float32
    )
    cross_inner = jnp.sum(cross_weights * grad_cross_weights, axis=-1, keepdims=True)
    grad_cross_scores = (cross_weights * (grad_cross_weights - cross_inner)).astype(jnp.bfloat16)
    grad_cross_q = (
        jnp.einsum(
            "chqk,ckhd->cqhd", grad_cross_scores, cross_keys, preferred_element_type=jnp.float32
        )
        * scale
    )
    grad_cross_q = grad_cross_q.astype(jnp.bfloat16).reshape(rows, width)
    grad_cross_keys = (
        jnp.einsum(
            "chqk,cqhd->ckhd", grad_cross_scores, cross_q, preferred_element_type=jnp.float32
        )
        * scale
    )
    grad_cross_values = jnp.einsum(
        "chqk,cqhd->ckhd", cross_rounded, grad_cross_context, preferred_element_type=jnp.float32
    )
    grad_memory = jnp.stack([grad_cross_keys, grad_cross_values], axis=2).reshape(
        clips * TEXT, 2 * width
    )
    memory_term = lax.dot_general(
        text_rows.astype(jnp.float32),
        grad_memory,
        (((0,), (0,)), ((), ())),
        precision=lax.Precision.HIGHEST,
        preferred_element_type=jnp.float32,
    )
    query_term = product_left(normed_two, grad_cross_q)
    grad_normed_two = product_right(grad_cross_q, back_rest[2])
    grad_first, cross_gain_term, cross_bias_term = norm_two_back(grad_normed_two)
    grad_first = grad_second + grad_first
    rest_sums = (
        lax.psum_scatter(
            cross_gain_term.astype(jnp.bfloat16), "fsdp", scatter_dimension=0, tiled=True
        ).astype(jnp.float32),
        lax.psum_scatter(
            cross_bias_term.astype(jnp.bfloat16), "fsdp", scatter_dimension=0, tiled=True
        ).astype(jnp.float32),
        lax.psum_scatter(
            query_term.astype(jnp.bfloat16), "fsdp", scatter_dimension=0, tiled=True
        ).astype(jnp.float32),
        lax.psum_scatter(
            memory_term.astype(jnp.bfloat16), "fsdp", scatter_dimension=0, tiled=True
        ).astype(jnp.float32),
        lax.psum_scatter(
            cross_output_term.astype(jnp.bfloat16), "fsdp", scatter_dimension=0, tiled=True
        ).astype(jnp.float32),
        lax.psum_scatter(
            final_gain_term.astype(jnp.bfloat16), "fsdp", scatter_dimension=0, tiled=True
        ).astype(jnp.float32),
        lax.psum_scatter(
            final_bias_term.astype(jnp.bfloat16), "fsdp", scatter_dimension=0, tiled=True
        ).astype(jnp.float32),
        lax.psum_scatter(
            expand_term.astype(jnp.bfloat16), "fsdp", scatter_dimension=0, tiled=True
        ).astype(jnp.float32),
        lax.psum_scatter(
            contract_term.astype(jnp.bfloat16), "fsdp", scatter_dimension=0, tiled=True
        ).astype(jnp.float32),
    )
    back_self = (
        lax.all_gather(self_gain, "fsdp", axis=0, tiled=True),
        lax.all_gather(self_bias, "fsdp", axis=0, tiled=True),
        lax.all_gather(query_key_value, "fsdp", axis=0, tiled=True),
        lax.all_gather(self_output, "fsdp", axis=0, tiled=True),
    )
    grad_attended = grad_first.astype(jnp.bfloat16)
    self_output_term = product_left(context, grad_attended)
    grad_context = (
        product_right(grad_attended, back_self[3])
        .astype(jnp.bfloat16)
        .reshape(clips, frames, width)
    )
    grad_heads = lax.all_to_all(grad_context, "seq", split_axis=2, concat_axis=1, tiled=True)
    grad_heads = grad_heads.reshape(clips, length, heads_local, HD)
    grad_regrouped = causal_backward(queries, keys, values, logsum, grad_heads, rows_block, scale)
    grad_projected = lax.all_to_all(
        grad_regrouped, "seq", split_axis=1, concat_axis=3, tiled=True
    ).reshape(rows, 3 * width)
    qkv_term = product_left(normed_one, grad_projected)
    grad_normed_one = product_right(grad_projected, back_self[2])
    grad_hidden, gain_one_term, bias_one_term = norm_one_back(grad_normed_one)
    grad_hidden = grad_first + grad_hidden
    self_sums = (
        lax.psum_scatter(
            gain_one_term.astype(jnp.bfloat16), "fsdp", scatter_dimension=0, tiled=True
        ).astype(jnp.float32),
        lax.psum_scatter(
            bias_one_term.astype(jnp.bfloat16), "fsdp", scatter_dimension=0, tiled=True
        ).astype(jnp.float32),
        lax.psum_scatter(
            qkv_term.astype(jnp.bfloat16), "fsdp", scatter_dimension=0, tiled=True
        ).astype(jnp.float32),
        lax.psum_scatter(
            self_output_term.astype(jnp.bfloat16), "fsdp", scatter_dimension=0, tiled=True
        ).astype(jnp.float32),
    )
    finals = (
        lax.psum(self_sums[0].astype(jnp.bfloat16), "seq").astype(jnp.float32),
        lax.psum(self_sums[1].astype(jnp.bfloat16), "seq").astype(jnp.float32),
        lax.psum(self_sums[2].astype(jnp.bfloat16), "seq").astype(jnp.float32),
        lax.psum(self_sums[3].astype(jnp.bfloat16), "seq").astype(jnp.float32),
        lax.psum(rest_sums[0].astype(jnp.bfloat16), "seq").astype(jnp.float32),
        lax.psum(rest_sums[1].astype(jnp.bfloat16), "seq").astype(jnp.float32),
        lax.psum(rest_sums[2].astype(jnp.bfloat16), "seq").astype(jnp.float32),
        lax.psum(rest_sums[3].astype(jnp.bfloat16), "seq").astype(jnp.float32),
        lax.psum(rest_sums[4].astype(jnp.bfloat16), "seq").astype(jnp.float32),
        lax.psum(rest_sums[5].astype(jnp.bfloat16), "seq").astype(jnp.float32),
        lax.psum(rest_sums[6].astype(jnp.bfloat16), "seq").astype(jnp.float32),
        lax.psum(rest_sums[7].astype(jnp.bfloat16), "seq").astype(jnp.float32),
        lax.psum(rest_sums[8].astype(jnp.bfloat16), "seq").astype(jnp.float32),
    )
    layer_rms = jnp.sqrt(square_totals / entries)
    return (
        output.astype(jnp.bfloat16).reshape(clips, frames, width),
        grad_hidden.reshape(clips, frames, width),
        finals[0],
        finals[1],
        finals[2],
        finals[3],
        finals[4],
        finals[5],
        finals[6],
        finals[7],
        finals[8],
        finals[9],
        finals[10],
        finals[11],
        finals[12],
        layer_rms,
    )


QUERIES = 256


def both_heads(value):
    lane = lax.broadcasted_iota(jnp.int32, value.shape, 1)
    zero = jnp.zeros_like(value)
    return jnp.where(lane < HD, value, zero), jnp.where(lane < HD, zero, value)


def across(left, right):
    return lax.dot_general(left, right, (((1,), (1,)), ((), ())), preferred_element_type=F32)


def down(left, right):
    return lax.dot_general(left, right, (((0,), (0,)), ((), ())), preferred_element_type=F32)


def join_heads(pair):
    row = lax.broadcasted_iota(jnp.int32, pair[0].shape, 0)
    return jnp.where(row < HD, pair[0], pair[1])


def key_parts(block):
    return ([(0, block * QUERIES, False)] if block else []) + [
        (block * QUERIES, (block + 1) * QUERIES, True)
    ]


def masked_scores(keys, queries, diagonal):
    scores = across(keys, queries)
    if diagonal:
        key = lax.broadcasted_iota(jnp.int32, scores.shape, 0)
        query = lax.broadcasted_iota(jnp.int32, scores.shape, 1)
        scores = jnp.where(key <= query, scores, NEGATIVE)
    return scores


def attention_kernel(scale, q_ref, k_ref, v_ref, out_ref, logsum_ref):
    blocks = q_ref.shape[0] * q_ref.shape[2] // QUERIES
    k = k_ref[:, 0].reshape(-1, 2 * HD)
    v = v_ref[:, 0].reshape(-1, 2 * HD)
    for block in range(blocks):
        rows = slice(block * QUERIES, (block + 1) * QUERIES)
        queries = both_heads((q_ref[block, 0].astype(F32) * scale).astype(BF16))
        outs = []
        for head in range(2):
            parts = key_parts(block)
            scores = [masked_scores(k[a:b], queries[head], diagonal) for a, b, diagonal in parts]
            highest = functools.reduce(
                jnp.maximum, [jnp.max(part, axis=0, keepdims=True) for part in scores]
            )
            raised = [jnp.exp(part - highest) for part in scores]
            summed = sum(jnp.sum(part, axis=0, keepdims=True) for part in raised)
            total = sum(
                down(v[a:b], part.astype(BF16)) for (a, b, _), part in zip(parts, raised)
            )
            outs.append(total / summed)
            logsum_ref[0, 0, head : head + 1, rows] = highest + jnp.log(summed)
        out_ref[block, 0] = join_heads(outs).T.astype(BF16)


def attention_back_kernel(
    scale, q_ref, k_ref, v_ref, grad_ref, logsum_ref, out_ref, grad_keys, grad_values
):
    blocks = q_ref.shape[0] * q_ref.shape[2] // QUERIES
    frames = q_ref.shape[2]
    k = k_ref[:, 0].reshape(-1, 2 * HD)
    v = v_ref[:, 0].reshape(-1, 2 * HD)

    def columns(kind):
        return pl.ds(kind * 2 * HD, 2 * HD)

    for block in range(blocks):
        rows = slice(block * QUERIES, (block + 1) * QUERIES)
        queries = both_heads((q_ref[block, 0].astype(F32) * scale).astype(BF16))
        grads = both_heads(grad_ref[block, 0])
        parts = key_parts(block)
        query_grads = []
        held = [[], []]
        for head in range(2):
            logsum = logsum_ref[0, 0, head : head + 1, rows]
            weights, weighted = [], []
            for a, b, diagonal in parts:
                weight = jnp.exp(masked_scores(k[a:b], queries[head], diagonal) - logsum)
                weights.append(weight)
                weighted.append(weight * across(v[a:b], grads[head]))
            inner = sum(jnp.sum(part, axis=0, keepdims=True) for part in weighted)
            changes = [
                (term - weight * inner).astype(BF16) for term, weight in zip(weighted, weights)
            ]
            query_grads.append(sum(down(k[a:b], part) for (a, b, _), part in zip(parts, changes)))
            held[head] = [(weight.astype(BF16), change) for weight, change in zip(weights, changes)]
        out_ref[block, 0, :, columns(0)] = (join_heads(query_grads).T * scale).astype(BF16)
        for j, (a, b, diagonal) in enumerate(parts):
            value_term = sum(
                jnp.dot(held[head][j][0], grads[head], preferred_element_type=F32)
                for head in range(2)
            )
            key_term = sum(
                jnp.dot(held[head][j][1], queries[head], preferred_element_type=F32)
                for head in range(2)
            )
            if diagonal:
                grad_values[a:b] = value_term
                grad_keys[a:b] = key_term
            else:
                grad_values[a:b] += value_term
                grad_keys[a:b] += key_term
    out_ref[:, 0, :, columns(1)] = grad_keys[...].reshape(-1, frames, 2 * HD).astype(BF16)
    out_ref[:, 0, :, columns(2)] = grad_values[...].reshape(-1, frames, 2 * HD).astype(BF16)


X_LAG = 2
CORE_LAG = 4


def forward_kernel(plan, weights, scale, *refs):
    inputs = refs[:weights]
    vector_in, hidden_in = refs[weights : weights + 2]
    refs = refs[weights + 2 :]
    outputs = refs[:weights]
    vector_out, normed_out, heads, logsum_out, context = refs[weights : weights + 5]
    (
        vector_land,
        vector,
        hidden,
        normed,
        weight_buf,
        product_buf,
        q_buf,
        k_buf,
        v_buf,
        context_buf,
        logsum_buf,
        z_send,
        z_recv,
        y_sem,
        x_sem,
        c_sem,
        own_sem,
        vector_sem,
        load_sem,
        product_send,
        product_recv,
        block_sem,
        context_sem,
        context_own,
    ) = refs[weights + 5 :]
    seq = lax.axis_index("seq")
    fsdp = lax.axis_index("fsdp")
    x, c = seq // 2, seq % 2
    z, y = fsdp // 2, fsdp % 2
    x_seq = 2 * (1 - x) + c
    c_seq = 2 * x + 1 - c
    neighbours = (x_seq, c_seq, 3 - seq)
    y_fsdp = 2 * z + 1 - y
    chunks = len(plan)
    clips, pairs = logsum_buf.shape[:2]
    frames = hidden.shape[0] // clips

    def at_z(k):
        return (seq, 2 * ((z + k) % 4) + y)

    barrier = pltpu.get_barrier_semaphore()
    partners = [(other, fsdp) for other in neighbours] + [(seq, (fsdp + k) % 8) for k in range(1, 8)]
    for partner in partners:
        pl.semaphore_signal(barrier, inc=1, device_id=partner, device_id_type=MESH)
    pl.semaphore_wait(barrier, len(partners))

    def remote(source, target, send, recv, device):
        return pltpu.make_async_remote_copy(
            src_ref=source,
            dst_ref=target,
            send_sem=send,
            recv_sem=recv,
            device_id=device,
            device_id_type=MESH,
        )

    def over(region, sems, device):
        return remote(region, region, sems.at[0], sems.at[1], device)

    sends = []

    def send(copy):
        copy.start()
        sends.append(copy)

    def vector_copy(k):
        return remote(
            vector_in,
            vector_land.at[fsdp],
            vector_sem.at[0, k],
            vector_sem.at[1, k],
            (seq, (fsdp + k) % 8),
        )

    def vector_arrival(k):
        region = vector_land.at[(fsdp + 8 - k) % 8]
        return over(region, vector_sem.at[:, k], (seq, (fsdp + k) % 8))

    own_vector = pltpu.make_async_copy(vector_in, vector_land.at[fsdp], vector_sem.at[0, 0])
    hidden_load = pltpu.make_async_copy(hidden_in, hidden, vector_sem.at[1, 0])
    normed_store = pltpu.make_async_copy(normed, normed_out, vector_sem.at[1, 0])
    vector_store = pltpu.make_async_copy(vector, vector_out, vector_sem.at[0, 0])

    def norm():
        own_vector.wait()
        for k in range(1, 8):
            vector_arrival(k).wait_recv()
        hidden_load.wait()
        vector[...] = sum(vector_land[f] for f in range(8))
        vector_store.start()

        @pl.loop(0, hidden.shape[0] // 32)
        def _(block):
            rows = pl.ds(pl.multiple_of(block * 32, 32), 32)
            value = hidden[rows, :].astype(F32)
            center = value - jnp.mean(value, axis=1, keepdims=True)
            inverse = lax.rsqrt(jnp.mean(center * center, axis=1, keepdims=True) + 1e-05)
            normed[rows, :] = (center * inverse * vector[0:1, :] + vector[1:2, :]).astype(BF16)

        normed_store.start()

    def part(entry):
        weight, block, column, width, split = entry
        first = 2 * c + x if split else 2 * c
        return weight, block, pl.ds(column, width), pl.ds(first, 1 if split else 2)

    def own_copy(i):
        weight, block, columns, _ = part(plan[i])
        both = pl.ds(2 * c, 2)
        return pltpu.make_async_copy(
            inputs[weight].at[block, both, :, columns],
            outputs[weight].at[z, y, block, both, :, columns],
            own_sem.at[i],
        )

    def start_z(i):
        weight, block, columns, mine = part(plan[i])
        source = inputs[weight].at[block, mine, :, columns]
        target = outputs[weight].at[z, y, block, mine, :, columns]
        for k in (1, 2, 3):
            send(remote(source, target, z_send.at[i, k - 1], z_recv.at[i, k - 1], at_z(k)))
        own_copy(i).start()

    def start_y(i):
        weight, block, columns, mine = part(plan[i])
        output = outputs[weight]
        for k in (1, 2, 3):
            region = output.at[(z + 4 - k) % 4, y, block, mine, :, columns]
            remote(region, region, z_send.at[i, k - 1], z_recv.at[i, k - 1], at_z(k)).wait_recv()
        own_copy(i).wait()
        region = output.at[:, y, block, mine, :, columns]
        send(over(region, y_sem.at[:, i], (seq, y_fsdp)))

    def x_copies(i, quarter):
        weight, block, columns, _ = part(plan[i])
        rest = (block, pl.ds(quarter, 1), slice(None), columns)
        regions = [outputs[weight].at[(slice(None), 1 - y) + rest]]
        regions += [outputs[weight].at[((z + k) % 4, y) + rest] for k in (1, 2, 3)]
        return [
            over(region, x_sem.at[:, i, j], (x_seq, fsdp)) for j, region in enumerate(regions)
        ]

    def start_x(i):
        weight, block, columns, mine = part(plan[i])
        output = outputs[weight]
        region = output.at[:, 1 - y, block, mine, :, columns]
        over(region, y_sem.at[:, i], (seq, y_fsdp)).wait_recv()
        if plan[i][4]:
            for copy in x_copies(i, 2 * c + x):
                send(copy)
        region = output.at[:, :, block, mine, :, columns]
        send(over(region, c_sem.at[:, i, 0], (c_seq, fsdp)))

    def start_core(i):
        if plan[i][4]:
            weight, block, columns, _ = part(plan[i])
            for copy in x_copies(i, 2 * c + 1 - x):
                copy.wait_recv()
            region = outputs[weight].at[:, :, block, pl.ds(2 * c + 1 - x, 1), :, columns]
            send(over(region, c_sem.at[:, i, 1], (c_seq, fsdp)))

    def finish(i):
        weight, block, columns, _ = part(plan[i])
        other = 2 * (1 - c)
        output = outputs[weight]
        if plan[i][4]:
            for j, quarter in ((0, other + x), (1, other + 1 - x)):
                region = output.at[:, :, block, pl.ds(quarter, 1), :, columns]
                over(region, c_sem.at[:, i, j], (c_seq, fsdp)).wait_recv()
        else:
            region = output.at[:, :, block, pl.ds(other, 2), :, columns]
            over(region, c_sem.at[:, i, 0], (c_seq, fsdp)).wait_recv()

    def weight_load(i):
        region = outputs[0].at[:, :, 0, :, :, pl.ds(384 * i, 384)]
        return pltpu.make_async_copy(region, weight_buf.at[i % 2], load_sem.at[i % 2])

    def product_copy(i):
        kind, group = i // 4, i % 4
        target = heads.at[seq, :, pl.ds(384 * kind, 384)]
        away = remote(
            product_buf.at[i % 2],
            target,
            product_send.at[i],
            product_recv.at[kind, seq],
            (group, fsdp),
        )
        here = pltpu.make_async_copy(product_buf.at[i % 2], target, product_send.at[i])
        return group, away, here

    def start_product(i):
        group, away, here = product_copy(i)

        @pl.when(seq != group)
        def _():
            away.start()

        @pl.when(seq == group)
        def _():
            here.start()

    def wait_product(i):
        group, away, here = product_copy(i)

        @pl.when(seq != group)
        def _():
            away.wait_send()

        @pl.when(seq == group)
        def _():
            here.wait()

    def project(i):
        weight_load(i).wait()
        if i >= 2:
            wait_product(i - 2)
        right = weight_buf[i % 2].reshape(-1, 384)

        @pl.loop(0, normed.shape[0] // 256)
        def _(block):
            rows = pl.ds(pl.multiple_of(block * 256, 256), 256)
            out = jnp.dot(normed[rows, :], right, preferred_element_type=F32)
            product_buf[i % 2, rows, :] = out.astype(BF16)

        start_product(i)

    def wait_heads():
        for i in (10, 11):
            wait_product(i)
        for kind in range(3):
            for other in neighbours:
                region = heads.at[other, :, pl.ds(384 * kind, 384)]
                remote(
                    region, region, product_send.at[0], product_recv.at[kind, other], (other, fsdp)
                ).wait_recv()

    def block_loads(step):
        clip, pair = step // pairs, step % pairs
        return [
            pltpu.make_async_copy(
                heads.at[:, pl.ds(clip * frames, frames), pl.ds(384 * kind + 128 * pair, 128)],
                buffer.at[step % 2, :, 0],
                block_sem.at[kind, step % 2],
            )
            for kind, buffer in enumerate((q_buf, k_buf, v_buf))
        ]

    def start_blocks(step):
        for copy in block_loads(step):
            copy.start()

    def context_region(step, group):
        clip, pair = step // pairs, step % pairs
        column = pl.multiple_of(group * 384 + pair * 128, 128)
        return context.at[pl.ds(clip * frames, frames), pl.ds(column, 128)]

    def context_copy(step, which):
        other = neighbours[which]
        return remote(
            context_buf.at[step % 2, other, 0],
            context_region(step, seq),
            context_sem.at[0, step, which],
            context_sem.at[1, step, which],
            (other, fsdp),
        )

    def context_here(step):
        return pltpu.make_async_copy(
            context_buf.at[step % 2, seq, 0], context_region(step, seq), context_own.at[step]
        )

    def context_sent(step):
        for which in range(3):
            context_copy(step, which).wait_send()
        context_here(step).wait()

    def attend(step):
        for copy in block_loads(step):
            copy.wait()
        if step + 1 < clips * pairs:
            start_blocks(step + 1)
        if step >= 2:
            context_sent(step - 2)
        slot = step % 2
        attention_kernel(
            scale,
            q_buf.at[slot],
            k_buf.at[slot],
            v_buf.at[slot],
            context_buf.at[slot],
            logsum_buf.at[step // pairs, step % pairs],
        )
        for which in range(3):
            context_copy(step, which).start()
        context_here(step).start()

    steps = clips * pairs
    projections = 12
    attention_start = projections + CORE_LAG + 5
    beside = {2: [norm]}
    for i in range(projections):
        beside.setdefault(i + CORE_LAG + 2, []).extend(
            [functools.partial(finish, i), lambda i=i: weight_load(i).start()]
        )
        beside.setdefault(i + CORE_LAG + 3, []).insert(0, functools.partial(project, i))
    beside.setdefault(attention_start, []).extend([wait_heads, lambda: start_blocks(0)])
    for step in range(steps):
        beside.setdefault(attention_start + 1 + 2 * step, []).append(functools.partial(attend, step))

    hidden_load.start()
    own_vector.start()
    for k in range(1, 8):
        send(vector_copy(k))
    ahead = 3
    for i in range(ahead):
        start_z(i)
    for t in range(chunks + CORE_LAG):
        if t + ahead < chunks:
            start_z(t + ahead)
        if t < chunks:
            start_y(t)
        if 0 <= t - X_LAG < chunks:
            start_x(t - X_LAG)
        if 0 <= t - CORE_LAG < chunks:
            start_core(t - CORE_LAG)
        for run in beside.pop(t, []):
            run()
    for i in range(projections, chunks):
        finish(i)
    for copy in sends:
        copy.wait_send()
    normed_store.wait()
    vector_store.wait()
    for step in (steps - 2, steps - 1):
        context_sent(step)
    for step in range(steps):
        for which in range(3):
            region = context_region(step, neighbours[which])
            over(region, context_sem.at[:, step, which], (neighbours[which], fsdp)).wait_recv()
    pltpu.sync_copy(logsum_buf, logsum_out)


def forward_plan(shapes):
    places = []
    for weight, (rows, columns) in enumerate(shapes):
        blocks = rows // 192
        for block in range(blocks):
            last = weight == len(shapes) - 1 and block == blocks - 1
            width = 384 if weight == 0 or last else 768
            places += [(weight, block, column, width) for column in range(0, columns, width)]
    return tuple(
        place + ((len(places) - 1 - i) * 2 % 5 >= 2,) for i, place in enumerate(places)
    )


def forward(shards, vectors, hidden, clips, scale):
    shapes = [shard.shape for shard in shards]
    plan = forward_plan(shapes)
    chunks, weights = len(plan), len(shards)
    rows, width = hidden.shape
    frames, group = rows // clips, width // 4
    pairs = group // (2 * HD)
    inputs = [shard.reshape(depth // 192, 4, 48, columns) for shard, (depth, columns) in zip(shards, shapes)]
    inputs += [vectors, hidden]
    out_shapes = [
        jax.ShapeDtypeStruct((4, 2, depth // 192, 4, 48, columns), BF16) for depth, columns in shapes
    ]
    logsum_shape = (clips, pairs, 1, 1, 2, 4 * frames)
    out_shapes += [
        jax.ShapeDtypeStruct(vectors.shape, F32),
        jax.ShapeDtypeStruct(hidden.shape, BF16),
        jax.ShapeDtypeStruct((4, rows, 3 * group), BF16),
        jax.ShapeDtypeStruct(logsum_shape, F32),
        jax.ShapeDtypeStruct(hidden.shape, BF16),
    ]
    anywhere = pl.BlockSpec(memory_space=pl.ANY)
    dma = pltpu.SemaphoreType.DMA
    pair_block = pltpu.VMEM((2, 4, 1, frames, 2 * HD), BF16)
    results = pl.pallas_call(
        functools.partial(forward_kernel, plan, weights, scale),
        out_shape=out_shapes,
        in_specs=[anywhere] * len(inputs),
        out_specs=[anywhere] * len(out_shapes),
        scratch_shapes=[
            pltpu.VMEM((8,) + vectors.shape, F32),
            pltpu.VMEM(vectors.shape, F32),
            pltpu.VMEM(hidden.shape, BF16),
            pltpu.VMEM(hidden.shape, BF16),
            pltpu.VMEM((2, 4, 2, 4, 48, 384), BF16),
            pltpu.VMEM((2, rows, 384), BF16),
            pair_block,
            pair_block,
            pair_block,
            pair_block,
            pltpu.VMEM(logsum_shape, F32),
            dma((chunks, 3)),
            dma((chunks, 3)),
            dma((2, chunks)),
            dma((2, chunks, 4)),
            dma((2, chunks, 2)),
            dma((chunks,)),
            dma((2, 8)),
            dma((2,)),
            dma((12,)),
            dma((3, 4)),
            dma((3, 2)),
            dma((2, clips * pairs, 3)),
            dma((clips * pairs,)),
        ],
        compiler_params=pltpu.CompilerParams(
            collective_id=1, has_side_effects=True, vmem_limit_bytes=60 << 20
        ),
        name="forward",
    )(*inputs)
    wholes = [
        result.reshape(8 * depth, columns) for result, (depth, columns) in zip(results, shapes)
    ]
    vector, normed, heads, logsum, context = results[weights:]
    return wholes, vector, normed, heads, logsum, context


def place_vectors(vectors):
    stacked = jnp.stack([vector.astype(F32) for vector in vectors])
    count, shard = stacked.shape
    whole = jnp.zeros((8, 8 * shard), F32)
    return lax.dynamic_update_slice(whole, stacked, (0, lax.axis_index("fsdp") * shard))


def text_weights(queries, keys):
    scores = across(keys, queries)
    raised = jnp.exp(scores - jnp.max(scores, axis=0, keepdims=True))
    return raised / jnp.sum(raised, axis=0, keepdims=True)


def pair_columns(pair):
    return slice(pair * 2 * HD, (pair + 1) * 2 * HD)


def text_attention_kernel(scale, q_ref, memory_ref, out_ref):
    pairs = q_ref.shape[1] // (2 * HD)
    for pair in range(pairs):
        queries = both_heads((q_ref[:, pair_columns(pair)].astype(F32) * scale).astype(BF16))
        k = memory_ref[:, pair_columns(pair)]
        v = memory_ref[:, pair_columns(pairs + pair)]
        outs = [down(v, text_weights(part, k).astype(BF16)) for part in queries]
        out_ref[:, pair_columns(pair)] = join_heads(outs).T.astype(BF16)


def head_rows(value):
    return jnp.concatenate(both_heads(value), 0)


def join_rows(value):
    rows = value.shape[1] // 2
    return join_heads((value[:, :rows], value[:, rows:])).T


def text_attention_back_kernel(scale, q_ref, memory_ref, grad_ref, q_out, memory_out):
    pairs = q_ref.shape[1] // (2 * HD)
    for pair in range(pairs):
        queries = head_rows((q_ref[:, pair_columns(pair)].astype(F32) * scale).astype(BF16))
        grads = head_rows(grad_ref[:, pair_columns(pair)])
        k = memory_ref[:, pair_columns(pair)]
        v = memory_ref[:, pair_columns(pairs + pair)]
        weights = text_weights(queries, k)
        weighted = weights * across(v, grads)
        inner = jnp.sum(weighted, axis=0, keepdims=True)
        change = (weighted - weights * inner).astype(BF16)
        key_grad = jnp.dot(change, queries, preferred_element_type=F32)
        value_grad = jnp.dot(weights.astype(BF16), grads, preferred_element_type=F32)
        q_out[:, pair_columns(pair)] = (join_rows(down(k, change)) * scale).astype(BF16)
        memory_out[:, pair_columns(pair)] = key_grad.astype(BF16)
        memory_out[:, pair_columns(pairs + pair)] = value_grad.astype(BF16)


def text_attention(clips, scale, queries, memory, grad=None):
    spec = lambda value: pl.BlockSpec(
        (value.shape[0] // clips, value.shape[1]), lambda clip: (clip, 0)
    )
    back = grad is not None
    operands = (queries, memory) + ((grad,) if back else ())
    results = (queries, memory) if back else (queries,)
    size = memory.shape[0] // clips * queries.size
    outs = pl.pallas_call(
        functools.partial(text_attention_back_kernel if back else text_attention_kernel, scale),
        grid=(clips,),
        out_shape=[jax.ShapeDtypeStruct(value.shape, BF16) for value in results],
        in_specs=[spec(value) for value in operands],
        out_specs=[spec(value) for value in results],
        compiler_params=pltpu.CompilerParams(vmem_limit_bytes=32 << 20),
        cost_estimate=pl.CostEstimate(
            flops=(20 if back else 8) * size,
            bytes_accessed=2 * sum(value.size for value in operands + results),
            transcendentals=size // HD,
        ),
        name="text_attention_back" if back else "text_attention",
    )(*operands)
    return outs if back else outs[0]


PIECE = (192, 384)
EARLY = 32
AFTER_LAG = 0
OVER_X = 1
STAGES = 7
SLOTS = 6


def sum_kernel(plan, weights, scale, *refs):
    chunks = len(plan)
    late = chunks - 3
    lefts, rights = refs[:weights], refs[weights : 2 * weights - 1]
    refs = refs[2 * weights - 1 :]
    regrouped, context_grad, logsum_in, projection, hidden_in, grad_in, gain_in, vector_in = refs[:8]
    outputs = refs[8 : 8 + weights]
    heads, hidden_out, vector_out = refs[8 + weights : 11 + weights]
    (
        mine,
        c_out,
        c_in,
        x_in,
        y_in,
        second_in,
        z_in,
        early_z_in,
        early_y_in,
        early_x_in,
        total,
        fx_in,
        fc_in,
        stage,
        left_buf,
        right_buf,
        weight_buf,
        normed_grad,
        hidden,
        grad,
        gain,
        q_buf,
        k_buf,
        v_buf,
        context_buf,
        logsum,
        heads_buf,
        key_grads,
        value_grads,
        vector,
        vector_got,
        vector_z,
        c_sem,
        x_sem,
        y_sem,
        second_x_sem,
        second_y_sem,
        z_sem,
        early_sem,
        fx_sem,
        fc_sem,
        stage_sem,
        load_sem,
        vector_sem,
        heads_sem,
        heads_own_sem,
        block_sem,
        own_sem,
    ) = refs[11 + weights :]
    rights = rights + (heads,)
    seq = lax.axis_index("seq")
    fsdp = lax.axis_index("fsdp")
    x, c = seq // 2, seq % 2
    z, y = fsdp // 2, fsdp % 2
    x_device = (2 * (1 - x) + c, fsdp)
    c_device = (2 * x + 1 - c, fsdp)
    far_device = (3 - seq, fsdp)
    y_device = (seq, 2 * z + 1 - y)

    def z_device(k):
        return (seq, 2 * ((z + k) % 4) + y)

    barrier = pltpu.get_barrier_semaphore()
    partners = [x_device, c_device, far_device, y_device] + [z_device(k) for k in (1, 2, 3)]
    for partner in partners:
        pl.semaphore_signal(barrier, inc=1, device_id=partner, device_id_type=MESH)
    pl.semaphore_wait(barrier, len(partners))

    def remote(source, target, sems, device):
        return pltpu.make_async_remote_copy(
            src_ref=source,
            dst_ref=target,
            send_sem=sems.at[0],
            recv_sem=sems.at[1],
            device_id=device,
            device_id_type=MESH,
        )

    def columns(block):
        return pl.ds(pl.multiple_of(block * 384, 128), 384)

    neighbours = (x_device, c_device, far_device)
    clips, pairs = logsum.shape[:2]
    frames = context_grad.shape[1] // clips
    steps = clips * pairs

    def block_loads(step):
        rows = pl.ds(pl.multiple_of(step // pairs * frames, frames), frames)
        first = step % pairs * 2 * HD
        places = [(regrouped, q_buf, 0), (regrouped, k_buf, 384), (regrouped, v_buf, 768)]
        places.append((context_grad, context_buf, 0))
        return [
            pltpu.make_async_copy(
                source.at[:, rows, pl.ds(pl.multiple_of(column + first, 128), 128)],
                buffer.at[:, 0],
                block_sem.at[j],
            )
            for j, (source, buffer, column) in enumerate(places)
        ]

    def heads_region(step, kind, group):
        rows = pl.ds(pl.multiple_of(step // pairs * frames, frames), frames)
        column = (kind * 4 + group) * 384 + step % pairs * 2 * HD
        return heads.at[rows, pl.ds(pl.multiple_of(column, 128), 128)]

    def heads_send(step, which, kind):
        other = neighbours[which]
        return remote(
            heads_buf.at[other[0], 0, :, pl.ds(kind * 128, 128)],
            heads_region(step, kind, seq),
            heads_sem.at[:, step, which, kind],
            other,
        )

    def heads_arrival(step, which, kind):
        region = heads_region(step, kind, neighbours[which][0])
        return remote(region, region, heads_sem.at[:, step, which, kind], neighbours[which])

    def heads_own(step, kind):
        return pltpu.make_async_copy(
            heads_buf.at[seq, 0, :, pl.ds(kind * 128, 128)],
            heads_region(step, kind, seq),
            heads_own_sem.at[step, kind],
        )

    logsum_load = pltpu.make_async_copy(logsum_in, logsum, block_sem.at[4])

    def attention_step(t):
        @pl.when(t == 0)
        def _():
            logsum_load.wait()

        @pl.when(jnp.logical_and(t >= 1, t <= steps))
        def _():
            for kind in range(3):
                heads_own(t - 1, kind).wait()
                for which in range(3):
                    heads_send(t - 1, which, kind).wait_send()

        @pl.when(t < steps)
        def _():
            for copy in block_loads(t):
                copy.wait()
            attention_back_kernel(
                scale,
                q_buf,
                k_buf,
                v_buf,
                context_buf,
                logsum.at[t // pairs, t % pairs],
                heads_buf,
                key_grads,
                value_grads,
            )
            for kind in range(3):
                for which in range(3):
                    heads_send(t, which, kind).start()
                heads_own(t, kind).start()

        @pl.when(t + 1 < steps)
        def _():
            for copy in block_loads(t + 1):
                copy.start()

    def whole(kind):
        return pltpu.make_async_copy(
            projection.at[:, pl.ds(kind * 1536, 1536)], weight_buf, own_sem.at[3]
        )

    operands = [
        pltpu.make_async_copy(hidden_in, hidden, own_sem.at[4]),
        pltpu.make_async_copy(grad_in, grad, own_sem.at[5]),
        pltpu.make_async_copy(gain_in, gain, own_sem.at[6]),
        pltpu.make_async_copy(vector_in, vector.at[0], own_sem.at[7]),
    ]

    def loads(j):
        weight, column = plan[j]
        slot = j % 2
        return [
            pltpu.make_async_copy(lefts[weight], left_buf.at[slot], load_sem.at[0, slot]),
            pltpu.make_async_copy(
                rights[weight].at[:, pl.ds(column, 1536)], right_buf.at[slot], load_sem.at[1, slot]
            ),
        ]

    def start_loads(i):
        for j in range(chunks):

            @pl.when(i == j)
            def _():
                if j >= late:
                    for step in range(steps):
                        for which in range(3):
                            heads_arrival(step, which, j - late).wait_recv()
                for copy in loads(j):
                    copy.start()

    def wait_loads(i):
        for j in range(chunks):

            @pl.when(i == j)
            def _():
                for copy in loads(j):
                    copy.wait()

    def multiply(i, half, target, slot):
        buffer = i % 2
        right = right_buf.at[buffer, :, pl.ds(pl.multiple_of(half * 768, 128), 768)]

        @pl.loop(0, 4)
        def _(zz):
            out = down(left_buf[buffer, :, columns(zz)], right[...]).astype(BF16)
            for q in range(2):
                for yy in range(2):
                    target[slot, q, zz, yy] = out[192 * yy : 192 * yy + 192, 384 * q : 384 * q + 384]

    def multiply_back(i):
        for kind in range(3):

            @pl.when(i == late + kind)
            def _():
                whole(kind).wait()

                @pl.loop(0, right_buf.shape[1] // 128)
                def _(block):
                    rows = pl.ds(pl.multiple_of(block * 128, 128), 128)
                    term = across(right_buf[i % 2, rows, :], weight_buf[...])
                    if kind:
                        normed_grad[rows, :] += term
                    else:
                        normed_grad[rows, :] = term

                if kind < 2:
                    whole(kind + 1).start()

    def norm_back():
        for copy in operands:
            copy.wait()

        def block(index, terms):
            rows = pl.ds(pl.multiple_of(index * 32, 32), 32)
            value = hidden[rows, :].astype(F32)
            center = value - jnp.mean(value, axis=1, keepdims=True)
            inverse = lax.rsqrt(jnp.mean(center * center, axis=1, keepdims=True) + 1e-05)
            normed = center * inverse
            change = normed_grad[rows, :]
            scaled = change * gain[0:1, :]
            first_mean = jnp.mean(scaled, axis=1, keepdims=True)
            second_mean = jnp.mean(scaled * normed, axis=1, keepdims=True)
            grad[rows, :] += inverse * (scaled - first_mean - normed * second_mean)
            gains, biases = terms
            return (
                gains + jnp.sum(change * normed, axis=0, keepdims=True),
                biases + jnp.sum(change, axis=0, keepdims=True),
            )

        zero = jnp.zeros((1, gain.shape[1]), F32)
        gains, biases = lax.fori_loop(0, hidden.shape[0] // 32, block, (zero, zero))
        vector[0, 0:1, :] = gains
        vector[0, 1:2, :] = biases

    def add_to(slot, q, zz, yy, rows, other):
        here = mine[slot, q, zz, yy, rows].astype(F32)
        mine[slot, q, zz, yy, rows] = (here + other.astype(F32)).astype(BF16)

    early_rows = pl.ds(0, EARLY)
    other_rows = pl.ds(EARLY, PIECE[0] - EARLY)

    def c_copy(i):
        return remote(c_out.at[i % 2], c_in.at[i % 2], c_sem.at[:, i % 2], c_device)

    def x_copy(i, count):
        region = pl.ds(0, count)
        return remote(
            mine.at[i % 5, 1 - x, region, :, other_rows],
            x_in.at[i % 4, region],
            x_sem.at[:, i % 4],
            x_device,
        )

    def y_copy(i, count):
        return remote(
            mine.at[i % 5, :, pl.ds(count, 4 - count), 1 - y, other_rows],
            y_in.at[i % 4, :, pl.ds(0, 4 - count)],
            y_sem.at[:, i % 4],
            y_device,
        )

    def second_y_copy(i, count):
        region = pl.ds(0, count)
        return remote(
            mine.at[i % 5, x, region, 1 - y, other_rows],
            second_in.at[i % 5, region],
            second_y_sem.at[:, i % 5],
            y_device,
        )

    def second_x_copy(i, count):
        region = pl.ds(count, 4 - count)
        return remote(
            mine.at[i % 5, 1 - x, region, y, other_rows],
            second_in.at[i % 5, region],
            second_x_sem.at[:, i % 5],
            x_device,
        )

    def z_copy(i, k):
        return remote(
            mine.at[i % 5, x, (z + k) % 4, y, other_rows],
            z_in.at[i % 4, k - 1],
            z_sem.at[:, i % 4, k - 1],
            z_device(k),
        )

    def early_z_copy(i, k):
        return remote(
            mine.at[i % 5, :, (z + k) % 4, :, early_rows],
            early_z_in.at[i % 4, k - 1],
            early_sem.at[:, i % 4, k - 1],
            z_device(k),
        )

    def early_y_copy(i):
        return remote(
            mine.at[i % 5, :, z, 1 - y, early_rows],
            early_y_in.at[i % 4],
            early_sem.at[:, i % 4, 3],
            y_device,
        )

    def early_x_copy(i):
        return remote(
            mine.at[i % 5, 1 - x, z, y, early_rows],
            early_x_in.at[i % 4],
            early_sem.at[:, i % 4, 4],
            x_device,
        )

    def fx_copy(i):
        slot = i % SLOTS
        return remote(total.at[slot], fx_in.at[slot], fx_sem.at[:, slot], x_device)

    def fc_copy(i, which):
        slot = i % SLOTS
        source = fx_in.at[slot] if which else total.at[slot]
        return remote(source, fc_in.at[slot, which], fc_sem.at[:, slot, which], c_device)

    def begin(i):
        wait_loads(i)

        @pl.when(i >= 2)
        def _():
            c_copy(i - 2).wait_send()

        multiply(i, 1 - c, c_out, i % 2)
        c_copy(i).start()
        multiply(i, c, mine, i % 5)
        multiply_back(i)

    def first(i):
        c_copy(i).wait_recv()

        def add_c(q, zz, yy, rows):
            add_to(i % 5, q, zz, yy, rows, c_in[i % 2, q, zz, yy, rows])

        for k in (1, 2, 3):
            for q in range(2):
                for yy in range(2):
                    add_c(q, (z + k) % 4, yy, early_rows)
            early_z_copy(i, k).start()

        def run(i, count):
            @pl.loop(0, count)
            def _(zz):
                for yy in range(2):
                    add_c(1 - x, zz, yy, other_rows)

            x_copy(i, count).start()

            @pl.loop(count, 4)
            def _(zz):
                for q in range(2):
                    add_c(q, zz, 1 - y, other_rows)

            y_copy(i, count).start()

            @pl.loop(0, count)
            def _(zz):
                for yy in range(2):
                    add_c(x, zz, yy, other_rows)

            @pl.loop(count, 4)
            def _(zz):
                for q in range(2):
                    add_c(q, zz, y, other_rows)

        run(i, OVER_X)
        for q in range(2):
            for yy in range(2):
                add_c(q, z, yy, early_rows)

    def second(i):
        own, slot = i % 5, i % 4

        def run(i, count):
            def add_x(yy):
                @pl.loop(0, count)
                def _(zz):
                    add_to(own, x, zz, yy, other_rows, x_in[slot, zz, yy])

            def add_y(q):
                @pl.loop(count, 4)
                def _(zz):
                    add_to(own, q, zz, y, other_rows, y_in[slot, q, zz - count])

            x_copy(i, count).wait()
            add_x(1 - y)
            second_y_copy(i, count).start()
            y_copy(i, count).wait()
            add_y(1 - x)
            second_x_copy(i, count).start()
            add_x(y)
            add_y(x)

        run(i, OVER_X)
        for k in (1, 2, 3):
            early_z_copy(i, k).wait()

        def add_early(q, yy):
            others = [early_z_in[slot, k, q, yy].astype(F32) for k in range(3)]
            add_to(own, q, z, yy, early_rows, others[0] + others[1] + others[2])

        for q in range(2):
            add_early(q, 1 - y)
        early_y_copy(i).start()
        for q in range(2):
            add_early(q, y)

    def third(i):
        own, slot = i % 5, i % 4

        def run(i, count):
            second_y_copy(i, count).wait()
            second_x_copy(i, count).wait()

        run(i, OVER_X)
        for k in (1, 2, 3):
            zz = (z + k) % 4
            add_to(own, x, zz, y, other_rows, second_in[own, zz])
            z_copy(i, k).start()
        early_y_copy(i).wait()
        add_to(own, 1 - x, z, y, early_rows, early_y_in[slot, 1 - x])
        early_x_copy(i).start()
        add_to(own, x, z, y, early_rows, early_y_in[slot, x])

    def fourth(i):
        own, slot = i % 5, i % 4
        result = mine[own, x, z, y, other_rows].astype(F32) + second_in[own, z].astype(F32)
        for k in (1, 2, 3):
            z_copy(i, k).wait()
            result = result + z_in[slot, k - 1].astype(F32)
        total[i % SLOTS, other_rows] = result.astype(BF16)
        early_x_copy(i).wait()
        result = mine[own, x, z, y, early_rows].astype(F32) + early_x_in[slot].astype(F32)
        total[i % SLOTS, early_rows] = result.astype(BF16)
        fx_copy(i).start()
        fc_copy(i, 0).start()

    def fifth(i):
        fx_copy(i).wait()
        fc_copy(i, 1).start()

    def store(j):
        weight, column = plan[j]
        return pltpu.make_async_copy(
            stage.at[j % 2], outputs[weight].at[:, pl.ds(column, 1536)], stage_sem.at[j % 2]
        )

    def sixth(i):
        slot = i % SLOTS
        for j in range(2, chunks):

            @pl.when(i == j)
            def _():
                store(j - 2).wait()

        def put(quarter, value):
            stage[i % 2, :, columns(quarter)] = value

        fc_copy(i, 0).wait()
        fc_copy(i, 1).wait()
        put(2 * c + x, total[slot])
        put(2 * c + 1 - x, fx_in[slot])
        put(2 * (1 - c) + x, fc_in[slot, 0])
        put(2 * (1 - c) + 1 - x, fc_in[slot, 1])
        for j in range(chunks):

            @pl.when(i == j)
            def _():
                store(j).start()

    def vector_copy(leg):
        device = (c_device, x_device, y_device)[leg]
        return remote(vector.at[leg], vector_got.at[leg], vector_sem.at[:, leg], device)

    def vector_z_copy(k):
        return remote(vector_z.at[z], vector_z.at[z], vector_sem.at[:, 2 + k], z_device(k))

    def vector_arrival(k):
        source = (z + 4 - k) % 4
        return remote(vector_z.at[source], vector_z.at[source], vector_sem.at[:, 2 + k], z_device(k))

    hidden_store = pltpu.make_async_copy(grad, hidden_out, own_sem.at[5])

    def vector_step(step):
        @pl.when(step == 0)
        def _():
            norm_back()
            hidden_store.start()
            vector_copy(0).start()

        for leg in range(3):

            @pl.when(step == leg + 1)
            def _():
                vector_copy(leg).wait()
                both = vector[leg] + vector_got[leg]
                if leg < 2:
                    vector[leg + 1] = both
                    vector_copy(leg + 1).start()
                else:
                    vector_z[z] = both
                    for k in (1, 2, 3):
                        vector_z_copy(k).start()

        @pl.when(step == 4)
        def _():
            for k in (1, 2, 3):
                vector_z_copy(k).wait_send()
                vector_arrival(k).wait_recv()
            vector[0] = vector_z[0] + vector_z[1] + vector_z[2] + vector_z[3]
            pltpu.sync_copy(vector.at[0], vector_out)

    start_loads(0)
    for copy in block_loads(0):
        copy.start()
    logsum_load.start()
    whole(0).start()
    for copy in operands:
        copy.start()

    @pl.loop(0, chunks + STAGES - 1)
    def _(t):
        @pl.when(t + 1 < chunks)
        def _():
            start_loads(t + 1)

        for lag, run in ((1, first), (0, begin), (2, second), (3, third), (4, fourth), (5, fifth), (6, sixth)):
            i = t - lag

            @pl.when(jnp.logical_and(i >= 0, i < chunks))
            def _():
                run(i)

            if lag == AFTER_LAG:
                attention_step(t)

        vector_step(t - chunks)

    for j in (chunks - 2, chunks - 1):
        c_copy(j).wait_send()
        store(j).wait()
    hidden_store.wait()


def sum_products(
    lefts, rights, regrouped, context_grad, logsum, projection, hidden, grad, gain, vectors, scale
):
    weights = len(lefts)
    widths = [right.shape[1] for right in rights] + [projection.shape[1]]
    plan = [
        (weight, column)
        for weight, width in enumerate(widths)
        for column in range(0, width, 1536)
    ]
    depth, width = hidden.shape
    out_shapes = [
        jax.ShapeDtypeStruct((left.shape[1] // 8, columns), BF16)
        for left, columns in zip(lefts, widths)
    ]
    out_shapes += [
        jax.ShapeDtypeStruct((depth, widths[-1]), BF16),
        jax.ShapeDtypeStruct(grad.shape, F32),
        jax.ShapeDtypeStruct(vectors.shape, F32),
    ]
    inputs = (
        *lefts,
        *rights,
        regrouped,
        context_grad,
        logsum,
        projection,
        hidden,
        grad,
        gain,
        vectors,
    )
    clips, pairs, *_, length = logsum.shape
    frames = depth // clips
    pair_block = pltpu.VMEM((4, 1, frames, 2 * HD), BF16)
    pair_grads = pltpu.VMEM((length, 2 * HD), F32)
    anywhere = pl.BlockSpec(memory_space=pl.ANY)
    dma = pltpu.SemaphoreType.DMA
    rest = PIECE[0] - EARLY
    block = lambda *lead, rows=PIECE[0]: pltpu.VMEM(lead + (rows, PIECE[1]), BF16)
    results = pl.pallas_call(
        functools.partial(sum_kernel, tuple(plan), weights, scale),
        out_shape=out_shapes,
        in_specs=[anywhere] * len(inputs),
        out_specs=[anywhere] * len(out_shapes),
        scratch_shapes=[
            block(5, 2, 4, 2),
            block(2, 2, 4, 2),
            block(2, 2, 4, 2),
            block(4, OVER_X, 2, rows=rest),
            block(4, 2, 4 - OVER_X, rows=rest),
            block(5, 4, rows=rest),
            block(4, 3, rows=rest),
            block(4, 3, 2, 2, rows=EARLY),
            block(4, 2, rows=EARLY),
            block(4, rows=EARLY),
            block(SLOTS),
            block(SLOTS),
            block(SLOTS, 2),
            pltpu.VMEM((2, 192, 1536), BF16),
            pltpu.VMEM((2, depth, 1536), BF16),
            pltpu.VMEM((2, depth, 1536), BF16),
            pltpu.VMEM((width, 1536), BF16),
            pltpu.VMEM((depth, width), F32),
            pltpu.VMEM((depth, width), BF16),
            pltpu.VMEM((depth, width), F32),
            pltpu.VMEM(gain.shape, F32),
            pair_block,
            pair_block,
            pair_block,
            pair_block,
            pltpu.VMEM(logsum.shape, F32),
            pltpu.VMEM((4, 1, frames, 3 * 2 * HD), BF16),
            pair_grads,
            pair_grads,
            pltpu.VMEM((3,) + vectors.shape, F32),
            pltpu.VMEM((3,) + vectors.shape, F32),
            pltpu.VMEM((4,) + vectors.shape, F32),
            dma((2, 2)),
            dma((2, 4)),
            dma((2, 4)),
            dma((2, 5)),
            dma((2, 5)),
            dma((2, 4, 3)),
            dma((2, 4, 5)),
            dma((2, SLOTS)),
            dma((2, SLOTS, 2)),
            dma((2,)),
            dma((2, 2)),
            dma((2, 6)),
            dma((2, clips * pairs, 3, 3)),
            dma((clips * pairs, 3)),
            dma((5,)),
            dma((8,)),
        ],
        compiler_params=pltpu.CompilerParams(
            collective_id=3, has_side_effects=True, vmem_limit_bytes=60 << 20
        ),
        name="sum_products",
    )(*inputs)
    return results[:weights], results[-2], results[-1]


def on_blocks(
    hidden_states,
    text_states,
    self_gain,
    self_bias,
    query_key_value,
    self_output,
    cross_gain,
    cross_bias,
    cross_query,
    cross_memory,
    cross_output,
    final_gain,
    final_bias,
    expand_weight,
    contract_weight,
    output_cotangent,
):
    clips, frames, width = hidden_states.shape
    rows = clips * frames
    groups = lax.axis_size("seq")
    fsdp_count = lax.axis_size("fsdp")
    scale = HD ** (-0.5)
    entries = rows * groups * fsdp_count * width
    group_width = width // groups

    gains = (self_gain, self_bias, cross_gain, cross_bias, final_gain, final_bias)
    wholes, gains, normed_one, regrouped, logsum, context = forward(
        (
            query_key_value,
            self_output,
            cross_query,
            cross_memory,
            cross_output,
            expand_weight,
            contract_weight,
        ),
        place_vectors(gains),
        hidden_states.reshape(rows, width),
        clips,
        scale,
    )
    (
        qkv_whole,
        self_output_whole,
        cross_query_whole,
        cross_memory_whole,
        cross_output_whole,
        expand_whole,
        contract_whole,
    ) = wholes
    hidden = hidden_states.reshape(rows, width).astype(F32)
    attended = product(context, self_output_whole)
    first = hidden + attended
    normed_two, norm_two_back = jax.vjp(layer_norm, first, gains[2], gains[3])
    normed_two = normed_two.astype(BF16)
    cross_q = product(normed_two, cross_query_whole).astype(BF16)
    text_rows = text_states.reshape(clips * TEXT, width)
    memory = product(text_rows, cross_memory_whole).astype(BF16)
    cross_context = text_attention(clips, scale, cross_q, memory)
    crossed = product(cross_context, cross_output_whole)
    second = first + crossed
    normed_three, norm_three_back = jax.vjp(layer_norm, second, gains[4], gains[5])
    normed_three = normed_three.astype(BF16)
    preact = product(normed_three, expand_whole)
    below = 0.5 + 0.5 * lax.erf(preact * 0.5**0.5)
    density = jnp.exp(preact * preact * -0.5) * (0.5 / jnp.pi) ** 0.5
    activated = (preact * below).astype(BF16)
    slope = (below + preact * density).astype(BF16)
    upstream = output_cotangent.reshape(rows, width).astype(F32)
    grad_mixed = output_cotangent.reshape(rows, width)
    contract_term = product_left(activated, grad_mixed).astype(BF16)
    grad_mixed, contract_term, contract_whole = lax.optimization_barrier(
        (grad_mixed, contract_term, contract_whole)
    )
    contract_part = lax.psum_scatter(
        contract_term, ("fsdp", "seq"), scatter_dimension=0, tiled=True
    )
    grad_activated = product_right(grad_mixed, contract_whole)
    grad_preact = (grad_activated * slope.astype(F32)).astype(BF16)
    grad_normed_three = product_right(grad_preact, expand_whole)
    grad_second, final_gain_term, final_bias_term = norm_three_back(grad_normed_three)
    grad_second = upstream + grad_second
    grad_crossed = grad_second.astype(BF16)
    grad_cross_context = product_right(grad_crossed, cross_output_whole).astype(BF16)
    grad_cross_q, grad_memory = text_attention(clips, scale, cross_q, memory, grad_cross_context)
    grad_normed_two = product_right(grad_cross_q, cross_query_whole)
    grad_first, cross_gain_term, cross_bias_term = norm_two_back(grad_normed_two)
    grad_first = grad_second + grad_first
    grad_attended = grad_first.astype(BF16)
    grad_context = product_right(grad_attended, self_output_whole).astype(BF16)
    grad_context = grad_context.reshape(rows, groups, group_width).transpose(1, 0, 2)
    grad_context, activated = lax.optimization_barrier((grad_context, activated))
    grad_heads = lax.all_to_all(grad_context, "seq", split_axis=0, concat_axis=0, tiled=True)
    mixed = product(activated, contract_whole)
    output = second + mixed
    squares = jnp.stack(
        [
            jnp.sum(output * output),
            jnp.sum(attended * attended),
            jnp.sum(crossed * crossed),
            jnp.sum(mixed * mixed),
        ]
    )
    output = output.astype(BF16)
    zeros = jnp.zeros_like(cross_gain_term)
    terms = jnp.stack(
        [
            zeros,
            zeros,
            cross_gain_term,
            cross_bias_term,
            final_gain_term,
            final_bias_term,
            jnp.pad(squares, (0, width - 4)),
            zeros,
        ]
    )
    deep = lambda value: jnp.pad(value, ((0, rows - value.shape[0]), (0, 0)))
    text_operands = (deep(text_rows), deep(grad_memory))
    grad_heads, output, terms, text_operands = lax.optimization_barrier(
        (grad_heads, output, terms, text_operands)
    )
    gradients, grad_hidden, totals = sum_products(
        [normed_three, cross_context, normed_two, text_operands[0], context, normed_one],
        [grad_preact, grad_crossed, grad_cross_q, text_operands[1], grad_attended],
        regrouped,
        grad_heads,
        logsum,
        qkv_whole,
        hidden_states.reshape(rows, width),
        grad_first,
        jnp.broadcast_to(gains[0], (8, width)),
        terms,
        scale,
    )
    gradients, contract_part = lax.optimization_barrier((gradients, contract_part))
    contract_gradient = lax.all_gather(contract_part, "seq", axis=0, tiled=True)
    gradients = [gradient.astype(F32) for gradient in gradients]
    contract_gradient = contract_gradient.astype(F32)
    layer_rms = jnp.sqrt(totals[6, :4] / entries)
    shard = width // fsdp_count
    vector_gradients = lax.dynamic_slice_in_dim(
        totals, lax.axis_index("fsdp") * shard, shard, 1
    )
    return (
        output.reshape(clips, frames, width),
        grad_hidden.reshape(clips, frames, width),
        vector_gradients[0],
        vector_gradients[1],
        gradients[5],
        gradients[4],
        vector_gradients[2],
        vector_gradients[3],
        gradients[2],
        gradients[3],
        gradients[1],
        vector_gradients[4],
        vector_gradients[5],
        gradients[0],
        contract_gradient,
        layer_rms,
    )


def solution(mesh):
    shape = dict(mesh.shape)
    blocks = shape["seq"] == 4 and shape["fsdp"] == 8
    return jax.shard_map(
        on_blocks if blocks else on_any_mesh,
        mesh=mesh,
        in_specs=(
            P("fsdp", "seq", None),
            P("fsdp", None, None),
            P("fsdp"),
            P("fsdp"),
            P("fsdp", None),
            P("fsdp", None),
            P("fsdp"),
            P("fsdp"),
            P("fsdp", None),
            P("fsdp", None),
            P("fsdp", None),
            P("fsdp"),
            P("fsdp"),
            P("fsdp", None),
            P("fsdp", None),
            P("fsdp", "seq", None),
        ),
        out_specs=(
            P("fsdp", "seq", None),
            P("fsdp", "seq", None),
            P("fsdp"),
            P("fsdp"),
            P("fsdp", None),
            P("fsdp", None),
            P("fsdp"),
            P("fsdp"),
            P("fsdp", None),
            P("fsdp", None),
            P("fsdp", None),
            P("fsdp"),
            P("fsdp"),
            P("fsdp", None),
            P("fsdp", None),
            P(),
        ),
        check_vma=False,
    )
```
